32 devices in a mesh: space: 16 (over z, x, core), bead: 2 (over y).
Axes of the slice: x: 2, y: 2, z: 4, core: 2. Of those that a mesh axis runs over, the one named last changes fastest.
Arguments:
- positions: float32 [32, 3, 65536], P('bead', None, 'space'), may hold values from -5 to 5
- momenta: float32 [32, 3, 65536], P('bead', None, 'space'), may hold values from -12 to 12
- masses: float32 [65536], P('space'), may hold values from 1 to 16
- strengths: float32 [65536], P('space'), may hold values from 0.5 to 2
- bond_ends: int32 [2, 65536], P(None, 'space'), may hold values from 0 to 127
- angle_ends: int32 [3, 32768], P(None, 'space'), may hold values from 0 to 127
- neighbour_tiles: int32 [3, 512], P(None, 'space'), may hold values from 0 to 511, as said below
Outputs:
- new_positions: float32 [32, 3, 65536], P('bead', None, 'space')
- new_momenta: float32 [32, 3, 65536], P('bead', None, 'space')
The draws below stay inside these ranges and needn't reach their ends.
Inputs may be any that keep to these rules, and one draw needn't show every extreme that they name: `bond_ends`: entry [e, b] is the place within tile b // 128 of end e of bond b. `angle_ends`: entry [e, b] is the place within tile b // 64 of atom e of angle b. `neighbour_tiles`: column t names 3 different tiles, each within 2 tiles of t, counting around the ends (tile 512 - 1 lies next to tile 0).
All inputs are finite; a program needn't handle non-finite values.
Results may differ from the reference program's by a relative error of at most 0.0003.
Values sent between devices are 32-bit elements; how exact they have to be, the bound alone decides.
No kernel may reach another device: no remote copies, remote signals or barrier semaphores. Data moves between devices by JAX's collectives and lax.ppermute only.
A program may use at most 64 MiB of HBM per device.

```python
import math
import jax
import jax.numpy as jnp
import numpy as np
from jax import lax

BEADS = 32
KEPT = 4
SUBS = 3
TILE = 128
GT = 2
NBR = 3
BPT = 128
APT = 64
NA = 65536
NT_ALL = 512
NBONDS = 65536
NANGLES = 32768


spring_freq = 80.0


def bead_modes(number):
    within = np.arange(number)
    result = np.zeros((number, number))
    for column in range(number):
        if column == 0:
            result[:, column] = 1.0 / math.sqrt(number)
        elif 2 * column < number:
            result[:, column] = math.sqrt(2.0 / number) * np.cos(2 * np.pi * within * column / number)
        elif 2 * column == number:
            result[:, column] = (-1.0) ** within / math.sqrt(number)
        else:
            result[:, column] = math.sqrt(2.0 / number) * np.sin(2 * np.pi * within * column / number)
    return result


def draw_positions(key, part):
    table = jnp.asarray(bead_modes(BEADS), jnp.float32)
    freqs = 2.0 * spring_freq * np.sin(np.pi * np.arange(BEADS) / BEADS)
    safe = np.where(freqs > 0, freqs, 1.0)
    amps = jnp.asarray(np.where(freqs > 0, 1.0 / safe, 0.0), jnp.float32)
    centre_key = jax.random.fold_in(key, 11)
    mode_key = jax.random.fold_in(key, 23)
    centre = jax.random.truncated_normal(centre_key, -4.0, 4.0, (1, 3, NA), jnp.float32)
    modes = jax.random.uniform(mode_key, (BEADS, 3, NA), jnp.float32, -1.0, 1.0) * amps[:, None, None]
    spread = jnp.einsum('jk,kcl->jcl', table, modes, precision=lax.Precision.HIGHEST)
    return (centre + spread).astype(jnp.float32)


def draw_neighbour_tiles(key, part):
    width = 2 * GT + 1
    scores = jax.random.randint(key, (NT_ALL, width), 0, 2 ** 20) * width + jnp.arange(width, dtype=jnp.int32)[None, :]
    ranking = jnp.argsort(scores, axis=1, stable=True)[:, :NBR].astype(jnp.int32) - GT
    chosen = jnp.arange(NT_ALL, dtype=jnp.int32)[:, None] + ranking
    return jnp.mod(chosen, NT_ALL).T.astype(jnp.int32)


def place_ends(array, key, low, largest):
    place = [jax.random.randint(jax.random.fold_in(key, axis), (), 0, length) for axis, length in enumerate(array.shape)]
    longest = array.shape.index(max(array.shape))
    beside = place[:longest] + [(place[longest] + 1) % array.shape[longest]] + place[longest + 1:]
    return array.at[tuple(place)].set(low).at[tuple(beside)].set(largest)


def levels(stream_key, extent, pieces, least, high):
    def one(dim, blocks):
        heights = jax.random.uniform(jax.random.fold_in(jax.random.fold_in(stream_key, 6), dim), (blocks,), jnp.float32, least / len(pieces), high / len(pieces))
        return jnp.repeat(jnp.exp(heights), extent[dim] // blocks).reshape((-1,) + (1,) * (len(extent) - dim - 1))

    level = one(*pieces[0])
    for cut in pieces[1:]:
        level = level * one(*cut)
    return level


def noise(rng, extent, scale, limit, cuts=(), kind=jnp.bfloat16):
    entries = jax.random.normal(rng, extent, jnp.float32) * scale
    if len(cuts) > 0:
        entries = levels(rng, extent, cuts, -0.22, 0.18) * entries
    return jnp.clip(entries, min=-limit, max=limit).astype(kind)


def setup_inputs(seed: int = 0) -> dict:
    streams_of = jax.random.split(jax.random.key(seed), 8)
    return {
        "positions": draw_positions(jax.random.fold_in(streams_of[7], 71), 0),
        "momenta": noise(streams_of[1], (BEADS, 3, NA), 2.0, 12.0, ((0, 2), (2, 16)), jnp.float32),
        "masses": jnp.clip(jnp.exp(math.log(16.0) - 2.7725887 * jax.random.uniform(streams_of[2], (NA,), jnp.float32) ** levels(streams_of[2], (NA,), ((0, 16),), -0.2, 0.2)), 1.0, 16.0),
        "strengths": jnp.clip(jnp.exp(math.log(2.0) - 1.3862944 * jax.random.uniform(streams_of[3], (NA,), jnp.float32) ** levels(streams_of[3], (NA,), ((0, 16),), -0.2, 0.2)), 0.5, 2.0),
        "bond_ends": place_ends(jax.random.randint(streams_of[4], (2, NBONDS), 0, TILE), jax.random.fold_in(streams_of[4], 1), 0, TILE - 1).astype(jnp.int32),
        "angle_ends": place_ends(jax.random.randint(streams_of[5], (3, NANGLES), 0, TILE), jax.random.fold_in(streams_of[5], 1), 0, TILE - 1).astype(jnp.int32),
        "neighbour_tiles": draw_neighbour_tiles(jax.random.fold_in(streams_of[7], 71), 0),
    }


time_step = 0.3
spring_freq = 80.0
bond_stiff = 0.2
bond_rest = 1.0
angle_stiff = 0.1
angle_rest = 0.5
range_sq = 4.0
HIGH = lax.Precision.HIGHEST

def mode_table(number):
    within = np.arange(number)
    result = np.zeros((number, number))
    for column in range(number):
        if column == 0:
            result[:, column] = 1.0 / math.sqrt(number)
        elif 2 * column < number:
            result[:, column] = math.sqrt(2.0 / number) * np.cos(2 * np.pi * within * column / number)
        elif 2 * column == number:
            result[:, column] = (-1.0) ** within / math.sqrt(number)
        else:
            result[:, column] = math.sqrt(2.0 / number) * np.sin(2 * np.pi * within * column / number)
    return result

def contract_table(number, kept):
    larger = mode_table(number)
    smaller = mode_table(kept)
    chosen = [column if 2 * column <= kept else number - kept + column for column in range(kept)]
    return math.sqrt(kept / number) * smaller @ larger[:, chosen].T

def orbit_tables(number, interval):
    freqs = 2.0 * spring_freq * np.sin(np.pi * np.arange(number) / number)
    cosine = np.cos(freqs * interval)
    safe = np.where(freqs > 0, freqs, 1.0)
    gains = np.where(freqs > 0, np.sin(freqs * interval) / safe, interval)
    drags = freqs * np.sin(freqs * interval)
    return (cosine, gains, drags)

def propagate(current, moment, masses, modes_table, cosine, gains, drags):
    modes_pos = jnp.einsum('jk,jcl->kcl', modes_table, current, precision=HIGH)
    modes_mom = jnp.einsum('jk,jcl->kcl', modes_table, moment, precision=HIGH)
    moved_pos = cosine[:, None, None] * modes_pos + gains[:, None, None] * modes_mom / masses
    moved_mom = cosine[:, None, None] * modes_mom - drags[:, None, None] * masses * modes_pos
    return (jnp.einsum('jk,kcl->jcl', modes_table, moved_pos, precision=HIGH), jnp.einsum('jk,kcl->jcl', modes_table, moved_mom, precision=HIGH))

def pair_block(own_tiles, nearby, own_scale, nearby_scale):
    own_sq = lax.optimization_barrier(jnp.sum(own_tiles * own_tiles, axis=1))
    nearby_sq = lax.optimization_barrier(jnp.sum(nearby * nearby, axis=1))
    inner = jnp.einsum('cxta,cxtn->ctan', own_tiles, nearby, precision=HIGH)
    distance = own_sq[..., None] + nearby_sq[:, :, None, :] - 2.0 * inner
    weight = jnp.exp(-distance / range_sq) * nearby_scale[None, :, None, :]
    weight_sum = lax.optimization_barrier(jnp.sum(weight, axis=3))
    pulled = jnp.einsum('ctan,cxtn->cxta', weight, nearby, precision=HIGH)
    return 2.0 / range_sq * own_scale[None, None] * (own_tiles * weight_sum[:, None] - pulled)

def tile_forces(extended, scale_ext, own_first, tile_count, local_nbr):
    kept = extended.shape[0]
    tiled = extended.reshape(kept, 3, -1, TILE)
    scale_tiles = scale_ext.reshape(-1, TILE)
    group_size = math.gcd(tile_count, 8)
    rounds = tile_count // group_size
    width = local_nbr.shape[1]

    def one_group(offset):
        own_tiles = lax.dynamic_slice_in_dim(tiled, own_first + offset, group_size, 2)
        own_scale = lax.dynamic_slice_in_dim(scale_tiles, own_first + offset, group_size, 0)
        chosen = lax.dynamic_slice_in_dim(local_nbr, offset, group_size, 0).reshape(-1)
        nearby = jnp.take(tiled, chosen, axis=2).reshape(kept, 3, group_size, width * TILE)
        nearby_scale = jnp.take(scale_tiles, chosen, axis=0).reshape(group_size, width * TILE)
        return pair_block(own_tiles, nearby, own_scale, nearby_scale)
    offsets = jnp.arange(rounds, dtype=jnp.int32) * group_size
    result = lax.map(one_group, offsets)
    return jnp.moveaxis(result, 0, 2).reshape(kept, 3, tile_count * TILE)

def bonded(current, bond_ends, angle_ends):
    bond_base = jnp.arange(bond_ends.shape[1], dtype=jnp.int32) // BPT * TILE
    one_end = bond_base + bond_ends[0]
    other_end = bond_base + bond_ends[1]
    stretch = current[:, :, one_end] - current[:, :, other_end]
    factor = bond_stiff * (lax.optimization_barrier(jnp.sum(stretch * stretch, axis=1, keepdims=True)) - bond_rest)
    push = -factor * stretch
    forces = jnp.zeros_like(current).at[:, :, one_end].add(push).at[:, :, other_end].add(-push)
    angle_base = jnp.arange(angle_ends.shape[1], dtype=jnp.int32) // APT * TILE
    outer_one = angle_base + angle_ends[0]
    centre = angle_base + angle_ends[1]
    outer_two = angle_base + angle_ends[2]
    to_first = current[:, :, outer_one] - current[:, :, centre]
    to_last = current[:, :, outer_two] - current[:, :, centre]
    factor = angle_stiff * (lax.optimization_barrier(jnp.sum(to_first * to_last, axis=1, keepdims=True)) - angle_rest)
    forces = forces.at[:, :, outer_one].add(-factor * to_last)
    forces = forces.at[:, :, outer_two].add(-factor * to_first)
    forces = forces.at[:, :, centre].add(factor * (to_first + to_last))
    return forces

def reference(positions, momenta, masses, strengths, bond_ends, angle_ends, neighbour_tiles):
    interval = time_step / SUBS
    modes_table = jnp.asarray(mode_table(BEADS), jnp.float32)
    contract = jnp.asarray(contract_table(BEADS, KEPT), jnp.float32)
    expand = BEADS / KEPT * contract.T
    cos_np, gain_np, drag_np = orbit_tables(BEADS, interval)
    cosine = jnp.asarray(cos_np, jnp.float32)
    gains = jnp.asarray(gain_np, jnp.float32)
    drags = jnp.asarray(drag_np, jnp.float32)

    def nonbonded(current):
        contracted = jnp.einsum('kj,jcl->kcl', contract, current, precision=HIGH)
        nearby = tile_forces(contracted, strengths, 0, NT_ALL, neighbour_tiles.T.astype(jnp.int32))
        return jnp.einsum('jk,kcl->jcl', expand, nearby, precision=HIGH)
    current = positions
    moment = momenta + 0.5 * time_step * nonbonded(current)
    pushed = bonded(current, bond_ends, angle_ends)
    for substep in range(SUBS):
        moment = moment + 0.5 * interval * pushed
        current, moment = propagate(current, moment, masses, modes_table, cosine, gains, drags)
        pushed = bonded(current, bond_ends, angle_ends)
        moment = moment + 0.5 * interval * pushed
    moment = moment + 0.5 * time_step * nonbonded(current)
    return (current, moment)
```

```python
import functools
import math

import jax
import jax.numpy as jnp
import numpy as np
from jax import lax
from jax.experimental import pallas as pl
from jax.experimental.pallas import tpu as pltpu
from jax.sharding import PartitionSpec as P

BEADS = 32
KEPT = 4
SUBS = 3
TILE = 128
GT = 2
BPT = 128
APT = 64
ROWS = 4 * KEPT

time_step = 0.3
spring_freq = 80.0
bond_stiff = 0.2
bond_rest = 1.0
angle_stiff = 0.1
angle_rest = 0.5
range_sq = 4.0
HIGH = lax.Precision.HIGHEST
F32 = jnp.float32
BF16 = jnp.bfloat16


def mode_table(number):
    within = np.arange(number)
    result = np.zeros((number, number))
    for column in range(number):
        if column == 0:
            result[:, column] = 1.0 / math.sqrt(number)
        elif 2 * column < number:
            result[:, column] = math.sqrt(2.0 / number) * np.cos(
                2 * np.pi * within * column / number
            )
        elif 2 * column == number:
            result[:, column] = (-1.0) ** within / math.sqrt(number)
        else:
            result[:, column] = math.sqrt(2.0 / number) * np.sin(
                2 * np.pi * within * column / number
            )
    return result


def contract_table(number, kept):
    larger = mode_table(number)
    smaller = mode_table(kept)
    chosen = [column if 2 * column <= kept else number - kept + column for column in range(kept)]
    return math.sqrt(kept / number) * smaller @ larger[:, chosen].T


def motion_table(number, interval):
    freqs = 2.0 * spring_freq * np.sin(np.pi * np.arange(number) / number)
    modes = mode_table(number)
    safe = np.where(freqs > 0, freqs, 1.0)
    gains = np.where(freqs > 0, np.sin(freqs * interval) / safe, interval)
    drags = freqs * np.sin(freqs * interval)
    stay = modes @ np.diag(np.cos(freqs * interval)) @ modes.T
    gain = modes @ np.diag(gains) @ modes.T
    drag = modes @ np.diag(drags) @ modes.T
    return np.block([[stay, gain], [-drag, stay]])


def np_split(table, parts):
    out, rest = [], np.asarray(table, np.float64)
    for _ in range(parts):
        piece = rest.astype(np.float32).astype(jnp.bfloat16)
        out.append(piece)
        rest = rest - piece.astype(np.float64)
    return out


def stacked_left(table, parts=3):
    pieces = np_split(table, parts)
    zero = np.zeros_like(pieces[0])
    return np.concatenate(
        [
            np.concatenate([pieces[i]] * (parts - i) + [zero] * i, axis=1)
            for i in range(parts)
        ],
        axis=0,
    )


def split(x, parts):
    out = []
    for i in range(parts):
        piece = x.astype(BF16)
        out.append(piece)
        if i < parts - 1:
            x = x - piece.astype(F32)
    return out


def mm(left, right):
    return jnp.dot(left, right, preferred_element_type=F32)


def exact(left, x, parts=3):
    out = mm(left, jnp.concatenate(split(x, parts), axis=0))
    rows = out.shape[0] // parts
    total = out[:rows]
    for i in range(1, parts):
        total = total + out[i * rows : (i + 1) * rows]
    return total


def contract_rows(beads):
    table = contract_table(BEADS, KEPT)
    tables = []
    for turn in range(0, BEADS, beads):
        order = (np.arange(BEADS) + turn) % BEADS
        tables.append(table[:, order])
    return tables


def contract_left(table):
    out = np.zeros((ROWS, 3 * table.shape[1]))
    for c in range(KEPT):
        for k in range(3):
            out[4 * c + 1 + k, k * table.shape[1] : (k + 1) * table.shape[1]] = table[c]
    return out


def expand_left(table):
    return BEADS / KEPT * contract_left(table).T


def partial_kernel(left, pos, logs, out):
    comps, beads, lanes = pos.shape
    width = min(lanes, 512)
    row = lax.broadcasted_iota(jnp.int32, (ROWS, width), 0)
    for at in range(0, lanes, width):
        x = jnp.concatenate([pos[c, :, at : at + width] for c in range(comps)], axis=0)
        c16 = exact(left[...], x)
        out[:, at : at + width] = jnp.where(row == 0, logs[:, at : at + width], c16)


def partial_contract(left, pos, logs):
    lanes = pos.shape[2]
    return pl.pallas_call(
        partial_kernel,
        out_shape=jax.ShapeDtypeStruct((ROWS, lanes), F32),
        cost_estimate=pl.CostEstimate(
            flops=2 * 48 * 144 * lanes, bytes_accessed=4 * pos.size, transcendentals=0
        ),
        name="partial_contract",
    )(left, pos, logs)


def pair_kernel(seg_sizes, own_count, *refs):
    own_pos, nbr_pos = refs[:2]
    total = sum(n for _, n in seg_sizes)
    count = sum(n for n, _ in seg_sizes)
    seg_refs = refs[2 : 2 + count]
    out, feat_i, feat_m, feat_p, base = refs[2 + count :]
    row = lax.broadcasted_iota(jnp.int32, (ROWS, TILE), 0)
    slot = row % 4
    scale = math.sqrt(2.0 * math.log2(math.e) / range_sq)
    same = (
        lax.broadcasted_iota(jnp.int32, (ROWS, ROWS), 0) // 4
        == lax.broadcasted_iota(jnp.int32, (ROWS, ROWS), 1) // 4
    ).astype(F32)

    def features(tile, c16):
        base[tile] = c16
        logs = c16[0:1]
        place = jnp.where(slot == 0, 0.0, c16)
        scaled = place * scale
        high, low = [piece.astype(F32) for piece in split(scaled, 2)]
        square = jnp.dot(same, scaled * scaled, precision=HIGH, preferred_element_type=F32)
        half = -0.5 * square

        def three(x):
            a, b, c = [piece.astype(F32) for piece in split(x, 3)]
            return jnp.where(slot == 0, a, jnp.where(slot == 1, b, jnp.where(slot == 2, c, 0.0)))

        ones = jnp.where(slot == 3, 0.0, 1.0)
        mine = jnp.concatenate([high, high, low, low, three(half), ones], axis=0)
        theirs = jnp.concatenate(
            [high, low, high, low, ones, three(half + logs), ones, ones], axis=0
        )
        feat_i[tile] = mine.astype(BF16)
        feat_m[tile] = jnp.transpose(theirs, (1, 0)).astype(BF16)
        one = jnp.ones((ROWS, TILE), F32)
        p_high, p_low = [piece.astype(F32) for piece in split(place, 2)]
        feat_p[tile] = jnp.concatenate([one, p_high, p_low], axis=0).astype(BF16)

    tile = 0
    at = 0
    for number, tiles in seg_sizes:
        group = seg_refs[at : at + number]
        at += number
        for i in range(tiles):
            c16 = group[0][:, i * TILE : (i + 1) * TILE]
            for other in group[1:]:
                more = other[:, i * TILE : (i + 1) * TILE]
                c16 = c16 + jnp.where(row == 0, 0.0, more)
            features(tile, c16)
            tile += 1
    assert tile == total

    groups = 6
    wide_row = lax.broadcasted_iota(jnp.int32, (groups * ROWS, TILE), 0)
    pick = [((wide_row % ROWS) // 4 == c).astype(BF16) for c in range(KEPT)]
    owner = row // 4

    def one_tile(t, carry):
        mine = own_pos[t]
        features_i = feat_i[mine]
        right = jnp.concatenate([features_i * pick[c] for c in range(KEPT)], axis=1)
        right = jnp.concatenate([right, jnp.zeros((2 * ROWS, KEPT * TILE), BF16)], axis=0)
        total_p = None
        for u in range(3):
            near = nbr_pos[3 * t + u]
            power = mm(feat_m[near], right)
            weight = jnp.exp2(power)
            w_high, w_low = split(weight, 2)
            left = feat_p[near]
            pulled = mm(
                jnp.concatenate([left, left], axis=1), jnp.concatenate([w_high, w_low], axis=0)
            )
            total_p = pulled if total_p is None else total_p + pulled
        sums = total_p[:ROWS]
        pulls = total_p[ROWS : 2 * ROWS] + total_p[2 * ROWS :]
        c16 = base[mine]
        factor = (2.0 / range_sq) * jnp.exp2(c16[0:1])
        result = jnp.zeros((ROWS, TILE), F32)
        for c in range(KEPT):
            lanes = slice(c * TILE, (c + 1) * TILE)
            force = factor * (c16 * sums[:, lanes] - pulls[:, lanes])
            result = jnp.where((owner == c) & (slot > 0), force, result)
        out[:, pl.ds(pl.multiple_of(t * TILE, TILE), TILE)] = result
        return carry

    lax.fori_loop(0, own_count, one_tile, 0)


def pair_forces(segments, own_pos, nbr_pos):
    sizes = tuple((len(group), group[0].shape[1] // TILE) for group in segments)
    total = sum(n for _, n in sizes)
    own_count = own_pos.shape[0]
    flat = [array for group in segments for array in group]
    grid_spec = pltpu.PrefetchScalarGridSpec(
        num_scalar_prefetch=2,
        grid=(1,),
        in_specs=[pl.BlockSpec(a.shape, lambda i, *_: (0, 0)) for a in flat],
        out_specs=pl.BlockSpec((ROWS, own_count * TILE), lambda i, *_: (0, 0)),
        scratch_shapes=[
            pltpu.VMEM((total, 6 * ROWS, TILE), BF16),
            pltpu.VMEM((total, TILE, 8 * ROWS), BF16),
            pltpu.VMEM((total, 3 * ROWS, TILE), BF16),
            pltpu.VMEM((total, ROWS, TILE), F32),
        ],
    )
    return pl.pallas_call(
        functools.partial(pair_kernel, sizes, own_count),
        grid_spec=grid_spec,
        out_shape=jax.ShapeDtypeStruct((ROWS, own_count * TILE), F32),
        cost_estimate=pl.CostEstimate(
            flops=own_count * 3 * 2 * TILE * 4 * TILE * 400,
            bytes_accessed=4 * ROWS * TILE * (total + own_count),
            transcendentals=own_count * 3 * TILE * 4 * TILE,
        ),
        name="pair_forces",
    )(own_pos, nbr_pos, *flat)


def step_kernel(parts, group, *refs):
    at = 1
    pos, mom = refs[at : at + 2]
    at += 2
    received = refs[at : at + parts - 1]
    at += parts - 1
    force, mass, ends, hot, motion, expand, contract, logs = refs[at : at + 8]
    at += 8
    outs = refs[at : at + parts]
    c_out = refs[at + parts]
    interval = time_step / SUBS
    width = group * TILE
    motion_l = motion[...]
    masses = mass[...]
    inverse = 1.0 / masses

    def gathered(ref_index, own):
        pieces = [own] + [r[ref_index] for r in received]
        return pieces[0] if parts == 1 else jnp.concatenate(pieces, axis=0)

    q = [gathered(c, pos[c]) for c in range(3)]
    p = [gathered(3 + c, mom[c]) for c in range(3)]
    kick = exact(expand[...], force[...])
    v = [
        (p[c] + 0.5 * time_step * kick[c * BEADS : (c + 1) * BEADS]) * inverse for c in range(3)
    ]
    places = []
    for t in range(group):
        places.append([jnp.broadcast_to(ends[t, e : e + 1], (3 * BEADS, TILE)) for e in range(4)])

    def take(x, index):
        return jnp.take_along_axis(x, index, axis=1, mode="promise_in_bounds")

    def bonded(q):
        forces = []
        for t in range(group):
            lanes = slice(t * TILE, (t + 1) * TILE)
            rows = jnp.concatenate([q[c][:, lanes] for c in range(3)], axis=0)
            one, other, outer, centre = places[t]
            stretch = take(rows, one) - take(rows, other)
            arms = take(rows, outer) - take(rows, centre)
            s = [stretch[c * BEADS : (c + 1) * BEADS] for c in range(3)]
            a = [arms[c * BEADS : (c + 1) * BEADS] for c in range(3)]
            length = s[0] * s[0] + s[1] * s[1] + s[2] * s[2]
            g = bond_stiff * (length - bond_rest)
            turned = [pltpu.roll(x, APT, 1) for x in a]
            inner = a[0] * turned[0] + a[1] * turned[1] + a[2] * turned[2]
            h = angle_stiff * (inner - angle_rest)
            bonds = jnp.concatenate([g * x for x in s], axis=0)
            angles = jnp.concatenate([h * x for x in a], axis=0)
            both = jnp.concatenate([bonds, angles], axis=1)
            out = mm(jnp.concatenate(split(both, 2), axis=0), hot[t])
            forces.append(out[: 3 * BEADS] + out[3 * BEADS :])
        return [
            jnp.concatenate([f[c * BEADS : (c + 1) * BEADS] for f in forces], axis=1)
            for c in range(3)
        ]

    for sub in range(SUBS):
        pushed = bonded(q)
        factor = (0.5 if sub == 0 else 1.0) * interval * inverse
        v = [v[c] + factor * pushed[c] for c in range(3)]
        for c in range(3):
            moved = exact(motion_l, jnp.concatenate([q[c], v[c]], axis=0))
            q[c], v[c] = moved[:BEADS], moved[BEADS:]
    pushed = bonded(q)
    p = [masses * v[c] + (0.5 * interval) * pushed[c] for c in range(3)]
    beads = BEADS // parts
    for i in range(parts):
        for c in range(3):
            outs[i][c] = q[c][i * beads : (i + 1) * beads]
            outs[i][3 + c] = p[c][i * beads : (i + 1) * beads]
    rows = jnp.concatenate(q, axis=0)
    c16 = exact(contract[...], rows, 2)
    row = lax.broadcasted_iota(jnp.int32, (ROWS, width), 0)
    c_out[...] = jnp.where(row == 0, logs[...], c16)


def substeps(chunk, chunks, bead_index, pos, mom, received, force, mass, ends, hot, motion, expand, contract, logs):
    if received:
        parts, lanes = 1 + len(received), received[0].shape[2]
    else:
        parts, lanes = 1, pos.shape[2]
    tiles = lanes // TILE
    group = math.gcd(tiles, 2)
    width = group * TILE
    steps = tiles // group
    beads = BEADS // parts
    per_block = chunks * steps

    def own(i, b):
        return (0, 0, (b[0] * per_block + chunk * steps + i) if received else i)

    def block(i, b):
        return (0, chunk * steps + i)

    grid_spec = pltpu.PrefetchScalarGridSpec(
        num_scalar_prefetch=1,
        grid=(steps,),
        in_specs=[pl.BlockSpec((3, beads, width), own)] * 2
        + [pl.BlockSpec((6, beads, width), lambda i, b: (0, 0, i))] * (parts - 1)
        + [
            pl.BlockSpec((ROWS, width), block),
            pl.BlockSpec((1, width), block),
            pl.BlockSpec((group, 4, TILE), lambda i, b: (chunk * steps + i, 0, 0)),
            pl.BlockSpec((group, 2 * TILE, TILE), lambda i, b: (chunk * steps + i, 0, 0)),
            pl.BlockSpec(motion.shape, lambda i, b: (0, 0)),
            pl.BlockSpec(expand.shape, lambda i, b: (0, 0)),
            pl.BlockSpec(contract.shape, lambda i, b: (0, 0)),
            pl.BlockSpec((1, width), block),
        ],
        out_specs=[pl.BlockSpec((6, beads, width), lambda i, b: (0, 0, i))] * parts
        + [pl.BlockSpec((ROWS, width), lambda i, b: (0, i))],
    )
    return pl.pallas_call(
        functools.partial(step_kernel, parts, group),
        grid_spec=grid_spec,
        out_shape=[jax.ShapeDtypeStruct((6, beads, lanes), F32)] * parts
        + [jax.ShapeDtypeStruct((ROWS, lanes), F32)],
        cost_estimate=pl.CostEstimate(
            flops=tiles * 4 * 40_000_000, bytes_accessed=4 * 12 * BEADS * lanes, transcendentals=0
        ),
        name="substeps",
    )(bead_index, pos, mom, *received, force, mass, ends, hot, motion, expand, contract, logs)


def finish_kernel(sizes, offsets, expand, force, *refs):
    count = len(sizes)
    parts = refs[:count]
    pos, mom = refs[count:]
    beads = pos.shape[1]
    for i, lanes in enumerate(sizes):
        start = pl.multiple_of(offsets[i], TILE)
        where = pl.ds(start, lanes)
        kick = exact(expand[...], force[:, where])
        for c in range(3):
            pos[c, :, where] = parts[i][c]
            mom[c, :, where] = (
                parts[i][3 + c] + 0.5 * time_step * kick[c * beads : (c + 1) * beads]
            )


def finish(parts, offsets, expand, force, beads):
    slab = force.shape[1]
    shape = (3, beads, slab)
    grid_spec = pltpu.PrefetchScalarGridSpec(
        num_scalar_prefetch=1,
        grid=(1,),
        in_specs=[
            pl.BlockSpec(expand.shape, lambda i, o: (0, 0)),
            pl.BlockSpec(force.shape, lambda i, o: (0, 0)),
        ]
        + [pl.BlockSpec(a.shape, lambda i, o: (0, 0, 0)) for a in parts],
        out_specs=[pl.BlockSpec(shape, lambda i, o: (0, 0, 0))] * 2,
    )
    return pl.pallas_call(
        functools.partial(finish_kernel, tuple(a.shape[2] for a in parts)),
        grid_spec=grid_spec,
        out_shape=[jax.ShapeDtypeStruct(shape, F32)] * 2,
        cost_estimate=pl.CostEstimate(
            flops=2 * 144 * 48 * slab, bytes_accessed=4 * 12 * beads * slab, transcendentals=0
        ),
        name="finish",
    )(offsets, expand, force, *parts)


def body(positions, momenta, masses, strengths, bond_ends, angle_ends, neighbour_tiles):
    beads, _, slab = positions.shape
    bead_count = lax.axis_size("bead")
    bead = lax.axis_index("bead")
    space_count = lax.axis_size("space")
    space = lax.axis_index("space")
    block = slab // bead_count
    slab_tiles = slab // TILE
    block_tiles = block // TILE
    all_tiles = slab_tiles * space_count
    rim = GT * TILE
    chunks = 2 if block_tiles % 4 == 0 else 1
    lanes = block // chunks
    interval = time_step / SUBS
    pair = bead_count == 2

    pos = positions.transpose(1, 0, 2)
    mom = momenta.transpose(1, 0, 2)
    logs = jnp.log2(strengths)[None, :]
    turned = contract_rows(beads)
    table = contract_table(BEADS, KEPT)
    own_tables = [table[:, i * beads : (i + 1) * beads] for i in range(bead_count)]

    def at_bead(tables):
        return lax.dynamic_index_in_dim(jnp.asarray(np.stack(tables)), bead, 0, keepdims=False)

    partial_left = at_bead([stacked_left(contract_left(t)) for t in own_tables])
    finish_left = at_bead([stacked_left(expand_left(t)) for t in own_tables])
    contract_l = at_bead([stacked_left(contract_left(t), 2) for t in turned])
    expand_l = at_bead([stacked_left(expand_left(t)) for t in turned])
    motion = jnp.asarray(stacked_left(motion_table(BEADS, interval)))

    def lanes_of(x, start, size):
        return lax.dynamic_slice_in_dim(x, start, size, x.ndim - 1)

    part = partial_contract(partial_left, pos, logs)

    shifted = jnp.mod(neighbour_tiles - space * slab_tiles + GT, all_tiles) - GT
    slab_ids = jnp.arange(slab_tiles, dtype=jnp.int32)
    left_of, right_of = shifted < 0, shifted >= slab_tiles
    flipped = [
        (s * 2 + b, ((s + (1 if b else -1)) % space_count) * 2 + (1 - b))
        for s in range(space_count)
        for b in range(2)
    ]
    near_side = [
        (s * 2 + b, ((s + (-1 if b else 1)) % space_count) * 2 + b)
        for s in range(space_count)
        for b in range(2)
    ]
    far_side = [
        (s * 2 + b, ((s + (1 if b else -1)) % space_count) * 2 + b)
        for s in range(space_count)
        for b in range(2)
    ]

    def rims(x):
        up = [(i, (i + 1) % space_count) for i in range(space_count)]
        down = [((i + 1) % space_count, i) for i in range(space_count)]
        return (
            lax.ppermute(x[:, slab - rim :], "space", up),
            lax.ppermute(x[:, :rim], "space", down),
        )

    if pair:
        first = bead * (block_tiles - GT)
        size = block + rim
        mine = lanes_of(part, first * TILE, size)
        head, tail = part[:, :rim], part[:, slab - rim :]
        theirs = lax.ppermute(
            lanes_of(part, (block_tiles - GT - first) * TILE, size), "bead", [(0, 1), (1, 0)]
        )
        straight = lax.ppermute(jnp.where(bead == 0, tail, head), ("space", "bead"), near_side)
        across = lax.ppermute(jnp.where(bead == 0, head, tail), ("space", "bead"), flipped)
        segments = [[mine, theirs], [straight, across]]
        outside = block_tiles + GT
        where = jnp.where(
            left_of,
            shifted + GT + outside,
            jnp.where(right_of, shifted - slab_tiles + outside, shifted - first),
        )
        own_where = slab_ids - first
    else:
        summed = lax.psum(part, "bead")
        summed = jnp.where(lax.broadcasted_iota(jnp.int32, summed.shape, 0) == 0, logs, summed)
        segments = [[summed], *[[x] for x in rims(summed)]]
        where = jnp.where(left_of, shifted + GT + slab_tiles, jnp.where(right_of, shifted + GT, shifted))
        own_where = slab_ids
    my_where = lanes_of(where, bead * block_tiles, block_tiles)
    my_own = lanes_of(own_where, bead * block_tiles, block_tiles)

    arrived = []
    for chunk in range(chunks):
        pieces = []
        for d in range(1, bead_count):
            owner = jnp.mod(bead - d, bead_count)
            start = owner * block + chunk * lanes
            piece = jnp.concatenate([lanes_of(pos, start, lanes), lanes_of(mom, start, lanes)], 0)
            pieces.append(
                lax.ppermute(piece, "bead", [(i, (i - d) % bead_count) for i in range(bead_count)])
            )
        arrived.append(pieces)

    my_bonds = lanes_of(bond_ends, bead * block_tiles * BPT, block_tiles * BPT)
    my_angles = lanes_of(angle_ends, bead * block_tiles * APT, block_tiles * APT)
    bonds = my_bonds.reshape(2, block_tiles, BPT)
    angles = my_angles.reshape(3, block_tiles, APT)
    outer = jnp.concatenate([angles[0], angles[2]], 1)
    centre = jnp.concatenate([angles[1], angles[1]], 1)
    ends = jnp.stack([bonds[0], bonds[1], outer, centre], 1)
    gains = jnp.concatenate([bonds[1], centre], 1)
    losses = jnp.concatenate([bonds[0], angles[2], angles[0]], 1)
    place = lax.broadcasted_iota(jnp.int32, (1, 1, TILE), 2)
    hot = ((gains[..., None] == place).astype(F32) - (losses[..., None] == place).astype(F32)).astype(BF16)
    my_mass = lanes_of(masses, bead * block, block)[None, :]
    my_logs = lanes_of(logs, bead * block, block)

    force = pair_forces(segments, my_own, my_where.T.reshape(-1))

    aligned = beads % 8 == 0
    index = jnp.reshape(bead, (1,)).astype(jnp.int32)
    own_out, sends, contracted = [], [], []
    for chunk in range(chunks):
        if aligned:
            sources = (pos, mom, arrived[chunk])
        else:
            start = bead * block + chunk * lanes
            q_all = [lanes_of(pos, start, lanes)] + [x[:3] for x in arrived[chunk]]
            p_all = [lanes_of(mom, start, lanes)] + [x[3:] for x in arrived[chunk]]
            sources = (jnp.concatenate(q_all, 1), jnp.concatenate(p_all, 1), [])
        *outs, c16 = substeps(
            chunk, chunks, index, *sources, force, my_mass, ends, hot, motion, expand_l, contract_l, my_logs
        )
        if not aligned:
            outs = [outs[0][:, d * beads : (d + 1) * beads] for d in range(bead_count)]
        own_out.append(outs[0])
        sends.append(outs[1:])
        contracted.append(c16)

    def send_back(chunk):
        return [
            lax.ppermute(x, "bead", [(i, (i + d) % bead_count) for i in range(bead_count)])
            for d, x in enumerate(sends[chunk], 1)
        ]

    returned = [send_back(chunk) for chunk in range(chunks - 1)]
    c16 = jnp.concatenate(contracted, 1) if chunks > 1 else contracted[0]
    if pair:
        edge = jnp.where(bead == 0, c16[:, :rim], c16[:, block - rim :])
        theirs = lax.ppermute(c16, "bead", [(0, 1), (1, 0)])
        straight = lax.ppermute(edge, ("space", "bead"), far_side)
        across = lax.ppermute(edge, ("space", "bead"), flipped)
        segments = [[c16], [theirs], [straight], [across]]
        left_at = jnp.where(bead == 0, slab_tiles + GT, slab_tiles)
        right_at = jnp.where(bead == 0, slab_tiles, slab_tiles + GT)
        inside = jnp.mod(shifted - bead * block_tiles, slab_tiles)
        where = jnp.where(
            left_of,
            shifted + GT + left_at,
            jnp.where(right_of, shifted - slab_tiles + right_at, inside),
        )
        own_where = jnp.mod(slab_ids - bead * block_tiles, slab_tiles)
    else:
        gathered = lax.all_gather(c16, "bead", axis=1, tiled=True)
        segments = [[gathered], *[[x] for x in rims(gathered)]]
    returned.append(send_back(chunks - 1))
    force = pair_forces(segments, own_where, where.T.reshape(-1))

    arrays, offsets = [], []
    for chunk in range(chunks):
        for d, x in enumerate([own_out[chunk]] + returned[chunk]):
            arrays.append(x)
            offsets.append(jnp.mod(bead - d, bead_count) * block + chunk * lanes)
    new_pos, new_mom = finish(
        arrays, jnp.stack(offsets).astype(jnp.int32), finish_left, force, beads
    )
    return new_pos.transpose(1, 0, 2), new_mom.transpose(1, 0, 2)


def solution(mesh):
    placed = (
        P("bead", None, "space"),
        P("bead", None, "space"),
        P("space"),
        P("space"),
        P(None, "space"),
        P(None, "space"),
        P(None, "space"),
    )
    return jax.shard_map(
        body,
        mesh=mesh,
        in_specs=placed,
        out_specs=(P("bead", None, "space"), P("bead", None, "space")),
        check_vma=False,
    )
```

```python
import functools
import math

import jax
import jax.numpy as jnp
import numpy as np
from jax import lax
from jax.experimental import pallas as pl
from jax.experimental.pallas import tpu as pltpu
from jax.sharding import PartitionSpec as P

BEADS = 32
KEPT = 4
SUBS = 3
TILE = 128
GT = 2
BPT = 128
APT = 64
ROWS = 4 * KEPT

time_step = 0.3
spring_freq = 80.0
bond_stiff = 0.2
bond_rest = 1.0
angle_stiff = 0.1
angle_rest = 0.5
range_sq = 4.0
HIGH = lax.Precision.HIGHEST
F32 = jnp.float32
BF16 = jnp.bfloat16


def mode_table(number):
    within = np.arange(number)
    result = np.zeros((number, number))
    for column in range(number):
        if column == 0:
            result[:, column] = 1.0 / math.sqrt(number)
        elif 2 * column < number:
            result[:, column] = math.sqrt(2.0 / number) * np.cos(
                2 * np.pi * within * column / number
            )
        elif 2 * column == number:
            result[:, column] = (-1.0) ** within / math.sqrt(number)
        else:
            result[:, column] = math.sqrt(2.0 / number) * np.sin(
                2 * np.pi * within * column / number
            )
    return result


def contract_table(number, kept):
    larger = mode_table(number)
    smaller = mode_table(kept)
    chosen = [column if 2 * column <= kept else number - kept + column for column in range(kept)]
    return math.sqrt(kept / number) * smaller @ larger[:, chosen].T


def motion_table(number, interval):
    freqs = 2.0 * spring_freq * np.sin(np.pi * np.arange(number) / number)
    modes = mode_table(number)
    safe = np.where(freqs > 0, freqs, 1.0)
    gains = np.where(freqs > 0, np.sin(freqs * interval) / safe, interval)
    drags = freqs * np.sin(freqs * interval)
    stay = modes @ np.diag(np.cos(freqs * interval)) @ modes.T
    gain = modes @ np.diag(gains) @ modes.T
    drag = modes @ np.diag(drags) @ modes.T
    return np.block([[stay, gain], [-drag, stay]])


def np_split(table, parts):
    out, rest = [], np.asarray(table, np.float64)
    for _ in range(parts):
        piece = rest.astype(np.float32).astype(jnp.bfloat16)
        out.append(piece)
        rest = rest - piece.astype(np.float64)
    return out


def stacked_left(table, parts=3):
    pieces = np_split(table, parts)
    zero = np.zeros_like(pieces[0])
    return np.concatenate(
        [
            np.concatenate([pieces[i]] * (parts - i) + [zero] * i, axis=1)
            for i in range(parts)
        ],
        axis=0,
    )


def split(x, parts):
    out = []
    for i in range(parts):
        piece = x.astype(BF16)
        out.append(piece)
        if i < parts - 1:
            x = x - piece.astype(F32)
    return out


def mm(left, right):
    return jnp.dot(left, right, preferred_element_type=F32)


def exact(left, x, parts=3):
    out = mm(left, jnp.concatenate(split(x, parts), axis=0))
    rows = out.shape[0] // parts
    total = out[:rows]
    for i in range(1, parts):
        total = total + out[i * rows : (i + 1) * rows]
    return total


def contract_rows(beads):
    table = contract_table(BEADS, KEPT)
    tables = []
    for turn in range(0, BEADS, beads):
        order = (np.arange(BEADS) + turn) % BEADS
        tables.append(table[:, order])
    return tables


def contract_left(table):
    out = np.zeros((ROWS, 3 * table.shape[1]))
    for c in range(KEPT):
        for k in range(3):
            out[4 * c + 1 + k, k * table.shape[1] : (k + 1) * table.shape[1]] = table[c]
    return out


def expand_left(table):
    return BEADS / KEPT * contract_left(table).T


def begin_kernel(pair, chunks, info, left, pos, mom, scal, *outs):
    comps, beads, lanes = pos.shape
    tables = left[...]
    width = min(lanes, 512)
    row = lax.broadcasted_iota(jnp.int32, (ROWS, width), 0)
    whole = outs[0] if not pair else outs[-1]
    for at in range(0, lanes, width):
        x = jnp.concatenate([pos[c, :, at : at + width] for c in range(comps)], axis=0)
        c16 = exact(tables, x)
        whole[:, at : at + width] = jnp.where(row == 0, scal[1:2, at : at + width], c16)
    if not pair:
        return
    mine, theirs, straight, across = outs[:4]
    pieces = outs[4:-1]
    block, rim = lanes // 2, GT * TILE
    size = block + rim

    def sides(bead):
        first, other = (0, block - rim) if bead == 0 else (block - rim, 0)
        mine[...] = whole[:, first : first + size]
        theirs[...] = whole[:, other : other + size]
        head, tail = whole[:, :rim], whole[:, lanes - rim :]
        straight[...] = tail if bead == 0 else head
        across[...] = head if bead == 0 else tail
        start = block if bead == 0 else 0
        step = block // chunks
        for i in range(chunks):
            where = slice(start + i * step, start + (i + 1) * step)
            pieces[i][:3] = pos[:, :, where]
            pieces[i][3:] = mom[:, :, where]

    for bead in range(2):
        pl.when(info[0] == bead)(functools.partial(sides, bead))


def begin(pair, chunks, info, left, pos, mom, scal):
    beads, lanes = pos.shape[1:]
    full = lambda shape: pl.BlockSpec(shape, lambda i, s: (0,) * len(shape))
    if pair:
        block, rim = lanes // 2, GT * TILE
        shapes = [(ROWS, block + rim)] * 2 + [(ROWS, rim)] * 2
        shapes += [(6, beads, block // chunks)] * chunks
        scratch = [pltpu.VMEM((ROWS, lanes), F32)]
    else:
        shapes, scratch = [(ROWS, lanes)], []
    grid_spec = pltpu.PrefetchScalarGridSpec(
        num_scalar_prefetch=1,
        grid=(1,),
        in_specs=[
            pl.BlockSpec((None,) + left.shape[1:], lambda i, s: (s[0], 0, 0)),
            full(pos.shape),
            full(mom.shape),
            full(scal.shape),
        ],
        out_specs=[full(s) for s in shapes],
        scratch_shapes=scratch,
    )
    return pl.pallas_call(
        functools.partial(begin_kernel, pair, chunks),
        grid_spec=grid_spec,
        out_shape=[jax.ShapeDtypeStruct(s, F32) for s in shapes],
        cost_estimate=pl.CostEstimate(
            flops=2 * 48 * 144 * lanes, bytes_accessed=12 * pos.size, transcendentals=0
        ),
        name="begin",
    )(info, left, pos, mom, scal)


def prepare_kernel(group, bonds, angles, ends, hot):
    lane = lax.broadcasted_iota(jnp.int32, (1, TILE), 1)
    atom = lax.broadcasted_iota(jnp.int32, (TILE, 2 * TILE), 0)
    low = lane < APT

    def merge(first, second, odd):
        a = pltpu.roll(first, APT, 1) if odd else first
        b = second if odd else pltpu.roll(second, APT, 1)
        return jnp.where(low, a, b)

    for t in range(group):
        one = bonds[0:1, t * TILE : (t + 1) * TILE]
        other = bonds[1:2, t * TILE : (t + 1) * TILE]
        odd = t % 2
        window = slice((t // 2) * TILE, (t // 2 + 1) * TILE)
        first, middle, last = [angles[e : e + 1, window] for e in range(3)]
        outer = merge(first, last, odd)
        opposite = merge(last, first, odd)
        centre = merge(middle, middle, odd)
        ends[t] = jnp.concatenate([one, other, outer, centre], axis=0)
        gains = jnp.concatenate([other, centre], axis=1)
        losses = jnp.concatenate([one, opposite], axis=1)
        table = (atom == gains).astype(F32) - (atom == losses).astype(F32)
        hot[t] = table.astype(BF16)


def prepare(info, bond_ends, angle_ends, block_tiles):
    group = math.gcd(block_tiles, 4)
    steps = block_tiles // group
    grid_spec = pltpu.PrefetchScalarGridSpec(
        num_scalar_prefetch=1,
        grid=(steps,),
        in_specs=[
            pl.BlockSpec((2, group * BPT), lambda i, s: (0, s[0] * steps + i)),
            pl.BlockSpec((3, group * APT), lambda i, s: (0, s[0] * steps + i)),
        ],
        out_specs=[
            pl.BlockSpec((group, 4, TILE), lambda i, s: (i, 0, 0)),
            pl.BlockSpec((group, TILE, 2 * TILE), lambda i, s: (i, 0, 0)),
        ],
    )
    return pl.pallas_call(
        lambda info, *refs: prepare_kernel(group, *refs),
        grid_spec=grid_spec,
        out_shape=[
            jax.ShapeDtypeStruct((block_tiles, 4, TILE), jnp.int32),
            jax.ShapeDtypeStruct((block_tiles, TILE, 2 * TILE), BF16),
        ],
        cost_estimate=pl.CostEstimate(
            flops=block_tiles * 200_000, bytes_accessed=block_tiles * 80_000, transcendentals=0
        ),
        name="prepare",
    )(info, bond_ends, angle_ends)


def pair_kernel(spots, seg_sizes, own_count, info, nbr, *refs):
    total = sum(n for _, n in seg_sizes)
    count = sum(n for n, _ in seg_sizes)
    seg_refs = refs[:count]
    out, feat_i, feat_m, feat_p, base, weights_a, weights_b = refs[count:]
    column, own_spot, spot = spots(info)
    row = lax.broadcasted_iota(jnp.int32, (ROWS, TILE), 0)
    slot = row % 4
    scale = math.sqrt(2.0 * math.log2(math.e) / range_sq)
    same = (
        lax.broadcasted_iota(jnp.int32, (ROWS, ROWS), 0) // 4
        == lax.broadcasted_iota(jnp.int32, (ROWS, ROWS), 1) // 4
    ).astype(F32)

    def features(tile, c16):
        base[tile] = c16
        logs = c16[0:1]
        place = jnp.where(slot == 0, 0.0, c16)
        scaled = place * scale
        high, low = [piece.astype(F32) for piece in split(scaled, 2)]
        square = jnp.dot(same, scaled * scaled, precision=HIGH, preferred_element_type=F32)
        half = -0.5 * square

        def three(x):
            a, b, c = [piece.astype(F32) for piece in split(x, 3)]
            return jnp.where(slot == 0, a, jnp.where(slot == 1, b, jnp.where(slot == 2, c, 0.0)))

        ones = jnp.where(slot == 3, 0.0, 1.0)
        mine = jnp.concatenate([high, high, low, low, three(half), ones], axis=0)
        theirs = jnp.concatenate(
            [high, low, high, low, ones, three(half + logs), ones, ones], axis=0
        )
        feat_i[tile] = mine.astype(BF16)
        feat_m[tile] = jnp.transpose(theirs, (1, 0)).astype(BF16)
        one = jnp.ones((ROWS, TILE), F32)
        p_high, p_low = [piece.astype(F32) for piece in split(place, 2)]
        feat_p[tile] = jnp.concatenate([one, p_high, p_low], axis=0).astype(BF16)

    tile = 0
    at = 0
    for number, tiles in seg_sizes:
        group = seg_refs[at : at + number]
        at += number
        for i in range(tiles):
            c16 = group[0][:, i * TILE : (i + 1) * TILE]
            for other in group[1:]:
                more = other[:, i * TILE : (i + 1) * TILE]
                c16 = c16 + jnp.where(row == 0, 0.0, more)
            features(tile, c16)
            tile += 1
    assert tile == total

    groups = 6
    wide_row = lax.broadcasted_iota(jnp.int32, (groups * ROWS, TILE), 0)
    pick = [((wide_row % ROWS) // 4 == c).astype(BF16) for c in range(KEPT)]
    owner = row // 4

    def near(t, u):
        return spot(nbr[u, column + t])

    def weigh(t, weights):
        features_i = feat_i[own_spot(t)]
        right = jnp.concatenate([features_i * pick[c] for c in range(KEPT)], axis=1)
        right = jnp.concatenate([right, jnp.zeros((2 * ROWS, KEPT * TILE), BF16)], axis=0)
        left = jnp.concatenate([feat_m[near(t, u)] for u in range(3)], axis=0)
        power = mm(left, right)
        for u in range(3):
            high, low = split(jnp.exp2(power[u * TILE : (u + 1) * TILE]), 2)
            weights[2 * u * TILE : (2 * u + 1) * TILE] = high
            weights[(2 * u + 1) * TILE : (2 * u + 2) * TILE] = low

    def pull(t, weights):
        left = []
        for u in range(3):
            piece = feat_p[near(t, u)]
            left += [piece, piece]
        total_p = mm(jnp.concatenate(left, axis=1), weights[...])
        sums = total_p[:ROWS]
        pulls = total_p[ROWS : 2 * ROWS] + total_p[2 * ROWS :]
        c16 = base[own_spot(t)]
        factor = (2.0 / range_sq) * jnp.exp2(c16[0:1])
        result = jnp.zeros((ROWS, TILE), F32)
        for c in range(KEPT):
            lanes = slice(c * TILE, (c + 1) * TILE)
            force = factor * (c16 * sums[:, lanes] - pulls[:, lanes])
            result = jnp.where((owner == c) & (slot > 0), force, result)
        out[:, pl.ds(pl.multiple_of(t * TILE, TILE), TILE)] = result

    weigh(0, weights_a)

    def two_tiles(i, carry):
        t = 2 * i
        weigh(t + 1, weights_b)
        pull(t, weights_a)
        weigh(jnp.minimum(t + 2, own_count - 1), weights_a)
        pull(t + 1, weights_b)
        return carry

    lax.fori_loop(0, own_count // 2, two_tiles, 0)


def pair_forces(spots, segments, own_count, info, neighbour_tiles):
    sizes = tuple((len(group), group[0].shape[1] // TILE) for group in segments)
    total = sum(n for _, n in sizes)
    assert own_count % 2 == 0
    flat = [array for group in segments for array in group]
    grid_spec = pltpu.PrefetchScalarGridSpec(
        num_scalar_prefetch=2,
        grid=(1,),
        in_specs=[pl.BlockSpec(a.shape, lambda i, *_: (0, 0)) for a in flat],
        out_specs=pl.BlockSpec((ROWS, own_count * TILE), lambda i, *_: (0, 0)),
        scratch_shapes=[
            pltpu.VMEM((total, 6 * ROWS, TILE), BF16),
            pltpu.VMEM((total, TILE, 8 * ROWS), BF16),
            pltpu.VMEM((total, 3 * ROWS, TILE), BF16),
            pltpu.VMEM((total, ROWS, TILE), F32),
            pltpu.VMEM((6 * TILE, KEPT * TILE), BF16),
            pltpu.VMEM((6 * TILE, KEPT * TILE), BF16),
        ],
    )
    return pl.pallas_call(
        functools.partial(pair_kernel, spots, sizes, own_count),
        grid_spec=grid_spec,
        out_shape=jax.ShapeDtypeStruct((ROWS, own_count * TILE), F32),
        cost_estimate=pl.CostEstimate(
            flops=own_count * 3 * 2 * TILE * 4 * TILE * 400,
            bytes_accessed=4 * ROWS * TILE * (total + own_count),
            transcendentals=own_count * 3 * TILE * 4 * TILE,
        ),
        name="pair_forces",
    )(info, neighbour_tiles, *flat)


def step_kernel(parts, group, with_edge, has_before, info, *refs):
    at = 0
    pos, mom = refs[at : at + 2]
    at += 2
    received = refs[at : at + parts - 1]
    at += parts - 1
    force, scal, ends, hot, motion, expand, contract = refs[at : at + 7]
    at += 7
    if has_before:
        before = refs[at]
        at += 1
    outs = refs[at : at + parts]
    c_out = refs[at + parts]
    interval = time_step / SUBS
    width = group * TILE
    motion_l = motion[...]
    masses = scal[0:1]
    inverse = 1.0 / masses

    def gathered(ref_index, own):
        pieces = [own] + [r[ref_index] for r in received]
        return pieces[0] if parts == 1 else jnp.concatenate(pieces, axis=0)

    q = [gathered(c, pos[c]) for c in range(3)]
    p = [gathered(3 + c, mom[c]) for c in range(3)]
    kick = exact(expand[...], force[...])
    v = [
        (p[c] + 0.5 * time_step * kick[c * BEADS : (c + 1) * BEADS]) * inverse for c in range(3)
    ]
    places = []
    for t in range(group):
        places.append([jnp.broadcast_to(ends[t, e : e + 1], (3 * BEADS, TILE)) for e in range(4)])

    def take(x, index):
        return jnp.take_along_axis(x, index, axis=1, mode="promise_in_bounds")

    def bonded(q):
        forces = []
        for t in range(group):
            lanes = slice(t * TILE, (t + 1) * TILE)
            rows = jnp.concatenate([q[c][:, lanes] for c in range(3)], axis=0)
            one, other, outer, centre = places[t]
            stretch = take(rows, one) - take(rows, other)
            arms = take(rows, outer) - take(rows, centre)
            s = [stretch[c * BEADS : (c + 1) * BEADS] for c in range(3)]
            a = [arms[c * BEADS : (c + 1) * BEADS] for c in range(3)]
            length = s[0] * s[0] + s[1] * s[1] + s[2] * s[2]
            g = bond_stiff * (length - bond_rest)
            turned = [pltpu.roll(x, APT, 1) for x in a]
            inner = a[0] * turned[0] + a[1] * turned[1] + a[2] * turned[2]
            h = angle_stiff * (inner - angle_rest)
            bonds = jnp.concatenate([g * x for x in s], axis=0)
            angles = jnp.concatenate([h * x for x in a], axis=0)
            both = jnp.concatenate([bonds, angles], axis=1)
            out = lax.dot_general(
                jnp.concatenate(split(both, 2), axis=0),
                hot[t],
                (((1,), (1,)), ((), ())),
                preferred_element_type=F32,
            )
            forces.append(out[: 3 * BEADS] + out[3 * BEADS :])
        return [
            jnp.concatenate([f[c * BEADS : (c + 1) * BEADS] for f in forces], axis=1)
            for c in range(3)
        ]

    for sub in range(SUBS):
        pushed = bonded(q)
        factor = (0.5 if sub == 0 else 1.0) * interval * inverse
        v = [v[c] + factor * pushed[c] for c in range(3)]
        for c in range(3):
            moved = exact(motion_l, jnp.concatenate([q[c], v[c]], axis=0))
            q[c], v[c] = moved[:BEADS], moved[BEADS:]
    pushed = bonded(q)
    p = [masses * v[c] + (0.5 * interval) * pushed[c] for c in range(3)]
    beads = BEADS // parts
    for i in range(parts):
        for c in range(3):
            outs[i][c] = q[c][i * beads : (i + 1) * beads]
            outs[i][3 + c] = p[c][i * beads : (i + 1) * beads]
    rows = jnp.concatenate(q, axis=0)
    c16 = exact(contract[...], rows, 2)
    row = lax.broadcasted_iota(jnp.int32, (ROWS, width), 0)
    c16 = jnp.where(row == 0, scal[1:2], c16)
    c_out[...] = c16
    if with_edge:
        rim = GT * TILE
        head = before[:, :rim] if has_before else c16[:, :rim]
        refs[-1][...] = jnp.where(info[0] == 0, head, c16[:, width - rim :])


def substeps(chunk, chunks, info, pos, mom, received, force, scal, ends, hot, motion, expand, contract, edge, before):
    if received:
        parts, lanes = 1 + len(received), received[0].shape[2]
    else:
        parts, lanes = 1, pos.shape[2]
    tiles = lanes // TILE
    group = tiles if edge else math.gcd(tiles, 8)
    width = group * TILE
    steps = tiles // group
    beads = BEADS // parts
    per_block = chunks * steps
    own_block = bool(received)

    def own(i, s):
        return (0, 0, (s[0] * per_block + chunk * steps + i) if own_block else i)

    def block(i, s):
        return (0, chunk * steps + i)

    def table(x):
        return pl.BlockSpec((None,) + x.shape[1:], lambda i, s: (s[0], 0, 0))

    extra = [before] if before is not None else []
    shapes = [(6, beads, lanes)] * parts + [(ROWS, lanes)]
    out_specs = [pl.BlockSpec((6, beads, width), lambda i, s: (0, 0, i))] * parts
    out_specs += [pl.BlockSpec((ROWS, width), lambda i, s: (0, i))]
    if edge:
        shapes.append((ROWS, GT * TILE))
        out_specs.append(pl.BlockSpec((ROWS, GT * TILE), lambda i, s: (0, 0)))
    grid_spec = pltpu.PrefetchScalarGridSpec(
        num_scalar_prefetch=1,
        grid=(steps,),
        in_specs=[pl.BlockSpec((3, beads, width), own)] * 2
        + [pl.BlockSpec((6, beads, width), lambda i, s: (0, 0, i))] * (parts - 1)
        + [
            pl.BlockSpec((ROWS, width), block),
            pl.BlockSpec((2, width), lambda i, s: (0, s[0] * per_block + chunk * steps + i)),
            pl.BlockSpec((group, 4, TILE), lambda i, s: (chunk * steps + i, 0, 0)),
            pl.BlockSpec((group, TILE, 2 * TILE), lambda i, s: (chunk * steps + i, 0, 0)),
            pl.BlockSpec(motion.shape, lambda i, s: (0, 0)),
            table(expand),
            table(contract),
        ]
        + [pl.BlockSpec(x.shape, lambda i, s: (0, 0)) for x in extra],
        out_specs=out_specs,
    )
    return pl.pallas_call(
        functools.partial(step_kernel, parts, group, edge, before is not None),
        grid_spec=grid_spec,
        out_shape=[jax.ShapeDtypeStruct(s, F32) for s in shapes],
        cost_estimate=pl.CostEstimate(
            flops=tiles * 4 * 40_000_000, bytes_accessed=4 * 12 * BEADS * lanes, transcendentals=0
        ),
        name="substeps",
    )(info, pos, mom, *received, force, scal, ends, hot, motion, expand, contract, *extra)


def finish_kernel(chunks, info, expand, force, *refs):
    pos, mom = refs[-2:]
    parts = refs[:-2]
    count = len(parts) // 2
    bead_count = count // chunks
    lanes = parts[0].shape[2]
    for i in range(count):
        chunk, distance = divmod(i, bead_count)
        block = lax.rem(info[0] + bead_count - distance, bead_count)
        start = pl.multiple_of(block * (chunks * lanes) + chunk * lanes, TILE)
        where = pl.ds(start, lanes)
        kick = exact(expand[...], force[:, where])
        pos[0, :, where] = parts[2 * i][0]
        mom[0, :, where] = parts[2 * i + 1][0] + 0.5 * time_step * kick


def finish(chunks, info, parts, expand, force):
    slab = force.shape[1]
    beads, lanes = parts[0].shape[1:]
    grid_spec = pltpu.PrefetchScalarGridSpec(
        num_scalar_prefetch=1,
        grid=(3,),
        in_specs=[
            pl.BlockSpec((None, None) + expand.shape[2:], lambda i, s: (s[0], i, 0, 0)),
            pl.BlockSpec(force.shape, lambda i, s: (0, 0)),
        ]
        + [
            pl.BlockSpec((1, beads, lanes), lambda i, s: (i, 0, 0)),
            pl.BlockSpec((1, beads, lanes), lambda i, s: (3 + i, 0, 0)),
        ]
        * len(parts),
        out_specs=[pl.BlockSpec((1, beads, slab), lambda i, s: (i, 0, 0))] * 2,
    )
    return pl.pallas_call(
        functools.partial(finish_kernel, chunks),
        grid_spec=grid_spec,
        out_shape=[jax.ShapeDtypeStruct((3, beads, slab), F32)] * 2,
        cost_estimate=pl.CostEstimate(
            flops=2 * 144 * 48 * slab, bytes_accessed=4 * 12 * beads * slab, transcendentals=0
        ),
        name="finish",
    )(info, expand, force, *[x for part in parts for x in (part, part)])


def body(positions, momenta, masses, strengths, bond_ends, angle_ends, neighbour_tiles):
    beads, _, slab = positions.shape
    bead_count = lax.axis_size("bead")
    bead = lax.axis_index("bead")
    space_count = lax.axis_size("space")
    space = lax.axis_index("space")
    block = slab // bead_count
    slab_tiles = slab // TILE
    block_tiles = block // TILE
    all_tiles = slab_tiles * space_count
    rim = GT * TILE
    chunks = 2 if block_tiles % 4 == 0 else 1
    lanes = block // chunks
    interval = time_step / SUBS
    pair = bead_count == 2

    pos = positions.transpose(1, 0, 2)
    mom = momenta.transpose(1, 0, 2)
    info = jnp.stack([bead, space]).astype(jnp.int32)
    scal = jnp.stack([masses, jnp.log2(strengths)])
    turned = contract_rows(beads)
    table = contract_table(BEADS, KEPT)
    own_tables = [table[:, i * beads : (i + 1) * beads] for i in range(bead_count)]

    def stack(tables):
        return jnp.asarray(np.stack(tables))

    begin_left = stack([stacked_left(contract_left(t)) for t in own_tables])
    finish_left = stack(
        [
            np.stack(
                [stacked_left(expand_left(t)[c * beads : (c + 1) * beads]) for c in range(3)]
            )
            for t in own_tables
        ]
    )
    contract_l = stack([stacked_left(contract_left(t), 2) for t in turned])
    expand_l = stack([stacked_left(expand_left(t)) for t in turned])
    motion = jnp.asarray(stacked_left(motion_table(BEADS, interval)))

    def lanes_of(x, start, size):
        return lax.dynamic_slice_in_dim(x, start, size, x.ndim - 1)

    def permutation(step, flip):
        return [
            (s * 2 + b, ((s + step(b)) % space_count) * 2 + (b ^ flip))
            for s in range(space_count)
            for b in range(2)
        ]

    def rims(x):
        up = [(i, (i + 1) % space_count) for i in range(space_count)]
        down = [((i + 1) % space_count, i) for i in range(space_count)]
        return (
            lax.ppermute(x[:, slab - rim :], "space", up),
            lax.ppermute(x[:, :rim], "space", down),
        )

    def relative(tile, info):
        x = tile - info[1] * slab_tiles
        x = jnp.where(x >= all_tiles - GT, x - all_tiles, x)
        return jnp.where(x < -GT, x + all_tiles, x)

    def spots_first(info):
        first = info[0] * (block_tiles - GT)
        outside = block_tiles + GT

        def spot(tile):
            x = relative(tile, info)
            right = jnp.where(x >= slab_tiles, x - slab_tiles + outside, x - first)
            return jnp.where(x < 0, x + GT + outside, right)

        return info[0] * block_tiles, lambda t: t + info[0] * GT, spot

    def spots_last(info):
        left_at = slab_tiles + jnp.where(info[0] == 0, GT, 0)
        right_at = slab_tiles + jnp.where(info[0] == 0, 0, GT)

        def turn(x):
            x = x - info[0] * block_tiles
            return jnp.where(x < 0, x + slab_tiles, x)

        def spot(tile):
            x = relative(tile, info)
            right = jnp.where(x >= slab_tiles, x - slab_tiles + right_at, turn(x))
            return jnp.where(x < 0, x + GT + left_at, right)

        return 0, turn, spot

    def spots_slab(first):
        def spots(info):
            start = info[0] * block_tiles if first else 0

            def spot(tile):
                x = relative(tile, info)
                return jnp.where(x < 0, x + GT + slab_tiles, jnp.where(x >= slab_tiles, x + GT, x))

            return start, lambda t: t + start, spot

        return spots

    arrived = [[] for _ in range(chunks)]
    if pair:
        mine, theirs, straight, across, *pieces = begin(
            True, chunks, info, begin_left, pos, mom, scal
        )
        theirs = lax.ppermute(theirs, "bead", [(0, 1), (1, 0)])
        straight = lax.ppermute(
            straight, ("space", "bead"), permutation(lambda b: -1 if b else 1, 0)
        )
        across = lax.ppermute(
            across, ("space", "bead"), permutation(lambda b: 1 if b else -1, 1)
        )
        segments = [[mine, theirs], [straight, across]]
        arrived = [[lax.ppermute(piece, "bead", [(0, 1), (1, 0)])] for piece in pieces]
        spots = spots_first
    else:
        (part,) = begin(False, chunks, info, begin_left, pos, mom, scal)
        summed = lax.psum(part, "bead")
        first_row = lax.broadcasted_iota(jnp.int32, summed.shape, 0) == 0
        summed = jnp.where(first_row, scal[1:2], summed)
        segments = [[summed], *[[x] for x in rims(summed)]]
        spots = spots_slab(True)
        for chunk in range(chunks):
            for d in range(1, bead_count):
                start = jnp.mod(bead - d, bead_count) * block + chunk * lanes
                piece = jnp.concatenate(
                    [lanes_of(pos, start, lanes), lanes_of(mom, start, lanes)], 0
                )
                back = [(i, (i - d) % bead_count) for i in range(bead_count)]
                arrived[chunk].append(lax.ppermute(piece, "bead", back))

    ends, hot = prepare(info, bond_ends, angle_ends, block_tiles)
    force = pair_forces(spots, segments, block_tiles, info, neighbour_tiles)

    aligned = beads % 8 == 0
    own_out, sends, contracted = [], [], []
    edge = None
    for chunk in range(chunks):
        if aligned:
            sources = (pos, mom, arrived[chunk])
        else:
            start = bead * block + chunk * lanes
            q_all = [lanes_of(pos, start, lanes)] + [x[:3] for x in arrived[chunk]]
            p_all = [lanes_of(mom, start, lanes)] + [x[3:] for x in arrived[chunk]]
            sources = (jnp.concatenate(q_all, 1), jnp.concatenate(p_all, 1), [])
        last = pair and chunk == chunks - 1
        outs = substeps(
            chunk, chunks, info, *sources, force, scal, ends, hot, motion, expand_l, contract_l,
            last, contracted[0] if last and chunk else None,
        )
        if last:
            *outs, edge = outs
        *outs, c16 = outs
        if not aligned:
            outs = [outs[0][:, d * beads : (d + 1) * beads] for d in range(bead_count)]
        own_out.append(outs[0])
        sends.append(outs[1:])
        contracted.append(c16)

    def send_back(chunk):
        return [
            lax.ppermute(x, "bead", [(i, (i + d) % bead_count) for i in range(bead_count)])
            for d, x in enumerate(sends[chunk], 1)
        ]

    if pair:
        theirs = [lax.ppermute(x, "bead", [(0, 1), (1, 0)]) for x in contracted]
        straight = lax.ppermute(
            edge, ("space", "bead"), permutation(lambda b: 1 if b else -1, 0)
        )
        across = lax.ppermute(edge, ("space", "bead"), permutation(lambda b: 1 if b else -1, 1))
        segments = [[x] for x in contracted + theirs + [straight, across]]
        spots = spots_last
    else:
        c16 = jnp.concatenate(contracted, 1) if chunks > 1 else contracted[0]
        gathered = lax.all_gather(c16, "bead", axis=1, tiled=True)
        segments = [[gathered], *[[x] for x in rims(gathered)]]
        spots = spots_slab(False)
    returned = [send_back(chunk) for chunk in range(chunks)]
    force = pair_forces(spots, segments, slab_tiles, info, neighbour_tiles)

    parts = [x for chunk in range(chunks) for x in [own_out[chunk]] + returned[chunk]]
    new_pos, new_mom = finish(chunks, info, parts, finish_left, force)
    return new_pos.transpose(1, 0, 2), new_mom.transpose(1, 0, 2)


def solution(mesh):
    placed = (
        P("bead", None, "space"),
        P("bead", None, "space"),
        P("space"),
        P("space"),
        P(None, "space"),
        P(None, "space"),
        P(None, "space"),
    )
    return jax.shard_map(
        body,
        mesh=mesh,
        in_specs=placed,
        out_specs=(P("bead", None, "space"), P("bead", None, "space")),
        check_vma=False,
    )
```

```python
import functools
import math

import jax
import jax.numpy as jnp
import numpy as np
from jax import lax
from jax.experimental import pallas as pl
from jax.experimental.pallas import tpu as pltpu
from jax.sharding import PartitionSpec as P


BEADS = 32
KEPT = 4
SUBS = 3
TILE = 128
GT = 2
BPT = 128
APT = 64
ROWS = 4 * KEPT

time_step = 0.3
spring_freq = 80.0
bond_stiff = 0.2
bond_rest = 1.0
angle_stiff = 0.1
angle_rest = 0.5
range_sq = 4.0
HIGH = lax.Precision.HIGHEST
IN_VMEM = pl.BlockSpec(memory_space=pltpu.VMEM)
IN_SMEM = pl.BlockSpec(memory_space=pltpu.SMEM)
IN_SPACE = pltpu.MemorySpace.VMEM


def near(x):
    return pltpu.with_memory_space_constraint(x, IN_SPACE)


def vmem_out(shape, dtype):
    return IN_SPACE(shape, dtype)


COST = pl.CostEstimate(flops=10_000_000, bytes_accessed=100_000, transcendentals=0)
F32 = jnp.float32
BF16 = jnp.bfloat16


def mode_table(number):
    within = np.arange(number)
    result = np.zeros((number, number))
    for column in range(number):
        if column == 0:
            result[:, column] = 1.0 / math.sqrt(number)
        elif 2 * column < number:
            result[:, column] = math.sqrt(2.0 / number) * np.cos(
                2 * np.pi * within * column / number
            )
        elif 2 * column == number:
            result[:, column] = (-1.0) ** within / math.sqrt(number)
        else:
            result[:, column] = math.sqrt(2.0 / number) * np.sin(
                2 * np.pi * within * column / number
            )
    return result


def contract_table(number, kept):
    larger = mode_table(number)
    smaller = mode_table(kept)
    chosen = [column if 2 * column <= kept else number - kept + column for column in range(kept)]
    return math.sqrt(kept / number) * smaller @ larger[:, chosen].T


def motion_table(number, interval):
    freqs = 2.0 * spring_freq * np.sin(np.pi * np.arange(number) / number)
    modes = mode_table(number)
    safe = np.where(freqs > 0, freqs, 1.0)
    gains = np.where(freqs > 0, np.sin(freqs * interval) / safe, interval)
    drags = freqs * np.sin(freqs * interval)
    stay = modes @ np.diag(np.cos(freqs * interval)) @ modes.T
    gain = modes @ np.diag(gains) @ modes.T
    drag = modes @ np.diag(drags) @ modes.T
    return np.block([[stay, gain], [-drag, stay]])


def np_split(table, parts):
    out, rest = [], np.asarray(table, np.float64)
    for _ in range(parts):
        piece = rest.astype(np.float32).astype(jnp.bfloat16)
        out.append(piece)
        rest = rest - piece.astype(np.float64)
    return out


def stacked_left(table, parts=3):
    pieces = np_split(table, parts)
    zero = np.zeros_like(pieces[0])
    return np.concatenate(
        [
            np.concatenate([pieces[i]] * (parts - i) + [zero] * i, axis=1)
            for i in range(parts)
        ],
        axis=0,
    )


def split(x, parts):
    out = []
    for i in range(parts):
        piece = x.astype(BF16)
        out.append(piece)
        if i < parts - 1:
            x = x - piece.astype(F32)
    return out


def mm(left, right):
    return jnp.dot(left, right, preferred_element_type=F32)


def exact(left, x, parts=3):
    out = mm(left, jnp.concatenate(split(x, parts), axis=0))
    rows = out.shape[0] // parts
    total = out[:rows]
    for i in range(1, parts):
        total = total + out[i * rows : (i + 1) * rows]
    return total


def contract_rows(beads):
    table = contract_table(BEADS, KEPT)
    tables = []
    for turn in range(0, BEADS, beads):
        order = (np.arange(BEADS) + turn) % BEADS
        tables.append(table[:, order])
    return tables


def contract_left(table):
    out = np.zeros((ROWS, 3 * table.shape[1]))
    for c in range(KEPT):
        for k in range(3):
            out[4 * c + 1 + k, k * table.shape[1] : (k + 1) * table.shape[1]] = table[c]
    return out


def expand_left(table):
    return BEADS / KEPT * contract_left(table).T


def begin_kernel(pair, chunks, bead, left, strengths, pos, mom, *outs):
    comps, _, lanes = pos.shape
    step = pl.program_id(0)
    whole = outs[-1]
    x = jnp.concatenate([pos[c] for c in range(comps)], axis=0)
    c16 = exact(left[bead[0]], x)
    logs = math.log2(math.e) * jnp.log(strengths[...])
    logs = jnp.concatenate([logs[t : t + 1] for t in range(lanes // TILE)], axis=1)
    row = lax.broadcasted_iota(jnp.int32, (ROWS, lanes), 0)
    c16 = jnp.where(row == 0, logs, c16)
    whole[:, pl.ds(pl.multiple_of(step * lanes, TILE), lanes)] = c16
    if not pair:
        return
    mine, theirs, straight, across = outs[:4]
    targets = outs[4:-1]
    for i in range(2 * chunks):
        owner, chunk = divmod(i, chunks)

        def put(target):
            target[:3] = pos[...]
            target[3:] = mom[...]

        pl.when((step == i) & (bead[0] == owner))(functools.partial(put, targets[chunk]))
        pl.when((step == i) & (bead[0] != owner))(functools.partial(put, targets[chunks + chunk]))

    slab = whole.shape[1]
    block, rim = slab // 2, GT * TILE
    size = block + rim

    def sides(which):
        first, other = (0, block - rim) if which == 0 else (block - rim, 0)
        mine[...] = whole[:, first : first + size]
        theirs[...] = whole[:, other : other + size]
        head, tail = whole[:, :rim], whole[:, slab - rim :]
        straight[...] = tail if which == 0 else head
        across[...] = head if which == 0 else tail

    for which in range(2):
        pl.when((step == 2 * chunks - 1) & (bead[0] == which))(functools.partial(sides, which))


def begin(pair, chunks, bead, left, strengths, pos, mom):
    beads, slab = pos.shape[1:]
    if pair:
        block, rim = slab // 2, GT * TILE
        lanes = block // chunks
        shapes = [(ROWS, block + rim)] * 2 + [(ROWS, rim)] * 2
        shapes += [(6, beads, lanes)] * (2 * chunks)
        scratch = [pltpu.VMEM((ROWS, slab), F32)]
    else:
        lanes = math.gcd(slab, 1024)
        shapes, scratch = [(ROWS, slab)], []
    return pl.pallas_call(
        functools.partial(begin_kernel, pair, chunks),
        grid=(slab // lanes,),
        in_specs=[
            IN_SMEM,
            IN_VMEM,
            pl.BlockSpec((lanes // TILE, TILE), lambda i: (i, 0)),
            pl.BlockSpec((3, beads, lanes), lambda i: (0, 0, i)),
            pl.BlockSpec((3, beads, lanes), lambda i: (0, 0, i)),
        ],
        out_specs=[IN_VMEM] * len(shapes),
        scratch_shapes=scratch,
        out_shape=[vmem_out(s, F32) for s in shapes],
        cost_estimate=COST,
        name="begin",
    )(bead, left, strengths, pos, mom)


def prepare_kernel(group, bead, bonds, angles, ends, hot):
    lane = lax.broadcasted_iota(jnp.int32, (1, TILE), 1)
    atom = lax.broadcasted_iota(jnp.int32, (TILE, 2 * TILE), 0)
    low = lane < APT

    def merge(first, second, odd):
        a = pltpu.roll(first, APT, 1) if odd else first
        b = second if odd else pltpu.roll(second, APT, 1)
        return jnp.where(low, a, b)

    def tiles(i, carry):
        at = (bead[0] * (hot.shape[0] // group) + i) * group
        bond_rows = bonds[:, pl.ds(pl.multiple_of(at * BPT, BPT), group * BPT)]
        angle_rows = angles[:, pl.ds(pl.multiple_of(at * APT, TILE), group * APT)]
        for t in range(group):
            one = bond_rows[0:1, t * TILE : (t + 1) * TILE]
            other = bond_rows[1:2, t * TILE : (t + 1) * TILE]
            odd = t % 2
            window = slice((t // 2) * TILE, (t // 2 + 1) * TILE)
            first, middle, last = [angle_rows[e : e + 1, window] for e in range(3)]
            outer = merge(first, last, odd)
            opposite = merge(last, first, odd)
            centre = merge(middle, middle, odd)
            ends[i * group + t] = jnp.concatenate([one, other, outer, centre], axis=0)
            gains = jnp.concatenate([other, centre], axis=1)
            losses = jnp.concatenate([one, opposite], axis=1)
            table = (atom == gains).astype(F32) - (atom == losses).astype(F32)
            hot[i * group + t] = table.astype(BF16)
        return carry

    lax.fori_loop(0, hot.shape[0] // group, tiles, 0)


def prepare(bead, bond_ends, angle_ends, block_tiles):
    return pl.pallas_call(
        functools.partial(prepare_kernel, math.gcd(block_tiles, 4)),
        in_specs=[IN_SMEM, IN_VMEM, IN_VMEM],
        out_specs=[IN_VMEM] * 2,
        out_shape=[
            vmem_out((block_tiles, 4, TILE), jnp.int32),
            vmem_out((block_tiles, TILE, 2 * TILE), BF16),
        ],
        cost_estimate=COST,
        name="prepare",
    )(bead, bond_ends, angle_ends)


def pair_kernel(spots, seg_sizes, own_count, bead, space, nbr, *refs):
    total = sum(n for _, n in seg_sizes)
    count = sum(n for n, _ in seg_sizes)
    seg_refs = refs[:count]
    out, feat_i, feat_m, feat_p, base, weights_a, weights_b = refs[count:]
    column, own_spot, spot = spots((bead[0], space[0]))
    row = lax.broadcasted_iota(jnp.int32, (ROWS, TILE), 0)
    slot = row % 4
    scale = math.sqrt(2.0 * math.log2(math.e) / range_sq)
    same = (
        lax.broadcasted_iota(jnp.int32, (ROWS, ROWS), 0) // 4
        == lax.broadcasted_iota(jnp.int32, (ROWS, ROWS), 1) // 4
    ).astype(F32)

    def features(tile, c16):
        base[tile] = c16
        logs = c16[0:1]
        place = jnp.where(slot == 0, 0.0, c16)
        scaled = place * scale
        high, low = [piece.astype(F32) for piece in split(scaled, 2)]
        square = jnp.dot(same, scaled * scaled, precision=HIGH, preferred_element_type=F32)
        half = -0.5 * square

        def three(x):
            a, b, c = [piece.astype(F32) for piece in split(x, 3)]
            return jnp.where(slot == 0, a, jnp.where(slot == 1, b, jnp.where(slot == 2, c, 0.0)))

        ones = jnp.where(slot == 3, 0.0, 1.0)
        mine = jnp.concatenate([high, high, low, low, three(half), ones], axis=0)
        theirs = jnp.concatenate(
            [high, low, high, low, ones, three(half + logs), ones, ones], axis=0
        )
        feat_i[tile] = mine.astype(BF16)
        feat_m[tile] = jnp.transpose(theirs, (1, 0)).astype(BF16)
        one = jnp.ones((ROWS, TILE), F32)
        p_high, p_low = [piece.astype(F32) for piece in split(place, 2)]
        feat_p[tile] = jnp.concatenate([one, p_high, p_low], axis=0).astype(BF16)

    tile = 0
    at = 0
    for number, tiles in seg_sizes:
        group = seg_refs[at : at + number]
        at += number
        for i in range(tiles):
            lanes = slice(i * TILE, (i + 1) * TILE)
            c16 = group[0][:, lanes] if len(group[0].shape) == 2 else group[0][6, :, lanes]
            for other in group[1:]:
                more = other[:, i * TILE : (i + 1) * TILE]
                c16 = c16 + jnp.where(row == 0, 0.0, more)
            features(tile, c16)
            tile += 1
    assert tile == total

    groups = 6
    wide_row = lax.broadcasted_iota(jnp.int32, (groups * ROWS, TILE), 0)
    pick = [((wide_row % ROWS) // 4 == c).astype(BF16) for c in range(KEPT)]
    owner = row // 4

    def close(t, u):
        return spot(nbr[u, column + t])

    def weigh(t, weights):
        features_i = feat_i[own_spot(t)]
        right = jnp.concatenate([features_i * pick[c] for c in range(KEPT)], axis=1)
        right = jnp.concatenate([right, jnp.zeros((2 * ROWS, KEPT * TILE), BF16)], axis=0)
        left = jnp.concatenate([feat_m[close(t, u)] for u in range(3)], axis=0)
        power = mm(left, right)
        for u in range(3):
            high, low = split(jnp.exp2(power[u * TILE : (u + 1) * TILE]), 2)
            weights[2 * u * TILE : (2 * u + 1) * TILE] = high
            weights[(2 * u + 1) * TILE : (2 * u + 2) * TILE] = low

    def pull(t, weights):
        left = []
        for u in range(3):
            piece = feat_p[close(t, u)]
            left += [piece, piece]
        total_p = mm(jnp.concatenate(left, axis=1), weights[...])
        sums = total_p[:ROWS]
        pulls = total_p[ROWS : 2 * ROWS] + total_p[2 * ROWS :]
        c16 = base[own_spot(t)]
        factor = (2.0 / range_sq) * jnp.exp2(c16[0:1])
        result = jnp.zeros((ROWS, TILE), F32)
        for c in range(KEPT):
            lanes = slice(c * TILE, (c + 1) * TILE)
            force = factor * (c16 * sums[:, lanes] - pulls[:, lanes])
            result = jnp.where((owner == c) & (slot > 0), force, result)
        out[:, pl.ds(pl.multiple_of(t * TILE, TILE), TILE)] = result

    weigh(0, weights_a)

    def two_tiles(i, carry):
        t = 2 * i
        weigh(t + 1, weights_b)
        pull(t, weights_a)
        weigh(jnp.minimum(t + 2, own_count - 1), weights_a)
        pull(t + 1, weights_b)
        return carry

    lax.fori_loop(0, own_count // 2, two_tiles, 0)


def pair_forces(spots, segments, own_count, bead, space, neighbour_tiles):
    sizes = tuple((len(group), group[0].shape[-1] // TILE) for group in segments)
    total = sum(n for _, n in sizes)
    assert own_count % 2 == 0
    flat = [array for group in segments for array in group]
    return pl.pallas_call(
        functools.partial(pair_kernel, spots, sizes, own_count),
        in_specs=[IN_SMEM] * 3 + [IN_VMEM] * len(flat),
        out_specs=IN_VMEM,
        out_shape=vmem_out((ROWS, own_count * TILE), F32),
        scratch_shapes=[
            pltpu.VMEM((total, 6 * ROWS, TILE), BF16),
            pltpu.VMEM((total, TILE, 8 * ROWS), BF16),
            pltpu.VMEM((total, 3 * ROWS, TILE), BF16),
            pltpu.VMEM((total, ROWS, TILE), F32),
            pltpu.VMEM((6 * TILE, KEPT * TILE), BF16),
            pltpu.VMEM((6 * TILE, KEPT * TILE), BF16),
        ],
        cost_estimate=COST,
        name="pair_forces",
    )(bead, space, neighbour_tiles, *[near(x) for x in flat])


def step_kernel(parts, chunk, chunks, group, edge, bead, *refs):
    pieces = refs[:parts]
    force, mass_rows, strength_rows, ends, hot, motion, expand, contract = refs[parts : parts + 8]
    before = refs[parts + 8] if edge and chunk else None
    outs = refs[len(refs) - parts - 1 - edge :]
    c_out = outs[parts]
    interval = time_step / SUBS
    width = group * TILE
    first = chunk * group
    motion_l = motion[...]

    def per_atom(rows):
        at = (bead[0] * chunks + chunk) * group
        return jnp.concatenate([rows[pl.ds(at + t, 1), :] for t in range(group)], axis=1)

    masses = per_atom(mass_rows)
    inverse = 1.0 / masses

    def gathered(plane):
        if parts == 1:
            return pieces[0][plane]
        return jnp.concatenate([piece[plane] for piece in pieces], axis=0)

    q = [gathered(c) for c in range(3)]
    p = [gathered(3 + c) for c in range(3)]
    kick = exact(expand[bead[0]], force[:, first * TILE : first * TILE + width])
    v = [
        (p[c] + 0.5 * time_step * kick[c * BEADS : (c + 1) * BEADS]) * inverse for c in range(3)
    ]
    places = []
    for t in range(group):
        places.append([jnp.broadcast_to(ends[first + t, e : e + 1], (3 * BEADS, TILE)) for e in range(4)])

    def take(x, index):
        return jnp.take_along_axis(x, index, axis=1, mode="promise_in_bounds")

    def bonded(q):
        forces = []
        for t in range(group):
            lanes = slice(t * TILE, (t + 1) * TILE)
            rows = jnp.concatenate([q[c][:, lanes] for c in range(3)], axis=0)
            one, other, outer, centre = places[t]
            stretch = take(rows, one) - take(rows, other)
            arms = take(rows, outer) - take(rows, centre)
            s = [stretch[c * BEADS : (c + 1) * BEADS] for c in range(3)]
            a = [arms[c * BEADS : (c + 1) * BEADS] for c in range(3)]
            length = s[0] * s[0] + s[1] * s[1] + s[2] * s[2]
            g = bond_stiff * (length - bond_rest)
            turned = [pltpu.roll(x, APT, 1) for x in a]
            inner = a[0] * turned[0] + a[1] * turned[1] + a[2] * turned[2]
            h = angle_stiff * (inner - angle_rest)
            bonds = jnp.concatenate([g * x for x in s], axis=0)
            angles = jnp.concatenate([h * x for x in a], axis=0)
            both = jnp.concatenate([bonds, angles], axis=1)
            out = lax.dot_general(
                jnp.concatenate(split(both, 2), axis=0),
                hot[first + t],
                (((1,), (1,)), ((), ())),
                preferred_element_type=F32,
            )
            forces.append(out[: 3 * BEADS] + out[3 * BEADS :])
        return [
            jnp.concatenate([f[c * BEADS : (c + 1) * BEADS] for f in forces], axis=1)
            for c in range(3)
        ]

    for sub in range(SUBS):
        pushed = bonded(q)
        factor = (0.5 if sub == 0 else 1.0) * interval * inverse
        v = [v[c] + factor * pushed[c] for c in range(3)]
        for c in range(3):
            moved = exact(motion_l, jnp.concatenate([q[c], v[c]], axis=0))
            q[c], v[c] = moved[:BEADS], moved[BEADS:]
    pushed = bonded(q)
    p = [masses * v[c] + (0.5 * interval) * pushed[c] for c in range(3)]
    beads = BEADS // parts
    for i in range(parts):
        for c in range(3):
            outs[i][c] = q[c][i * beads : (i + 1) * beads]
            outs[i][3 + c] = p[c][i * beads : (i + 1) * beads]
    rows = jnp.concatenate(q, axis=0)
    c16 = exact(contract[bead[0]], rows, 2)
    row = lax.broadcasted_iota(jnp.int32, (ROWS, width), 0)
    logs = math.log2(math.e) * jnp.log(per_atom(strength_rows))
    c16 = jnp.where(row == 0, logs, c16)
    c_out[...] = c16
    for out in outs[1:parts]:
        if out.shape[0] == 7:
            out[6] = c16
    if edge:
        rim = GT * TILE
        head = c16[:, :rim] if before is None else before[:, :rim]
        outs[-1][...] = jnp.where(bead[0] == 0, head, c16[:, width - rim :])


def substeps(chunk, chunks, bead, pieces, force, mass, strength, ends, hot, motion, expand, contract, edge, before):
    parts = len(pieces)
    lanes = pieces[0].shape[2]
    beads = BEADS // parts
    extra = [before] if edge and chunk else []
    shapes = [(6, beads, lanes)] + [(7, beads, lanes)] * (parts - 1) + [(ROWS, lanes)]
    if edge:
        shapes.append((ROWS, GT * TILE))
    return pl.pallas_call(
        functools.partial(step_kernel, parts, chunk, chunks, lanes // TILE, int(edge)),
        in_specs=[IN_SMEM] + [IN_VMEM] * (parts + 8 + len(extra)),
        out_specs=[IN_VMEM] * len(shapes),
        out_shape=[vmem_out(s, F32) for s in shapes],
        cost_estimate=COST,
        name="substeps",
    )(
        bead,
        *[near(x) for x in pieces + [force]],
        mass,
        strength,
        near(ends),
        near(hot),
        motion,
        expand,
        contract,
        *[near(x) for x in extra],
    )


def finish_kernel(chunks, bead, expand, force, *refs):
    pos, mom = refs[-2:]
    parts = refs[:-2]
    bead_count = len(parts) // chunks
    lanes = parts[0].shape[2]
    comp = pl.program_id(0)
    table = expand[bead[0], comp]
    for i, part in enumerate(parts):
        chunk, distance = divmod(i, bead_count)
        block = lax.rem(bead[0] + bead_count - distance, bead_count)
        start = pl.multiple_of(block * (chunks * lanes) + chunk * lanes, TILE)
        where = pl.ds(start, lanes)
        pos[0, :, where] = part[comp]
        mom[0, :, where] = part[3 + comp] + 0.5 * time_step * exact(table, force[:, where])


def finish(chunks, bead, parts, expand, force):
    slab = force.shape[1]
    beads = parts[0].shape[1]
    return pl.pallas_call(
        functools.partial(finish_kernel, chunks),
        grid=(3,),
        in_specs=[IN_SMEM] + [IN_VMEM] * (2 + len(parts)),
        out_specs=[pl.BlockSpec((1, beads, slab), lambda i: (i, 0, 0))] * 2,
        out_shape=[jax.ShapeDtypeStruct((3, beads, slab), F32)] * 2,
        cost_estimate=COST,
        name="finish",
    )(bead, expand, near(force), *[near(x) for x in parts])


def body(positions, momenta, masses, strengths, bond_ends, angle_ends, neighbour_tiles):
    beads, _, slab = positions.shape
    bead_count = lax.axis_size("bead")
    bead = lax.axis_index("bead")
    space_count = lax.axis_size("space")
    space = lax.axis_index("space")
    block = slab // bead_count
    slab_tiles = slab // TILE
    block_tiles = block // TILE
    all_tiles = slab_tiles * space_count
    rim = GT * TILE
    chunks = 2 if block_tiles % 4 == 0 else 1
    lanes = block // chunks
    interval = time_step / SUBS
    pair = bead_count == 2

    pos = positions.transpose(1, 0, 2)
    mom = momenta.transpose(1, 0, 2)
    bead_at = jnp.reshape(bead, (1,)).astype(jnp.int32)
    space_at = jnp.reshape(space, (1,)).astype(jnp.int32)
    mass = masses.reshape(slab_tiles, TILE)
    strength = strengths.reshape(slab_tiles, TILE)
    turned = contract_rows(beads)
    table = contract_table(BEADS, KEPT)
    own_tables = [table[:, i * beads : (i + 1) * beads] for i in range(bead_count)]

    def stack(tables):
        return jnp.asarray(np.stack(tables))

    begin_left = stack([stacked_left(contract_left(t)) for t in own_tables])
    finish_left = stack(
        [
            np.stack(
                [stacked_left(expand_left(t)[c * beads : (c + 1) * beads]) for c in range(3)]
            )
            for t in own_tables
        ]
    )
    contract_l = stack([stacked_left(contract_left(t), 2) for t in turned])
    expand_l = stack([stacked_left(expand_left(t)) for t in turned])
    motion = jnp.asarray(stacked_left(motion_table(BEADS, interval)))

    def lanes_of(x, start, size):
        return lax.dynamic_slice_in_dim(x, start, size, x.ndim - 1)

    def permutation(step, flip):
        return [
            (s * 2 + b, ((s + step(b)) % space_count) * 2 + (b ^ flip))
            for s in range(space_count)
            for b in range(2)
        ]

    def rims(x):
        up = [(i, (i + 1) % space_count) for i in range(space_count)]
        down = [((i + 1) % space_count, i) for i in range(space_count)]
        return (
            lax.ppermute(x[:, slab - rim :], "space", up),
            lax.ppermute(x[:, :rim], "space", down),
        )

    def relative(tile, info):
        x = tile - info[1] * slab_tiles
        x = jnp.where(x >= all_tiles - GT, x - all_tiles, x)
        return jnp.where(x < -GT, x + all_tiles, x)

    def spots_first(info):
        first = info[0] * (block_tiles - GT)
        outside = block_tiles + GT

        def spot(tile):
            x = relative(tile, info)
            right = jnp.where(x >= slab_tiles, x - slab_tiles + outside, x - first)
            return jnp.where(x < 0, x + GT + outside, right)

        return info[0] * block_tiles, lambda t: t + info[0] * GT, spot

    def spots_last(info):
        left_at = slab_tiles + jnp.where(info[0] == 0, GT, 0)
        right_at = slab_tiles + jnp.where(info[0] == 0, 0, GT)

        def turn(x):
            x = x - info[0] * block_tiles
            return jnp.where(x < 0, x + slab_tiles, x)

        def spot(tile):
            x = relative(tile, info)
            right = jnp.where(x >= slab_tiles, x - slab_tiles + right_at, turn(x))
            return jnp.where(x < 0, x + GT + left_at, right)

        return 0, turn, spot

    def spots_slab(first):
        def spots(info):
            start = info[0] * block_tiles if first else 0

            def spot(tile):
                x = relative(tile, info)
                return jnp.where(x < 0, x + GT + slab_tiles, jnp.where(x >= slab_tiles, x + GT, x))

            return start, lambda t: t + start, spot

        return spots

    pieces = [[] for _ in range(chunks)]
    if pair:
        mine, theirs, straight, across, *blocks = begin(
            True, chunks, bead_at, begin_left, strength, pos, mom
        )
        theirs = lax.ppermute(theirs, "bead", SWAP)
        straight = lax.ppermute(
            straight, ("space", "bead"), permutation(lambda b: -1 if b else 1, 0)
        )
        across = lax.ppermute(across, ("space", "bead"), permutation(lambda b: 1 if b else -1, 1))
        segments = [[mine, theirs], [straight, across]]
        for chunk in range(chunks):
            other = lax.ppermute(blocks[chunks + chunk], "bead", SWAP)
            pieces[chunk] = [blocks[chunk], other]
        spots = spots_first
    else:
        (part,) = begin(False, chunks, bead_at, begin_left, strength, pos, mom)
        summed = lax.psum(part, "bead")
        first_row = lax.broadcasted_iota(jnp.int32, summed.shape, 0) == 0
        summed = jnp.where(first_row, jnp.log2(strengths)[None, :], summed)
        segments = [[summed], *[[x] for x in rims(summed)]]
        spots = spots_slab(True)
        for chunk in range(chunks):
            parts = []
            for d in range(bead_count):
                start = jnp.mod(bead - d, bead_count) * block + chunk * lanes
                piece = jnp.concatenate(
                    [lanes_of(pos, start, lanes), lanes_of(mom, start, lanes)], 0
                )
                back = [(i, (i - d) % bead_count) for i in range(bead_count)]
                parts.append(lax.ppermute(piece, "bead", back) if d else piece)
            pieces[chunk] = [jnp.concatenate(parts, 1)]

    ends, hot = prepare(bead_at, bond_ends, angle_ends, block_tiles)
    force = pair_forces(spots, segments, block_tiles, bead_at, space_at, neighbour_tiles)

    own_out, returned, contracted = [], [], []
    edge = None
    for chunk in range(chunks):
        last = pair and chunk == chunks - 1
        outs = substeps(
            chunk, chunks, bead_at, pieces[chunk], force, mass, strength, ends, hot, motion,
            expand_l, contract_l, last, contracted[0] if contracted else None,
        )
        if last:
            *outs, edge = outs
        *outs, c16 = outs
        if not pair:
            outs = [outs[0][:, d * beads : (d + 1) * beads] for d in range(bead_count)]
        own_out.append(outs[0])
        contracted.append(c16)
        back = []
        for d in range(1, bead_count):
            on = [(i, (i + d) % bead_count) for i in range(bead_count)]
            back.append(lax.ppermute(outs[d], "bead", on))
        returned.append(back)

    if pair:
        theirs = lax.ppermute(contracted[-1], "bead", SWAP)
        straight = lax.ppermute(edge, ("space", "bead"), permutation(lambda b: 1 if b else -1, 0))
        across = lax.ppermute(
            edge, ("space", "bead"), permutation(lambda b: 1 if b else -1, 1)
        )
        early = [x[0] for x in returned[:-1]]
        segments = [[x] for x in contracted + early + [theirs, straight, across]]
        spots = spots_last
    else:
        c16 = jnp.concatenate(contracted, 1) if chunks > 1 else contracted[0]
        everyone = lax.all_gather(c16, "bead", axis=1, tiled=True)
        segments = [[everyone], *[[x] for x in rims(everyone)]]
        spots = spots_slab(False)
    force = pair_forces(spots, segments, slab_tiles, bead_at, space_at, neighbour_tiles)

    parts = [x for chunk in range(chunks) for x in [own_out[chunk]] + returned[chunk]]
    new_pos, new_mom = finish(chunks, bead_at, parts, finish_left, force)
    return new_pos.transpose(1, 0, 2), new_mom.transpose(1, 0, 2)


SWAP = [(0, 1), (1, 0)]


def solution(mesh):
    placed = (
        P("bead", None, "space"),
        P("bead", None, "space"),
        P("space"),
        P("space"),
        P(None, "space"),
        P(None, "space"),
        P(None, "space"),
    )

    return jax.shard_map(
        body,
        mesh=mesh,
        in_specs=placed,
        out_specs=(P("bead", None, "space"), P("bead", None, "space")),
        check_vma=False,
    )
```

```python
import functools
import math

import jax
import jax.numpy as jnp
import numpy as np
from jax import lax
from jax.experimental import pallas as pl
from jax.experimental.pallas import tpu as pltpu
from jax.sharding import PartitionSpec as P


BEADS = 32
KEPT = 4
SUBS = 3
TILE = 128
GT = 2
BPT = 128
APT = 64
ROWS = 4 * KEPT

time_step = 0.3
spring_freq = 80.0
bond_stiff = 0.2
bond_rest = 1.0
angle_stiff = 0.1
angle_rest = 0.5
range_sq = 4.0
HIGH = lax.Precision.HIGHEST
IN_VMEM = pl.BlockSpec(memory_space=pltpu.VMEM)
IN_SMEM = pl.BlockSpec(memory_space=pltpu.SMEM)
IN_SPACE = pltpu.MemorySpace.VMEM


def near(x):
    return pltpu.with_memory_space_constraint(x, IN_SPACE)


def far(x):
    return pltpu.with_memory_space_constraint(x, pltpu.MemorySpace.HBM)


def vmem_out(shape, dtype):
    return IN_SPACE(shape, dtype)


PARAMS = pltpu.CompilerParams(vmem_limit_bytes=20 * 1024 * 1024)
COST = pl.CostEstimate(flops=10_000_000, bytes_accessed=100_000, transcendentals=0)
F32 = jnp.float32
BF16 = jnp.bfloat16


def mode_table(number):
    within = np.arange(number)
    result = np.zeros((number, number))
    for column in range(number):
        if column == 0:
            result[:, column] = 1.0 / math.sqrt(number)
        elif 2 * column < number:
            result[:, column] = math.sqrt(2.0 / number) * np.cos(
                2 * np.pi * within * column / number
            )
        elif 2 * column == number:
            result[:, column] = (-1.0) ** within / math.sqrt(number)
        else:
            result[:, column] = math.sqrt(2.0 / number) * np.sin(
                2 * np.pi * within * column / number
            )
    return result


def contract_table(number, kept):
    larger = mode_table(number)
    smaller = mode_table(kept)
    chosen = [column if 2 * column <= kept else number - kept + column for column in range(kept)]
    return math.sqrt(kept / number) * smaller @ larger[:, chosen].T


def motion_table(number, interval):
    freqs = 2.0 * spring_freq * np.sin(np.pi * np.arange(number) / number)
    modes = mode_table(number)
    safe = np.where(freqs > 0, freqs, 1.0)
    gains = np.where(freqs > 0, np.sin(freqs * interval) / safe, interval)
    drags = freqs * np.sin(freqs * interval)
    stay = modes @ np.diag(np.cos(freqs * interval)) @ modes.T
    gain = modes @ np.diag(gains) @ modes.T
    drag = modes @ np.diag(drags) @ modes.T
    return np.block([[stay, gain], [-drag, stay]])


def np_split(table, parts):
    out, rest = [], np.asarray(table, np.float64)
    for _ in range(parts):
        piece = rest.astype(np.float32).astype(jnp.bfloat16)
        out.append(piece)
        rest = rest - piece.astype(np.float64)
    return out


def stacked_left(table, parts=3):
    pieces = np_split(table, parts)
    zero = np.zeros_like(pieces[0])
    return np.concatenate(
        [
            np.concatenate([pieces[i]] * (parts - i) + [zero] * i, axis=1)
            for i in range(parts)
        ],
        axis=0,
    )


def split(x, parts):
    out = []
    for i in range(parts):
        piece = x.astype(BF16)
        out.append(piece)
        if i < parts - 1:
            x = x - piece.astype(F32)
    return out


def mm(left, right):
    return jnp.dot(left, right, preferred_element_type=F32)


def exact(left, x, parts=3):
    out = mm(left, jnp.concatenate(split(x, parts), axis=0))
    rows = out.shape[0] // parts
    total = out[:rows]
    for i in range(1, parts):
        total = total + out[i * rows : (i + 1) * rows]
    return total


def contract_rows(beads):
    table = contract_table(BEADS, KEPT)
    tables = []
    for turn in range(0, BEADS, beads):
        order = (np.arange(BEADS) + turn) % BEADS
        tables.append(table[:, order])
    return tables


def contract_left(table):
    out = np.zeros((ROWS, 3 * table.shape[1]))
    for c in range(KEPT):
        for k in range(3):
            out[4 * c + 1 + k, k * table.shape[1] : (k + 1) * table.shape[1]] = table[c]
    return out


def expand_left(table):
    return BEADS / KEPT * contract_left(table).T


def begin_kernel(chunks, bead, left, strengths, pos, mom, *refs):
    mine, theirs, straight, across = refs[:4]
    blocks = refs[4:-2]
    whole, sems = refs[-2:]
    lanes = blocks[0].shape[2]
    slab = whole.shape[1]
    starts, copies = [], []
    for i in range(2 * chunks):
        owner = bead[0] if i < chunks else 1 - bead[0]
        starts.append(pl.multiple_of((owner * chunks + i % chunks) * lanes, TILE))
    for half, source in enumerate((pos, mom)):
        for i, block in enumerate(blocks):
            copy = pltpu.make_async_copy(
                source.at[:, :, pl.ds(starts[i], lanes)],
                block.at[pl.ds(3 * half, 3)],
                sems.at[half * len(blocks) + i],
            )
            copy.start()
            copies.append(copy)
    table = left[bead[0]]
    logs = math.log2(math.e) * jnp.log(strengths[...])
    for t in range(slab // TILE):
        whole[0:1, t * TILE : (t + 1) * TILE] = logs[t : t + 1]
    for i, block in enumerate(blocks):
        copies[i].wait()
        x = jnp.concatenate([block[c] for c in range(3)], axis=0)
        where = pl.ds(starts[i], lanes)
        row = lax.broadcasted_iota(jnp.int32, (ROWS, lanes), 0)
        whole[:, where] = jnp.where(row == 0, whole[:, where], exact(table, x))

    block, rim = slab // 2, GT * TILE
    size = block + rim

    def sides(which):
        first, other = (0, block - rim) if which == 0 else (block - rim, 0)
        mine[...] = whole[:, first : first + size]
        theirs[...] = whole[:, other : other + size]
        head, tail = whole[:, :rim], whole[:, slab - rim :]
        straight[...] = tail if which == 0 else head
        across[...] = head if which == 0 else tail

    for which in range(2):
        pl.when(bead[0] == which)(functools.partial(sides, which))
    for copy in copies[len(blocks) :]:
        copy.wait()


def begin(chunks, bead, left, strengths, pos, mom):
    beads, slab = pos.shape[1:]
    block, rim = slab // 2, GT * TILE
    lanes = block // chunks
    shapes = [(ROWS, block + rim)] * 2 + [(ROWS, rim)] * 2
    shapes += [(6, beads, lanes)] * (2 * chunks)
    return pl.pallas_call(
        functools.partial(begin_kernel, chunks),
        in_specs=[IN_SMEM, IN_VMEM, IN_VMEM] + [pl.BlockSpec(memory_space=pl.ANY)] * 2,
        out_specs=[IN_VMEM] * len(shapes),
        out_shape=[vmem_out(s, F32) for s in shapes],
        scratch_shapes=[
            pltpu.VMEM((ROWS, slab), F32),
            pltpu.SemaphoreType.DMA((4 * chunks,)),
        ],
        compiler_params=PARAMS,
        cost_estimate=COST,
        name="begin",
    )(bead, left, strengths, far(pos), far(mom))


def partial_kernel(bead, left, strengths, pos, out):
    comps, _, lanes = pos.shape
    logs = math.log2(math.e) * jnp.log(strengths[...])
    logs = jnp.concatenate([logs[t : t + 1] for t in range(lanes // TILE)], axis=1)
    row = lax.broadcasted_iota(jnp.int32, (ROWS, lanes), 0)
    x = jnp.concatenate([pos[c] for c in range(comps)], axis=0)
    out[...] = jnp.where(row == 0, logs, exact(left[bead[0]], x))


def partial_rows(bead, left, strengths, pos):
    beads, slab = pos.shape[1:]
    lanes = math.gcd(slab, 1024)
    return pl.pallas_call(
        partial_kernel,
        grid=(slab // lanes,),
        in_specs=[
            IN_SMEM,
            IN_VMEM,
            pl.BlockSpec((lanes // TILE, TILE), lambda i: (i, 0)),
            pl.BlockSpec((3, beads, lanes), lambda i: (0, 0, i)),
        ],
        out_specs=pl.BlockSpec((ROWS, lanes), lambda i: (0, i)),
        out_shape=jax.ShapeDtypeStruct((ROWS, slab), F32),
        name="partial_rows",
    )(bead, left, strengths, pos)


def prepare_kernel(group, bead, bonds, angles, ends, hot):
    lane = lax.broadcasted_iota(jnp.int32, (1, TILE), 1)
    atom = lax.broadcasted_iota(jnp.int32, (TILE, 2 * TILE), 0)
    low = lane < APT

    def merge(first, second, odd):
        a = pltpu.roll(first, APT, 1) if odd else first
        b = second if odd else pltpu.roll(second, APT, 1)
        return jnp.where(low, a, b)

    def tiles(i, carry):
        at = (bead[0] * (hot.shape[0] // group) + i) * group
        bond_rows = bonds[:, pl.ds(pl.multiple_of(at * BPT, BPT), group * BPT)]
        angle_rows = angles[:, pl.ds(pl.multiple_of(at * APT, TILE), group * APT)]
        for t in range(group):
            one = bond_rows[0:1, t * TILE : (t + 1) * TILE]
            other = bond_rows[1:2, t * TILE : (t + 1) * TILE]
            odd = t % 2
            window = slice((t // 2) * TILE, (t // 2 + 1) * TILE)
            first, middle, last = [angle_rows[e : e + 1, window] for e in range(3)]
            outer = merge(first, last, odd)
            opposite = merge(last, first, odd)
            centre = merge(middle, middle, odd)
            ends[i * group + t] = jnp.concatenate([one, other, outer, centre], axis=0)
            gains = jnp.concatenate([other, centre], axis=1)
            losses = jnp.concatenate([one, opposite], axis=1)
            table = (atom == gains).astype(F32) - (atom == losses).astype(F32)
            hot[i * group + t] = table.astype(BF16)
        return carry

    lax.fori_loop(0, hot.shape[0] // group, tiles, 0)


def prepare(bead, bond_ends, angle_ends, block_tiles):
    return pl.pallas_call(
        functools.partial(prepare_kernel, math.gcd(block_tiles, 4)),
        in_specs=[IN_SMEM, IN_VMEM, IN_VMEM],
        out_specs=[IN_VMEM] * 2,
        out_shape=[
            vmem_out((block_tiles, 4, TILE), jnp.int32),
            vmem_out((block_tiles, TILE, 2 * TILE), BF16),
        ],
        compiler_params=PARAMS,
        cost_estimate=COST,
        name="prepare",
    )(bead, bond_ends, angle_ends)


def pair_kernel(spots, seg_sizes, own_count, bead, space, nbr, *refs):
    total = sum(n for *_, n in seg_sizes)
    count = sum(n for n, *_ in seg_sizes)
    seg_refs = refs[:count]
    out, feat_i, feat_m, feat_p, base, weights_a, weights_b = refs[count:]
    column, own_spot, spot = spots((bead[0], space[0]))
    row = lax.broadcasted_iota(jnp.int32, (ROWS, TILE), 0)
    slot = row % 4
    scale = math.sqrt(2.0 * math.log2(math.e) / range_sq)
    same = (
        lax.broadcasted_iota(jnp.int32, (ROWS, ROWS), 0) // 4
        == lax.broadcasted_iota(jnp.int32, (ROWS, ROWS), 1) // 4
    ).astype(F32)

    def features(tile, c16):
        base[tile] = c16
        logs = c16[0:1]
        place = jnp.where(slot == 0, 0.0, c16)
        scaled = place * scale
        high, low = [piece.astype(F32) for piece in split(scaled, 2)]
        square = jnp.dot(same, scaled * scaled, precision=HIGH, preferred_element_type=F32)
        half = -0.5 * square

        def three(x):
            a, b, c = [piece.astype(F32) for piece in split(x, 3)]
            return jnp.where(slot == 0, a, jnp.where(slot == 1, b, jnp.where(slot == 2, c, 0.0)))

        ones = jnp.where(slot == 3, 0.0, 1.0)
        mine = jnp.concatenate([high, high, low, low, three(half), ones], axis=0)
        theirs = jnp.concatenate(
            [high, low, high, low, ones, three(half + logs), ones, ones], axis=0
        )
        feat_i[tile] = mine.astype(BF16)
        feat_m[tile] = jnp.transpose(theirs, (1, 0)).astype(BF16)
        one = jnp.ones((ROWS, TILE), F32)
        p_high, p_low = [piece.astype(F32) for piece in split(place, 2)]
        feat_p[tile] = jnp.concatenate([one, p_high, p_low], axis=0).astype(BF16)

    tile = 0
    at = 0
    for number, begins, tiles in seg_sizes:
        group = seg_refs[at : at + number]
        at += number
        for i in range(begins, begins + tiles):
            c16 = group[0][:, i * TILE : (i + 1) * TILE]
            for other in group[1:]:
                more = other[:, i * TILE : (i + 1) * TILE]
                c16 = c16 + jnp.where(row == 0, 0.0, more)
            features(tile, c16)
            tile += 1
    assert tile == total

    groups = 6
    wide_row = lax.broadcasted_iota(jnp.int32, (groups * ROWS, TILE), 0)
    pick = [((wide_row % ROWS) // 4 == c).astype(BF16) for c in range(KEPT)]
    owner = row // 4

    def close(t, u):
        return spot(nbr[u, column(t)])

    def weigh(t, weights):
        features_i = feat_i[own_spot(t)]
        right = jnp.concatenate([features_i * pick[c] for c in range(KEPT)], axis=1)
        right = jnp.concatenate([right, jnp.zeros((2 * ROWS, KEPT * TILE), BF16)], axis=0)
        left = jnp.concatenate([feat_m[close(t, u)] for u in range(3)], axis=0)
        power = mm(left, right)
        for u in range(3):
            high, low = split(jnp.exp2(power[u * TILE : (u + 1) * TILE]), 2)
            weights[2 * u * TILE : (2 * u + 1) * TILE] = high
            weights[(2 * u + 1) * TILE : (2 * u + 2) * TILE] = low

    def pull(t, weights):
        left = []
        for u in range(3):
            piece = feat_p[close(t, u)]
            left += [piece, piece]
        total_p = mm(jnp.concatenate(left, axis=1), weights[...])
        sums = total_p[:ROWS]
        pulls = total_p[ROWS : 2 * ROWS] + total_p[2 * ROWS :]
        c16 = base[own_spot(t)]
        factor = (2.0 / range_sq) * jnp.exp2(c16[0:1])
        result = jnp.zeros((ROWS, TILE), F32)
        for c in range(KEPT):
            lanes = slice(c * TILE, (c + 1) * TILE)
            force = factor * (c16 * sums[:, lanes] - pulls[:, lanes])
            result = jnp.where((owner == c) & (slot > 0), force, result)
        out[:, pl.ds(pl.multiple_of(t * TILE, TILE), TILE)] = result

    weigh(0, weights_a)

    def two_tiles(i, carry):
        t = 2 * i
        weigh(t + 1, weights_b)
        pull(t, weights_a)
        weigh(jnp.minimum(t + 2, own_count - 1), weights_a)
        pull(t + 1, weights_b)
        return carry

    lax.fori_loop(0, own_count // 2, two_tiles, 0)


def pair_forces(spots, segments, own_count, bead, space, neighbour_tiles):
    sizes = tuple((len(group), start, tiles) for group, start, tiles in segments)
    total = sum(n for *_, n in sizes)
    assert own_count % 2 == 0
    flat = [array for group, *_ in segments for array in group]
    return pl.pallas_call(
        functools.partial(pair_kernel, spots, sizes, own_count),
        in_specs=[IN_SMEM] * 3 + [IN_VMEM] * len(flat),
        out_specs=IN_VMEM,
        out_shape=vmem_out((ROWS, own_count * TILE), F32),
        scratch_shapes=[
            pltpu.VMEM((total, 6 * ROWS, TILE), BF16),
            pltpu.VMEM((total, TILE, 8 * ROWS), BF16),
            pltpu.VMEM((total, 3 * ROWS, TILE), BF16),
            pltpu.VMEM((total, ROWS, TILE), F32),
            pltpu.VMEM((6 * TILE, KEPT * TILE), BF16),
            pltpu.VMEM((6 * TILE, KEPT * TILE), BF16),
        ],
        compiler_params=PARAMS,
        cost_estimate=COST,
        name="pair_forces",
    )(bead, space, neighbour_tiles, *[near(x) for x in flat])


def step_kernel(parts, chunk, chunks, group, edge, bead, *refs):
    pieces = refs[:parts]
    force, mass_rows, strength_rows, ends, hot, motion, expand, contract = refs[parts : parts + 8]
    before = refs[parts + 8] if edge and chunk else None
    outs = refs[len(refs) - parts - 1 - 2 * edge :]
    c_out = outs[parts]
    interval = time_step / SUBS
    width = group * TILE
    first = chunk * group
    motion_l = motion[...]

    def per_atom(rows):
        at = (bead[0] * chunks + chunk) * group
        return jnp.concatenate([rows[pl.ds(at + t, 1), :] for t in range(group)], axis=1)

    masses = per_atom(mass_rows)
    inverse = 1.0 / masses

    def gathered(plane):
        if parts == 1:
            return pieces[0][plane]
        return jnp.concatenate([piece[plane] for piece in pieces], axis=0)

    q = [gathered(c) for c in range(3)]
    p = [gathered(3 + c) for c in range(3)]
    kick = exact(expand[bead[0]], force[:, first * TILE : first * TILE + width])
    v = [
        (p[c] + 0.5 * time_step * kick[c * BEADS : (c + 1) * BEADS]) * inverse for c in range(3)
    ]
    places = []
    for t in range(group):
        places.append([jnp.broadcast_to(ends[first + t, e : e + 1], (3 * BEADS, TILE)) for e in range(4)])

    def take(x, index):
        return jnp.take_along_axis(x, index, axis=1, mode="promise_in_bounds")

    def bonded(q):
        forces = []
        for t in range(group):
            lanes = slice(t * TILE, (t + 1) * TILE)
            rows = jnp.concatenate([q[c][:, lanes] for c in range(3)], axis=0)
            one, other, outer, centre = places[t]
            stretch = take(rows, one) - take(rows, other)
            arms = take(rows, outer) - take(rows, centre)
            s = [stretch[c * BEADS : (c + 1) * BEADS] for c in range(3)]
            a = [arms[c * BEADS : (c + 1) * BEADS] for c in range(3)]
            length = s[0] * s[0] + s[1] * s[1] + s[2] * s[2]
            g = bond_stiff * (length - bond_rest)
            turned = [pltpu.roll(x, APT, 1) for x in a]
            inner = a[0] * turned[0] + a[1] * turned[1] + a[2] * turned[2]
            h = angle_stiff * (inner - angle_rest)
            bonds = jnp.concatenate([g * x for x in s], axis=0)
            angles = jnp.concatenate([h * x for x in a], axis=0)
            both = jnp.concatenate([bonds, angles], axis=1)
            out = lax.dot_general(
                jnp.concatenate(split(both, 2), axis=0),
                hot[first + t],
                (((1,), (1,)), ((), ())),
                preferred_element_type=F32,
            )
            forces.append(out[: 3 * BEADS] + out[3 * BEADS :])
        return [
            jnp.concatenate([f[c * BEADS : (c + 1) * BEADS] for f in forces], axis=1)
            for c in range(3)
        ]

    for sub in range(SUBS):
        pushed = bonded(q)
        factor = (0.5 if sub == 0 else 1.0) * interval * inverse
        v = [v[c] + factor * pushed[c] for c in range(3)]
        for c in range(3):
            moved = exact(motion_l, jnp.concatenate([q[c], v[c]], axis=0))
            q[c], v[c] = moved[:BEADS], moved[BEADS:]
    pushed = bonded(q)
    p = [masses * v[c] + (0.5 * interval) * pushed[c] for c in range(3)]
    beads = BEADS // parts
    for i in range(parts):
        for c in range(3):
            outs[i][c] = q[c][i * beads : (i + 1) * beads]
            outs[i][3 + c] = p[c][i * beads : (i + 1) * beads]
    rows = jnp.concatenate(q, axis=0)
    c16 = exact(contract[bead[0]], rows, 2)
    row = lax.broadcasted_iota(jnp.int32, (ROWS, width), 0)
    logs = math.log2(math.e) * jnp.log(per_atom(strength_rows))
    c16 = jnp.where(row == 0, logs, c16)
    c_out[...] = c16
    if edge:
        rim = GT * TILE
        head = c16[:, :rim] if before is None else before[:, :rim]
        tail = c16[:, width - rim :]
        outs[-2][...] = jnp.where(bead[0] == 0, tail, head)
        outs[-1][...] = jnp.where(bead[0] == 0, head, tail)


def substeps(chunk, chunks, bead, pieces, force, mass, strength, ends, hot, motion, expand, contract, edge, before):
    parts = len(pieces)
    lanes = pieces[0].shape[2]
    beads = BEADS // parts
    extra = [before] if edge and chunk else []
    shapes = [(6, beads, lanes)] * parts + [(ROWS, lanes)]
    if edge:
        shapes += [(ROWS, GT * TILE)] * 2
    return pl.pallas_call(
        functools.partial(step_kernel, parts, chunk, chunks, lanes // TILE, int(edge)),
        in_specs=[IN_SMEM] + [IN_VMEM] * (parts + 8 + len(extra)),
        out_specs=[IN_VMEM] * len(shapes),
        out_shape=[vmem_out(s, F32) for s in shapes],
        compiler_params=PARAMS,
        cost_estimate=COST,
        name="substeps",
    )(
        bead,
        *[near(x) for x in pieces + [force]],
        mass,
        strength,
        near(ends),
        near(hot),
        motion,
        expand,
        contract,
        *[near(x) for x in extra],
    )


def finish_kernel(chunks, bead, expand, force, *refs):
    pos, mom = refs[-2:]
    parts = refs[:-2]
    bead_count = len(parts) // chunks
    lanes = parts[0].shape[2]
    comp = pl.program_id(0)
    table = expand[bead[0], comp]
    for i, part in enumerate(parts):
        chunk, distance = divmod(i, bead_count)
        block = lax.rem(bead[0] + bead_count - distance, bead_count)
        start = pl.multiple_of(block * (chunks * lanes) + chunk * lanes, TILE)
        where = pl.ds(start, lanes)
        pos[0, :, where] = part[comp]
        mom[0, :, where] = part[3 + comp] + 0.5 * time_step * exact(table, force[:, where])


def finish(chunks, bead, parts, expand, force):
    slab = force.shape[1]
    beads = parts[0].shape[1]
    return pl.pallas_call(
        functools.partial(finish_kernel, chunks),
        grid=(3,),
        in_specs=[IN_SMEM] + [IN_VMEM] * (2 + len(parts)),
        out_specs=[pl.BlockSpec((1, beads, slab), lambda i: (i, 0, 0))] * 2,
        out_shape=[jax.ShapeDtypeStruct((3, beads, slab), F32)] * 2,
        compiler_params=PARAMS,
        cost_estimate=COST,
        name="finish",
    )(bead, expand, near(force), *[near(x) for x in parts])


def finish_block_kernel(chunks, bead, expand, inner, outer, *refs):
    parts = refs[:chunks]
    pos, mom = refs[-2:]
    lanes = parts[0].shape[2]
    rim = GT * TILE
    comp = pl.program_id(0)
    force = jnp.concatenate([outer[:, :rim], inner[...], outer[:, rim:]], axis=1)
    kick = 0.5 * time_step * exact(expand[bead[0], comp], force)
    for chunk, part in enumerate(parts):
        where = slice(chunk * lanes, (chunk + 1) * lanes)
        pos[0, :, where] = part[comp]
        mom[0, :, where] = part[3 + comp] + kick[:, where]


def finish_block(bead, distance, parts, expand, inner, outer, before):
    beads, lanes = parts[0].shape[1:]
    block = lanes * len(parts)
    anywhere = [pl.BlockSpec(memory_space=pl.ANY)] * len(before)
    whole = pl.BlockSpec(memory_space=pltpu.VMEM)
    grid_spec = pltpu.PrefetchScalarGridSpec(
        num_scalar_prefetch=1,
        grid=(3,),
        in_specs=[whole] * (3 + len(parts)) + anywhere,
        out_specs=[
            pl.BlockSpec((1, beads, block), lambda i, b: (i, 0, lax.rem(b[0] + distance, 2)))
        ]
        * 2,
    )
    at = 4 + len(parts)
    return pl.pallas_call(
        functools.partial(finish_block_kernel, len(parts)),
        grid_spec=grid_spec,
        out_shape=[jax.ShapeDtypeStruct((3, beads, 2 * block), F32)] * 2,
        input_output_aliases={at + i: i for i in range(len(before))},
        compiler_params=PARAMS,
        cost_estimate=COST,
        name="finish_block",
    )(bead, expand, near(inner), near(outer), *[near(x) for x in parts], *before)


def body(positions, momenta, masses, strengths, bond_ends, angle_ends, neighbour_tiles):
    beads, _, slab = positions.shape
    bead_count = lax.axis_size("bead")
    bead = lax.axis_index("bead")
    space_count = lax.axis_size("space")
    space = lax.axis_index("space")
    block = slab // bead_count
    slab_tiles = slab // TILE
    block_tiles = block // TILE
    all_tiles = slab_tiles * space_count
    rim = GT * TILE
    chunks = 2 if block_tiles % 4 == 0 else 1
    lanes = block // chunks
    interval = time_step / SUBS
    pair = bead_count == 2

    pos = positions.transpose(1, 0, 2)
    mom = momenta.transpose(1, 0, 2)
    bead_at = jnp.reshape(bead, (1,)).astype(jnp.int32)
    space_at = jnp.reshape(space, (1,)).astype(jnp.int32)
    mass = masses.reshape(slab_tiles, TILE)
    strength = strengths.reshape(slab_tiles, TILE)
    turned = contract_rows(beads)
    table = contract_table(BEADS, KEPT)
    own_tables = [table[:, i * beads : (i + 1) * beads] for i in range(bead_count)]

    def stack(tables):
        return jnp.asarray(np.stack(tables))

    begin_left = stack([stacked_left(contract_left(t)) for t in own_tables])
    finish_left = stack(
        [
            np.stack(
                [stacked_left(expand_left(t)[c * beads : (c + 1) * beads]) for c in range(3)]
            )
            for t in own_tables
        ]
    )
    contract_l = stack([stacked_left(contract_left(t), 2) for t in turned])
    expand_l = stack([stacked_left(expand_left(t)) for t in turned])
    motion = jnp.asarray(stacked_left(motion_table(BEADS, interval)))

    def lanes_of(x, start, size):
        return lax.dynamic_slice_in_dim(x, start, size, x.ndim - 1)

    def permutation(step, flip):
        return [
            (s * 2 + b, ((s + step(b)) % space_count) * 2 + (b ^ flip))
            for s in range(space_count)
            for b in range(2)
        ]

    def rims(x):
        up = [(i, (i + 1) % space_count) for i in range(space_count)]
        down = [((i + 1) % space_count, i) for i in range(space_count)]
        return (
            lax.ppermute(x[:, slab - rim :], "space", up),
            lax.ppermute(x[:, :rim], "space", down),
        )

    def relative(tile, info):
        x = tile - info[1] * slab_tiles
        x = jnp.where(x >= all_tiles - GT, x - all_tiles, x)
        return jnp.where(x < -GT, x + all_tiles, x)

    def spots_first(info):
        first = info[0] * (block_tiles - GT)
        outside = block_tiles + GT

        def spot(tile):
            x = relative(tile, info)
            right = jnp.where(x >= slab_tiles, x - slab_tiles + outside, x - first)
            return jnp.where(x < 0, x + GT + outside, right)

        return lambda t: t + info[0] * block_tiles, lambda t: t + info[0] * GT, spot

    def spots_inner(info):
        def spot(tile):
            return relative(tile, info) - info[0] * block_tiles

        return lambda t: t + GT + info[0] * block_tiles, lambda t: t + GT, spot

    def spots_outer(info):
        bead_at = 4 * GT
        far_at = bead_at + GT
        left_at = jnp.where(info[0] == 0, far_at, bead_at)
        right_at = jnp.where(info[0] == 0, bead_at, far_at)

        def own(t):
            return jnp.where(t < GT, t, t + block_tiles - 2 * GT)

        def place(x):
            return jnp.where(x < 2 * GT, x, x - (block_tiles - 4 * GT))

        def spot(tile):
            x = relative(tile, info) - info[0] * block_tiles
            right = jnp.where(x >= block_tiles, x - block_tiles + right_at, place(x))
            return jnp.where(x < 0, x + GT + left_at, right)

        return lambda t: own(t) + info[0] * block_tiles, lambda t: place(own(t)), spot

    def spots_slab(first):
        def spots(info):
            start = info[0] * block_tiles if first else 0

            def spot(tile):
                x = relative(tile, info)
                return jnp.where(x < 0, x + GT + slab_tiles, jnp.where(x >= slab_tiles, x + GT, x))

            return lambda t: t + start, lambda t: t + start, spot

        return spots

    pieces = [[] for _ in range(chunks)]
    if pair:
        mine, theirs, straight, across, *blocks = begin(
            chunks, bead_at, begin_left, strength, pos, mom
        )
        theirs = lax.ppermute(theirs, "bead", SWAP)
        straight = lax.ppermute(
            straight, ("space", "bead"), permutation(lambda b: -1 if b else 1, 0)
        )
        across = lax.ppermute(across, ("space", "bead"), permutation(lambda b: 1 if b else -1, 1))
        segments = [([mine, theirs], 0, block_tiles + GT), ([straight, across], 0, GT)]
        for chunk in range(chunks):
            other = lax.ppermute(blocks[chunks + chunk], "bead", SWAP)
            pieces[chunk] = [blocks[chunk], other]
        spots = spots_first
    else:
        part = partial_rows(bead_at, begin_left, strength, pos)
        summed = lax.psum(part, "bead")
        first_row = lax.broadcasted_iota(jnp.int32, summed.shape, 0) == 0
        summed = jnp.where(first_row, jnp.log2(strengths)[None, :], summed)
        segments = [([summed], 0, slab_tiles), *[([x], 0, GT) for x in rims(summed)]]
        spots = spots_slab(True)
        for chunk in range(chunks):
            parts = []
            for d in range(bead_count):
                start = jnp.mod(bead - d, bead_count) * block + chunk * lanes
                piece = jnp.concatenate(
                    [lanes_of(pos, start, lanes), lanes_of(mom, start, lanes)], 0
                )
                back = [(i, (i - d) % bead_count) for i in range(bead_count)]
                parts.append(lax.ppermute(piece, "bead", back) if d else piece)
            pieces[chunk] = [jnp.concatenate(parts, 1)]

    ends, hot = prepare(bead_at, bond_ends, angle_ends, block_tiles)
    force = pair_forces(spots, segments, block_tiles, bead_at, space_at, neighbour_tiles)

    own_out, returned, contracted = [], [], []
    for chunk in range(chunks):
        last = pair and chunk == chunks - 1
        outs = substeps(
            chunk, chunks, bead_at, pieces[chunk], force, mass, strength, ends, hot, motion,
            expand_l, contract_l, last, contracted[0] if contracted else None,
        )
        if last:
            *outs, bead_edge, far_edge = outs
        *outs, c16 = outs
        if not pair:
            outs = [outs[0][:, d * beads : (d + 1) * beads] for d in range(bead_count)]
        own_out.append(outs[0])
        contracted.append(c16)
        back = []
        for d in range(1, bead_count):
            on = [(i, (i + d) % bead_count) for i in range(bead_count)]
            back.append(lax.ppermute(outs[d], "bead", on))
        returned.append(back)

    if not pair:
        c16 = jnp.concatenate(contracted, 1) if chunks > 1 else contracted[0]
        everyone = lax.all_gather(c16, "bead", axis=1, tiled=True)
        segments = [([everyone], 0, slab_tiles), *[([x], 0, GT) for x in rims(everyone)]]
        force = pair_forces(
            spots_slab(False), segments, slab_tiles, bead_at, space_at, neighbour_tiles
        )
        parts = [x for chunk in range(chunks) for x in [own_out[chunk]] + returned[chunk]]
        new_pos, new_mom = finish(chunks, bead_at, parts, finish_left, force)
        return new_pos.transpose(1, 0, 2), new_mom.transpose(1, 0, 2)

    beside = lax.ppermute(bead_edge, "bead", SWAP)
    across = lax.ppermute(
        far_edge, ("space", "bead"), permutation(lambda b: 1 if b else -1, 1)
    )
    chunk_tiles = lanes // TILE
    segments = [([x], 0, chunk_tiles) for x in contracted]
    inner = pair_forces(
        spots_inner, segments, block_tiles - 2 * GT, bead_at, space_at, neighbour_tiles
    )
    segments = [
        ([contracted[0]], 0, 2 * GT),
        ([contracted[-1]], chunk_tiles - 2 * GT, 2 * GT),
        ([beside], 0, GT),
        ([across], 0, GT),
    ]
    outer = pair_forces(spots_outer, segments, 2 * GT, bead_at, space_at, neighbour_tiles)
    result = finish_block(bead_at, 0, own_out, finish_left, inner, outer, [])
    inner = lax.ppermute(inner, "bead", SWAP)
    outer = lax.ppermute(outer, "bead", SWAP)
    others = [x[0] for x in returned]
    new_pos, new_mom = finish_block(bead_at, 1, others, finish_left, inner, outer, result)
    return new_pos.transpose(1, 0, 2), new_mom.transpose(1, 0, 2)


SWAP = [(0, 1), (1, 0)]


def solution(mesh):
    placed = (
        P("bead", None, "space"),
        P("bead", None, "space"),
        P("space"),
        P("space"),
        P(None, "space"),
        P(None, "space"),
        P(None, "space"),
    )

    return jax.shard_map(
        body,
        mesh=mesh,
        in_specs=placed,
        out_specs=(P("bead", None, "space"), P("bead", None, "space")),
        check_vma=False,
    )
```

```python
import functools
import math

import jax
import jax.numpy as jnp
import numpy as np
from jax import lax
from jax.experimental import pallas as pl
from jax.experimental.pallas import tpu as pltpu
from jax.sharding import PartitionSpec as P


BEADS = 32
KEPT = 4
SUBS = 3
TILE = 128
GT = 2
BPT = 128
APT = 64
ROWS = 4 * KEPT

time_step = 0.3
spring_freq = 80.0
bond_stiff = 0.2
bond_rest = 1.0
angle_stiff = 0.1
angle_rest = 0.5
range_sq = 4.0
HIGH = lax.Precision.HIGHEST
IN_VMEM = pl.BlockSpec(memory_space=pltpu.VMEM)
IN_SMEM = pl.BlockSpec(memory_space=pltpu.SMEM)
IN_SPACE = pltpu.MemorySpace.VMEM


def near(x):
    return pltpu.with_memory_space_constraint(x, IN_SPACE)


def far(x):
    return pltpu.with_memory_space_constraint(x, pltpu.MemorySpace.HBM)


def vmem_out(shape, dtype):
    return IN_SPACE(shape, dtype)


PARAMS = pltpu.CompilerParams(vmem_limit_bytes=20 * 1024 * 1024)
COST = pl.CostEstimate(flops=10_000_000, bytes_accessed=100_000, transcendentals=0)
F32 = jnp.float32
BF16 = jnp.bfloat16


def mode_table(number):
    within = np.arange(number)
    result = np.zeros((number, number))
    for column in range(number):
        if column == 0:
            result[:, column] = 1.0 / math.sqrt(number)
        elif 2 * column < number:
            result[:, column] = math.sqrt(2.0 / number) * np.cos(
                2 * np.pi * within * column / number
            )
        elif 2 * column == number:
            result[:, column] = (-1.0) ** within / math.sqrt(number)
        else:
            result[:, column] = math.sqrt(2.0 / number) * np.sin(
                2 * np.pi * within * column / number
            )
    return result


def contract_table(number, kept):
    larger = mode_table(number)
    smaller = mode_table(kept)
    chosen = [column if 2 * column <= kept else number - kept + column for column in range(kept)]
    return math.sqrt(kept / number) * smaller @ larger[:, chosen].T


def motion_table(number, interval):
    freqs = 2.0 * spring_freq * np.sin(np.pi * np.arange(number) / number)
    modes = mode_table(number)
    safe = np.where(freqs > 0, freqs, 1.0)
    gains = np.where(freqs > 0, np.sin(freqs * interval) / safe, interval)
    drags = freqs * np.sin(freqs * interval)
    stay = modes @ np.diag(np.cos(freqs * interval)) @ modes.T
    gain = modes @ np.diag(gains) @ modes.T
    drag = modes @ np.diag(drags) @ modes.T
    return np.block([[stay, gain], [-drag, stay]])


def np_split(table, parts):
    out, rest = [], np.asarray(table, np.float64)
    for _ in range(parts):
        piece = rest.astype(np.float32).astype(jnp.bfloat16)
        out.append(piece)
        rest = rest - piece.astype(np.float64)
    return out


def stacked_left(table, parts=3):
    pieces = np_split(table, parts)
    zero = np.zeros_like(pieces[0])
    return np.concatenate(
        [
            np.concatenate([pieces[i]] * (parts - i) + [zero] * i, axis=1)
            for i in range(parts)
        ],
        axis=0,
    )


def split(x, parts):
    out = []
    for i in range(parts):
        piece = x.astype(BF16)
        out.append(piece)
        if i < parts - 1:
            x = x - piece.astype(F32)
    return out


def mm(left, right):
    return jnp.dot(left, right, preferred_element_type=F32)


def exact(left, x, parts=3):
    out = mm(left, jnp.concatenate(split(x, parts), axis=0))
    rows = out.shape[0] // parts
    total = out[:rows]
    for i in range(1, parts):
        total = total + out[i * rows : (i + 1) * rows]
    return total


def contract_rows(beads):
    table = contract_table(BEADS, KEPT)
    tables = []
    for turn in range(0, BEADS, beads):
        order = (np.arange(BEADS) + turn) % BEADS
        tables.append(table[:, order])
    return tables


def contract_left(table):
    out = np.zeros((ROWS, 3 * table.shape[1]))
    for c in range(KEPT):
        for k in range(3):
            out[4 * c + 1 + k, k * table.shape[1] : (k + 1) * table.shape[1]] = table[c]
    return out


def expand_left(table):
    return BEADS / KEPT * contract_left(table).T


def begin_kernel(chunks, bead, left, strengths, pos, mom, *refs):
    mine, theirs, straight = refs[:3]
    blocks = refs[3:-4]
    whole, table, rows, sems = refs[-4:]
    lanes = blocks[0].shape[2]
    slab = whole.shape[1]
    starts, copies = [], []
    for i in range(2 * chunks):
        owner = bead[0] if i < chunks else 1 - bead[0]
        starts.append(pl.multiple_of((owner * chunks + i % chunks) * lanes, TILE))
    for half, source in enumerate((pos, mom)):
        for i, block in enumerate(blocks):
            copy = pltpu.make_async_copy(
                source.at[:, :, pl.ds(starts[i], lanes)],
                block.at[pl.ds(3 * half, 3)],
                sems.at[half * len(blocks) + i],
            )
            copy.start()
            copies.append(copy)
    small = [
        pltpu.make_async_copy(left.at[bead[0]], table, sems.at[len(copies)]),
        pltpu.make_async_copy(strengths, rows, sems.at[len(copies) + 1]),
    ]
    for copy in small:
        copy.start()
    for copy in small:
        copy.wait()
    logs = math.log2(math.e) * jnp.log(rows[...])
    for t in range(slab // TILE):
        whole[0:1, t * TILE : (t + 1) * TILE] = logs[t : t + 1]
    for i, block in enumerate(blocks):
        copies[i].wait()
        x = jnp.concatenate([block[c] for c in range(3)], axis=0)
        where = pl.ds(starts[i], lanes)
        row = lax.broadcasted_iota(jnp.int32, (ROWS, lanes), 0)
        whole[:, where] = jnp.where(row == 0, whole[:, where], exact(table[...], x))

    block, rim = slab // 2, GT * TILE
    size = block + rim

    def sides(which):
        first, other = (0, block - rim) if which == 0 else (block - rim, 0)
        mine[...] = whole[:, first : first + size]
        theirs[:, :size] = whole[:, other : other + size]
        head, tail = whole[:, :rim], whole[:, slab - rim :]
        straight[...] = tail if which == 0 else head
        theirs[:, size:] = head if which == 0 else tail

    for which in range(2):
        pl.when(bead[0] == which)(functools.partial(sides, which))
    for copy in copies[len(blocks) :]:
        copy.wait()


def begin(chunks, bead, left, strengths, pos, mom):
    beads, slab = pos.shape[1:]
    block, rim = slab // 2, GT * TILE
    lanes = block // chunks
    shapes = [(ROWS, block + rim), (ROWS, block + 2 * rim), (ROWS, rim)]
    shapes += [(6, beads, lanes)] * (2 * chunks)
    return pl.pallas_call(
        functools.partial(begin_kernel, chunks),
        in_specs=[IN_SMEM] + [pl.BlockSpec(memory_space=pl.ANY)] * 4,
        out_specs=[IN_VMEM] * len(shapes),
        out_shape=[vmem_out(s, F32) for s in shapes],
        scratch_shapes=[
            pltpu.VMEM((ROWS, slab), F32),
            pltpu.VMEM(left.shape[1:], left.dtype),
            pltpu.VMEM(strengths.shape, F32),
            pltpu.SemaphoreType.DMA((4 * chunks + 2,)),
        ],
        compiler_params=PARAMS,
        cost_estimate=COST,
        name="begin",
    )(bead, far(left), far(strengths), far(pos), far(mom))


def partial_kernel(bead, left, strengths, pos, out):
    comps, _, lanes = pos.shape
    logs = math.log2(math.e) * jnp.log(strengths[...])
    logs = jnp.concatenate([logs[t : t + 1] for t in range(lanes // TILE)], axis=1)
    row = lax.broadcasted_iota(jnp.int32, (ROWS, lanes), 0)
    x = jnp.concatenate([pos[c] for c in range(comps)], axis=0)
    out[...] = jnp.where(row == 0, logs, exact(left[bead[0]], x))


def partial_rows(bead, left, strengths, pos):
    beads, slab = pos.shape[1:]
    lanes = math.gcd(slab, 1024)
    return pl.pallas_call(
        partial_kernel,
        grid=(slab // lanes,),
        in_specs=[
            IN_SMEM,
            IN_VMEM,
            pl.BlockSpec((lanes // TILE, TILE), lambda i: (i, 0)),
            pl.BlockSpec((3, beads, lanes), lambda i: (0, 0, i)),
        ],
        out_specs=pl.BlockSpec((ROWS, lanes), lambda i: (0, i)),
        out_shape=jax.ShapeDtypeStruct((ROWS, slab), F32),
        name="partial_rows",
    )(bead, left, strengths, pos)


def prepare_kernel(group, bead, bonds, angles, ends, hot):
    lane = lax.broadcasted_iota(jnp.int32, (1, TILE), 1)
    atom = lax.broadcasted_iota(jnp.int32, (TILE, 2 * TILE), 0)
    low = lane < APT

    def merge(first, second, odd):
        a = pltpu.roll(first, APT, 1) if odd else first
        b = second if odd else pltpu.roll(second, APT, 1)
        return jnp.where(low, a, b)

    def tiles(i, carry):
        at = (bead[0] * (hot.shape[0] // group) + i) * group
        bond_rows = bonds[:, pl.ds(pl.multiple_of(at * BPT, BPT), group * BPT)]
        angle_rows = angles[:, pl.ds(pl.multiple_of(at * APT, TILE), group * APT)]
        for t in range(group):
            one = bond_rows[0:1, t * TILE : (t + 1) * TILE]
            other = bond_rows[1:2, t * TILE : (t + 1) * TILE]
            odd = t % 2
            window = slice((t // 2) * TILE, (t // 2 + 1) * TILE)
            first, middle, last = [angle_rows[e : e + 1, window] for e in range(3)]
            outer = merge(first, last, odd)
            opposite = merge(last, first, odd)
            centre = merge(middle, middle, odd)
            ends[i * group + t] = jnp.concatenate([one, other, outer, centre], axis=0)
            gains = jnp.concatenate([other, centre], axis=1)
            losses = jnp.concatenate([one, opposite], axis=1)
            table = (atom == gains).astype(F32) - (atom == losses).astype(F32)
            hot[i * group + t] = table.astype(BF16)
        return carry

    lax.fori_loop(0, hot.shape[0] // group, tiles, 0)


def prepare(bead, bond_ends, angle_ends, block_tiles):
    return pl.pallas_call(
        functools.partial(prepare_kernel, math.gcd(block_tiles, 4)),
        in_specs=[IN_SMEM, IN_VMEM, IN_VMEM],
        out_specs=[IN_VMEM] * 2,
        out_shape=[
            vmem_out((block_tiles, 4, TILE), jnp.int32),
            vmem_out((block_tiles, TILE, 2 * TILE), BF16),
        ],
        compiler_params=PARAMS,
        cost_estimate=COST,
        name="prepare",
    )(bead, bond_ends, angle_ends)


def pair_kernel(spots, seg_sizes, own_count, bead, space, nbr, *refs):
    total = sum(n for *_, n in seg_sizes)
    count = sum(n for n, *_ in seg_sizes)
    seg_refs = refs[:count]
    out, feat_i, feat_m, feat_p, base, weights_a, weights_b = refs[count:]
    column, own_spot, spot = spots((bead[0], space[0]))
    row = lax.broadcasted_iota(jnp.int32, (ROWS, TILE), 0)
    slot = row % 4
    scale = math.sqrt(2.0 * math.log2(math.e) / range_sq)
    same = (
        lax.broadcasted_iota(jnp.int32, (ROWS, ROWS), 0) // 4
        == lax.broadcasted_iota(jnp.int32, (ROWS, ROWS), 1) // 4
    ).astype(F32)

    def features(tile, c16):
        base[tile] = c16
        logs = c16[0:1]
        place = jnp.where(slot == 0, 0.0, c16)
        scaled = place * scale
        high, low = [piece.astype(F32) for piece in split(scaled, 2)]
        square = jnp.dot(same, scaled * scaled, precision=HIGH, preferred_element_type=F32)
        half = -0.5 * square

        def three(x):
            a, b, c = [piece.astype(F32) for piece in split(x, 3)]
            return jnp.where(slot == 0, a, jnp.where(slot == 1, b, jnp.where(slot == 2, c, 0.0)))

        ones = jnp.where(slot == 3, 0.0, 1.0)
        mine = jnp.concatenate([high, high, low, low, three(half), ones], axis=0)
        theirs = jnp.concatenate(
            [high, low, high, low, ones, three(half + logs), ones, ones], axis=0
        )
        feat_i[tile] = mine.astype(BF16)
        feat_m[tile] = jnp.transpose(theirs, (1, 0)).astype(BF16)
        one = jnp.ones((ROWS, TILE), F32)
        p_high, p_low = [piece.astype(F32) for piece in split(place, 2)]
        feat_p[tile] = jnp.concatenate([one, p_high, p_low], axis=0).astype(BF16)

    tile = 0
    at = 0
    for number, begins, tiles in seg_sizes:
        group = seg_refs[at : at + number]
        at += number
        for i in range(begins, begins + tiles):
            c16 = group[0][:, i * TILE : (i + 1) * TILE]
            for other in group[1:]:
                more = other[:, i * TILE : (i + 1) * TILE]
                c16 = c16 + jnp.where(row == 0, 0.0, more)
            features(tile, c16)
            tile += 1
    assert tile == total

    groups = 6
    wide_row = lax.broadcasted_iota(jnp.int32, (groups * ROWS, TILE), 0)
    pick = [((wide_row % ROWS) // 4 == c).astype(BF16) for c in range(KEPT)]
    owner = row // 4

    def close(t, u):
        return spot(nbr[u, column(t)])

    def weigh(t, weights):
        features_i = feat_i[own_spot(t)]
        right = jnp.concatenate([features_i * pick[c] for c in range(KEPT)], axis=1)
        right = jnp.concatenate([right, jnp.zeros((2 * ROWS, KEPT * TILE), BF16)], axis=0)
        left = jnp.concatenate([feat_m[close(t, u)] for u in range(3)], axis=0)
        power = mm(left, right)
        for u in range(3):
            high, low = split(jnp.exp2(power[u * TILE : (u + 1) * TILE]), 2)
            weights[2 * u * TILE : (2 * u + 1) * TILE] = high
            weights[(2 * u + 1) * TILE : (2 * u + 2) * TILE] = low

    def pull(t, weights):
        left = []
        for u in range(3):
            piece = feat_p[close(t, u)]
            left += [piece, piece]
        total_p = mm(jnp.concatenate(left, axis=1), weights[...])
        sums = total_p[:ROWS]
        pulls = total_p[ROWS : 2 * ROWS] + total_p[2 * ROWS :]
        c16 = base[own_spot(t)]
        factor = (2.0 / range_sq) * jnp.exp2(c16[0:1])
        result = jnp.zeros((ROWS, TILE), F32)
        for c in range(KEPT):
            lanes = slice(c * TILE, (c + 1) * TILE)
            force = factor * (c16 * sums[:, lanes] - pulls[:, lanes])
            result = jnp.where((owner == c) & (slot > 0), force, result)
        out[:, pl.ds(pl.multiple_of(t * TILE, TILE), TILE)] = result

    weigh(0, weights_a)

    def two_tiles(i, carry):
        t = 2 * i
        weigh(t + 1, weights_b)
        pull(t, weights_a)
        weigh(jnp.minimum(t + 2, own_count - 1), weights_a)
        pull(t + 1, weights_b)
        return carry

    lax.fori_loop(0, own_count // 2, two_tiles, 0)


def pair_forces(spots, segments, own_count, bead, space, neighbour_tiles):
    sizes = tuple((len(group), start, tiles) for group, start, tiles in segments)
    total = sum(n for *_, n in sizes)
    assert own_count % 2 == 0
    flat = [array for group, *_ in segments for array in group]
    return pl.pallas_call(
        functools.partial(pair_kernel, spots, sizes, own_count),
        in_specs=[IN_SMEM] * 3 + [IN_VMEM] * len(flat),
        out_specs=IN_VMEM,
        out_shape=vmem_out((ROWS, own_count * TILE), F32),
        scratch_shapes=[
            pltpu.VMEM((total, 6 * ROWS, TILE), BF16),
            pltpu.VMEM((total, TILE, 8 * ROWS), BF16),
            pltpu.VMEM((total, 3 * ROWS, TILE), BF16),
            pltpu.VMEM((total, ROWS, TILE), F32),
            pltpu.VMEM((6 * TILE, KEPT * TILE), BF16),
            pltpu.VMEM((6 * TILE, KEPT * TILE), BF16),
        ],
        compiler_params=PARAMS,
        cost_estimate=COST,
        name="pair_forces",
    )(bead, space, far(neighbour_tiles), *[near(x) for x in flat])


def step_kernel(parts, chunk, chunks, group, edge, bead, *refs):
    pieces = refs[:parts]
    force, mass_rows, strength_rows, ends, hot, motion, expand, contract = refs[parts : parts + 8]
    before = refs[parts + 8] if edge and chunk else None
    outs = refs[len(refs) - parts - 1 - 2 * edge :]
    c_out = outs[parts]
    interval = time_step / SUBS
    width = group * TILE
    first = chunk * group
    motion_l = motion[...]

    def per_atom(rows):
        at = (bead[0] * chunks + chunk) * group
        return jnp.concatenate([rows[pl.ds(at + t, 1), :] for t in range(group)], axis=1)

    masses = per_atom(mass_rows)
    inverse = 1.0 / masses

    def gathered(plane):
        if parts == 1:
            return pieces[0][plane]
        return jnp.concatenate([piece[plane] for piece in pieces], axis=0)

    q = [gathered(c) for c in range(3)]
    p = [gathered(3 + c) for c in range(3)]
    kick = exact(expand[bead[0]], force[:, first * TILE : first * TILE + width])
    v = [
        (p[c] + 0.5 * time_step * kick[c * BEADS : (c + 1) * BEADS]) * inverse for c in range(3)
    ]
    places = []
    for t in range(group):
        places.append([jnp.broadcast_to(ends[first + t, e : e + 1], (3 * BEADS, TILE)) for e in range(4)])

    def take(x, index):
        return jnp.take_along_axis(x, index, axis=1, mode="promise_in_bounds")

    def bonded(q):
        forces = []
        for t in range(group):
            lanes = slice(t * TILE, (t + 1) * TILE)
            rows = jnp.concatenate([q[c][:, lanes] for c in range(3)], axis=0)
            one, other, outer, centre = places[t]
            stretch = take(rows, one) - take(rows, other)
            arms = take(rows, outer) - take(rows, centre)
            s = [stretch[c * BEADS : (c + 1) * BEADS] for c in range(3)]
            a = [arms[c * BEADS : (c + 1) * BEADS] for c in range(3)]
            length = s[0] * s[0] + s[1] * s[1] + s[2] * s[2]
            g = bond_stiff * (length - bond_rest)
            turned = [pltpu.roll(x, APT, 1) for x in a]
            inner = a[0] * turned[0] + a[1] * turned[1] + a[2] * turned[2]
            h = angle_stiff * (inner - angle_rest)
            bonds = jnp.concatenate([g * x for x in s], axis=0)
            angles = jnp.concatenate([h * x for x in a], axis=0)
            both = jnp.concatenate([bonds, angles], axis=1)
            out = lax.dot_general(
                jnp.concatenate(split(both, 2), axis=0),
                hot[first + t],
                (((1,), (1,)), ((), ())),
                preferred_element_type=F32,
            )
            forces.append(out[: 3 * BEADS] + out[3 * BEADS :])
        return [
            jnp.concatenate([f[c * BEADS : (c + 1) * BEADS] for f in forces], axis=1)
            for c in range(3)
        ]

    for sub in range(SUBS):
        pushed = bonded(q)
        factor = (0.5 if sub == 0 else 1.0) * interval * inverse
        v = [v[c] + factor * pushed[c] for c in range(3)]
        for c in range(3):
            moved = exact(motion_l, jnp.concatenate([q[c], v[c]], axis=0))
            q[c], v[c] = moved[:BEADS], moved[BEADS:]
    pushed = bonded(q)
    p = [masses * v[c] + (0.5 * interval) * pushed[c] for c in range(3)]
    beads = BEADS // parts
    for i in range(parts):
        for c in range(3):
            outs[i][c] = q[c][i * beads : (i + 1) * beads]
            outs[i][3 + c] = p[c][i * beads : (i + 1) * beads]
    rows = jnp.concatenate(q, axis=0)
    c16 = exact(contract[bead[0]], rows, 2)
    row = lax.broadcasted_iota(jnp.int32, (ROWS, width), 0)
    logs = math.log2(math.e) * jnp.log(per_atom(strength_rows))
    c16 = jnp.where(row == 0, logs, c16)
    c_out[...] = c16
    if edge:
        rim = GT * TILE
        head = c16[:, :rim] if before is None else before[:, :rim]
        tail = c16[:, width - rim :]
        outs[-2][...] = jnp.where(bead[0] == 0, tail, head)
        outs[-1][...] = jnp.where(bead[0] == 0, head, tail)


def substeps(chunk, chunks, bead, pieces, force, mass, strength, ends, hot, motion, expand, contract, edge, before):
    parts = len(pieces)
    lanes = pieces[0].shape[2]
    beads = BEADS // parts
    extra = [before] if edge and chunk else []
    shapes = [(6, beads, lanes)] * parts + [(ROWS, lanes)]
    if edge:
        shapes += [(ROWS, GT * TILE)] * 2
    return pl.pallas_call(
        functools.partial(step_kernel, parts, chunk, chunks, lanes // TILE, int(edge)),
        in_specs=[IN_SMEM] + [IN_VMEM] * (parts + 8 + len(extra)),
        out_specs=[IN_VMEM] * len(shapes),
        out_shape=[vmem_out(s, F32) for s in shapes],
        compiler_params=PARAMS,
        cost_estimate=COST,
        name="substeps",
    )(
        bead,
        *[near(x) for x in pieces + [force]],
        mass,
        strength,
        near(ends),
        near(hot),
        motion,
        expand,
        contract,
        *[near(x) for x in extra],
    )


def finish_kernel(chunks, bead, expand, force, *refs):
    pos, mom = refs[-2:]
    parts = refs[:-2]
    bead_count = len(parts) // chunks
    lanes = parts[0].shape[2]
    comp = pl.program_id(0)
    table = expand[bead[0], comp]
    for i, part in enumerate(parts):
        chunk, distance = divmod(i, bead_count)
        block = lax.rem(bead[0] + bead_count - distance, bead_count)
        start = pl.multiple_of(block * (chunks * lanes) + chunk * lanes, TILE)
        where = pl.ds(start, lanes)
        pos[0, :, where] = part[comp]
        mom[0, :, where] = part[3 + comp] + 0.5 * time_step * exact(table, force[:, where])


def finish(chunks, bead, parts, expand, force):
    slab = force.shape[1]
    beads = parts[0].shape[1]
    return pl.pallas_call(
        functools.partial(finish_kernel, chunks),
        grid=(3,),
        in_specs=[IN_SMEM] + [IN_VMEM] * (2 + len(parts)),
        out_specs=[pl.BlockSpec((1, beads, slab), lambda i: (i, 0, 0))] * 2,
        out_shape=[jax.ShapeDtypeStruct((3, beads, slab), F32)] * 2,
        compiler_params=PARAMS,
        cost_estimate=COST,
        name="finish",
    )(bead, expand, near(force), *[near(x) for x in parts])


def finish_block_kernel(chunks, owner, moves, count, bead, expand, inner, outer, *refs):
    parts = refs[:count]
    pos, mom, held, sems = refs[-4:]
    lanes = parts[0].shape[2]
    rim = GT * TILE
    blocks = [bead[0], 1 - bead[0]]

    def where(owner, chunk):
        return pl.ds(pl.multiple_of((blocks[owner] * chunks + chunk) * lanes, TILE), lanes)

    copies = []

    def copy(source, target):
        copies.append(pltpu.make_async_copy(source, target, sems.at[len(copies)]))
        copies[-1].start()

    for part, move_owner, chunk in moves:
        copy(parts[part].at[pl.ds(0, 3)], pos.at[:, :, where(move_owner, chunk)])
    force = jnp.concatenate([outer[:, :rim], inner[...], outer[:, rim:]], axis=1)
    for chunk in range(chunks):
        lane = slice(chunk * lanes, (chunk + 1) * lanes)
        for c in range(3):
            kick = 0.5 * time_step * exact(expand[bead[0], c], force[:, lane])
            held[c, :, lane] = parts[chunk][3 + c] + kick
        copy(held.at[:, :, pl.ds(chunk * lanes, lanes)], mom.at[:, :, where(owner, chunk)])
    for waiting in copies:
        waiting.wait()


def finish_block(chunks, owner, moves, bead, parts, expand, inner, outer, before):
    beads, lanes = parts[0].shape[1:]
    block = lanes * chunks
    anywhere = pl.BlockSpec(memory_space=pl.ANY)
    at = 4 + len(parts)
    return pl.pallas_call(
        functools.partial(finish_block_kernel, chunks, owner, moves, len(parts)),
        in_specs=[IN_SMEM] + [IN_VMEM] * (3 + len(parts)) + [anywhere] * len(before),
        out_specs=[anywhere] * 2,
        out_shape=[pltpu.MemorySpace.HBM((3, beads, 2 * block), F32)] * 2,
        scratch_shapes=[
            pltpu.VMEM((3, beads, block), F32),
            pltpu.SemaphoreType.DMA((len(moves) + chunks,)),
        ],
        input_output_aliases={at + i: i for i in range(len(before))},
        compiler_params=PARAMS,
        cost_estimate=COST,
        name="finish_block",
    )(
        bead,
        expand,
        near(inner),
        near(outer),
        *[near(x) for x in parts],
        *[far(x) for x in before],
    )


def body(positions, momenta, masses, strengths, bond_ends, angle_ends, neighbour_tiles):
    beads, _, slab = positions.shape
    bead_count = lax.axis_size("bead")
    bead = lax.axis_index("bead")
    space_count = lax.axis_size("space")
    space = lax.axis_index("space")
    block = slab // bead_count
    slab_tiles = slab // TILE
    block_tiles = block // TILE
    all_tiles = slab_tiles * space_count
    rim = GT * TILE
    chunks = 2 if block_tiles % 4 == 0 else 1
    lanes = block // chunks
    interval = time_step / SUBS
    pair = bead_count == 2

    pos = positions.transpose(1, 0, 2)
    mom = momenta.transpose(1, 0, 2)
    bead_at = jnp.reshape(bead, (1,)).astype(jnp.int32)
    space_at = jnp.reshape(space, (1,)).astype(jnp.int32)
    mass = masses.reshape(slab_tiles, TILE)
    strength = strengths.reshape(slab_tiles, TILE)
    turned = contract_rows(beads)
    table = contract_table(BEADS, KEPT)
    own_tables = [table[:, i * beads : (i + 1) * beads] for i in range(bead_count)]

    def stack(tables):
        return jnp.asarray(np.stack(tables))

    begin_left = stack([stacked_left(contract_left(t)) for t in own_tables])
    finish_left = stack(
        [
            np.stack(
                [stacked_left(expand_left(t)[c * beads : (c + 1) * beads]) for c in range(3)]
            )
            for t in own_tables
        ]
    )
    contract_l = stack([stacked_left(contract_left(t), 2) for t in turned])
    expand_l = stack([stacked_left(expand_left(t)) for t in turned])
    motion = jnp.asarray(stacked_left(motion_table(BEADS, interval)))

    def lanes_of(x, start, size):
        return lax.dynamic_slice_in_dim(x, start, size, x.ndim - 1)

    def permutation(step, flip):
        return [
            (s * 2 + b, ((s + step(b)) % space_count) * 2 + (b ^ flip))
            for s in range(space_count)
            for b in range(2)
        ]

    def rims(x):
        up = [(i, (i + 1) % space_count) for i in range(space_count)]
        down = [((i + 1) % space_count, i) for i in range(space_count)]
        return (
            lax.ppermute(x[:, slab - rim :], "space", up),
            lax.ppermute(x[:, :rim], "space", down),
        )

    def relative(tile, info):
        x = tile - info[1] * slab_tiles
        x = jnp.where(x >= all_tiles - GT, x - all_tiles, x)
        return jnp.where(x < -GT, x + all_tiles, x)

    def spots_first(info):
        first = info[0] * (block_tiles - GT)
        outside = block_tiles + GT

        def spot(tile):
            x = relative(tile, info)
            right = jnp.where(x >= slab_tiles, x - slab_tiles + outside, x - first)
            return jnp.where(x < 0, x + GT + outside, right)

        return lambda t: t + info[0] * block_tiles, lambda t: t + info[0] * GT, spot

    def spots_inner(info):
        def spot(tile):
            return relative(tile, info) - info[0] * block_tiles

        return lambda t: t + GT + info[0] * block_tiles, lambda t: t + GT, spot

    def spots_outer(info):
        bead_at = 4 * GT
        far_at = bead_at + GT
        left_at = jnp.where(info[0] == 0, far_at, bead_at)
        right_at = jnp.where(info[0] == 0, bead_at, far_at)

        def own(t):
            return jnp.where(t < GT, t, t + block_tiles - 2 * GT)

        def place(x):
            return jnp.where(x < 2 * GT, x, x - (block_tiles - 4 * GT))

        def spot(tile):
            x = relative(tile, info) - info[0] * block_tiles
            right = jnp.where(x >= block_tiles, x - block_tiles + right_at, place(x))
            return jnp.where(x < 0, x + GT + left_at, right)

        return lambda t: own(t) + info[0] * block_tiles, lambda t: place(own(t)), spot

    def spots_slab(first):
        def spots(info):
            start = info[0] * block_tiles if first else 0

            def spot(tile):
                x = relative(tile, info)
                return jnp.where(x < 0, x + GT + slab_tiles, jnp.where(x >= slab_tiles, x + GT, x))

            return lambda t: t + start, lambda t: t + start, spot

        return spots

    pieces = [[] for _ in range(chunks)]
    if pair:
        mine, theirs, straight, *blocks = begin(
            chunks, bead_at, begin_left, strength, pos, mom
        )
        theirs = lax.ppermute(theirs, "bead", SWAP)
        for chunk in range(chunks):
            other = lax.ppermute(blocks[chunks + chunk], "bead", SWAP)
            pieces[chunk] = [blocks[chunk], other]
        more = theirs[:, block + rim :]
        row = lax.broadcasted_iota(jnp.int32, more.shape, 0)
        straight = straight + jnp.where(row == 0, 0.0, more)
        straight = lax.ppermute(
            straight, ("space", "bead"), permutation(lambda b: -1 if b else 1, 0)
        )
        segments = [([mine, theirs], 0, block_tiles + GT), ([straight], 0, GT)]
        spots = spots_first
    else:
        part = partial_rows(bead_at, begin_left, strength, pos)
        summed = lax.psum(part, "bead")
        first_row = lax.broadcasted_iota(jnp.int32, summed.shape, 0) == 0
        summed = jnp.where(first_row, jnp.log2(strengths)[None, :], summed)
        segments = [([summed], 0, slab_tiles), *[([x], 0, GT) for x in rims(summed)]]
        spots = spots_slab(True)
        for chunk in range(chunks):
            parts = []
            for d in range(bead_count):
                start = jnp.mod(bead - d, bead_count) * block + chunk * lanes
                piece = jnp.concatenate(
                    [lanes_of(pos, start, lanes), lanes_of(mom, start, lanes)], 0
                )
                back = [(i, (i - d) % bead_count) for i in range(bead_count)]
                parts.append(lax.ppermute(piece, "bead", back) if d else piece)
            pieces[chunk] = [jnp.concatenate(parts, 1)]

    ends, hot = prepare(bead_at, bond_ends, angle_ends, block_tiles)
    force = pair_forces(spots, segments, block_tiles, bead_at, space_at, neighbour_tiles)

    own_out, returned, contracted = [], [], []
    for chunk in range(chunks):
        last = pair and chunk == chunks - 1
        outs = substeps(
            chunk, chunks, bead_at, pieces[chunk], force, mass, strength, ends, hot, motion,
            expand_l, contract_l, last, contracted[0] if contracted else None,
        )
        if last:
            *outs, bead_edge, far_edge = outs
        *outs, c16 = outs
        if not pair:
            outs = [outs[0][:, d * beads : (d + 1) * beads] for d in range(bead_count)]
        own_out.append(outs[0])
        contracted.append(c16)
        back = []
        for d in range(1, bead_count):
            on = [(i, (i + d) % bead_count) for i in range(bead_count)]
            back.append(lax.ppermute(outs[d], "bead", on))
        returned.append(back)

    if not pair:
        c16 = jnp.concatenate(contracted, 1) if chunks > 1 else contracted[0]
        everyone = lax.all_gather(c16, "bead", axis=1, tiled=True)
        segments = [([everyone], 0, slab_tiles), *[([x], 0, GT) for x in rims(everyone)]]
        force = pair_forces(
            spots_slab(False), segments, slab_tiles, bead_at, space_at, neighbour_tiles
        )
        parts = [x for chunk in range(chunks) for x in [own_out[chunk]] + returned[chunk]]
        new_pos, new_mom = finish(chunks, bead_at, parts, finish_left, force)
        return new_pos.transpose(1, 0, 2), new_mom.transpose(1, 0, 2)

    beside = lax.ppermute(bead_edge, "bead", SWAP)
    across = lax.ppermute(
        far_edge, ("space", "bead"), permutation(lambda b: 1 if b else -1, 1)
    )
    chunk_tiles = lanes // TILE
    segments = [([x], 0, chunk_tiles) for x in contracted]
    inner = pair_forces(
        spots_inner, segments, block_tiles - 2 * GT, bead_at, space_at, neighbour_tiles
    )
    segments = [
        ([contracted[0]], 0, 2 * GT),
        ([contracted[-1]], chunk_tiles - 2 * GT, 2 * GT),
        ([beside], 0, GT),
        ([across], 0, GT),
    ]
    outer = pair_forces(spots_outer, segments, 2 * GT, bead_at, space_at, neighbour_tiles)
    others = [x[0] for x in returned]
    moves = [(i, 0, i) for i in range(chunks)]
    moves += [(chunks + i, 1, i) for i in range(chunks - 1)]
    result = finish_block(
        chunks, 0, moves, bead_at, own_out + others[:-1], finish_left, inner, outer, []
    )
    inner = lax.ppermute(inner, "bead", SWAP)
    outer = lax.ppermute(outer, "bead", SWAP)
    moves = [(chunks - 1, 1, chunks - 1)]
    new_pos, new_mom = finish_block(
        chunks, 1, moves, bead_at, others, finish_left, inner, outer, result
    )
    return new_pos.transpose(1, 0, 2), new_mom.transpose(1, 0, 2)


SWAP = [(0, 1), (1, 0)]


def solution(mesh):
    placed = (
        P("bead", None, "space"),
        P("bead", None, "space"),
        P("space"),
        P("space"),
        P(None, "space"),
        P(None, "space"),
        P(None, "space"),
    )

    return jax.shard_map(
        body,
        mesh=mesh,
        in_specs=placed,
        out_specs=(P("bead", None, "space"), P("bead", None, "space")),
        check_vma=False,
    )
```

```python
import functools
import math

import jax
import jax.numpy as jnp
import numpy as np
from jax import lax
from jax.experimental import pallas as pl
from jax.experimental.pallas import tpu as pltpu
from jax.sharding import PartitionSpec as P


BEADS = 32
KEPT = 4
SUBS = 3
TILE = 128
GT = 2
BPT = 128
APT = 64
ROWS = 4 * KEPT

time_step = 0.3
spring_freq = 80.0
bond_stiff = 0.2
bond_rest = 1.0
angle_stiff = 0.1
angle_rest = 0.5
range_sq = 4.0
HIGH = lax.Precision.HIGHEST
IN_VMEM = pl.BlockSpec(memory_space=pltpu.VMEM)
IN_SMEM = pl.BlockSpec(memory_space=pltpu.SMEM)
IN_SPACE = pltpu.MemorySpace.VMEM


def near(x):
    return pltpu.with_memory_space_constraint(x, IN_SPACE)


def far(x):
    return pltpu.with_memory_space_constraint(x, pltpu.MemorySpace.HBM)


def vmem_out(shape, dtype):
    return IN_SPACE(shape, dtype)


PARAMS = pltpu.CompilerParams(vmem_limit_bytes=20 * 1024 * 1024)
COST = pl.CostEstimate(flops=10_000_000, bytes_accessed=100_000, transcendentals=0)
F32 = jnp.float32
BF16 = jnp.bfloat16


def mode_table(number):
    within = np.arange(number)
    result = np.zeros((number, number))
    for column in range(number):
        if column == 0:
            result[:, column] = 1.0 / math.sqrt(number)
        elif 2 * column < number:
            result[:, column] = math.sqrt(2.0 / number) * np.cos(
                2 * np.pi * within * column / number
            )
        elif 2 * column == number:
            result[:, column] = (-1.0) ** within / math.sqrt(number)
        else:
            result[:, column] = math.sqrt(2.0 / number) * np.sin(
                2 * np.pi * within * column / number
            )
    return result


def contract_table(number, kept):
    larger = mode_table(number)
    smaller = mode_table(kept)
    chosen = [column if 2 * column <= kept else number - kept + column for column in range(kept)]
    return math.sqrt(kept / number) * smaller @ larger[:, chosen].T


def motion_table(number, interval):
    freqs = 2.0 * spring_freq * np.sin(np.pi * np.arange(number) / number)
    modes = mode_table(number)
    safe = np.where(freqs > 0, freqs, 1.0)
    gains = np.where(freqs > 0, np.sin(freqs * interval) / safe, interval)
    drags = freqs * np.sin(freqs * interval)
    stay = modes @ np.diag(np.cos(freqs * interval)) @ modes.T
    gain = modes @ np.diag(gains) @ modes.T
    drag = modes @ np.diag(drags) @ modes.T
    return np.block([[stay, gain], [-drag, stay]])


def np_split(table, parts):
    out, rest = [], np.asarray(table, np.float64)
    for _ in range(parts):
        piece = rest.astype(np.float32).astype(jnp.bfloat16)
        out.append(piece)
        rest = rest - piece.astype(np.float64)
    return out


def stacked_left(table, parts=3):
    pieces = np_split(table, parts)
    zero = np.zeros_like(pieces[0])
    return np.concatenate(
        [
            np.concatenate([pieces[i]] * (parts - i) + [zero] * i, axis=1)
            for i in range(parts)
        ],
        axis=0,
    )


def split(x, parts):
    out = []
    for i in range(parts):
        piece = x.astype(BF16)
        out.append(piece)
        if i < parts - 1:
            x = x - piece.astype(F32)
    return out


def mm(left, right):
    return jnp.dot(left, right, preferred_element_type=F32)


def exact(left, x, parts=3):
    out = mm(left, jnp.concatenate(split(x, parts), axis=0))
    rows = out.shape[0] // parts
    total = out[:rows]
    for i in range(1, parts):
        total = total + out[i * rows : (i + 1) * rows]
    return total


def contract_rows(beads):
    table = contract_table(BEADS, KEPT)
    tables = []
    for turn in range(0, BEADS, beads):
        order = (np.arange(BEADS) + turn) % BEADS
        tables.append(table[:, order])
    return tables


def contract_left(table):
    out = np.zeros((ROWS, 3 * table.shape[1]))
    for c in range(KEPT):
        for k in range(3):
            out[4 * c + 1 + k, k * table.shape[1] : (k + 1) * table.shape[1]] = table[c]
    return out


def expand_left(table):
    return BEADS / KEPT * contract_left(table).T


def begin_kernel(chunks, bead, left, strengths, pos, *refs):
    mine, theirs, straight = refs[:3]
    blocks = refs[3:-4]
    whole, table, rows, sems = refs[-4:]
    lanes = blocks[0].shape[2]
    slab = whole.shape[1]
    starts, copies = [], []
    for i in range(2 * chunks):
        owner = bead[0] if i < chunks else 1 - bead[0]
        starts.append(pl.multiple_of((owner * chunks + i % chunks) * lanes, TILE))
    for i, block in enumerate(blocks):
        copy = pltpu.make_async_copy(
            pos.at[:, :, pl.ds(starts[i], lanes)], block.at[pl.ds(0, 3)], sems.at[i]
        )
        copy.start()
        copies.append(copy)
    small = [
        pltpu.make_async_copy(left.at[bead[0]], table, sems.at[len(copies)]),
        pltpu.make_async_copy(strengths, rows, sems.at[len(copies) + 1]),
    ]
    for copy in small:
        copy.start()
    for copy in small:
        copy.wait()
    logs = math.log2(math.e) * jnp.log(rows[...])
    for t in range(slab // TILE):
        whole[0:1, t * TILE : (t + 1) * TILE] = logs[t : t + 1]
    for i, block in enumerate(blocks):
        copies[i].wait()
        x = jnp.concatenate([block[c] for c in range(3)], axis=0)
        where = pl.ds(starts[i], lanes)
        row = lax.broadcasted_iota(jnp.int32, (ROWS, lanes), 0)
        whole[:, where] = jnp.where(row == 0, whole[:, where], exact(table[...], x))

    block, rim = slab // 2, GT * TILE
    size = block + rim

    def sides(which):
        first, other = (0, block - rim) if which == 0 else (block - rim, 0)
        mine[...] = whole[:, first : first + size]
        theirs[:, :size] = whole[:, other : other + size]
        head, tail = whole[:, :rim], whole[:, slab - rim :]
        straight[...] = tail if which == 0 else head
        theirs[:, size:] = head if which == 0 else tail

    for which in range(2):
        pl.when(bead[0] == which)(functools.partial(sides, which))


def fetch_kernel(chunks, bead, mom, *refs):
    blocks = refs[2 * chunks : 4 * chunks]
    sems = refs[-1]
    lanes = blocks[0].shape[2]
    copies = []
    for i, block in reversed(list(enumerate(blocks))):
        owner = bead[0] if i < chunks else 1 - bead[0]
        start = pl.multiple_of((owner * chunks + i % chunks) * lanes, TILE)
        copy = pltpu.make_async_copy(
            mom.at[:, :, pl.ds(start, lanes)], block.at[pl.ds(3, 3)], sems.at[i]
        )
        copy.start()
        copies.append(copy)
    for copy in copies:
        copy.wait()


def fetch(chunks, bead, mom, blocks):
    return pl.pallas_call(
        functools.partial(fetch_kernel, chunks),
        in_specs=[IN_SMEM] + [pl.BlockSpec(memory_space=pl.ANY)] + [IN_VMEM] * len(blocks),
        out_specs=[IN_VMEM] * len(blocks),
        out_shape=[vmem_out(x.shape, F32) for x in blocks],
        scratch_shapes=[pltpu.SemaphoreType.DMA((len(blocks),))],
        input_output_aliases={2 + i: i for i in range(len(blocks))},
        compiler_params=PARAMS,
        cost_estimate=COST,
        name="fetch",
    )(bead, far(mom), *[near(x) for x in blocks])


def begin(chunks, bead, left, strengths, pos):
    beads, slab = pos.shape[1:]
    block, rim = slab // 2, GT * TILE
    lanes = block // chunks
    shapes = [(ROWS, block + rim), (ROWS, block + 2 * rim), (ROWS, rim)]
    shapes += [(6, beads, lanes)] * (2 * chunks)
    return pl.pallas_call(
        functools.partial(begin_kernel, chunks),
        in_specs=[IN_SMEM] + [pl.BlockSpec(memory_space=pl.ANY)] * 3,
        out_specs=[IN_VMEM] * len(shapes),
        out_shape=[vmem_out(s, F32) for s in shapes],
        scratch_shapes=[
            pltpu.VMEM((ROWS, slab), F32),
            pltpu.VMEM(left.shape[1:], left.dtype),
            pltpu.VMEM(strengths.shape, F32),
            pltpu.SemaphoreType.DMA((2 * chunks + 2,)),
        ],
        compiler_params=PARAMS,
        cost_estimate=COST,
        name="begin",
    )(bead, far(left), far(strengths), far(pos))


def partial_kernel(bead, left, strengths, pos, out):
    comps, _, lanes = pos.shape
    logs = math.log2(math.e) * jnp.log(strengths[...])
    logs = jnp.concatenate([logs[t : t + 1] for t in range(lanes // TILE)], axis=1)
    row = lax.broadcasted_iota(jnp.int32, (ROWS, lanes), 0)
    x = jnp.concatenate([pos[c] for c in range(comps)], axis=0)
    out[...] = jnp.where(row == 0, logs, exact(left[bead[0]], x))


def partial_rows(bead, left, strengths, pos):
    beads, slab = pos.shape[1:]
    lanes = math.gcd(slab, 1024)
    return pl.pallas_call(
        partial_kernel,
        grid=(slab // lanes,),
        in_specs=[
            IN_SMEM,
            IN_VMEM,
            pl.BlockSpec((lanes // TILE, TILE), lambda i: (i, 0)),
            pl.BlockSpec((3, beads, lanes), lambda i: (0, 0, i)),
        ],
        out_specs=pl.BlockSpec((ROWS, lanes), lambda i: (0, i)),
        out_shape=jax.ShapeDtypeStruct((ROWS, slab), F32),
        name="partial_rows",
    )(bead, left, strengths, pos)


def prepare_kernel(group, bead, bonds, angles, ends, hot):
    lane = lax.broadcasted_iota(jnp.int32, (1, TILE), 1)
    atom = lax.broadcasted_iota(jnp.int32, (TILE, 2 * TILE), 0)
    low = lane < APT

    def merge(first, second, odd):
        a = pltpu.roll(first, APT, 1) if odd else first
        b = second if odd else pltpu.roll(second, APT, 1)
        return jnp.where(low, a, b)

    def tiles(i, carry):
        at = (bead[0] * (hot.shape[0] // group) + i) * group
        bond_rows = bonds[:, pl.ds(pl.multiple_of(at * BPT, BPT), group * BPT)]
        angle_rows = angles[:, pl.ds(pl.multiple_of(at * APT, TILE), group * APT)]
        for t in range(group):
            one = bond_rows[0:1, t * TILE : (t + 1) * TILE]
            other = bond_rows[1:2, t * TILE : (t + 1) * TILE]
            odd = t % 2
            window = slice((t // 2) * TILE, (t // 2 + 1) * TILE)
            first, middle, last = [angle_rows[e : e + 1, window] for e in range(3)]
            outer = merge(first, last, odd)
            opposite = merge(last, first, odd)
            centre = merge(middle, middle, odd)
            ends[i * group + t] = jnp.concatenate([one, other, outer, centre], axis=0)
            gains = jnp.concatenate([other, centre], axis=1)
            losses = jnp.concatenate([one, opposite], axis=1)
            table = (atom == gains).astype(F32) - (atom == losses).astype(F32)
            hot[i * group + t] = table.astype(BF16)
        return carry

    lax.fori_loop(0, hot.shape[0] // group, tiles, 0)


def prepare(bead, bond_ends, angle_ends, block_tiles):
    return pl.pallas_call(
        functools.partial(prepare_kernel, math.gcd(block_tiles, 4)),
        in_specs=[IN_SMEM, IN_VMEM, IN_VMEM],
        out_specs=[IN_VMEM] * 2,
        out_shape=[
            vmem_out((block_tiles, 4, TILE), jnp.int32),
            vmem_out((block_tiles, TILE, 2 * TILE), BF16),
        ],
        compiler_params=PARAMS,
        cost_estimate=COST,
        name="prepare",
    )(bead, bond_ends, angle_ends)


def pair_kernel(spots, seg_sizes, own_count, bead, space, nbr, *refs):
    total = sum(n for *_, n in seg_sizes)
    count = sum(n for n, *_ in seg_sizes)
    seg_refs = refs[:count]
    out, feat_i, feat_m, feat_p, base, weights_a, weights_b = refs[count:]
    column, own_spot, spot = spots((bead[0], space[0]))
    row = lax.broadcasted_iota(jnp.int32, (ROWS, TILE), 0)
    slot = row % 4
    scale = math.sqrt(2.0 * math.log2(math.e) / range_sq)
    same = (
        lax.broadcasted_iota(jnp.int32, (ROWS, ROWS), 0) // 4
        == lax.broadcasted_iota(jnp.int32, (ROWS, ROWS), 1) // 4
    ).astype(F32)

    def features(tile, c16):
        base[tile] = c16
        logs = c16[0:1]
        place = jnp.where(slot == 0, 0.0, c16)
        scaled = place * scale
        high, low = [piece.astype(F32) for piece in split(scaled, 2)]
        square = jnp.dot(same, scaled * scaled, precision=HIGH, preferred_element_type=F32)
        half = -0.5 * square

        def three(x):
            a, b, c = [piece.astype(F32) for piece in split(x, 3)]
            return jnp.where(slot == 0, a, jnp.where(slot == 1, b, jnp.where(slot == 2, c, 0.0)))

        ones = jnp.where(slot == 3, 0.0, 1.0)
        mine = jnp.concatenate([high, high, low, low, three(half), ones], axis=0)
        theirs = jnp.concatenate(
            [high, low, high, low, ones, three(half + logs), ones, ones], axis=0
        )
        feat_i[tile] = mine.astype(BF16)
        feat_m[tile] = jnp.transpose(theirs, (1, 0)).astype(BF16)
        one = jnp.ones((ROWS, TILE), F32)
        p_high, p_low = [piece.astype(F32) for piece in split(place, 2)]
        feat_p[tile] = jnp.concatenate([one, p_high, p_low], axis=0).astype(BF16)

    tile = 0
    at = 0
    for number, begins, tiles in seg_sizes:
        group = seg_refs[at : at + number]
        at += number
        for i in range(begins, begins + tiles):
            c16 = group[0][:, i * TILE : (i + 1) * TILE]
            for other in group[1:]:
                more = other[:, i * TILE : (i + 1) * TILE]
                c16 = c16 + jnp.where(row == 0, 0.0, more)
            features(tile, c16)
            tile += 1
    assert tile == total

    groups = 6
    wide_row = lax.broadcasted_iota(jnp.int32, (groups * ROWS, TILE), 0)
    pick = [((wide_row % ROWS) // 4 == c).astype(BF16) for c in range(KEPT)]
    owner = row // 4

    def close(t, u):
        return spot(nbr[u, column(t)])

    def weigh(t, weights):
        features_i = feat_i[own_spot(t)]
        right = jnp.concatenate([features_i * pick[c] for c in range(KEPT)], axis=1)
        right = jnp.concatenate([right, jnp.zeros((2 * ROWS, KEPT * TILE), BF16)], axis=0)
        left = jnp.concatenate([feat_m[close(t, u)] for u in range(3)], axis=0)
        power = mm(left, right)
        for u in range(3):
            high, low = split(jnp.exp2(power[u * TILE : (u + 1) * TILE]), 2)
            weights[2 * u * TILE : (2 * u + 1) * TILE] = high
            weights[(2 * u + 1) * TILE : (2 * u + 2) * TILE] = low

    def pull(t, weights):
        left = []
        for u in range(3):
            piece = feat_p[close(t, u)]
            left += [piece, piece]
        total_p = mm(jnp.concatenate(left, axis=1), weights[...])
        sums = total_p[:ROWS]
        pulls = total_p[ROWS : 2 * ROWS] + total_p[2 * ROWS :]
        c16 = base[own_spot(t)]
        factor = (2.0 / range_sq) * jnp.exp2(c16[0:1])
        result = jnp.zeros((ROWS, TILE), F32)
        for c in range(KEPT):
            lanes = slice(c * TILE, (c + 1) * TILE)
            force = factor * (c16 * sums[:, lanes] - pulls[:, lanes])
            result = jnp.where((owner == c) & (slot > 0), force, result)
        out[:, pl.ds(pl.multiple_of(t * TILE, TILE), TILE)] = result

    weigh(0, weights_a)

    def two_tiles(i, carry):
        t = 2 * i
        weigh(t + 1, weights_b)
        pull(t, weights_a)
        weigh(jnp.minimum(t + 2, own_count - 1), weights_a)
        pull(t + 1, weights_b)
        return carry

    lax.fori_loop(0, own_count // 2, two_tiles, 0)


def pair_forces(spots, segments, own_count, bead, space, neighbour_tiles):
    sizes = tuple((len(group), start, tiles) for group, start, tiles in segments)
    total = sum(n for *_, n in sizes)
    assert own_count % 2 == 0
    flat = [array for group, *_ in segments for array in group]
    return pl.pallas_call(
        functools.partial(pair_kernel, spots, sizes, own_count),
        in_specs=[IN_SMEM] * 3 + [IN_VMEM] * len(flat),
        out_specs=IN_VMEM,
        out_shape=vmem_out((ROWS, own_count * TILE), F32),
        scratch_shapes=[
            pltpu.VMEM((total, 6 * ROWS, TILE), BF16),
            pltpu.VMEM((total, TILE, 8 * ROWS), BF16),
            pltpu.VMEM((total, 3 * ROWS, TILE), BF16),
            pltpu.VMEM((total, ROWS, TILE), F32),
            pltpu.VMEM((6 * TILE, KEPT * TILE), BF16),
            pltpu.VMEM((6 * TILE, KEPT * TILE), BF16),
        ],
        compiler_params=PARAMS,
        cost_estimate=COST,
        name="pair_forces",
    )(bead, space, far(neighbour_tiles), *[near(x) for x in flat])


def whole_force(inner, outer):
    rim = GT * TILE
    return jnp.concatenate([outer[:, :rim], inner[...], outer[:, rim:]], axis=1)


def step_kernel(parts, forces, chunk, chunks, group, edge, bead, *refs):
    pieces = refs[:parts]
    force = refs[parts] if forces == 1 else whole_force(*refs[parts : parts + 2])
    at = parts + forces
    mass_rows, strength_rows, ends, hot, motion, expand, contract = refs[at : at + 7]
    before = refs[at + 7] if edge and chunk else None
    outs = refs[len(refs) - parts - 1 - 2 * edge :]
    c_out = outs[parts]
    interval = time_step / SUBS
    width = group * TILE
    first = chunk * group
    motion_l = motion[...]

    def per_atom(rows):
        at = (bead[0] * chunks + chunk) * group
        return jnp.concatenate([rows[pl.ds(at + t, 1), :] for t in range(group)], axis=1)

    masses = per_atom(mass_rows)
    inverse = 1.0 / masses

    def gathered(plane):
        if parts == 1:
            return pieces[0][plane]
        return jnp.concatenate([piece[plane] for piece in pieces], axis=0)

    q = [gathered(c) for c in range(3)]
    p = [gathered(3 + c) for c in range(3)]
    kick = exact(expand[bead[0]], force[:, first * TILE : first * TILE + width])
    v = [
        (p[c] + 0.5 * time_step * kick[c * BEADS : (c + 1) * BEADS]) * inverse for c in range(3)
    ]
    places = []
    for t in range(group):
        places.append([jnp.broadcast_to(ends[first + t, e : e + 1], (3 * BEADS, TILE)) for e in range(4)])

    def take(x, index):
        return jnp.take_along_axis(x, index, axis=1, mode="promise_in_bounds")

    def bonded(q):
        forces = []
        for t in range(group):
            lanes = slice(t * TILE, (t + 1) * TILE)
            rows = jnp.concatenate([q[c][:, lanes] for c in range(3)], axis=0)
            one, other, outer, centre = places[t]
            stretch = take(rows, one) - take(rows, other)
            arms = take(rows, outer) - take(rows, centre)
            s = [stretch[c * BEADS : (c + 1) * BEADS] for c in range(3)]
            a = [arms[c * BEADS : (c + 1) * BEADS] for c in range(3)]
            length = s[0] * s[0] + s[1] * s[1] + s[2] * s[2]
            g = bond_stiff * (length - bond_rest)
            turned = [pltpu.roll(x, APT, 1) for x in a]
            inner = a[0] * turned[0] + a[1] * turned[1] + a[2] * turned[2]
            h = angle_stiff * (inner - angle_rest)
            bonds = jnp.concatenate([g * x for x in s], axis=0)
            angles = jnp.concatenate([h * x for x in a], axis=0)
            both = jnp.concatenate([bonds, angles], axis=1)
            out = lax.dot_general(
                jnp.concatenate(split(both, 2), axis=0),
                hot[first + t],
                (((1,), (1,)), ((), ())),
                preferred_element_type=F32,
            )
            forces.append(out[: 3 * BEADS] + out[3 * BEADS :])
        return [
            jnp.concatenate([f[c * BEADS : (c + 1) * BEADS] for f in forces], axis=1)
            for c in range(3)
        ]

    for sub in range(SUBS):
        pushed = bonded(q)
        factor = (0.5 if sub == 0 else 1.0) * interval * inverse
        v = [v[c] + factor * pushed[c] for c in range(3)]
        for c in range(3):
            moved = exact(motion_l, jnp.concatenate([q[c], v[c]], axis=0))
            q[c], v[c] = moved[:BEADS], moved[BEADS:]
    pushed = bonded(q)
    p = [masses * v[c] + (0.5 * interval) * pushed[c] for c in range(3)]
    beads = BEADS // parts
    for i in range(parts):
        for c in range(3):
            outs[i][c] = q[c][i * beads : (i + 1) * beads]
            outs[i][3 + c] = p[c][i * beads : (i + 1) * beads]
    rows = jnp.concatenate(q, axis=0)
    c16 = exact(contract[bead[0]], rows, 2)
    row = lax.broadcasted_iota(jnp.int32, (ROWS, width), 0)
    logs = math.log2(math.e) * jnp.log(per_atom(strength_rows))
    c16 = jnp.where(row == 0, logs, c16)
    c_out[...] = c16
    if edge:
        rim = GT * TILE
        head = c16[:, :rim] if before is None else before[:, :rim]
        tail = c16[:, width - rim :]
        outs[-2][...] = jnp.where(bead[0] == 0, tail, head)
        outs[-1][...] = jnp.where(bead[0] == 0, head, tail)


def substeps(chunk, chunks, bead, pieces, force, mass, strength, ends, hot, motion, expand, contract, edge, before):
    parts = len(pieces)
    lanes = pieces[0].shape[2]
    beads = BEADS // parts
    extra = [before] if edge and chunk else []
    shapes = [(6, beads, lanes)] * parts + [(ROWS, lanes)]
    if edge:
        shapes += [(ROWS, GT * TILE)] * 2
    return pl.pallas_call(
        functools.partial(
            step_kernel, parts, len(force), chunk, chunks, lanes // TILE, int(edge)
        ),
        in_specs=[IN_SMEM] + [IN_VMEM] * (parts + len(force) + 7 + len(extra)),
        out_specs=[IN_VMEM] * len(shapes),
        out_shape=[vmem_out(s, F32) for s in shapes],
        compiler_params=PARAMS,
        cost_estimate=COST,
        name="substeps",
    )(
        bead,
        *[near(x) for x in pieces + force],
        mass,
        strength,
        near(ends),
        near(hot),
        motion,
        expand,
        contract,
        *[near(x) for x in extra],
    )


def finish_kernel(chunks, bead, expand, force, *refs):
    pos, mom = refs[-2:]
    parts = refs[:-2]
    bead_count = len(parts) // chunks
    lanes = parts[0].shape[2]
    comp = pl.program_id(0)
    table = expand[bead[0], comp]
    for i, part in enumerate(parts):
        chunk, distance = divmod(i, bead_count)
        block = lax.rem(bead[0] + bead_count - distance, bead_count)
        start = pl.multiple_of(block * (chunks * lanes) + chunk * lanes, TILE)
        where = pl.ds(start, lanes)
        pos[0, :, where] = part[comp]
        mom[0, :, where] = part[3 + comp] + 0.5 * time_step * exact(table, force[:, where])


def finish(chunks, bead, parts, expand, force):
    slab = force.shape[1]
    beads = parts[0].shape[1]
    return pl.pallas_call(
        functools.partial(finish_kernel, chunks),
        grid=(3,),
        in_specs=[IN_SMEM] + [IN_VMEM] * (2 + len(parts)),
        out_specs=[pl.BlockSpec((1, beads, slab), lambda i: (i, 0, 0))] * 2,
        out_shape=[jax.ShapeDtypeStruct((3, beads, slab), F32)] * 2,
        compiler_params=PARAMS,
        cost_estimate=COST,
        name="finish",
    )(bead, expand, near(force), *[near(x) for x in parts])


def finish_block_kernel(chunks, owner, moves, count, bead, expand, inner, outer, *refs):
    parts = refs[:count]
    pos, mom, held, sems = refs[-4:]
    lanes = parts[0].shape[2]
    blocks = [bead[0], 1 - bead[0]]

    def where(owner, chunk):
        return pl.ds(pl.multiple_of((blocks[owner] * chunks + chunk) * lanes, TILE), lanes)

    copies = []

    def copy(source, target):
        copies.append(pltpu.make_async_copy(source, target, sems.at[len(copies)]))
        copies[-1].start()

    for part, move_owner, chunk in moves:
        copy(parts[part].at[pl.ds(0, 3)], pos.at[:, :, where(move_owner, chunk)])
    force = whole_force(inner, outer)
    for chunk in range(chunks):
        lane = slice(chunk * lanes, (chunk + 1) * lanes)
        for c in range(3):
            kick = 0.5 * time_step * exact(expand[bead[0], c], force[:, lane])
            held[c, :, lane] = parts[chunk][3 + c] + kick
        copy(held.at[:, :, pl.ds(chunk * lanes, lanes)], mom.at[:, :, where(owner, chunk)])
    for waiting in copies:
        waiting.wait()


def finish_block(chunks, owner, moves, bead, parts, expand, inner, outer, before):
    beads, lanes = parts[0].shape[1:]
    block = lanes * chunks
    anywhere = pl.BlockSpec(memory_space=pl.ANY)
    at = 4 + len(parts)
    return pl.pallas_call(
        functools.partial(finish_block_kernel, chunks, owner, moves, len(parts)),
        in_specs=[IN_SMEM] + [IN_VMEM] * (3 + len(parts)) + [anywhere] * len(before),
        out_specs=[anywhere] * 2,
        out_shape=[pltpu.MemorySpace.HBM((3, beads, 2 * block), F32)] * 2,
        scratch_shapes=[
            pltpu.VMEM((3, beads, block), F32),
            pltpu.SemaphoreType.DMA((len(moves) + chunks,)),
        ],
        input_output_aliases={at + i: i for i in range(len(before))},
        compiler_params=PARAMS,
        cost_estimate=COST,
        name="finish_block",
    )(
        bead,
        expand,
        near(inner),
        near(outer),
        *[near(x) for x in parts],
        *[far(x) for x in before],
    )


def body(positions, momenta, masses, strengths, bond_ends, angle_ends, neighbour_tiles):
    beads, _, slab = positions.shape
    bead_count = lax.axis_size("bead")
    bead = lax.axis_index("bead")
    space_count = lax.axis_size("space")
    space = lax.axis_index("space")
    block = slab // bead_count
    slab_tiles = slab // TILE
    block_tiles = block // TILE
    all_tiles = slab_tiles * space_count
    rim = GT * TILE
    chunks = 2 if block_tiles % 4 == 0 else 1
    lanes = block // chunks
    interval = time_step / SUBS
    pair = bead_count == 2

    pos = positions.transpose(1, 0, 2)
    mom = momenta.transpose(1, 0, 2)
    bead_at = jnp.reshape(bead, (1,)).astype(jnp.int32)
    space_at = jnp.reshape(space, (1,)).astype(jnp.int32)
    mass = masses.reshape(slab_tiles, TILE)
    strength = strengths.reshape(slab_tiles, TILE)
    turned = contract_rows(beads)
    table = contract_table(BEADS, KEPT)
    own_tables = [table[:, i * beads : (i + 1) * beads] for i in range(bead_count)]

    def stack(tables):
        return jnp.asarray(np.stack(tables))

    begin_left = stack([stacked_left(contract_left(t)) for t in own_tables])
    finish_left = stack(
        [
            np.stack(
                [stacked_left(expand_left(t)[c * beads : (c + 1) * beads]) for c in range(3)]
            )
            for t in own_tables
        ]
    )
    contract_l = stack([stacked_left(contract_left(t), 2) for t in turned])
    expand_l = stack([stacked_left(expand_left(t)) for t in turned])
    motion = jnp.asarray(stacked_left(motion_table(BEADS, interval)))

    def lanes_of(x, start, size):
        return lax.dynamic_slice_in_dim(x, start, size, x.ndim - 1)

    def permutation(step, flip):
        return [
            (s * 2 + b, ((s + step(b)) % space_count) * 2 + (b ^ flip))
            for s in range(space_count)
            for b in range(2)
        ]

    def rims(x):
        up = [(i, (i + 1) % space_count) for i in range(space_count)]
        down = [((i + 1) % space_count, i) for i in range(space_count)]
        return (
            lax.ppermute(x[:, slab - rim :], "space", up),
            lax.ppermute(x[:, :rim], "space", down),
        )

    def relative(tile, info):
        x = tile - info[1] * slab_tiles
        x = jnp.where(x >= all_tiles - GT, x - all_tiles, x)
        return jnp.where(x < -GT, x + all_tiles, x)

    def spots_first(inner):
        def spots(info):
            first = info[0] * (block_tiles - GT)
            outside = block_tiles + GT

            def own(t):
                return t + GT if inner else jnp.where(t < GT, t, t + block_tiles - 2 * GT)

            def spot(tile):
                x = relative(tile, info)
                right = jnp.where(x >= slab_tiles, x - slab_tiles + outside, x - first)
                return jnp.where(x < 0, x + GT + outside, right)

            return lambda t: own(t) + info[0] * block_tiles, lambda t: own(t) + info[0] * GT, spot

        return spots

    def spots_inner(info):
        def spot(tile):
            return relative(tile, info) - info[0] * block_tiles

        return lambda t: t + GT + info[0] * block_tiles, lambda t: t + GT, spot

    def spots_outer(info):
        bead_at = 4 * GT
        far_at = bead_at + GT
        left_at = jnp.where(info[0] == 0, far_at, bead_at)
        right_at = jnp.where(info[0] == 0, bead_at, far_at)

        def own(t):
            return jnp.where(t < GT, t, t + block_tiles - 2 * GT)

        def place(x):
            return jnp.where(x < 2 * GT, x, x - (block_tiles - 4 * GT))

        def spot(tile):
            x = relative(tile, info) - info[0] * block_tiles
            right = jnp.where(x >= block_tiles, x - block_tiles + right_at, place(x))
            return jnp.where(x < 0, x + GT + left_at, right)

        return lambda t: own(t) + info[0] * block_tiles, lambda t: place(own(t)), spot

    def spots_slab(first):
        def spots(info):
            start = info[0] * block_tiles if first else 0

            def spot(tile):
                x = relative(tile, info)
                return jnp.where(x < 0, x + GT + slab_tiles, jnp.where(x >= slab_tiles, x + GT, x))

            return lambda t: t + start, lambda t: t + start, spot

        return spots

    pieces = [[] for _ in range(chunks)]
    if pair:
        mine, theirs, straight, *blocks = begin(
            chunks, bead_at, begin_left, strength, pos
        )
        theirs = lax.ppermute(theirs, "bead", SWAP)
        blocks = fetch(chunks, bead_at, mom, blocks)
        for chunk in range(chunks):
            other = lax.ppermute(blocks[chunks + chunk], "bead", SWAP)
            pieces[chunk] = [blocks[chunk], other]
        more = theirs[:, block + rim :]
        row = lax.broadcasted_iota(jnp.int32, more.shape, 0)
        straight = straight + jnp.where(row == 0, 0.0, more)
        straight = lax.ppermute(
            straight, ("space", "bead"), permutation(lambda b: -1 if b else 1, 0)
        )
        inside = [([mine, theirs], 0, block_tiles + GT)]
        rim_tiles = [([straight], 0, GT)]
    else:
        part = partial_rows(bead_at, begin_left, strength, pos)
        summed = lax.psum(part, "bead")
        first_row = lax.broadcasted_iota(jnp.int32, summed.shape, 0) == 0
        summed = jnp.where(first_row, jnp.log2(strengths)[None, :], summed)
        segments = [([summed], 0, slab_tiles), *[([x], 0, GT) for x in rims(summed)]]
        spots = spots_slab(True)
        for chunk in range(chunks):
            parts = []
            for d in range(bead_count):
                start = jnp.mod(bead - d, bead_count) * block + chunk * lanes
                piece = jnp.concatenate(
                    [lanes_of(pos, start, lanes), lanes_of(mom, start, lanes)], 0
                )
                back = [(i, (i - d) % bead_count) for i in range(bead_count)]
                parts.append(lax.ppermute(piece, "bead", back) if d else piece)
            pieces[chunk] = [jnp.concatenate(parts, 1)]

    ends, hot = prepare(bead_at, bond_ends, angle_ends, block_tiles)
    if pair:
        ids = bead_at, space_at, neighbour_tiles
        inner = pair_forces(spots_first(True), inside, block_tiles - 2 * GT, *ids)
        outer = pair_forces(spots_first(False), inside + rim_tiles, 2 * GT, *ids)
        force = [inner, outer]
    else:
        force = [pair_forces(spots, segments, block_tiles, bead_at, space_at, neighbour_tiles)]

    own_out, returned, contracted = [], [], []
    for chunk in range(chunks):
        last = pair and chunk == chunks - 1
        outs = substeps(
            chunk, chunks, bead_at, pieces[chunk], force, mass, strength, ends, hot, motion,
            expand_l, contract_l, last, contracted[0] if contracted else None,
        )
        if last:
            *outs, bead_edge, far_edge = outs
        *outs, c16 = outs
        if not pair:
            outs = [outs[0][:, d * beads : (d + 1) * beads] for d in range(bead_count)]
        own_out.append(outs[0])
        contracted.append(c16)
        back = []
        for d in range(1, bead_count):
            on = [(i, (i + d) % bead_count) for i in range(bead_count)]
            back.append(lax.ppermute(outs[d], "bead", on))
        returned.append(back)

    if not pair:
        c16 = jnp.concatenate(contracted, 1) if chunks > 1 else contracted[0]
        everyone = lax.all_gather(c16, "bead", axis=1, tiled=True)
        segments = [([everyone], 0, slab_tiles), *[([x], 0, GT) for x in rims(everyone)]]
        force = pair_forces(
            spots_slab(False), segments, slab_tiles, bead_at, space_at, neighbour_tiles
        )
        parts = [x for chunk in range(chunks) for x in [own_out[chunk]] + returned[chunk]]
        new_pos, new_mom = finish(chunks, bead_at, parts, finish_left, force)
        return new_pos.transpose(1, 0, 2), new_mom.transpose(1, 0, 2)

    beside = lax.ppermute(bead_edge, "bead", SWAP)
    across = lax.ppermute(
        far_edge, ("space", "bead"), permutation(lambda b: 1 if b else -1, 1)
    )
    chunk_tiles = lanes // TILE
    segments = [([x], 0, chunk_tiles) for x in contracted]
    inner = pair_forces(
        spots_inner, segments, block_tiles - 2 * GT, bead_at, space_at, neighbour_tiles
    )
    segments = [
        ([contracted[0]], 0, 2 * GT),
        ([contracted[-1]], chunk_tiles - 2 * GT, 2 * GT),
        ([beside], 0, GT),
        ([across], 0, GT),
    ]
    outer = pair_forces(spots_outer, segments, 2 * GT, bead_at, space_at, neighbour_tiles)
    others = [x[0] for x in returned]
    moves = [(i, 0, i) for i in range(chunks)]
    moves += [(chunks + i, 1, i) for i in range(chunks - 1)]
    result = finish_block(
        chunks, 0, moves, bead_at, own_out + others[:-1], finish_left, inner, outer, []
    )
    inner = lax.ppermute(inner, "bead", SWAP)
    outer = lax.ppermute(outer, "bead", SWAP)
    moves = [(chunks - 1, 1, chunks - 1)]
    new_pos, new_mom = finish_block(
        chunks, 1, moves, bead_at, others, finish_left, inner, outer, result
    )
    return new_pos.transpose(1, 0, 2), new_mom.transpose(1, 0, 2)


SWAP = [(0, 1), (1, 0)]


def solution(mesh):
    placed = (
        P("bead", None, "space"),
        P("bead", None, "space"),
        P("space"),
        P("space"),
        P(None, "space"),
        P(None, "space"),
        P(None, "space"),
    )

    return jax.shard_map(
        body,
        mesh=mesh,
        in_specs=placed,
        out_specs=(P("bead", None, "space"), P("bead", None, "space")),
        check_vma=False,
    )
```

```python
import functools
import math

import jax
import jax.numpy as jnp
import numpy as np
from jax import lax
from jax.experimental import pallas as pl
from jax.experimental.pallas import tpu as pltpu
from jax.sharding import PartitionSpec as P


BEADS = 32
KEPT = 4
SUBS = 3
TILE = 128
GT = 2
BPT = 128
APT = 64
ROWS = 4 * KEPT
LOGS = 3 * KEPT

time_step = 0.3
spring_freq = 80.0
bond_stiff = 0.2
bond_rest = 1.0
angle_stiff = 0.1
angle_rest = 0.5
range_sq = 4.0
HIGH = lax.Precision.HIGHEST
IN_VMEM = pl.BlockSpec(memory_space=pltpu.VMEM)
IN_SMEM = pl.BlockSpec(memory_space=pltpu.SMEM)
IN_SPACE = pltpu.MemorySpace.VMEM


def near(x):
    return pltpu.with_memory_space_constraint(x, IN_SPACE)


def far(x):
    return pltpu.with_memory_space_constraint(x, pltpu.MemorySpace.HBM)


def vmem_out(shape, dtype):
    return IN_SPACE(shape, dtype)


PARAMS = pltpu.CompilerParams(vmem_limit_bytes=20 * 1024 * 1024)
COST = pl.CostEstimate(flops=10_000_000, bytes_accessed=100_000, transcendentals=0)
F32 = jnp.float32
BF16 = jnp.bfloat16


def mode_table(number):
    within = np.arange(number)
    result = np.zeros((number, number))
    for column in range(number):
        if column == 0:
            result[:, column] = 1.0 / math.sqrt(number)
        elif 2 * column < number:
            result[:, column] = math.sqrt(2.0 / number) * np.cos(
                2 * np.pi * within * column / number
            )
        elif 2 * column == number:
            result[:, column] = (-1.0) ** within / math.sqrt(number)
        else:
            result[:, column] = math.sqrt(2.0 / number) * np.sin(
                2 * np.pi * within * column / number
            )
    return result


def contract_table(number, kept):
    larger = mode_table(number)
    smaller = mode_table(kept)
    chosen = [column if 2 * column <= kept else number - kept + column for column in range(kept)]
    return math.sqrt(kept / number) * smaller @ larger[:, chosen].T


def motion_table(number, interval):
    freqs = 2.0 * spring_freq * np.sin(np.pi * np.arange(number) / number)
    modes = mode_table(number)
    safe = np.where(freqs > 0, freqs, 1.0)
    gains = np.where(freqs > 0, np.sin(freqs * interval) / safe, interval)
    drags = freqs * np.sin(freqs * interval)
    stay = modes @ np.diag(np.cos(freqs * interval)) @ modes.T
    gain = modes @ np.diag(gains) @ modes.T
    drag = modes @ np.diag(drags) @ modes.T
    return np.block([[stay, gain], [-drag, stay]])


def np_split(table, parts):
    out, rest = [], np.asarray(table, np.float64)
    for _ in range(parts):
        piece = rest.astype(np.float32).astype(jnp.bfloat16)
        out.append(piece)
        rest = rest - piece.astype(np.float64)
    return out


def stacked_left(table, parts=3):
    pieces = np_split(table, parts)
    zero = np.zeros_like(pieces[0])
    return np.concatenate(
        [
            np.concatenate([pieces[i]] * (parts - i) + [zero] * i, axis=1)
            for i in range(parts)
        ],
        axis=0,
    )


def split(x, parts):
    out = []
    for i in range(parts):
        piece = x.astype(BF16)
        out.append(piece)
        if i < parts - 1:
            x = x - piece.astype(F32)
    return out


def mm(left, right):
    return jnp.dot(left, right, preferred_element_type=F32)


def exact(left, x, parts=3):
    out = mm(left, jnp.concatenate(split(x, parts), axis=0))
    rows = out.shape[0] // parts
    total = out[:rows]
    for i in range(1, parts):
        total = total + out[i * rows : (i + 1) * rows]
    return total


def packed_left(table):
    high, mid, low = np_split(table, 3)
    zero = np.zeros_like(high)
    return np.concatenate(
        [
            np.concatenate([high, high, high, mid], axis=1),
            np.concatenate([low, mid, zero, zero], axis=1),
        ],
        axis=0,
    )


def packed_exact(left, x):
    high, mid, low = split(x, 3)
    out = mm(left, jnp.concatenate([high, mid, low, high], axis=0))
    rows = out.shape[0] // 2
    return out[:rows] + out[rows:]


def contract_rows(beads):
    table = contract_table(BEADS, KEPT)
    tables = []
    for turn in range(0, BEADS, beads):
        order = (np.arange(BEADS) + turn) % BEADS
        tables.append(table[:, order])
    return tables


def contract_left(table):
    out = np.zeros((ROWS, 3 * table.shape[1]))
    for c in range(KEPT):
        for k in range(3):
            out[k * KEPT + c, k * table.shape[1] : (k + 1) * table.shape[1]] = table[c]
    return out


def expand_left(table):
    return BEADS / KEPT * contract_left(table).T


def pack_rows(target, x):
    lanes = x.shape[1]
    target[:, :lanes] = x[:8]
    target[:4, lanes:] = x[8:12, : lanes // 2]
    target[4:, lanes:] = x[8:12, lanes // 2 :]


def unpacked(x):
    lanes = x.shape[1] * 2 // 3
    last = jnp.concatenate([x[:4, lanes:], x[4:, lanes:]], axis=1)
    return jnp.concatenate([x[:, :lanes], last, jnp.zeros_like(last)], axis=0)


def begin_kernel(chunks, bead, left, strengths, pos, *refs):
    mine, theirs, straight = refs[:3]
    blocks = refs[3:-4]
    whole, table, rows, sems = refs[-4:]
    lanes = blocks[0].shape[2]
    slab = whole.shape[1]
    starts, copies = [], []
    for i in range(2 * chunks):
        owner = bead[0] if i < chunks else 1 - bead[0]
        starts.append(pl.multiple_of((owner * chunks + i % chunks) * lanes, TILE))
    for i, block in enumerate(blocks):
        copy = pltpu.make_async_copy(
            pos.at[:, :, pl.ds(starts[i], lanes)], block, sems.at[i]
        )
        copy.start()
        copies.append(copy)
    small = [
        pltpu.make_async_copy(left.at[bead[0]], table, sems.at[len(copies)]),
        pltpu.make_async_copy(strengths, rows, sems.at[len(copies) + 1]),
    ]
    for copy in small:
        copy.start()
    for copy in small:
        copy.wait()
    logs = math.log2(math.e) * jnp.log(rows[...])
    for t in range(slab // TILE):
        whole[LOGS : LOGS + 1, t * TILE : (t + 1) * TILE] = logs[t : t + 1]
    for i, block in enumerate(blocks):
        copies[i].wait()
        x = jnp.concatenate([block[c] for c in range(3)], axis=0)
        where = pl.ds(starts[i], lanes)
        row = lax.broadcasted_iota(jnp.int32, (ROWS, lanes), 0)
        whole[:, where] = jnp.where(row == LOGS, whole[:, where], exact(table[...], x))

    block, rim = slab // 2, GT * TILE
    size = block + rim

    def sides(which):
        first, other = (0, block - rim) if which == 0 else (block - rim, 0)
        mine[...] = whole[:, first : first + size]
        head, tail = whole[:, :rim], whole[:, slab - rim :]
        straight[...] = tail if which == 0 else head
        relay = head if which == 0 else tail
        pack_rows(theirs, jnp.concatenate([whole[:, other : other + size], relay], axis=1))

    for which in range(2):
        pl.when(bead[0] == which)(functools.partial(sides, which))


def fetch_kernel(chunks, bead, mom, *refs):
    *blocks, sems = refs
    lanes = blocks[0].shape[2]
    copies = []
    for i, block in reversed(list(enumerate(blocks))):
        owner = bead[0] if i < chunks else 1 - bead[0]
        start = pl.multiple_of((owner * chunks + i % chunks) * lanes, TILE)
        copy = pltpu.make_async_copy(mom.at[:, :, pl.ds(start, lanes)], block, sems.at[i])
        copy.start()
        copies.append(copy)
    for copy in copies:
        copy.wait()


def fetch(chunks, bead, mom):
    beads, slab = mom.shape[1:]
    count = 2 * chunks
    return pl.pallas_call(
        functools.partial(fetch_kernel, chunks),
        in_specs=[IN_SMEM, pl.BlockSpec(memory_space=pl.ANY)],
        out_specs=[IN_VMEM] * count,
        out_shape=[vmem_out((3, beads, slab // count), F32)] * count,
        scratch_shapes=[pltpu.SemaphoreType.DMA((count,))],
        compiler_params=PARAMS,
        cost_estimate=COST,
        name="fetch",
    )(bead, far(mom))


def begin(chunks, bead, left, strengths, pos):
    beads, slab = pos.shape[1:]
    block, rim = slab // 2, GT * TILE
    lanes = block // chunks
    shapes = [(ROWS, block + rim), (8, 3 * (block + 2 * rim) // 2), (ROWS, rim)]
    shapes += [(3, beads, lanes)] * (2 * chunks)
    return pl.pallas_call(
        functools.partial(begin_kernel, chunks),
        in_specs=[IN_SMEM] + [pl.BlockSpec(memory_space=pl.ANY)] * 3,
        out_specs=[IN_VMEM] * len(shapes),
        out_shape=[vmem_out(s, F32) for s in shapes],
        scratch_shapes=[
            pltpu.VMEM((ROWS, slab), F32),
            pltpu.VMEM(left.shape[1:], left.dtype),
            pltpu.VMEM(strengths.shape, F32),
            pltpu.SemaphoreType.DMA((2 * chunks + 2,)),
        ],
        compiler_params=PARAMS,
        cost_estimate=COST,
        name="begin",
    )(bead, far(left), far(strengths), far(pos))


def relay_kernel(own, received, out):
    rim = GT * TILE
    size = received.shape[1] * 2 // 3
    more = jnp.concatenate([received[:, size - rim : size], received[4:, -rim:]], axis=0)
    out[...] = own[...] + jnp.concatenate([more, jnp.zeros_like(more[:4])], axis=0)


def relay(own, received):
    return pl.pallas_call(
        relay_kernel,
        in_specs=[IN_VMEM] * 2,
        out_specs=IN_VMEM,
        out_shape=vmem_out(own.shape, F32),
        compiler_params=PARAMS,
        cost_estimate=COST,
        name="relay",
    )(near(own), near(received))


def partial_kernel(bead, left, strengths, pos, out):
    comps, _, lanes = pos.shape
    logs = math.log2(math.e) * jnp.log(strengths[...])
    logs = jnp.concatenate([logs[t : t + 1] for t in range(lanes // TILE)], axis=1)
    row = lax.broadcasted_iota(jnp.int32, (ROWS, lanes), 0)
    x = jnp.concatenate([pos[c] for c in range(comps)], axis=0)
    out[...] = jnp.where(row == LOGS, logs, exact(left[bead[0]], x))


def partial_rows(bead, left, strengths, pos):
    beads, slab = pos.shape[1:]
    lanes = math.gcd(slab, 1024)
    return pl.pallas_call(
        partial_kernel,
        grid=(slab // lanes,),
        in_specs=[
            IN_SMEM,
            IN_VMEM,
            pl.BlockSpec((lanes // TILE, TILE), lambda i: (i, 0)),
            pl.BlockSpec((3, beads, lanes), lambda i: (0, 0, i)),
        ],
        out_specs=pl.BlockSpec((ROWS, lanes), lambda i: (0, i)),
        out_shape=jax.ShapeDtypeStruct((ROWS, slab), F32),
        name="partial_rows",
    )(bead, left, strengths, pos)


def prepare_kernel(group, bead, bonds, angles, hot):
    lane = lax.broadcasted_iota(jnp.int32, (1, TILE), 1)
    atom = lax.broadcasted_iota(jnp.int32, (TILE, 2 * TILE), 0)
    low = lane < APT

    def merge(first, second, odd):
        a = pltpu.roll(first, APT, 1) if odd else first
        b = second if odd else pltpu.roll(second, APT, 1)
        return jnp.where(low, a, b)

    def tiles(i, carry):
        at = (bead[0] * (hot.shape[0] // group) + i) * group
        bond_rows = bonds[:, pl.ds(pl.multiple_of(at * BPT, BPT), group * BPT)]
        angle_rows = angles[:, pl.ds(pl.multiple_of(at * APT, TILE), group * APT)]
        for t in range(group):
            one = bond_rows[0:1, t * TILE : (t + 1) * TILE]
            other = bond_rows[1:2, t * TILE : (t + 1) * TILE]
            odd = t % 2
            window = slice((t // 2) * TILE, (t // 2 + 1) * TILE)
            first, middle, last = [angle_rows[e : e + 1, window] for e in range(3)]
            opposite = merge(last, first, odd)
            centre = merge(middle, middle, odd)
            gains = jnp.concatenate([other, centre], axis=1)
            losses = jnp.concatenate([one, opposite], axis=1)
            table = (atom == gains).astype(F32) - (atom == losses).astype(F32)
            hot[i * group + t] = table.astype(BF16)
        return carry

    lax.fori_loop(0, hot.shape[0] // group, tiles, 0)


def prepare(bead, bond_ends, angle_ends, block_tiles):
    return pl.pallas_call(
        functools.partial(prepare_kernel, math.gcd(block_tiles, 4)),
        in_specs=[IN_SMEM, IN_VMEM, IN_VMEM],
        out_specs=IN_VMEM,
        out_shape=vmem_out((block_tiles, TILE, 2 * TILE), BF16),
        compiler_params=PARAMS,
        cost_estimate=COST,
        name="prepare",
    )(bead, bond_ends, angle_ends)


def pair_kernel(spots, seg_sizes, own_count, packed, bead, space, nbr, *refs):
    total = sum(n for *_, n in seg_sizes)
    count = sum(n for n, *_ in seg_sizes)
    seg_refs = refs[:count]
    target, feat_i, feat_m, feat_p, base, *weights, held = refs[count:]
    out = held if packed else target
    column, own_spot, spot = spots((bead[0], space[0]))
    row = lax.broadcasted_iota(jnp.int32, (ROWS, TILE), 0)
    slot = row // KEPT
    scale = math.sqrt(2.0 * math.log2(math.e) / range_sq)
    same = (
        lax.broadcasted_iota(jnp.int32, (ROWS, ROWS), 0) % KEPT
        == lax.broadcasted_iota(jnp.int32, (ROWS, ROWS), 1) % KEPT
    ).astype(F32)

    def features(tile, c16):
        base[tile] = c16
        logs = c16[LOGS : LOGS + 1]
        place = jnp.where(slot == 3, 0.0, c16)
        scaled = place * scale
        high, low = [piece.astype(F32) for piece in split(scaled, 2)]
        square = jnp.dot(same, scaled * scaled, precision=HIGH, preferred_element_type=F32)
        half = -0.5 * square

        def three(x):
            a, b, c = [piece.astype(F32) for piece in split(x, 3)]
            return jnp.where(slot == 0, a, jnp.where(slot == 1, b, jnp.where(slot == 2, c, 0.0)))

        ones = jnp.where(slot == 3, 0.0, 1.0)
        mine = jnp.concatenate([high, high, low, low, three(half), ones], axis=0)
        theirs = jnp.concatenate(
            [high, low, high, low, ones, three(half + logs), ones, ones], axis=0
        )
        feat_i[tile] = mine.astype(BF16)
        feat_m[tile] = jnp.transpose(theirs, (1, 0)).astype(BF16)
        one = jnp.ones((ROWS, TILE), F32)
        p_high, p_low = [piece.astype(F32) for piece in split(place, 2)]
        feat_p[tile] = jnp.concatenate([one, p_high, p_low], axis=0).astype(BF16)

    def piece(ref, begins, i):
        moving = callable(begins)
        at = (begins(bead[0]) if moving else begins) + i

        def lanes(tile):
            if moving:
                return pl.ds(pl.multiple_of(tile * TILE, TILE), TILE)
            return slice(tile * TILE, (tile + 1) * TILE)

        if ref.shape[0] == ROWS:
            return ref[:, lanes(at)]
        tiles = ref.shape[1] * 2 // 3 // TILE
        half = tiles // 2
        upper = at >= half
        last = ref[:, lanes(tiles + jnp.where(upper, at - half, at))]
        last = jnp.where(upper, last[4:], last[:4])
        return jnp.concatenate([ref[:, lanes(at)], last, jnp.zeros_like(last)], axis=0)

    tile = 0
    at = 0
    for number, begins, tiles in seg_sizes:
        group = seg_refs[at : at + number]
        at += number
        for i in range(tiles):
            c16 = piece(group[0], begins, i)
            for other in group[1:]:
                c16 = c16 + piece(other, begins, i)
            features(tile, c16)
            tile += 1
    assert tile == total

    groups = 6
    wide_row = lax.broadcasted_iota(jnp.int32, (groups * ROWS, TILE), 0)
    pick = [(wide_row % KEPT == c).astype(BF16) for c in range(KEPT)]
    owner = row % KEPT

    def close(t, u):
        return spot(nbr[u, column(t)])

    def weigh(t, weights):
        features_i = feat_i[own_spot(t)]
        right = jnp.concatenate([features_i * pick[c] for c in range(KEPT)], axis=1)
        right = jnp.concatenate([right, jnp.zeros((2 * ROWS, KEPT * TILE), BF16)], axis=0)
        left = jnp.concatenate([feat_m[close(t, u)] for u in range(3)], axis=0)
        power = mm(left, right)
        for u in range(3):
            high, low = split(jnp.exp2(power[u * TILE : (u + 1) * TILE]), 2)
            weights[2 * u * TILE : (2 * u + 1) * TILE] = high
            weights[(2 * u + 1) * TILE : (2 * u + 2) * TILE] = low

    def pull(t, weights):
        left = []
        for u in range(3):
            piece = feat_p[close(t, u)]
            left += [piece, piece]
        total_p = mm(jnp.concatenate(left, axis=1), weights[...])
        sums = total_p[:ROWS]
        pulls = total_p[ROWS : 2 * ROWS] + total_p[2 * ROWS :]
        c16 = base[own_spot(t)]
        factor = (2.0 / range_sq) * jnp.exp2(c16[LOGS : LOGS + 1])
        result = jnp.zeros((ROWS, TILE), F32)
        for c in range(KEPT):
            lanes = slice(c * TILE, (c + 1) * TILE)
            force = factor * (c16 * sums[:, lanes] - pulls[:, lanes])
            result = jnp.where((owner == c) & (slot < 3), force, result)
        lane = t * TILE if isinstance(t, int) else pl.multiple_of(t * TILE, TILE)
        out[:, pl.ds(lane, TILE)] = result

    unroll = math.gcd(own_count, 4)
    weigh(0, weights[0])

    def some_tiles(t, last):
        for j in range(unroll):
            if not (last and j == unroll - 1):
                weigh(t + j + 1, weights[(j + 1) % 2])
            pull(t + j, weights[j % 2])

    def loop(i, carry):
        some_tiles(unroll * i, False)
        return carry

    lax.fori_loop(0, own_count // unroll - 1, loop, 0)
    some_tiles(own_count - unroll, True)
    if packed:
        pack_rows(target, held[...])


def pair_forces(spots, segments, own_count, bead, space, neighbour_tiles, packed=False):
    sizes = tuple((len(group), start, tiles) for group, start, tiles in segments)
    total = sum(n for *_, n in sizes)
    assert own_count % 2 == 0
    flat = [array for group, *_ in segments for array in group]
    return pl.pallas_call(
        functools.partial(pair_kernel, spots, sizes, own_count, packed),
        in_specs=[IN_SMEM] * 3 + [IN_VMEM] * len(flat),
        out_specs=IN_VMEM,
        out_shape=vmem_out(
            (8, 3 * own_count * TILE // 2) if packed else (ROWS, own_count * TILE), F32
        ),
        scratch_shapes=[
            pltpu.VMEM((total, 6 * ROWS, TILE), BF16),
            pltpu.VMEM((total, TILE, 8 * ROWS), BF16),
            pltpu.VMEM((total, 3 * ROWS, TILE), BF16),
            pltpu.VMEM((total, ROWS, TILE), F32),
            pltpu.VMEM((6 * TILE, KEPT * TILE), BF16),
            pltpu.VMEM((6 * TILE, KEPT * TILE), BF16),
            pltpu.VMEM((ROWS, own_count * TILE), F32),
        ],
        compiler_params=PARAMS,
        cost_estimate=COST,
        name="pair_forces",
    )(bead, space, far(neighbour_tiles), *[near(x) for x in flat])


def whole_force(inner, outer):
    rim = GT * TILE
    inner, outer = unpacked(inner[...]), unpacked(outer[...])
    return jnp.concatenate([outer[:, :rim], inner, outer[:, rim:]], axis=1)


def step_kernel(parts, forces, chunk, chunks, group, edge, bead, *refs):
    pieces = refs[: 2 * parts]
    at = 2 * parts
    force = refs[at] if forces == 1 else whole_force(*refs[at : at + 2])
    at += forces
    mass_rows, strength_rows, hot, motion, expand, contract = refs[at : at + 6]
    before = refs[at + 6] if edge and chunk else None
    outs = refs[len(refs) - parts - 1 - 2 * edge :]
    c_out = outs[parts]
    interval = time_step / SUBS
    width = group * TILE
    first = chunk * group
    motion_l = motion[...]

    def per_atom(rows):
        at = (bead[0] * chunks + chunk) * group
        return jnp.concatenate([rows[pl.ds(at + t, 1), :] for t in range(group)], axis=1)

    masses = per_atom(mass_rows)
    inverse = 1.0 / masses

    def gathered(kind, c):
        if parts == 1:
            return pieces[kind][c]
        return jnp.concatenate([piece[c] for piece in pieces[kind::2]], axis=0)

    q = [gathered(0, c) for c in range(3)]
    p = [gathered(1, c) for c in range(3)]
    kick = exact(expand[bead[0]], force[:, first * TILE : first * TILE + width])
    v = [
        (p[c] + 0.5 * time_step * kick[c * BEADS : (c + 1) * BEADS]) * inverse for c in range(3)
    ]

    def bonded(q):
        forces = []
        for t in range(group):
            lanes = slice(t * TILE, (t + 1) * TILE)
            rows = jnp.concatenate([q[c][:, lanes] for c in range(3)], axis=0)
            seen = mm(jnp.concatenate(split(rows, 2), axis=0), hot[first + t])
            seen = seen[: 3 * BEADS] + seen[3 * BEADS :]
            stretch, arms = seen[:, :TILE], seen[:, TILE:]
            s = [stretch[c * BEADS : (c + 1) * BEADS] for c in range(3)]
            a = [arms[c * BEADS : (c + 1) * BEADS] for c in range(3)]
            length = s[0] * s[0] + s[1] * s[1] + s[2] * s[2]
            g = bond_stiff * (bond_rest - length)
            turned = [pltpu.roll(x, APT, 1) for x in a]
            inner = a[0] * turned[0] + a[1] * turned[1] + a[2] * turned[2]
            h = angle_stiff * (angle_rest - inner)
            bonds = jnp.concatenate([g * x for x in s], axis=0)
            angles = jnp.concatenate([h * x for x in turned], axis=0)
            both = jnp.concatenate([bonds, angles], axis=1)
            out = lax.dot_general(
                jnp.concatenate(split(both, 2), axis=0),
                hot[first + t],
                (((1,), (1,)), ((), ())),
                preferred_element_type=F32,
            )
            forces.append(out[: 3 * BEADS] + out[3 * BEADS :])
        return [
            jnp.concatenate([f[c * BEADS : (c + 1) * BEADS] for f in forces], axis=1)
            for c in range(3)
        ]

    for sub in range(SUBS):
        pushed = bonded(q)
        factor = (0.5 if sub == 0 else 1.0) * interval * inverse
        v = [v[c] + factor * pushed[c] for c in range(3)]
        for c in range(3):
            moved = packed_exact(motion_l, jnp.concatenate([q[c], v[c]], axis=0))
            q[c], v[c] = moved[:BEADS], moved[BEADS:]
    pushed = bonded(q)
    p = [masses * v[c] + (0.5 * interval) * pushed[c] for c in range(3)]
    beads = BEADS // parts
    for i in range(parts):
        for c in range(3):
            outs[i][c] = q[c][i * beads : (i + 1) * beads]
            outs[i][3 + c] = p[c][i * beads : (i + 1) * beads]
    rows = jnp.concatenate(q, axis=0)
    c16 = exact(contract[bead[0]], rows, 2)
    row = lax.broadcasted_iota(jnp.int32, (ROWS, width), 0)
    logs = math.log2(math.e) * jnp.log(per_atom(strength_rows))
    c16 = jnp.where(row == LOGS, logs, c16)
    c_out[...] = c16
    if edge:
        rim = GT * TILE
        head = c16[:, :rim] if before is None else before[:, :rim]
        tail = c16[:, width - rim :]
        outs[-2][...] = jnp.where(bead[0] == 0, tail, head)
        outs[-1][...] = jnp.where(bead[0] == 0, head, tail)


def substeps(chunk, chunks, bead, pieces, force, mass, strength, hot, motion, expand, contract, edge, before):
    parts = len(pieces) // 2
    lanes = pieces[0].shape[2]
    beads = BEADS // parts
    extra = [before] if edge and chunk else []
    shapes = [(6, beads, lanes)] * parts + [(ROWS, lanes)]
    if edge:
        shapes += [(ROWS, GT * TILE)] * 2
    return pl.pallas_call(
        functools.partial(
            step_kernel, parts, len(force), chunk, chunks, lanes // TILE, int(edge)
        ),
        in_specs=[IN_SMEM] + [IN_VMEM] * (2 * parts + len(force) + 6 + len(extra)),
        out_specs=[IN_VMEM] * len(shapes),
        out_shape=[vmem_out(s, F32) for s in shapes],
        compiler_params=PARAMS,
        cost_estimate=COST,
        name="substeps",
    )(
        bead,
        *[near(x) for x in pieces + force],
        mass,
        strength,
        near(hot),
        motion,
        expand,
        contract,
        *[near(x) for x in extra],
    )


def finish_kernel(chunks, bead, expand, force, *refs):
    pos, mom = refs[-2:]
    parts = refs[:-2]
    bead_count = len(parts) // chunks
    lanes = parts[0].shape[2]
    comp = pl.program_id(0)
    table = expand[bead[0], comp]
    for i, part in enumerate(parts):
        chunk, distance = divmod(i, bead_count)
        block = lax.rem(bead[0] + bead_count - distance, bead_count)
        start = pl.multiple_of(block * (chunks * lanes) + chunk * lanes, TILE)
        where = pl.ds(start, lanes)
        pos[0, :, where] = part[comp]
        mom[0, :, where] = part[3 + comp] + 0.5 * time_step * exact(table, force[:, where])


def finish(chunks, bead, parts, expand, force):
    slab = force.shape[1]
    beads = parts[0].shape[1]
    return pl.pallas_call(
        functools.partial(finish_kernel, chunks),
        grid=(3,),
        in_specs=[IN_SMEM] + [IN_VMEM] * (2 + len(parts)),
        out_specs=[pl.BlockSpec((1, beads, slab), lambda i: (i, 0, 0))] * 2,
        out_shape=[jax.ShapeDtypeStruct((3, beads, slab), F32)] * 2,
        compiler_params=PARAMS,
        cost_estimate=COST,
        name="finish",
    )(bead, expand, near(force), *[near(x) for x in parts])


def finish_block_kernel(chunks, owner, moves, count, bead, expand, inner, outer, *refs):
    parts = refs[:count]
    pos, mom, held, sems = refs[-4:]
    lanes = parts[0].shape[2]
    blocks = [bead[0], 1 - bead[0]]

    def where(owner, chunk):
        return pl.ds(pl.multiple_of((blocks[owner] * chunks + chunk) * lanes, TILE), lanes)

    copies = []

    def copy(source, target):
        copies.append(pltpu.make_async_copy(source, target, sems.at[len(copies)]))
        copies[-1].start()

    for part, move_owner, chunk in moves:
        copy(parts[part].at[pl.ds(0, 3)], pos.at[:, :, where(move_owner, chunk)])
    force = whole_force(inner, outer)
    for chunk in range(chunks):
        lane = slice(chunk * lanes, (chunk + 1) * lanes)
        for c in range(3):
            kick = 0.5 * time_step * exact(expand[bead[0], c], force[:, lane])
            held[c, :, lane] = parts[chunk][3 + c] + kick
        copy(held.at[:, :, pl.ds(chunk * lanes, lanes)], mom.at[:, :, where(owner, chunk)])
    for waiting in copies:
        waiting.wait()


def finish_block(chunks, owner, moves, bead, parts, expand, inner, outer, before):
    beads, lanes = parts[0].shape[1:]
    block = lanes * chunks
    anywhere = pl.BlockSpec(memory_space=pl.ANY)
    at = 4 + len(parts)
    return pl.pallas_call(
        functools.partial(finish_block_kernel, chunks, owner, moves, len(parts)),
        in_specs=[IN_SMEM] + [IN_VMEM] * (3 + len(parts)) + [anywhere] * len(before),
        out_specs=[anywhere] * 2,
        out_shape=[pltpu.MemorySpace.HBM((3, beads, 2 * block), F32)] * 2,
        scratch_shapes=[
            pltpu.VMEM((3, beads, block), F32),
            pltpu.SemaphoreType.DMA((len(moves) + chunks,)),
        ],
        input_output_aliases={at + i: i for i in range(len(before))},
        compiler_params=PARAMS,
        cost_estimate=COST,
        name="finish_block",
    )(
        bead,
        expand,
        near(inner),
        near(outer),
        *[near(x) for x in parts],
        *[far(x) for x in before],
    )


def body(positions, momenta, masses, strengths, bond_ends, angle_ends, neighbour_tiles):
    beads, _, slab = positions.shape
    bead_count = lax.axis_size("bead")
    bead = lax.axis_index("bead")
    space_count = lax.axis_size("space")
    space = lax.axis_index("space")
    block = slab // bead_count
    slab_tiles = slab // TILE
    block_tiles = block // TILE
    all_tiles = slab_tiles * space_count
    rim = GT * TILE
    chunks = 2 if block_tiles % 4 == 0 else 1
    lanes = block // chunks
    interval = time_step / SUBS
    pair = bead_count == 2

    pos = positions.transpose(1, 0, 2)
    mom = momenta.transpose(1, 0, 2)
    bead_at = jnp.reshape(bead, (1,)).astype(jnp.int32)
    space_at = jnp.reshape(space, (1,)).astype(jnp.int32)
    mass = masses.reshape(slab_tiles, TILE)
    strength = strengths.reshape(slab_tiles, TILE)
    turned = contract_rows(beads)
    table = contract_table(BEADS, KEPT)
    own_tables = [table[:, i * beads : (i + 1) * beads] for i in range(bead_count)]

    def stack(tables):
        return jnp.asarray(np.stack(tables))

    begin_left = stack([stacked_left(contract_left(t)) for t in own_tables])
    finish_left = stack(
        [
            np.stack(
                [stacked_left(expand_left(t)[c * beads : (c + 1) * beads]) for c in range(3)]
            )
            for t in own_tables
        ]
    )
    contract_l = stack([stacked_left(contract_left(t), 2) for t in turned])
    expand_l = stack([stacked_left(expand_left(t)) for t in turned])
    motion = jnp.asarray(packed_left(motion_table(BEADS, interval)))

    def lanes_of(x, start, size):
        return lax.dynamic_slice_in_dim(x, start, size, x.ndim - 1)

    def permutation(step, flip):
        return [
            (s * 2 + b, ((s + step(b)) % space_count) * 2 + (b ^ flip))
            for s in range(space_count)
            for b in range(2)
        ]

    def rims(x):
        up = [(i, (i + 1) % space_count) for i in range(space_count)]
        down = [((i + 1) % space_count, i) for i in range(space_count)]
        return (
            lax.ppermute(x[:, slab - rim :], "space", up),
            lax.ppermute(x[:, :rim], "space", down),
        )

    def relative(tile, info):
        x = tile - info[1] * slab_tiles
        x = jnp.where(x >= all_tiles - GT, x - all_tiles, x)
        return jnp.where(x < -GT, x + all_tiles, x)

    def spots_inner(info):
        def spot(tile):
            return relative(tile, info) - info[0] * block_tiles

        return lambda t: t + GT + info[0] * block_tiles, lambda t: t + GT, spot

    def spots_outer(info):
        bead_at = 4 * GT
        far_at = bead_at + GT
        left_at = jnp.where(info[0] == 0, far_at, bead_at)
        right_at = jnp.where(info[0] == 0, bead_at, far_at)

        def own(t):
            return jnp.where(t < GT, t, t + block_tiles - 2 * GT)

        def place(x):
            return jnp.where(x < 2 * GT, x, x - (block_tiles - 4 * GT))

        def spot(tile):
            x = relative(tile, info) - info[0] * block_tiles
            right = jnp.where(x >= block_tiles, x - block_tiles + right_at, place(x))
            return jnp.where(x < 0, x + GT + left_at, right)

        return lambda t: own(t) + info[0] * block_tiles, lambda t: place(own(t)), spot

    def spots_slab(first):
        def spots(info):
            start = info[0] * block_tiles if first else 0

            def spot(tile):
                x = relative(tile, info)
                return jnp.where(x < 0, x + GT + slab_tiles, jnp.where(x >= slab_tiles, x + GT, x))

            return lambda t: t + start, lambda t: t + start, spot

        return spots

    pieces = [[] for _ in range(chunks)]
    if pair:
        mine, theirs, straight, *blocks = begin(
            chunks, bead_at, begin_left, strength, pos
        )
        theirs = lax.ppermute(theirs, "bead", SWAP)
        moments = fetch(chunks, bead_at, mom)
        for chunk in range(chunks):
            other = lax.ppermute(blocks[chunks + chunk], "bead", SWAP)
            moment = lax.ppermute(moments[chunks + chunk], "bead", SWAP)
            pieces[chunk] = [blocks[chunk], moments[chunk], other, moment]
        straight = relay(straight, theirs)
        straight = lax.ppermute(
            straight, ("space", "bead"), permutation(lambda b: -1 if b else 1, 0)
        )
        both = [mine, theirs]
        inside = [(both, lambda b: b * GT, block_tiles)]
        rim_tiles = [
            (both, lambda b: b * GT, 2 * GT),
            (both, lambda b: b * GT + block_tiles - 2 * GT, 2 * GT),
            (both, lambda b: (1 - b) * block_tiles, GT),
            ([straight], 0, GT),
        ]
    else:
        part = partial_rows(bead_at, begin_left, strength, pos)
        summed = lax.psum(part, "bead")
        logs_row = lax.broadcasted_iota(jnp.int32, summed.shape, 0) == LOGS
        summed = jnp.where(logs_row, jnp.log2(strengths)[None, :], summed)
        segments = [([summed], 0, slab_tiles), *[([x], 0, GT) for x in rims(summed)]]
        spots = spots_slab(True)
        for chunk in range(chunks):
            parts = []
            for d in range(bead_count):
                start = jnp.mod(bead - d, bead_count) * block + chunk * lanes
                piece = jnp.concatenate(
                    [lanes_of(pos, start, lanes), lanes_of(mom, start, lanes)], 0
                )
                back = [(i, (i - d) % bead_count) for i in range(bead_count)]
                parts.append(lax.ppermute(piece, "bead", back) if d else piece)
            whole = jnp.concatenate(parts, 1)
            pieces[chunk] = [whole[:3], whole[3:]]

    hot = prepare(bead_at, bond_ends, angle_ends, block_tiles)
    if pair:
        ids = bead_at, space_at, neighbour_tiles
        inner = pair_forces(spots_inner, inside, block_tiles - 2 * GT, *ids, True)
        outer = pair_forces(spots_outer, rim_tiles, 2 * GT, *ids, True)
        force = [inner, outer]
    else:
        force = [pair_forces(spots, segments, block_tiles, bead_at, space_at, neighbour_tiles)]

    own_out, returned, contracted = [], [], []
    for chunk in range(chunks):
        last = pair and chunk == chunks - 1
        outs = substeps(
            chunk, chunks, bead_at, pieces[chunk], force, mass, strength, hot, motion,
            expand_l, contract_l, last, contracted[0] if contracted else None,
        )
        if last:
            *outs, bead_edge, far_edge = outs
        *outs, c16 = outs
        if not pair:
            outs = [outs[0][:, d * beads : (d + 1) * beads] for d in range(bead_count)]
        own_out.append(outs[0])
        contracted.append(c16)
        back = []
        for d in range(1, bead_count):
            on = [(i, (i + d) % bead_count) for i in range(bead_count)]
            back.append(lax.ppermute(outs[d], "bead", on))
        returned.append(back)

    if not pair:
        c16 = jnp.concatenate(contracted, 1) if chunks > 1 else contracted[0]
        everyone = lax.all_gather(c16, "bead", axis=1, tiled=True)
        segments = [([everyone], 0, slab_tiles), *[([x], 0, GT) for x in rims(everyone)]]
        force = pair_forces(
            spots_slab(False), segments, slab_tiles, bead_at, space_at, neighbour_tiles
        )
        parts = [x for chunk in range(chunks) for x in [own_out[chunk]] + returned[chunk]]
        new_pos, new_mom = finish(chunks, bead_at, parts, finish_left, force)
        return new_pos.transpose(1, 0, 2), new_mom.transpose(1, 0, 2)

    beside = lax.ppermute(bead_edge, "bead", SWAP)
    across = lax.ppermute(
        far_edge, ("space", "bead"), permutation(lambda b: 1 if b else -1, 1)
    )
    chunk_tiles = lanes // TILE
    segments = [([x], 0, chunk_tiles) for x in contracted]
    inner = pair_forces(spots_inner, segments, block_tiles - 2 * GT, *ids, True)
    segments = [
        ([contracted[0]], 0, 2 * GT),
        ([contracted[-1]], chunk_tiles - 2 * GT, 2 * GT),
        ([beside], 0, GT),
        ([across], 0, GT),
    ]
    outer = pair_forces(spots_outer, segments, 2 * GT, *ids, True)
    others = [x[0] for x in returned]
    moves = [(i, 0, i) for i in range(chunks)]
    moves += [(chunks + i, 1, i) for i in range(chunks - 1)]
    result = finish_block(
        chunks, 0, moves, bead_at, own_out + others[:-1], finish_left, inner, outer, []
    )
    inner = lax.ppermute(inner, "bead", SWAP)
    outer = lax.ppermute(outer, "bead", SWAP)
    moves = [(chunks - 1, 1, chunks - 1)]
    new_pos, new_mom = finish_block(
        chunks, 1, moves, bead_at, others, finish_left, inner, outer, result
    )
    return new_pos.transpose(1, 0, 2), new_mom.transpose(1, 0, 2)


SWAP = [(0, 1), (1, 0)]


def solution(mesh):
    placed = (
        P("bead", None, "space"),
        P("bead", None, "space"),
        P("space"),
        P("space"),
        P(None, "space"),
        P(None, "space"),
        P(None, "space"),
    )

    return jax.shard_map(
        body,
        mesh=mesh,
        in_specs=placed,
        out_specs=(P("bead", None, "space"), P("bead", None, "space")),
        check_vma=False,
    )
```

```python
import functools
import math

import jax
import jax.numpy as jnp
import numpy as np
from jax import lax
from jax.experimental import pallas as pl
from jax.experimental.pallas import tpu as pltpu
from jax.sharding import PartitionSpec as P


BEADS = 32
KEPT = 4
SUBS = 3
TILE = 128
GT = 2
BPT = 128
APT = 64
ROWS = 4 * KEPT
LOGS = 3 * KEPT

time_step = 0.3
spring_freq = 80.0
bond_stiff = 0.2
bond_rest = 1.0
angle_stiff = 0.1
angle_rest = 0.5
range_sq = 4.0
HIGH = lax.Precision.HIGHEST
IN_VMEM = pl.BlockSpec(memory_space=pltpu.VMEM)
IN_SMEM = pl.BlockSpec(memory_space=pltpu.SMEM)
IN_SPACE = pltpu.MemorySpace.VMEM


def near(x):
    return pltpu.with_memory_space_constraint(x, IN_SPACE)


def far(x):
    return pltpu.with_memory_space_constraint(x, pltpu.MemorySpace.HBM)


def vmem_out(shape, dtype):
    return IN_SPACE(shape, dtype)


PARAMS = pltpu.CompilerParams(vmem_limit_bytes=20 * 1024 * 1024)
COST = pl.CostEstimate(flops=10_000_000, bytes_accessed=100_000, transcendentals=0)
F32 = jnp.float32
BF16 = jnp.bfloat16


def mode_table(number):
    within = np.arange(number)
    result = np.zeros((number, number))
    for column in range(number):
        if column == 0:
            result[:, column] = 1.0 / math.sqrt(number)
        elif 2 * column < number:
            result[:, column] = math.sqrt(2.0 / number) * np.cos(
                2 * np.pi * within * column / number
            )
        elif 2 * column == number:
            result[:, column] = (-1.0) ** within / math.sqrt(number)
        else:
            result[:, column] = math.sqrt(2.0 / number) * np.sin(
                2 * np.pi * within * column / number
            )
    return result


def contract_table(number, kept):
    larger = mode_table(number)
    smaller = mode_table(kept)
    chosen = [column if 2 * column <= kept else number - kept + column for column in range(kept)]
    return math.sqrt(kept / number) * smaller @ larger[:, chosen].T


def motion_table(number, interval):
    freqs = 2.0 * spring_freq * np.sin(np.pi * np.arange(number) / number)
    modes = mode_table(number)
    safe = np.where(freqs > 0, freqs, 1.0)
    gains = np.where(freqs > 0, np.sin(freqs * interval) / safe, interval)
    drags = freqs * np.sin(freqs * interval)
    stay = modes @ np.diag(np.cos(freqs * interval)) @ modes.T
    gain = modes @ np.diag(gains) @ modes.T
    drag = modes @ np.diag(drags) @ modes.T
    return np.block([[stay, gain], [-drag, stay]])


def np_split(table, parts):
    out, rest = [], np.asarray(table, np.float64)
    for _ in range(parts):
        piece = rest.astype(np.float32).astype(jnp.bfloat16)
        out.append(piece)
        rest = rest - piece.astype(np.float64)
    return out


def stacked_left(table, parts=3):
    pieces = np_split(table, parts)
    zero = np.zeros_like(pieces[0])
    return np.concatenate(
        [
            np.concatenate([pieces[i]] * (parts - i) + [zero] * i, axis=1)
            for i in range(parts)
        ],
        axis=0,
    )


def split(x, parts):
    out = []
    for i in range(parts):
        piece = x.astype(BF16)
        out.append(piece)
        if i < parts - 1:
            x = x - piece.astype(F32)
    return out


def mm(left, right):
    return jnp.dot(left, right, preferred_element_type=F32)


def exact(left, x, parts=3):
    out = mm(left, jnp.concatenate(split(x, parts), axis=0))
    rows = out.shape[0] // parts
    total = out[:rows]
    for i in range(1, parts):
        total = total + out[i * rows : (i + 1) * rows]
    return total


def packed_left(table):
    high, mid, low = np_split(table, 3)
    zero = np.zeros_like(high)
    return np.concatenate(
        [
            np.concatenate([high, high, high, mid], axis=1),
            np.concatenate([low, mid, zero, zero], axis=1),
        ],
        axis=0,
    )


def packed_exact(left, x):
    high, mid, low = split(x, 3)
    out = mm(left, jnp.concatenate([high, mid, low, high], axis=0))
    rows = out.shape[0] // 2
    return out[:rows] + out[rows:]


def contract_rows(beads):
    table = contract_table(BEADS, KEPT)
    tables = []
    for turn in range(0, BEADS, beads):
        order = (np.arange(BEADS) + turn) % BEADS
        tables.append(table[:, order])
    return tables


def contract_left(table):
    out = np.zeros((ROWS, 3 * table.shape[1]))
    for c in range(KEPT):
        for k in range(3):
            out[k * KEPT + c, k * table.shape[1] : (k + 1) * table.shape[1]] = table[c]
    return out


def expand_left(table):
    return BEADS / KEPT * contract_left(table).T


def pack_rows(target, x):
    lanes = x.shape[1]
    target[:, :lanes] = x[:8]
    target[:4, lanes:] = x[8:12, : lanes // 2]
    target[4:, lanes:] = x[8:12, lanes // 2 :]


def unpacked(x):
    lanes = x.shape[1] * 2 // 3
    last = jnp.concatenate([x[:4, lanes:], x[4:, lanes:]], axis=1)
    return jnp.concatenate([x[:, :lanes], last, jnp.zeros_like(last)], axis=0)


def begin_kernel(chunks, bead, left, strengths, pos, *refs):
    mine, theirs, straight = refs[:3]
    whole, table, rows, spare, sems = refs[-5:]
    blocks = list(refs[3:-5]) + [spare.at[i] for i in range(chunks)]
    lanes = blocks[0].shape[2]
    slab = whole.shape[1]
    starts, copies = [], []
    for i in range(2 * chunks):
        owner = bead[0] if i < chunks else 1 - bead[0]
        starts.append(pl.multiple_of((owner * chunks + i % chunks) * lanes, TILE))
    for i, block in enumerate(blocks):
        copy = pltpu.make_async_copy(
            pos.at[:, :, pl.ds(starts[i], lanes)], block, sems.at[i]
        )
        copy.start()
        copies.append(copy)
    small = [
        pltpu.make_async_copy(left.at[bead[0]], table, sems.at[len(copies)]),
        pltpu.make_async_copy(strengths, rows, sems.at[len(copies) + 1]),
    ]
    for copy in small:
        copy.start()
    for copy in small:
        copy.wait()
    logs = math.log2(math.e) * jnp.log(rows[...])
    for t in range(slab // TILE):
        whole[LOGS : LOGS + 1, t * TILE : (t + 1) * TILE] = logs[t : t + 1]
    for i, block in enumerate(blocks):
        copies[i].wait()
        x = jnp.concatenate([block[c] for c in range(3)], axis=0)
        where = pl.ds(starts[i], lanes)
        row = lax.broadcasted_iota(jnp.int32, (ROWS, lanes), 0)
        whole[:, where] = jnp.where(row == LOGS, whole[:, where], exact(table[...], x))

    block, rim = slab // 2, GT * TILE
    size = block + rim

    def sides(which):
        first, other = (0, block - rim) if which == 0 else (block - rim, 0)
        mine[...] = whole[:, first : first + size]
        head, tail = whole[:, :rim], whole[:, slab - rim :]
        straight[...] = tail if which == 0 else head
        relay = head if which == 0 else tail
        pack_rows(theirs, jnp.concatenate([whole[:, other : other + size], relay], axis=1))

    for which in range(2):
        pl.when(bead[0] == which)(functools.partial(sides, which))


def fetch_kernel(moves, chunks, bead, pos, mom, *refs):
    *blocks, sems = refs
    lanes = blocks[0].shape[2]
    copies = []
    for i, (block, plane, source, owner, chunk) in enumerate(moves):
        side = bead[0] if owner == 0 else 1 - bead[0]
        start = pl.multiple_of((side * chunks + chunk) * lanes, TILE)
        copy = pltpu.make_async_copy(
            (pos, mom)[source].at[:, :, pl.ds(start, lanes)],
            blocks[block].at[pl.ds(plane, 3)],
            sems.at[i],
        )
        copy.start()
        copies.append(copy)
    for copy in copies:
        copy.wait()


def fetch(moves, planes, chunks, bead, pos, mom):
    beads, slab = mom.shape[1:]
    lanes = slab // (2 * chunks)
    return pl.pallas_call(
        functools.partial(fetch_kernel, moves, chunks),
        in_specs=[IN_SMEM] + [pl.BlockSpec(memory_space=pl.ANY)] * 2,
        out_specs=[IN_VMEM] * len(planes),
        out_shape=[vmem_out((n, beads, lanes), F32) for n in planes],
        scratch_shapes=[pltpu.SemaphoreType.DMA((len(moves),))],
        compiler_params=PARAMS,
        cost_estimate=COST,
        name="fetch",
    )(bead, far(pos), far(mom))


def begin(chunks, bead, left, strengths, pos):
    beads, slab = pos.shape[1:]
    block, rim = slab // 2, GT * TILE
    lanes = block // chunks
    shapes = [(ROWS, block + rim), (8, 3 * (block + 2 * rim) // 2), (ROWS, rim)]
    shapes += [(3, beads, lanes)] * chunks
    return pl.pallas_call(
        functools.partial(begin_kernel, chunks),
        in_specs=[IN_SMEM] + [pl.BlockSpec(memory_space=pl.ANY)] * 3,
        out_specs=[IN_VMEM] * len(shapes),
        out_shape=[vmem_out(s, F32) for s in shapes],
        scratch_shapes=[
            pltpu.VMEM((ROWS, slab), F32),
            pltpu.VMEM(left.shape[1:], left.dtype),
            pltpu.VMEM(strengths.shape, F32),
            pltpu.VMEM((chunks, 3, beads, lanes), F32),
            pltpu.SemaphoreType.DMA((2 * chunks + 2,)),
        ],
        compiler_params=PARAMS,
        cost_estimate=COST,
        name="begin",
    )(bead, far(left), far(strengths), far(pos))


def relay_kernel(own, received, out):
    rim = GT * TILE
    size = received.shape[1] * 2 // 3
    more = jnp.concatenate([received[:, size - rim : size], received[4:, -rim:]], axis=0)
    out[...] = own[...] + jnp.concatenate([more, jnp.zeros_like(more[:4])], axis=0)


def relay(own, received):
    return pl.pallas_call(
        relay_kernel,
        in_specs=[IN_VMEM] * 2,
        out_specs=IN_VMEM,
        out_shape=vmem_out(own.shape, F32),
        compiler_params=PARAMS,
        cost_estimate=COST,
        name="relay",
    )(near(own), near(received))


def partial_kernel(bead, left, strengths, pos, out):
    comps, _, lanes = pos.shape
    logs = math.log2(math.e) * jnp.log(strengths[...])
    logs = jnp.concatenate([logs[t : t + 1] for t in range(lanes // TILE)], axis=1)
    row = lax.broadcasted_iota(jnp.int32, (ROWS, lanes), 0)
    x = jnp.concatenate([pos[c] for c in range(comps)], axis=0)
    out[...] = jnp.where(row == LOGS, logs, exact(left[bead[0]], x))


def partial_rows(bead, left, strengths, pos):
    beads, slab = pos.shape[1:]
    lanes = math.gcd(slab, 1024)
    return pl.pallas_call(
        partial_kernel,
        grid=(slab // lanes,),
        in_specs=[
            IN_SMEM,
            IN_VMEM,
            pl.BlockSpec((lanes // TILE, TILE), lambda i: (i, 0)),
            pl.BlockSpec((3, beads, lanes), lambda i: (0, 0, i)),
        ],
        out_specs=pl.BlockSpec((ROWS, lanes), lambda i: (0, i)),
        out_shape=jax.ShapeDtypeStruct((ROWS, slab), F32),
        name="partial_rows",
    )(bead, left, strengths, pos)


def prepare_kernel(group, bead, bonds, angles, hot):
    lane = lax.broadcasted_iota(jnp.int32, (1, TILE), 1)
    atom = lax.broadcasted_iota(jnp.int32, (TILE, 2 * TILE), 0)
    low = lane < APT

    def merge(first, second, odd):
        a = pltpu.roll(first, APT, 1) if odd else first
        b = second if odd else pltpu.roll(second, APT, 1)
        return jnp.where(low, a, b)

    def tiles(i, carry):
        at = (bead[0] * (hot.shape[0] // group) + i) * group
        bond_rows = bonds[:, pl.ds(pl.multiple_of(at * BPT, BPT), group * BPT)]
        angle_rows = angles[:, pl.ds(pl.multiple_of(at * APT, TILE), group * APT)]
        for t in range(group):
            one = bond_rows[0:1, t * TILE : (t + 1) * TILE]
            other = bond_rows[1:2, t * TILE : (t + 1) * TILE]
            odd = t % 2
            window = slice((t // 2) * TILE, (t // 2 + 1) * TILE)
            first, middle, last = [angle_rows[e : e + 1, window] for e in range(3)]
            opposite = merge(last, first, odd)
            centre = merge(middle, middle, odd)
            gains = jnp.concatenate([other, centre], axis=1)
            losses = jnp.concatenate([one, opposite], axis=1)
            table = (atom == gains).astype(F32) - (atom == losses).astype(F32)
            hot[i * group + t] = table.astype(BF16)
        return carry

    lax.fori_loop(0, hot.shape[0] // group, tiles, 0)


def prepare(bead, bond_ends, angle_ends, block_tiles):
    return pl.pallas_call(
        functools.partial(prepare_kernel, math.gcd(block_tiles, 4)),
        in_specs=[IN_SMEM, IN_VMEM, IN_VMEM],
        out_specs=IN_VMEM,
        out_shape=vmem_out((block_tiles, TILE, 2 * TILE), BF16),
        compiler_params=PARAMS,
        cost_estimate=COST,
        name="prepare",
    )(bead, bond_ends, angle_ends)


def pair_kernel(spots, seg_sizes, own_count, packed, bead, space, nbr, *refs):
    total = sum(n for *_, n in seg_sizes)
    count = sum(n for n, *_ in seg_sizes)
    seg_refs = refs[:count]
    target, feat_i, feat_m, feat_p, base, *weights, held = refs[count:]
    out = held if packed else target
    column, own_spot, spot = spots((bead[0], space[0]))
    row = lax.broadcasted_iota(jnp.int32, (ROWS, TILE), 0)
    slot = row // KEPT
    scale = math.sqrt(2.0 * math.log2(math.e) / range_sq)
    same = (
        lax.broadcasted_iota(jnp.int32, (ROWS, ROWS), 0) % KEPT
        == lax.broadcasted_iota(jnp.int32, (ROWS, ROWS), 1) % KEPT
    ).astype(F32)

    def features(tile, c16):
        base[tile] = c16
        logs = c16[LOGS : LOGS + 1]
        place = jnp.where(slot == 3, 0.0, c16)
        scaled = place * scale
        high, low = [piece.astype(F32) for piece in split(scaled, 2)]
        square = jnp.dot(same, scaled * scaled, precision=HIGH, preferred_element_type=F32)
        half = -0.5 * square

        def three(x):
            a, b, c = [piece.astype(F32) for piece in split(x, 3)]
            return jnp.where(slot == 0, a, jnp.where(slot == 1, b, jnp.where(slot == 2, c, 0.0)))

        ones = jnp.where(slot == 3, 0.0, 1.0)
        mine = jnp.concatenate([high, high, low, low, three(half), ones], axis=0)
        theirs = jnp.concatenate(
            [high, low, high, low, ones, three(half + logs), ones, ones], axis=0
        )
        feat_i[tile] = mine.astype(BF16)
        feat_m[tile] = jnp.transpose(theirs, (1, 0)).astype(BF16)
        one = jnp.ones((ROWS, TILE), F32)
        p_high, p_low = [piece.astype(F32) for piece in split(place, 2)]
        feat_p[tile] = jnp.concatenate([one, p_high, p_low], axis=0).astype(BF16)

    def piece(ref, begins, i):
        moving = callable(begins)
        at = (begins(bead[0]) if moving else begins) + i

        def lanes(tile):
            if moving:
                return pl.ds(pl.multiple_of(tile * TILE, TILE), TILE)
            return slice(tile * TILE, (tile + 1) * TILE)

        if ref.shape[0] == ROWS:
            return ref[:, lanes(at)]
        tiles = ref.shape[1] * 2 // 3 // TILE
        half = tiles // 2
        upper = at >= half
        last = ref[:, lanes(tiles + jnp.where(upper, at - half, at))]
        last = jnp.where(upper, last[4:], last[:4])
        return jnp.concatenate([ref[:, lanes(at)], last, jnp.zeros_like(last)], axis=0)

    tile = 0
    at = 0
    for number, begins, tiles in seg_sizes:
        group = seg_refs[at : at + number]
        at += number
        for i in range(tiles):
            c16 = piece(group[0], begins, i)
            for other in group[1:]:
                c16 = c16 + piece(other, begins, i)
            features(tile, c16)
            tile += 1
    assert tile == total

    groups = 6
    wide_row = lax.broadcasted_iota(jnp.int32, (groups * ROWS, TILE), 0)
    pick = [(wide_row % KEPT == c).astype(BF16) for c in range(KEPT)]
    owner = row % KEPT

    def close(t, u):
        return spot(nbr[u, column(t)])

    def weigh(t, weights):
        features_i = feat_i[own_spot(t)]
        right = jnp.concatenate([features_i * pick[c] for c in range(KEPT)], axis=1)
        right = jnp.concatenate([right, jnp.zeros((2 * ROWS, KEPT * TILE), BF16)], axis=0)
        left = jnp.concatenate([feat_m[close(t, u)] for u in range(3)], axis=0)
        power = mm(left, right)
        for u in range(3):
            high, low = split(jnp.exp2(power[u * TILE : (u + 1) * TILE]), 2)
            weights[2 * u * TILE : (2 * u + 1) * TILE] = high
            weights[(2 * u + 1) * TILE : (2 * u + 2) * TILE] = low

    def pull(t, weights):
        left = []
        for u in range(3):
            piece = feat_p[close(t, u)]
            left += [piece, piece]
        total_p = mm(jnp.concatenate(left, axis=1), weights[...])
        sums = total_p[:ROWS]
        pulls = total_p[ROWS : 2 * ROWS] + total_p[2 * ROWS :]
        c16 = base[own_spot(t)]
        factor = (2.0 / range_sq) * jnp.exp2(c16[LOGS : LOGS + 1])
        result = jnp.zeros((ROWS, TILE), F32)
        for c in range(KEPT):
            lanes = slice(c * TILE, (c + 1) * TILE)
            force = factor * (c16 * sums[:, lanes] - pulls[:, lanes])
            result = jnp.where((owner == c) & (slot < 3), force, result)
        lane = t * TILE if isinstance(t, int) else pl.multiple_of(t * TILE, TILE)
        out[:, pl.ds(lane, TILE)] = result

    unroll = math.gcd(own_count, 4)
    weigh(0, weights[0])

    def some_tiles(t, last):
        for j in range(unroll):
            if not (last and j == unroll - 1):
                weigh(t + j + 1, weights[(j + 1) % 2])
            pull(t + j, weights[j % 2])

    def loop(i, carry):
        some_tiles(unroll * i, False)
        return carry

    lax.fori_loop(0, own_count // unroll - 1, loop, 0)
    some_tiles(own_count - unroll, True)
    if packed:
        pack_rows(target, held[...])


def pair_forces(spots, segments, own_count, bead, space, neighbour_tiles, packed=False):
    sizes = tuple((len(group), start, tiles) for group, start, tiles in segments)
    total = sum(n for *_, n in sizes)
    assert own_count % 2 == 0
    flat = [array for group, *_ in segments for array in group]
    return pl.pallas_call(
        functools.partial(pair_kernel, spots, sizes, own_count, packed),
        in_specs=[IN_SMEM] * 3 + [IN_VMEM] * len(flat),
        out_specs=IN_VMEM,
        out_shape=vmem_out(
            (8, 3 * own_count * TILE // 2) if packed else (ROWS, own_count * TILE), F32
        ),
        scratch_shapes=[
            pltpu.VMEM((total, 6 * ROWS, TILE), BF16),
            pltpu.VMEM((total, TILE, 8 * ROWS), BF16),
            pltpu.VMEM((total, 3 * ROWS, TILE), BF16),
            pltpu.VMEM((total, ROWS, TILE), F32),
            pltpu.VMEM((6 * TILE, KEPT * TILE), BF16),
            pltpu.VMEM((6 * TILE, KEPT * TILE), BF16),
            pltpu.VMEM((ROWS, own_count * TILE), F32),
        ],
        compiler_params=PARAMS,
        cost_estimate=COST,
        name="pair_forces",
    )(bead, space, far(neighbour_tiles), *[near(x) for x in flat])


def whole_force(inner, outer):
    rim = GT * TILE
    inner, outer = unpacked(inner[...]), unpacked(outer[...])
    return jnp.concatenate([outer[:, :rim], inner, outer[:, rim:]], axis=1)


def step_kernel(parts, count, forces, chunk, chunks, group, edge, bead, *refs):
    pieces = refs[:count]
    at = count
    force = refs[at] if forces == 1 else whole_force(*refs[at : at + 2])
    at += forces
    mass_rows, strength_rows, hot, motion, expand, contract = refs[at : at + 6]
    before = refs[at + 6] if edge and chunk else None
    outs = refs[len(refs) - parts - 1 - 2 * edge :]
    c_out = outs[parts]
    interval = time_step / SUBS
    width = group * TILE
    first = chunk * group
    motion_l = motion[...]

    def per_atom(rows):
        at = (bead[0] * chunks + chunk) * group
        return jnp.concatenate([rows[pl.ds(at + t, 1), :] for t in range(group)], axis=1)

    masses = per_atom(mass_rows)
    inverse = 1.0 / masses

    places = [(piece, plane) for piece in pieces for plane in range(0, piece.shape[0], 3)]

    def gathered(kind, c):
        found = [piece[plane + c] for piece, plane in places[kind::2]]
        return found[0] if parts == 1 else jnp.concatenate(found, axis=0)

    q = [gathered(0, c) for c in range(3)]
    p = [gathered(1, c) for c in range(3)]
    kick = exact(expand[bead[0]], force[:, first * TILE : first * TILE + width])
    v = [
        (p[c] + 0.5 * time_step * kick[c * BEADS : (c + 1) * BEADS]) * inverse for c in range(3)
    ]

    def bonded(q):
        forces = []
        for t in range(group):
            lanes = slice(t * TILE, (t + 1) * TILE)
            rows = jnp.concatenate([q[c][:, lanes] for c in range(3)], axis=0)
            seen = mm(jnp.concatenate(split(rows, 2), axis=0), hot[first + t])
            seen = seen[: 3 * BEADS] + seen[3 * BEADS :]
            stretch, arms = seen[:, :TILE], seen[:, TILE:]
            s = [stretch[c * BEADS : (c + 1) * BEADS] for c in range(3)]
            a = [arms[c * BEADS : (c + 1) * BEADS] for c in range(3)]
            length = s[0] * s[0] + s[1] * s[1] + s[2] * s[2]
            g = bond_stiff * (bond_rest - length)
            turned = [pltpu.roll(x, APT, 1) for x in a]
            inner = a[0] * turned[0] + a[1] * turned[1] + a[2] * turned[2]
            h = angle_stiff * (angle_rest - inner)
            bonds = jnp.concatenate([g * x for x in s], axis=0)
            angles = jnp.concatenate([h * x for x in turned], axis=0)
            both = jnp.concatenate([bonds, angles], axis=1)
            out = lax.dot_general(
                jnp.concatenate(split(both, 2), axis=0),
                hot[first + t],
                (((1,), (1,)), ((), ())),
                preferred_element_type=F32,
            )
            forces.append(out[: 3 * BEADS] + out[3 * BEADS :])
        return [
            jnp.concatenate([f[c * BEADS : (c + 1) * BEADS] for f in forces], axis=1)
            for c in range(3)
        ]

    for sub in range(SUBS):
        pushed = bonded(q)
        factor = (0.5 if sub == 0 else 1.0) * interval * inverse
        v = [v[c] + factor * pushed[c] for c in range(3)]
        for c in range(3):
            moved = packed_exact(motion_l, jnp.concatenate([q[c], v[c]], axis=0))
            q[c], v[c] = moved[:BEADS], moved[BEADS:]
    pushed = bonded(q)
    p = [masses * v[c] + (0.5 * interval) * pushed[c] for c in range(3)]
    beads = BEADS // parts
    for i in range(parts):
        for c in range(3):
            outs[i][c] = q[c][i * beads : (i + 1) * beads]
            outs[i][3 + c] = p[c][i * beads : (i + 1) * beads]
    rows = jnp.concatenate(q, axis=0)
    c16 = exact(contract[bead[0]], rows, 2)
    row = lax.broadcasted_iota(jnp.int32, (ROWS, width), 0)
    logs = math.log2(math.e) * jnp.log(per_atom(strength_rows))
    c16 = jnp.where(row == LOGS, logs, c16)
    c_out[...] = c16
    if edge:
        rim = GT * TILE
        head = c16[:, :rim] if before is None else before[:, :rim]
        tail = c16[:, width - rim :]
        outs[-2][...] = jnp.where(bead[0] == 0, tail, head)
        outs[-1][...] = jnp.where(bead[0] == 0, head, tail)


def substeps(chunk, chunks, bead, pieces, force, mass, strength, hot, motion, expand, contract, edge, before):
    beads, lanes = pieces[0].shape[1:]
    parts = BEADS // beads
    extra = [before] if edge and chunk else []
    shapes = [(6, beads, lanes)] * parts + [(ROWS, lanes)]
    if edge:
        shapes += [(ROWS, GT * TILE)] * 2
    return pl.pallas_call(
        functools.partial(
            step_kernel, parts, len(pieces), len(force), chunk, chunks, lanes // TILE, int(edge)
        ),
        in_specs=[IN_SMEM] + [IN_VMEM] * (len(pieces) + len(force) + 6 + len(extra)),
        out_specs=[IN_VMEM] * len(shapes),
        out_shape=[vmem_out(s, F32) for s in shapes],
        compiler_params=PARAMS,
        cost_estimate=COST,
        name="substeps",
    )(
        bead,
        *[near(x) for x in pieces + force],
        mass,
        strength,
        near(hot),
        motion,
        expand,
        contract,
        *[near(x) for x in extra],
    )


def finish_kernel(chunks, bead, expand, force, *refs):
    pos, mom = refs[-2:]
    parts = refs[:-2]
    bead_count = len(parts) // chunks
    lanes = parts[0].shape[2]
    comp = pl.program_id(0)
    table = expand[bead[0], comp]
    for i, part in enumerate(parts):
        chunk, distance = divmod(i, bead_count)
        block = lax.rem(bead[0] + bead_count - distance, bead_count)
        start = pl.multiple_of(block * (chunks * lanes) + chunk * lanes, TILE)
        where = pl.ds(start, lanes)
        pos[0, :, where] = part[comp]
        mom[0, :, where] = part[3 + comp] + 0.5 * time_step * exact(table, force[:, where])


def finish(chunks, bead, parts, expand, force):
    slab = force.shape[1]
    beads = parts[0].shape[1]
    return pl.pallas_call(
        functools.partial(finish_kernel, chunks),
        grid=(3,),
        in_specs=[IN_SMEM] + [IN_VMEM] * (2 + len(parts)),
        out_specs=[pl.BlockSpec((1, beads, slab), lambda i: (i, 0, 0))] * 2,
        out_shape=[jax.ShapeDtypeStruct((3, beads, slab), F32)] * 2,
        compiler_params=PARAMS,
        cost_estimate=COST,
        name="finish",
    )(bead, expand, near(force), *[near(x) for x in parts])


def finish_block_kernel(chunks, owner, moves, count, bead, expand, inner, outer, *refs):
    parts = refs[:count]
    pos, mom, held, sems = refs[-4:]
    lanes = parts[0].shape[2]
    blocks = [bead[0], 1 - bead[0]]

    def where(owner, chunk):
        return pl.ds(pl.multiple_of((blocks[owner] * chunks + chunk) * lanes, TILE), lanes)

    copies = []

    def copy(source, target):
        copies.append(pltpu.make_async_copy(source, target, sems.at[len(copies)]))
        copies[-1].start()

    for part, move_owner, chunk in moves:
        copy(parts[part].at[pl.ds(0, 3)], pos.at[:, :, where(move_owner, chunk)])
    force = whole_force(inner, outer)
    for chunk in range(chunks):
        lane = slice(chunk * lanes, (chunk + 1) * lanes)
        for c in range(3):
            kick = 0.5 * time_step * exact(expand[bead[0], c], force[:, lane])
            held[c, :, lane] = parts[chunk][3 + c] + kick
        copy(held.at[:, :, pl.ds(chunk * lanes, lanes)], mom.at[:, :, where(owner, chunk)])
    for waiting in copies:
        waiting.wait()


def finish_block(chunks, owner, moves, bead, parts, expand, inner, outer, before):
    beads, lanes = parts[0].shape[1:]
    block = lanes * chunks
    anywhere = pl.BlockSpec(memory_space=pl.ANY)
    at = 4 + len(parts)
    return pl.pallas_call(
        functools.partial(finish_block_kernel, chunks, owner, moves, len(parts)),
        in_specs=[IN_SMEM] + [IN_VMEM] * (3 + len(parts)) + [anywhere] * len(before),
        out_specs=[anywhere] * 2,
        out_shape=[pltpu.MemorySpace.HBM((3, beads, 2 * block), F32)] * 2,
        scratch_shapes=[
            pltpu.VMEM((3, beads, block), F32),
            pltpu.SemaphoreType.DMA((len(moves) + chunks,)),
        ],
        input_output_aliases={at + i: i for i in range(len(before))},
        compiler_params=PARAMS,
        cost_estimate=COST,
        name="finish_block",
    )(
        bead,
        expand,
        near(inner),
        near(outer),
        *[near(x) for x in parts],
        *[far(x) for x in before],
    )


def body(positions, momenta, masses, strengths, bond_ends, angle_ends, neighbour_tiles):
    beads, _, slab = positions.shape
    bead_count = lax.axis_size("bead")
    bead = lax.axis_index("bead")
    space_count = lax.axis_size("space")
    space = lax.axis_index("space")
    block = slab // bead_count
    slab_tiles = slab // TILE
    block_tiles = block // TILE
    all_tiles = slab_tiles * space_count
    rim = GT * TILE
    chunks = 2 if block_tiles % 4 == 0 else 1
    lanes = block // chunks
    interval = time_step / SUBS
    pair = bead_count == 2

    pos = positions.transpose(1, 0, 2)
    mom = momenta.transpose(1, 0, 2)
    bead_at = jnp.reshape(bead, (1,)).astype(jnp.int32)
    space_at = jnp.reshape(space, (1,)).astype(jnp.int32)
    mass = masses.reshape(slab_tiles, TILE)
    strength = strengths.reshape(slab_tiles, TILE)
    turned = contract_rows(beads)
    table = contract_table(BEADS, KEPT)
    own_tables = [table[:, i * beads : (i + 1) * beads] for i in range(bead_count)]

    def stack(tables):
        return jnp.asarray(np.stack(tables))

    begin_left = stack([stacked_left(contract_left(t)) for t in own_tables])
    finish_left = stack(
        [
            np.stack(
                [stacked_left(expand_left(t)[c * beads : (c + 1) * beads]) for c in range(3)]
            )
            for t in own_tables
        ]
    )
    contract_l = stack([stacked_left(contract_left(t), 2) for t in turned])
    expand_l = stack([stacked_left(expand_left(t)) for t in turned])
    motion = jnp.asarray(packed_left(motion_table(BEADS, interval)))

    def lanes_of(x, start, size):
        return lax.dynamic_slice_in_dim(x, start, size, x.ndim - 1)

    def permutation(step, flip):
        return [
            (s * 2 + b, ((s + step(b)) % space_count) * 2 + (b ^ flip))
            for s in range(space_count)
            for b in range(2)
        ]

    def rims(x):
        up = [(i, (i + 1) % space_count) for i in range(space_count)]
        down = [((i + 1) % space_count, i) for i in range(space_count)]
        return (
            lax.ppermute(x[:, slab - rim :], "space", up),
            lax.ppermute(x[:, :rim], "space", down),
        )

    def relative(tile, info):
        x = tile - info[1] * slab_tiles
        x = jnp.where(x >= all_tiles - GT, x - all_tiles, x)
        return jnp.where(x < -GT, x + all_tiles, x)

    def spots_inner(info):
        def spot(tile):
            return relative(tile, info) - info[0] * block_tiles

        return lambda t: t + GT + info[0] * block_tiles, lambda t: t + GT, spot

    def spots_outer(info):
        bead_at = 4 * GT
        far_at = bead_at + GT
        left_at = jnp.where(info[0] == 0, far_at, bead_at)
        right_at = jnp.where(info[0] == 0, bead_at, far_at)

        def own(t):
            return jnp.where(t < GT, t, t + block_tiles - 2 * GT)

        def place(x):
            return jnp.where(x < 2 * GT, x, x - (block_tiles - 4 * GT))

        def spot(tile):
            x = relative(tile, info) - info[0] * block_tiles
            right = jnp.where(x >= block_tiles, x - block_tiles + right_at, place(x))
            return jnp.where(x < 0, x + GT + left_at, right)

        return lambda t: own(t) + info[0] * block_tiles, lambda t: place(own(t)), spot

    def spots_slab(first):
        def spots(info):
            start = info[0] * block_tiles if first else 0

            def spot(tile):
                x = relative(tile, info)
                return jnp.where(x < 0, x + GT + slab_tiles, jnp.where(x >= slab_tiles, x + GT, x))

            return lambda t: t + start, lambda t: t + start, spot

        return spots

    pieces = [[] for _ in range(chunks)]
    if pair:
        (lead,) = fetch([(0, 0, 0, 1, 0)], [3], chunks, bead_at, pos, mom)
        other = lax.ppermute(lead, "bead", SWAP)
        mine, theirs, straight, *own_q = begin(chunks, bead_at, begin_left, strength, pos)
        theirs = lax.ppermute(theirs, "bead", SWAP)
        moves = [(0, 0, 1, 1, 0)]
        for chunk in range(1, chunks):
            moves += [(chunk, 0, 0, 1, chunk), (chunk, 3, 1, 1, chunk)]
        moves += [(chunks + chunk, 0, 1, 0, chunk) for chunk in range(chunks)]
        planes = [3] + [6] * (chunks - 1) + [3] * chunks
        blocks = fetch(moves, planes, chunks, bead_at, pos, mom)
        for chunk in range(chunks):
            moment = lax.ppermute(blocks[chunk], "bead", SWAP)
            pieces[chunk] = [own_q[chunk], blocks[chunks + chunk]]
            pieces[chunk] += [moment] if chunk else [other, moment]
        straight = relay(straight, theirs)
        straight = lax.ppermute(
            straight, ("space", "bead"), permutation(lambda b: -1 if b else 1, 0)
        )
        both = [mine, theirs]
        inside = [(both, lambda b: b * GT, block_tiles)]
        rim_tiles = [
            (both, lambda b: b * GT, 2 * GT),
            (both, lambda b: b * GT + block_tiles - 2 * GT, 2 * GT),
            (both, lambda b: (1 - b) * block_tiles, GT),
            ([straight], 0, GT),
        ]
    else:
        part = partial_rows(bead_at, begin_left, strength, pos)
        summed = lax.psum(part, "bead")
        logs_row = lax.broadcasted_iota(jnp.int32, summed.shape, 0) == LOGS
        summed = jnp.where(logs_row, jnp.log2(strengths)[None, :], summed)
        segments = [([summed], 0, slab_tiles), *[([x], 0, GT) for x in rims(summed)]]
        spots = spots_slab(True)
        for chunk in range(chunks):
            parts = []
            for d in range(bead_count):
                start = jnp.mod(bead - d, bead_count) * block + chunk * lanes
                piece = jnp.concatenate(
                    [lanes_of(pos, start, lanes), lanes_of(mom, start, lanes)], 0
                )
                back = [(i, (i - d) % bead_count) for i in range(bead_count)]
                parts.append(lax.ppermute(piece, "bead", back) if d else piece)
            pieces[chunk] = [jnp.concatenate(parts, 1)]

    hot = prepare(bead_at, bond_ends, angle_ends, block_tiles)
    if pair:
        ids = bead_at, space_at, neighbour_tiles
        inner = pair_forces(spots_inner, inside, block_tiles - 2 * GT, *ids, True)
        outer = pair_forces(spots_outer, rim_tiles, 2 * GT, *ids, True)
        force = [inner, outer]
    else:
        force = [pair_forces(spots, segments, block_tiles, bead_at, space_at, neighbour_tiles)]

    own_out, returned, contracted = [], [], []
    for chunk in range(chunks):
        last = pair and chunk == chunks - 1
        outs = substeps(
            chunk, chunks, bead_at, pieces[chunk], force, mass, strength, hot, motion,
            expand_l, contract_l, last, contracted[0] if contracted else None,
        )
        if last:
            *outs, bead_edge, far_edge = outs
        *outs, c16 = outs
        if not pair:
            outs = [outs[0][:, d * beads : (d + 1) * beads] for d in range(bead_count)]
        own_out.append(outs[0])
        contracted.append(c16)
        back = []
        for d in range(1, bead_count):
            on = [(i, (i + d) % bead_count) for i in range(bead_count)]
            back.append(lax.ppermute(outs[d], "bead", on))
        returned.append(back)

    if not pair:
        c16 = jnp.concatenate(contracted, 1) if chunks > 1 else contracted[0]
        everyone = lax.all_gather(c16, "bead", axis=1, tiled=True)
        segments = [([everyone], 0, slab_tiles), *[([x], 0, GT) for x in rims(everyone)]]
        force = pair_forces(
            spots_slab(False), segments, slab_tiles, bead_at, space_at, neighbour_tiles
        )
        parts = [x for chunk in range(chunks) for x in [own_out[chunk]] + returned[chunk]]
        new_pos, new_mom = finish(chunks, bead_at, parts, finish_left, force)
        return new_pos.transpose(1, 0, 2), new_mom.transpose(1, 0, 2)

    beside = lax.ppermute(bead_edge, "bead", SWAP)
    across = lax.ppermute(
        far_edge, ("space", "bead"), permutation(lambda b: 1 if b else -1, 1)
    )
    chunk_tiles = lanes // TILE
    segments = [([x], 0, chunk_tiles) for x in contracted]
    inner = pair_forces(spots_inner, segments, block_tiles - 2 * GT, *ids, True)
    segments = [
        ([contracted[0]], 0, 2 * GT),
        ([contracted[-1]], chunk_tiles - 2 * GT, 2 * GT),
        ([beside], 0, GT),
        ([across], 0, GT),
    ]
    outer = pair_forces(spots_outer, segments, 2 * GT, *ids, True)
    others = [x[0] for x in returned]
    moves = [(i, 0, i) for i in range(chunks)]
    moves += [(chunks + i, 1, i) for i in range(chunks - 1)]
    result = finish_block(
        chunks, 0, moves, bead_at, own_out + others[:-1], finish_left, inner, outer, []
    )
    inner = lax.ppermute(inner, "bead", SWAP)
    outer = lax.ppermute(outer, "bead", SWAP)
    moves = [(chunks - 1, 1, chunks - 1)]
    new_pos, new_mom = finish_block(
        chunks, 1, moves, bead_at, others, finish_left, inner, outer, result
    )
    return new_pos.transpose(1, 0, 2), new_mom.transpose(1, 0, 2)


SWAP = [(0, 1), (1, 0)]


def solution(mesh):
    placed = (
        P("bead", None, "space"),
        P("bead", None, "space"),
        P("space"),
        P("space"),
        P(None, "space"),
        P(None, "space"),
        P(None, "space"),
    )

    return jax.shard_map(
        body,
        mesh=mesh,
        in_specs=placed,
        out_specs=(P("bead", None, "space"), P("bead", None, "space")),
        check_vma=False,
    )
```

```python
import functools
import math

import jax
import jax.numpy as jnp
import numpy as np
from jax import lax
from jax.experimental import pallas as pl
from jax.experimental.pallas import tpu as pltpu
from jax.sharding import PartitionSpec as P


BEADS = 32
KEPT = 4
SUBS = 3
TILE = 128
GT = 2
BPT = 128
APT = 64
ROWS = 4 * KEPT
LOGS = 3 * KEPT

time_step = 0.3
spring_freq = 80.0
bond_stiff = 0.2
bond_rest = 1.0
angle_stiff = 0.1
angle_rest = 0.5
range_sq = 4.0
HIGH = lax.Precision.HIGHEST
IN_VMEM = pl.BlockSpec(memory_space=pltpu.VMEM)
IN_SMEM = pl.BlockSpec(memory_space=pltpu.SMEM)
IN_SPACE = pltpu.MemorySpace.VMEM


def near(x):
    return pltpu.with_memory_space_constraint(x, IN_SPACE)


def far(x):
    return pltpu.with_memory_space_constraint(x, pltpu.MemorySpace.HBM)


def vmem_out(shape, dtype):
    return IN_SPACE(shape, dtype)


PARAMS = pltpu.CompilerParams(vmem_limit_bytes=20 * 1024 * 1024)
COST = pl.CostEstimate(flops=10_000_000, bytes_accessed=100_000, transcendentals=0)
F32 = jnp.float32
BF16 = jnp.bfloat16


def mode_table(number):
    within = np.arange(number)
    result = np.zeros((number, number))
    for column in range(number):
        if column == 0:
            result[:, column] = 1.0 / math.sqrt(number)
        elif 2 * column < number:
            result[:, column] = math.sqrt(2.0 / number) * np.cos(
                2 * np.pi * within * column / number
            )
        elif 2 * column == number:
            result[:, column] = (-1.0) ** within / math.sqrt(number)
        else:
            result[:, column] = math.sqrt(2.0 / number) * np.sin(
                2 * np.pi * within * column / number
            )
    return result


def contract_table(number, kept):
    larger = mode_table(number)
    smaller = mode_table(kept)
    chosen = [column if 2 * column <= kept else number - kept + column for column in range(kept)]
    return math.sqrt(kept / number) * smaller @ larger[:, chosen].T


def motion_table(number, interval):
    freqs = 2.0 * spring_freq * np.sin(np.pi * np.arange(number) / number)
    modes = mode_table(number)
    safe = np.where(freqs > 0, freqs, 1.0)
    gains = np.where(freqs > 0, np.sin(freqs * interval) / safe, interval)
    drags = freqs * np.sin(freqs * interval)
    stay = modes @ np.diag(np.cos(freqs * interval)) @ modes.T
    gain = modes @ np.diag(gains) @ modes.T
    drag = modes @ np.diag(drags) @ modes.T
    return np.block([[stay, gain], [-drag, stay]])


def np_split(table, parts):
    out, rest = [], np.asarray(table, np.float64)
    for _ in range(parts):
        piece = rest.astype(np.float32).astype(jnp.bfloat16)
        out.append(piece)
        rest = rest - piece.astype(np.float64)
    return out


def stacked_left(table, parts=3):
    pieces = np_split(table, parts)
    zero = np.zeros_like(pieces[0])
    return np.concatenate(
        [
            np.concatenate([pieces[i]] * (parts - i) + [zero] * i, axis=1)
            for i in range(parts)
        ],
        axis=0,
    )


def split(x, parts):
    out = []
    for i in range(parts):
        piece = x.astype(BF16)
        out.append(piece)
        if i < parts - 1:
            x = x - piece.astype(F32)
    return out


def mm(left, right):
    return jnp.dot(left, right, preferred_element_type=F32)


def exact(left, x, parts=3):
    out = mm(left, jnp.concatenate(split(x, parts), axis=0))
    rows = out.shape[0] // parts
    total = out[:rows]
    for i in range(1, parts):
        total = total + out[i * rows : (i + 1) * rows]
    return total


def packed_left(table):
    high, mid, low = np_split(table, 3)
    zero = np.zeros_like(high)
    return np.concatenate(
        [
            np.concatenate([high, high, high, mid], axis=1),
            np.concatenate([low, mid, zero, zero], axis=1),
        ],
        axis=0,
    )


def packed_exact(left, x):
    high, mid, low = split(x, 3)
    out = mm(left, jnp.concatenate([high, mid, low, high], axis=0))
    rows = out.shape[0] // 2
    return out[:rows] + out[rows:]


def contract_rows(beads):
    table = contract_table(BEADS, KEPT)
    tables = []
    for turn in range(0, BEADS, beads):
        order = (np.arange(BEADS) + turn) % BEADS
        tables.append(table[:, order])
    return tables


def contract_left(table):
    out = np.zeros((ROWS, 3 * table.shape[1]))
    for c in range(KEPT):
        for k in range(3):
            out[k * KEPT + c, k * table.shape[1] : (k + 1) * table.shape[1]] = table[c]
    return out


def expand_left(table):
    return BEADS / KEPT * contract_left(table).T


def pack_rows(target, x):
    lanes = x.shape[1]
    target[:, :lanes] = x[:8]
    target[:4, lanes:] = x[8:12, : lanes // 2]
    target[4:, lanes:] = x[8:12, lanes // 2 :]


def unpacked(x):
    lanes = x.shape[1] * 2 // 3
    last = jnp.concatenate([x[:4, lanes:], x[4:, lanes:]], axis=1)
    return jnp.concatenate([x[:, :lanes], last, jnp.zeros_like(last)], axis=0)


def begin_kernel(chunks, bead, left, strengths, pos, *refs):
    mine, theirs, straight = refs[:3]
    whole, table, rows, spare, sems = refs[-5:]
    blocks = list(refs[3:-5]) + [spare.at[i] for i in range(chunks)]
    lanes = blocks[0].shape[2]
    slab = whole.shape[1]
    starts, copies = [], []
    for i in range(2 * chunks):
        owner = bead[0] if i < chunks else 1 - bead[0]
        starts.append(pl.multiple_of((owner * chunks + i % chunks) * lanes, TILE))
    for i, block in enumerate(blocks):
        copy = pltpu.make_async_copy(
            pos.at[:, :, pl.ds(starts[i], lanes)], block, sems.at[i]
        )
        copy.start()
        copies.append(copy)
    small = [
        pltpu.make_async_copy(left.at[bead[0]], table, sems.at[len(copies)]),
        pltpu.make_async_copy(strengths, rows, sems.at[len(copies) + 1]),
    ]
    for copy in small:
        copy.start()
    for copy in small:
        copy.wait()
    logs = math.log2(math.e) * jnp.log(rows[...])
    for t in range(slab // TILE):
        whole[LOGS : LOGS + 1, t * TILE : (t + 1) * TILE] = logs[t : t + 1]
    for i, block in enumerate(blocks):
        copies[i].wait()
        x = jnp.concatenate([block[c] for c in range(3)], axis=0)
        where = pl.ds(starts[i], lanes)
        row = lax.broadcasted_iota(jnp.int32, (ROWS, lanes), 0)
        whole[:, where] = jnp.where(row == LOGS, whole[:, where], exact(table[...], x))

    block, rim = slab // 2, GT * TILE
    size = block + rim

    def sides(which):
        first, other = (0, block - rim) if which == 0 else (block - rim, 0)
        mine[...] = whole[:, first : first + size]
        head, tail = whole[:, :rim], whole[:, slab - rim :]
        straight[...] = tail if which == 0 else head
        relay = head if which == 0 else tail
        pack_rows(theirs, jnp.concatenate([whole[:, other : other + size], relay], axis=1))

    for which in range(2):
        pl.when(bead[0] == which)(functools.partial(sides, which))


def fetch_kernel(moves, chunks, bead, pos, mom, *refs):
    *blocks, sems = refs
    lanes = blocks[0].shape[2]
    copies = []
    for i, (block, plane, source, comp, comps, owner, chunk) in enumerate(moves):
        side = bead[0] if owner == 0 else 1 - bead[0]
        start = pl.multiple_of((side * chunks + chunk) * lanes, TILE)
        copy = pltpu.make_async_copy(
            (pos, mom)[source].at[pl.ds(comp, comps), :, pl.ds(start, lanes)],
            blocks[block].at[pl.ds(plane, comps)],
            sems.at[i],
        )
        copy.start()
        copies.append(copy)
    for copy in copies:
        copy.wait()


def fetch(moves, planes, chunks, bead, pos, mom):
    beads, slab = mom.shape[1:]
    lanes = slab // (2 * chunks)
    return pl.pallas_call(
        functools.partial(fetch_kernel, moves, chunks),
        in_specs=[IN_SMEM] + [pl.BlockSpec(memory_space=pl.ANY)] * 2,
        out_specs=[IN_VMEM] * len(planes),
        out_shape=[vmem_out((n, beads, lanes), F32) for n in planes],
        scratch_shapes=[pltpu.SemaphoreType.DMA((len(moves),))],
        compiler_params=PARAMS,
        cost_estimate=COST,
        name="fetch",
    )(bead, far(pos), far(mom))


def begin(chunks, bead, left, strengths, pos):
    beads, slab = pos.shape[1:]
    block, rim = slab // 2, GT * TILE
    lanes = block // chunks
    shapes = [(ROWS, block + rim), (8, 3 * (block + 2 * rim) // 2), (ROWS, rim)]
    shapes += [(3, beads, lanes)] * chunks
    return pl.pallas_call(
        functools.partial(begin_kernel, chunks),
        in_specs=[IN_SMEM] + [pl.BlockSpec(memory_space=pl.ANY)] * 3,
        out_specs=[IN_VMEM] * len(shapes),
        out_shape=[vmem_out(s, F32) for s in shapes],
        scratch_shapes=[
            pltpu.VMEM((ROWS, slab), F32),
            pltpu.VMEM(left.shape[1:], left.dtype),
            pltpu.VMEM(strengths.shape, F32),
            pltpu.VMEM((chunks, 3, beads, lanes), F32),
            pltpu.SemaphoreType.DMA((2 * chunks + 2,)),
        ],
        compiler_params=PARAMS,
        cost_estimate=COST,
        name="begin",
    )(bead, far(left), far(strengths), far(pos))


def relay_kernel(own, received, out):
    rim = GT * TILE
    size = received.shape[1] * 2 // 3
    more = jnp.concatenate([received[:, size - rim : size], received[4:, -rim:]], axis=0)
    out[...] = own[...] + jnp.concatenate([more, jnp.zeros_like(more[:4])], axis=0)


def relay(own, received):
    return pl.pallas_call(
        relay_kernel,
        in_specs=[IN_VMEM] * 2,
        out_specs=IN_VMEM,
        out_shape=vmem_out(own.shape, F32),
        compiler_params=PARAMS,
        cost_estimate=COST,
        name="relay",
    )(near(own), near(received))


def partial_kernel(bead, left, strengths, pos, out):
    comps, _, lanes = pos.shape
    logs = math.log2(math.e) * jnp.log(strengths[...])
    logs = jnp.concatenate([logs[t : t + 1] for t in range(lanes // TILE)], axis=1)
    row = lax.broadcasted_iota(jnp.int32, (ROWS, lanes), 0)
    x = jnp.concatenate([pos[c] for c in range(comps)], axis=0)
    out[...] = jnp.where(row == LOGS, logs, exact(left[bead[0]], x))


def partial_rows(bead, left, strengths, pos):
    beads, slab = pos.shape[1:]
    lanes = math.gcd(slab, 1024)
    return pl.pallas_call(
        partial_kernel,
        grid=(slab // lanes,),
        in_specs=[
            IN_SMEM,
            IN_VMEM,
            pl.BlockSpec((lanes // TILE, TILE), lambda i: (i, 0)),
            pl.BlockSpec((3, beads, lanes), lambda i: (0, 0, i)),
        ],
        out_specs=pl.BlockSpec((ROWS, lanes), lambda i: (0, i)),
        out_shape=jax.ShapeDtypeStruct((ROWS, slab), F32),
        name="partial_rows",
    )(bead, left, strengths, pos)


def prepare_kernel(group, bead, bonds, angles, hot):
    lane = lax.broadcasted_iota(jnp.int32, (1, TILE), 1)
    atom = lax.broadcasted_iota(jnp.int32, (TILE, 2 * TILE), 0)
    low = lane < APT

    def merge(first, second, odd):
        a = pltpu.roll(first, APT, 1) if odd else first
        b = second if odd else pltpu.roll(second, APT, 1)
        return jnp.where(low, a, b)

    def tiles(i, carry):
        at = (bead[0] * (hot.shape[0] // group) + i) * group
        bond_rows = bonds[:, pl.ds(pl.multiple_of(at * BPT, BPT), group * BPT)]
        angle_rows = angles[:, pl.ds(pl.multiple_of(at * APT, TILE), group * APT)]
        for t in range(group):
            one = bond_rows[0:1, t * TILE : (t + 1) * TILE]
            other = bond_rows[1:2, t * TILE : (t + 1) * TILE]
            odd = t % 2
            window = slice((t // 2) * TILE, (t // 2 + 1) * TILE)
            first, middle, last = [angle_rows[e : e + 1, window] for e in range(3)]
            opposite = merge(last, first, odd)
            centre = merge(middle, middle, odd)
            gains = jnp.concatenate([other, centre], axis=1)
            losses = jnp.concatenate([one, opposite], axis=1)
            table = (atom == gains).astype(F32) - (atom == losses).astype(F32)
            hot[i * group + t] = table.astype(BF16)
        return carry

    lax.fori_loop(0, hot.shape[0] // group, tiles, 0)


def prepare(bead, bond_ends, angle_ends, block_tiles):
    return pl.pallas_call(
        functools.partial(prepare_kernel, math.gcd(block_tiles, 4)),
        in_specs=[IN_SMEM, IN_VMEM, IN_VMEM],
        out_specs=IN_VMEM,
        out_shape=vmem_out((block_tiles, TILE, 2 * TILE), BF16),
        compiler_params=PARAMS,
        cost_estimate=COST,
        name="prepare",
    )(bead, bond_ends, angle_ends)


def pair_kernel(spots, seg_sizes, own_count, packed, bead, space, nbr, *refs):
    total = sum(n for *_, n in seg_sizes)
    count = sum(n for n, *_ in seg_sizes)
    seg_refs = refs[:count]
    target, feat_i, feat_m, feat_p, base, *weights, held = refs[count:]
    out = held if packed else target
    column, own_spot, spot = spots((bead[0], space[0]))
    row = lax.broadcasted_iota(jnp.int32, (ROWS, TILE), 0)
    slot = row // KEPT
    scale = math.sqrt(2.0 * math.log2(math.e) / range_sq)
    same = (
        lax.broadcasted_iota(jnp.int32, (ROWS, ROWS), 0) % KEPT
        == lax.broadcasted_iota(jnp.int32, (ROWS, ROWS), 1) % KEPT
    ).astype(F32)

    def features(tile, c16):
        base[tile] = c16
        logs = c16[LOGS : LOGS + 1]
        place = jnp.where(slot == 3, 0.0, c16)
        scaled = place * scale
        high, low = [piece.astype(F32) for piece in split(scaled, 2)]
        square = jnp.dot(same, scaled * scaled, precision=HIGH, preferred_element_type=F32)
        half = -0.5 * square

        def three(x):
            a, b, c = [piece.astype(F32) for piece in split(x, 3)]
            return jnp.where(slot == 0, a, jnp.where(slot == 1, b, jnp.where(slot == 2, c, 0.0)))

        ones = jnp.where(slot == 3, 0.0, 1.0)
        mine = jnp.concatenate([high, high, low, low, three(half), ones], axis=0)
        theirs = jnp.concatenate(
            [high, low, high, low, ones, three(half + logs), ones, ones], axis=0
        )
        feat_i[tile] = mine.astype(BF16)
        feat_m[tile] = jnp.transpose(theirs, (1, 0)).astype(BF16)
        one = jnp.ones((ROWS, TILE), F32)
        p_high, p_low = [piece.astype(F32) for piece in split(place, 2)]
        feat_p[tile] = jnp.concatenate([one, p_high, p_low], axis=0).astype(BF16)

    def piece(ref, begins, i):
        moving = callable(begins)
        at = (begins(bead[0]) if moving else begins) + i

        def lanes(tile):
            if moving:
                return pl.ds(pl.multiple_of(tile * TILE, TILE), TILE)
            return slice(tile * TILE, (tile + 1) * TILE)

        if ref.shape[0] == ROWS:
            return ref[:, lanes(at)]
        tiles = ref.shape[1] * 2 // 3 // TILE
        half = tiles // 2
        upper = at >= half
        last = ref[:, lanes(tiles + jnp.where(upper, at - half, at))]
        last = jnp.where(upper, last[4:], last[:4])
        return jnp.concatenate([ref[:, lanes(at)], last, jnp.zeros_like(last)], axis=0)

    tile = 0
    at = 0
    for number, begins, tiles in seg_sizes:
        group = seg_refs[at : at + number]
        at += number
        for i in range(tiles):
            c16 = piece(group[0], begins, i)
            for other in group[1:]:
                c16 = c16 + piece(other, begins, i)
            features(tile, c16)
            tile += 1
    assert tile == total

    groups = 6
    wide_row = lax.broadcasted_iota(jnp.int32, (groups * ROWS, TILE), 0)
    pick = [(wide_row % KEPT == c).astype(BF16) for c in range(KEPT)]
    owner = row % KEPT

    def close(t, u):
        return spot(nbr[u, column(t)])

    def weigh(t, weights):
        features_i = feat_i[own_spot(t)]
        right = jnp.concatenate([features_i * pick[c] for c in range(KEPT)], axis=1)
        right = jnp.concatenate([right, jnp.zeros((2 * ROWS, KEPT * TILE), BF16)], axis=0)
        left = jnp.concatenate([feat_m[close(t, u)] for u in range(3)], axis=0)
        power = mm(left, right)
        for u in range(3):
            high, low = split(jnp.exp2(power[u * TILE : (u + 1) * TILE]), 2)
            weights[2 * u * TILE : (2 * u + 1) * TILE] = high
            weights[(2 * u + 1) * TILE : (2 * u + 2) * TILE] = low

    def pull(t, weights):
        left = []
        for u in range(3):
            piece = feat_p[close(t, u)]
            left += [piece, piece]
        total_p = mm(jnp.concatenate(left, axis=1), weights[...])
        sums = total_p[:ROWS]
        pulls = total_p[ROWS : 2 * ROWS] + total_p[2 * ROWS :]
        c16 = base[own_spot(t)]
        factor = (2.0 / range_sq) * jnp.exp2(c16[LOGS : LOGS + 1])
        result = jnp.zeros((ROWS, TILE), F32)
        for c in range(KEPT):
            lanes = slice(c * TILE, (c + 1) * TILE)
            force = factor * (c16 * sums[:, lanes] - pulls[:, lanes])
            result = jnp.where((owner == c) & (slot < 3), force, result)
        lane = t * TILE if isinstance(t, int) else pl.multiple_of(t * TILE, TILE)
        out[:, pl.ds(lane, TILE)] = result

    unroll = math.gcd(own_count, 4)
    weigh(0, weights[0])

    def some_tiles(t, last):
        for j in range(unroll):
            if not (last and j == unroll - 1):
                weigh(t + j + 1, weights[(j + 1) % 2])
            pull(t + j, weights[j % 2])

    def loop(i, carry):
        some_tiles(unroll * i, False)
        return carry

    lax.fori_loop(0, own_count // unroll - 1, loop, 0)
    some_tiles(own_count - unroll, True)
    if packed:
        pack_rows(target, held[...])


def pair_forces(spots, segments, own_count, bead, space, neighbour_tiles, packed=False):
    sizes = tuple((len(group), start, tiles) for group, start, tiles in segments)
    total = sum(n for *_, n in sizes)
    assert own_count % 2 == 0
    flat = [array for group, *_ in segments for array in group]
    return pl.pallas_call(
        functools.partial(pair_kernel, spots, sizes, own_count, packed),
        in_specs=[IN_SMEM] * 3 + [IN_VMEM] * len(flat),
        out_specs=IN_VMEM,
        out_shape=vmem_out(
            (8, 3 * own_count * TILE // 2) if packed else (ROWS, own_count * TILE), F32
        ),
        scratch_shapes=[
            pltpu.VMEM((total, 6 * ROWS, TILE), BF16),
            pltpu.VMEM((total, TILE, 8 * ROWS), BF16),
            pltpu.VMEM((total, 3 * ROWS, TILE), BF16),
            pltpu.VMEM((total, ROWS, TILE), F32),
            pltpu.VMEM((6 * TILE, KEPT * TILE), BF16),
            pltpu.VMEM((6 * TILE, KEPT * TILE), BF16),
            pltpu.VMEM((ROWS, own_count * TILE), F32),
        ],
        compiler_params=PARAMS,
        cost_estimate=COST,
        name="pair_forces",
    )(bead, space, far(neighbour_tiles), *[near(x) for x in flat])


def whole_force(inner, outer):
    rim = GT * TILE
    inner, outer = unpacked(inner[...]), unpacked(outer[...])
    return jnp.concatenate([outer[:, :rim], inner, outer[:, rim:]], axis=1)


def step_kernel(parts, count, forces, chunk, chunks, group, edge, bead, *refs):
    pieces = refs[:count]
    at = count
    force = refs[at] if forces == 1 else whole_force(*refs[at : at + 2])
    at += forces
    mass_rows, strength_rows, hot, motion, expand, contract = refs[at : at + 6]
    before = refs[at + 6] if edge and chunk else None
    outs = refs[len(refs) - parts - 1 - 2 * edge :]
    c_out = outs[parts]
    interval = time_step / SUBS
    width = group * TILE
    first = chunk * group
    motion_l = motion[...]

    def per_atom(rows):
        at = (bead[0] * chunks + chunk) * group
        return jnp.concatenate([rows[pl.ds(at + t, 1), :] for t in range(group)], axis=1)

    masses = per_atom(mass_rows)
    inverse = 1.0 / masses

    planes = [(piece, plane) for piece in pieces for plane in range(piece.shape[0])]

    def gathered(kind, c):
        found = [planes[6 * part + 3 * kind + c] for part in range(parts)]
        found = [piece[plane] for piece, plane in found]
        return found[0] if parts == 1 else jnp.concatenate(found, axis=0)

    q = [gathered(0, c) for c in range(3)]
    p = [gathered(1, c) for c in range(3)]
    kick = exact(expand[bead[0]], force[:, first * TILE : first * TILE + width])
    v = [
        (p[c] + 0.5 * time_step * kick[c * BEADS : (c + 1) * BEADS]) * inverse for c in range(3)
    ]

    def bonded(q):
        forces = []
        for t in range(group):
            lanes = slice(t * TILE, (t + 1) * TILE)
            rows = jnp.concatenate([q[c][:, lanes] for c in range(3)], axis=0)
            seen = mm(jnp.concatenate(split(rows, 2), axis=0), hot[first + t])
            seen = seen[: 3 * BEADS] + seen[3 * BEADS :]
            stretch, arms = seen[:, :TILE], seen[:, TILE:]
            s = [stretch[c * BEADS : (c + 1) * BEADS] for c in range(3)]
            a = [arms[c * BEADS : (c + 1) * BEADS] for c in range(3)]
            length = s[0] * s[0] + s[1] * s[1] + s[2] * s[2]
            g = bond_stiff * (bond_rest - length)
            turned = [pltpu.roll(x, APT, 1) for x in a]
            inner = a[0] * turned[0] + a[1] * turned[1] + a[2] * turned[2]
            h = angle_stiff * (angle_rest - inner)
            bonds = jnp.concatenate([g * x for x in s], axis=0)
            angles = jnp.concatenate([h * x for x in turned], axis=0)
            both = jnp.concatenate([bonds, angles], axis=1)
            out = lax.dot_general(
                jnp.concatenate(split(both, 2), axis=0),
                hot[first + t],
                (((1,), (1,)), ((), ())),
                preferred_element_type=F32,
            )
            forces.append(out[: 3 * BEADS] + out[3 * BEADS :])
        return [
            jnp.concatenate([f[c * BEADS : (c + 1) * BEADS] for f in forces], axis=1)
            for c in range(3)
        ]

    for sub in range(SUBS):
        pushed = bonded(q)
        factor = (0.5 if sub == 0 else 1.0) * interval * inverse
        v = [v[c] + factor * pushed[c] for c in range(3)]
        for c in range(3):
            moved = packed_exact(motion_l, jnp.concatenate([q[c], v[c]], axis=0))
            q[c], v[c] = moved[:BEADS], moved[BEADS:]
    pushed = bonded(q)
    p = [masses * v[c] + (0.5 * interval) * pushed[c] for c in range(3)]
    beads = BEADS // parts
    for i in range(parts):
        for c in range(3):
            outs[i][c] = q[c][i * beads : (i + 1) * beads]
            outs[i][3 + c] = p[c][i * beads : (i + 1) * beads]
    rows = jnp.concatenate(q, axis=0)
    c16 = exact(contract[bead[0]], rows, 2)
    row = lax.broadcasted_iota(jnp.int32, (ROWS, width), 0)
    logs = math.log2(math.e) * jnp.log(per_atom(strength_rows))
    c16 = jnp.where(row == LOGS, logs, c16)
    c_out[...] = c16
    if edge:
        rim = GT * TILE
        head = c16[:, :rim] if before is None else before[:, :rim]
        tail = c16[:, width - rim :]
        outs[-2][...] = jnp.where(bead[0] == 0, tail, head)
        outs[-1][...] = jnp.where(bead[0] == 0, head, tail)


def substeps(chunk, chunks, bead, pieces, force, mass, strength, hot, motion, expand, contract, edge, before):
    beads, lanes = pieces[0].shape[1:]
    parts = BEADS // beads
    extra = [before] if edge and chunk else []
    shapes = [(6, beads, lanes)] * parts + [(ROWS, lanes)]
    if edge:
        shapes += [(ROWS, GT * TILE)] * 2
    return pl.pallas_call(
        functools.partial(
            step_kernel, parts, len(pieces), len(force), chunk, chunks, lanes // TILE, int(edge)
        ),
        in_specs=[IN_SMEM] + [IN_VMEM] * (len(pieces) + len(force) + 6 + len(extra)),
        out_specs=[IN_VMEM] * len(shapes),
        out_shape=[vmem_out(s, F32) for s in shapes],
        compiler_params=PARAMS,
        cost_estimate=COST,
        name="substeps",
    )(
        bead,
        *[near(x) for x in pieces + force],
        mass,
        strength,
        near(hot),
        motion,
        expand,
        contract,
        *[near(x) for x in extra],
    )


def finish_kernel(chunks, bead, expand, force, *refs):
    pos, mom = refs[-2:]
    parts = refs[:-2]
    bead_count = len(parts) // chunks
    lanes = parts[0].shape[2]
    comp = pl.program_id(0)
    table = expand[bead[0], comp]
    for i, part in enumerate(parts):
        chunk, distance = divmod(i, bead_count)
        block = lax.rem(bead[0] + bead_count - distance, bead_count)
        start = pl.multiple_of(block * (chunks * lanes) + chunk * lanes, TILE)
        where = pl.ds(start, lanes)
        pos[0, :, where] = part[comp]
        mom[0, :, where] = part[3 + comp] + 0.5 * time_step * exact(table, force[:, where])


def finish(chunks, bead, parts, expand, force):
    slab = force.shape[1]
    beads = parts[0].shape[1]
    return pl.pallas_call(
        functools.partial(finish_kernel, chunks),
        grid=(3,),
        in_specs=[IN_SMEM] + [IN_VMEM] * (2 + len(parts)),
        out_specs=[pl.BlockSpec((1, beads, slab), lambda i: (i, 0, 0))] * 2,
        out_shape=[jax.ShapeDtypeStruct((3, beads, slab), F32)] * 2,
        compiler_params=PARAMS,
        cost_estimate=COST,
        name="finish",
    )(bead, expand, near(force), *[near(x) for x in parts])


def finish_block_kernel(chunks, owner, moves, count, bead, expand, inner, outer, *refs):
    parts = refs[:count]
    pos, mom, held, sems = refs[-4:]
    lanes = parts[0].shape[2]
    blocks = [bead[0], 1 - bead[0]]

    def where(owner, chunk):
        return pl.ds(pl.multiple_of((blocks[owner] * chunks + chunk) * lanes, TILE), lanes)

    copies = []

    def copy(source, target):
        copies.append(pltpu.make_async_copy(source, target, sems.at[len(copies)]))
        copies[-1].start()

    for part, move_owner, chunk in moves:
        copy(parts[part].at[pl.ds(0, 3)], pos.at[:, :, where(move_owner, chunk)])
    force = whole_force(inner, outer)
    for chunk in range(chunks):
        lane = slice(chunk * lanes, (chunk + 1) * lanes)
        for c in range(3):
            kick = 0.5 * time_step * exact(expand[bead[0], c], force[:, lane])
            held[c, :, lane] = parts[chunk][3 + c] + kick
        copy(held.at[:, :, pl.ds(chunk * lanes, lanes)], mom.at[:, :, where(owner, chunk)])
    for waiting in copies:
        waiting.wait()


def finish_block(chunks, owner, moves, bead, parts, expand, inner, outer, before):
    beads, lanes = parts[0].shape[1:]
    block = lanes * chunks
    anywhere = pl.BlockSpec(memory_space=pl.ANY)
    at = 4 + len(parts)
    return pl.pallas_call(
        functools.partial(finish_block_kernel, chunks, owner, moves, len(parts)),
        in_specs=[IN_SMEM] + [IN_VMEM] * (3 + len(parts)) + [anywhere] * len(before),
        out_specs=[anywhere] * 2,
        out_shape=[pltpu.MemorySpace.HBM((3, beads, 2 * block), F32)] * 2,
        scratch_shapes=[
            pltpu.VMEM((3, beads, block), F32),
            pltpu.SemaphoreType.DMA((len(moves) + chunks,)),
        ],
        input_output_aliases={at + i: i for i in range(len(before))},
        compiler_params=PARAMS,
        cost_estimate=COST,
        name="finish_block",
    )(
        bead,
        expand,
        near(inner),
        near(outer),
        *[near(x) for x in parts],
        *[far(x) for x in before],
    )


def body(positions, momenta, masses, strengths, bond_ends, angle_ends, neighbour_tiles):
    beads, _, slab = positions.shape
    bead_count = lax.axis_size("bead")
    bead = lax.axis_index("bead")
    space_count = lax.axis_size("space")
    space = lax.axis_index("space")
    block = slab // bead_count
    slab_tiles = slab // TILE
    block_tiles = block // TILE
    all_tiles = slab_tiles * space_count
    rim = GT * TILE
    chunks = 2 if block_tiles % 4 == 0 else 1
    lanes = block // chunks
    interval = time_step / SUBS
    pair = bead_count == 2

    pos = positions.transpose(1, 0, 2)
    mom = momenta.transpose(1, 0, 2)
    bead_at = jnp.reshape(bead, (1,)).astype(jnp.int32)
    space_at = jnp.reshape(space, (1,)).astype(jnp.int32)
    mass = masses.reshape(slab_tiles, TILE)
    strength = strengths.reshape(slab_tiles, TILE)
    turned = contract_rows(beads)
    table = contract_table(BEADS, KEPT)
    own_tables = [table[:, i * beads : (i + 1) * beads] for i in range(bead_count)]

    def stack(tables):
        return jnp.asarray(np.stack(tables))

    begin_left = stack([stacked_left(contract_left(t)) for t in own_tables])
    finish_left = stack(
        [
            np.stack(
                [stacked_left(expand_left(t)[c * beads : (c + 1) * beads]) for c in range(3)]
            )
            for t in own_tables
        ]
    )
    contract_l = stack([stacked_left(contract_left(t), 2) for t in turned])
    expand_l = stack([stacked_left(expand_left(t)) for t in turned])
    motion = jnp.asarray(packed_left(motion_table(BEADS, interval)))

    def lanes_of(x, start, size):
        return lax.dynamic_slice_in_dim(x, start, size, x.ndim - 1)

    def permutation(step, flip):
        return [
            (s * 2 + b, ((s + step(b)) % space_count) * 2 + (b ^ flip))
            for s in range(space_count)
            for b in range(2)
        ]

    def rims(x):
        up = [(i, (i + 1) % space_count) for i in range(space_count)]
        down = [((i + 1) % space_count, i) for i in range(space_count)]
        return (
            lax.ppermute(x[:, slab - rim :], "space", up),
            lax.ppermute(x[:, :rim], "space", down),
        )

    def relative(tile, info):
        x = tile - info[1] * slab_tiles
        x = jnp.where(x >= all_tiles - GT, x - all_tiles, x)
        return jnp.where(x < -GT, x + all_tiles, x)

    def spots_inner(info):
        def spot(tile):
            return relative(tile, info) - info[0] * block_tiles

        return lambda t: t + GT + info[0] * block_tiles, lambda t: t + GT, spot

    def spots_outer(info):
        bead_at = 4 * GT
        far_at = bead_at + GT
        left_at = jnp.where(info[0] == 0, far_at, bead_at)
        right_at = jnp.where(info[0] == 0, bead_at, far_at)

        def own(t):
            return jnp.where(t < GT, t, t + block_tiles - 2 * GT)

        def place(x):
            return jnp.where(x < 2 * GT, x, x - (block_tiles - 4 * GT))

        def spot(tile):
            x = relative(tile, info) - info[0] * block_tiles
            right = jnp.where(x >= block_tiles, x - block_tiles + right_at, place(x))
            return jnp.where(x < 0, x + GT + left_at, right)

        return lambda t: own(t) + info[0] * block_tiles, lambda t: place(own(t)), spot

    def spots_slab(first):
        def spots(info):
            start = info[0] * block_tiles if first else 0

            def spot(tile):
                x = relative(tile, info)
                return jnp.where(x < 0, x + GT + slab_tiles, jnp.where(x >= slab_tiles, x + GT, x))

            return lambda t: t + start, lambda t: t + start, spot

        return spots

    pieces = [[] for _ in range(chunks)]
    if pair:
        (lead,) = fetch([(0, 0, 0, 0, 2, 1, 0)], [2], chunks, bead_at, pos, mom)
        other = lax.ppermute(lead, "bead", SWAP)
        mine, theirs, straight, *own_q = begin(chunks, bead_at, begin_left, strength, pos)
        theirs = lax.ppermute(theirs, "bead", SWAP)
        moves = [(0, 0, 0, 2, 1, 1, 0), (0, 1, 1, 0, 3, 1, 0)]
        blocks = fetch(moves, [4], chunks, bead_at, pos, mom)
        moves = []
        for chunk in range(1, chunks):
            moves += [(chunk - 1, 0, 0, 0, 3, 1, chunk), (chunk - 1, 3, 1, 0, 3, 1, chunk)]
        moves += [(chunks - 1 + chunk, 0, 1, 0, 3, 0, chunk) for chunk in range(chunks)]
        planes = [6] * (chunks - 1) + [3] * chunks
        blocks += fetch(moves, planes, chunks, bead_at, pos, mom)
        for chunk in range(chunks):
            moment = lax.ppermute(blocks[chunk], "bead", SWAP)
            pieces[chunk] = [own_q[chunk], blocks[chunks + chunk]]
            pieces[chunk] += [moment] if chunk else [other, moment]
        straight = relay(straight, theirs)
        straight = lax.ppermute(
            straight, ("space", "bead"), permutation(lambda b: -1 if b else 1, 0)
        )
        both = [mine, theirs]
        inside = [(both, lambda b: b * GT, block_tiles)]
        rim_tiles = [
            (both, lambda b: b * GT, 2 * GT),
            (both, lambda b: b * GT + block_tiles - 2 * GT, 2 * GT),
            (both, lambda b: (1 - b) * block_tiles, GT),
            ([straight], 0, GT),
        ]
    else:
        part = partial_rows(bead_at, begin_left, strength, pos)
        summed = lax.psum(part, "bead")
        logs_row = lax.broadcasted_iota(jnp.int32, summed.shape, 0) == LOGS
        summed = jnp.where(logs_row, jnp.log2(strengths)[None, :], summed)
        segments = [([summed], 0, slab_tiles), *[([x], 0, GT) for x in rims(summed)]]
        spots = spots_slab(True)
        for chunk in range(chunks):
            parts = []
            for d in range(bead_count):
                start = jnp.mod(bead - d, bead_count) * block + chunk * lanes
                piece = jnp.concatenate(
                    [lanes_of(pos, start, lanes), lanes_of(mom, start, lanes)], 0
                )
                back = [(i, (i - d) % bead_count) for i in range(bead_count)]
                parts.append(lax.ppermute(piece, "bead", back) if d else piece)
            pieces[chunk] = [jnp.concatenate(parts, 1)]

    hot = prepare(bead_at, bond_ends, angle_ends, block_tiles)
    if pair:
        ids = bead_at, space_at, neighbour_tiles
        inner = pair_forces(spots_inner, inside, block_tiles - 2 * GT, *ids, True)
        outer = pair_forces(spots_outer, rim_tiles, 2 * GT, *ids, True)
        force = [inner, outer]
    else:
        force = [pair_forces(spots, segments, block_tiles, bead_at, space_at, neighbour_tiles)]

    own_out, returned, contracted = [], [], []
    for chunk in range(chunks):
        last = pair and chunk == chunks - 1
        outs = substeps(
            chunk, chunks, bead_at, pieces[chunk], force, mass, strength, hot, motion,
            expand_l, contract_l, last, contracted[0] if contracted else None,
        )
        if last:
            *outs, bead_edge, far_edge = outs
        *outs, c16 = outs
        if not pair:
            outs = [outs[0][:, d * beads : (d + 1) * beads] for d in range(bead_count)]
        own_out.append(outs[0])
        contracted.append(c16)
        back = []
        for d in range(1, bead_count):
            on = [(i, (i + d) % bead_count) for i in range(bead_count)]
            back.append(lax.ppermute(outs[d], "bead", on))
        returned.append(back)

    if not pair:
        c16 = jnp.concatenate(contracted, 1) if chunks > 1 else contracted[0]
        everyone = lax.all_gather(c16, "bead", axis=1, tiled=True)
        segments = [([everyone], 0, slab_tiles), *[([x], 0, GT) for x in rims(everyone)]]
        force = pair_forces(
            spots_slab(False), segments, slab_tiles, bead_at, space_at, neighbour_tiles
        )
        parts = [x for chunk in range(chunks) for x in [own_out[chunk]] + returned[chunk]]
        new_pos, new_mom = finish(chunks, bead_at, parts, finish_left, force)
        return new_pos.transpose(1, 0, 2), new_mom.transpose(1, 0, 2)

    beside = lax.ppermute(bead_edge, "bead", SWAP)
    across = lax.ppermute(
        far_edge, ("space", "bead"), permutation(lambda b: 1 if b else -1, 1)
    )
    chunk_tiles = lanes // TILE
    segments = [([x], 0, chunk_tiles) for x in contracted]
    inner = pair_forces(spots_inner, segments, block_tiles - 2 * GT, *ids, True)
    segments = [
        ([contracted[0]], 0, 2 * GT),
        ([contracted[-1]], chunk_tiles - 2 * GT, 2 * GT),
        ([beside], 0, GT),
        ([across], 0, GT),
    ]
    outer = pair_forces(spots_outer, segments, 2 * GT, *ids, True)
    others = [x[0] for x in returned]
    moves = [(i, 0, i) for i in range(chunks)]
    moves += [(chunks + i, 1, i) for i in range(chunks - 1)]
    result = finish_block(
        chunks, 0, moves, bead_at, own_out + others[:-1], finish_left, inner, outer, []
    )
    inner = lax.ppermute(inner, "bead", SWAP)
    outer = lax.ppermute(outer, "bead", SWAP)
    moves = [(chunks - 1, 1, chunks - 1)]
    new_pos, new_mom = finish_block(
        chunks, 1, moves, bead_at, others, finish_left, inner, outer, result
    )
    return new_pos.transpose(1, 0, 2), new_mom.transpose(1, 0, 2)


SWAP = [(0, 1), (1, 0)]


def solution(mesh):
    placed = (
        P("bead", None, "space"),
        P("bead", None, "space"),
        P("space"),
        P("space"),
        P(None, "space"),
        P(None, "space"),
        P(None, "space"),
    )

    return jax.shard_map(
        body,
        mesh=mesh,
        in_specs=placed,
        out_specs=(P("bead", None, "space"), P("bead", None, "space")),
        check_vma=False,
    )
```

```python
import functools
import math

import jax
import jax.numpy as jnp
import numpy as np
from jax import lax
from jax.experimental import pallas as pl
from jax.experimental.pallas import tpu as pltpu
from jax.sharding import PartitionSpec as P


BEADS = 32
KEPT = 4
SUBS = 3
TILE = 128
GT = 2
BPT = 128
APT = 64
ROWS = 4 * KEPT
LOGS = 3 * KEPT

time_step = 0.3
spring_freq = 80.0
bond_stiff = 0.2
bond_rest = 1.0
angle_stiff = 0.1
angle_rest = 0.5
range_sq = 4.0
HIGH = lax.Precision.HIGHEST
IN_VMEM = pl.BlockSpec(memory_space=pltpu.VMEM)
IN_SMEM = pl.BlockSpec(memory_space=pltpu.SMEM)
IN_SPACE = pltpu.MemorySpace.VMEM


def near(x):
    return pltpu.with_memory_space_constraint(x, IN_SPACE)


def far(x):
    return pltpu.with_memory_space_constraint(x, pltpu.MemorySpace.HBM)


def vmem_out(shape, dtype):
    return IN_SPACE(shape, dtype)


PARAMS = pltpu.CompilerParams(vmem_limit_bytes=20 * 1024 * 1024)
COST = pl.CostEstimate(flops=10_000_000, bytes_accessed=100_000, transcendentals=0)
F32 = jnp.float32
BF16 = jnp.bfloat16


def mode_table(number):
    within = np.arange(number)
    result = np.zeros((number, number))
    for column in range(number):
        if column == 0:
            result[:, column] = 1.0 / math.sqrt(number)
        elif 2 * column < number:
            result[:, column] = math.sqrt(2.0 / number) * np.cos(
                2 * np.pi * within * column / number
            )
        elif 2 * column == number:
            result[:, column] = (-1.0) ** within / math.sqrt(number)
        else:
            result[:, column] = math.sqrt(2.0 / number) * np.sin(
                2 * np.pi * within * column / number
            )
    return result


def contract_table(number, kept):
    larger = mode_table(number)
    smaller = mode_table(kept)
    chosen = [column if 2 * column <= kept else number - kept + column for column in range(kept)]
    return math.sqrt(kept / number) * smaller @ larger[:, chosen].T


def motion_table(number, interval):
    freqs = 2.0 * spring_freq * np.sin(np.pi * np.arange(number) / number)
    modes = mode_table(number)
    safe = np.where(freqs > 0, freqs, 1.0)
    gains = np.where(freqs > 0, np.sin(freqs * interval) / safe, interval)
    drags = freqs * np.sin(freqs * interval)
    stay = modes @ np.diag(np.cos(freqs * interval)) @ modes.T
    gain = modes @ np.diag(gains) @ modes.T
    drag = modes @ np.diag(drags) @ modes.T
    return np.block([[stay, gain], [-drag, stay]])


def np_split(table, parts):
    out, rest = [], np.asarray(table, np.float64)
    for _ in range(parts):
        piece = rest.astype(np.float32).astype(jnp.bfloat16)
        out.append(piece)
        rest = rest - piece.astype(np.float64)
    return out


def stacked_left(table, parts=3):
    pieces = np_split(table, parts)
    zero = np.zeros_like(pieces[0])
    return np.concatenate(
        [
            np.concatenate([pieces[i]] * (parts - i) + [zero] * i, axis=1)
            for i in range(parts)
        ],
        axis=0,
    )


def split(x, parts):
    out = []
    for i in range(parts):
        piece = x.astype(BF16)
        out.append(piece)
        if i < parts - 1:
            x = x - piece.astype(F32)
    return out


def mm(left, right):
    return jnp.dot(left, right, preferred_element_type=F32)


def exact(left, x, parts=3):
    out = mm(left, jnp.concatenate(split(x, parts), axis=0))
    rows = out.shape[0] // parts
    total = out[:rows]
    for i in range(1, parts):
        total = total + out[i * rows : (i + 1) * rows]
    return total


def packed_left(table):
    high, mid, low = np_split(table, 3)
    zero = np.zeros_like(high)
    return np.concatenate(
        [
            np.concatenate([high, high, high, mid], axis=1),
            np.concatenate([low, mid, zero, zero], axis=1),
        ],
        axis=0,
    )


def packed_exact(left, x):
    high, mid, low = split(x, 3)
    out = mm(left, jnp.concatenate([high, mid, low, high], axis=0))
    rows = out.shape[0] // 2
    return out[:rows] + out[rows:]


def contract_rows(beads):
    table = contract_table(BEADS, KEPT)
    tables = []
    for turn in range(0, BEADS, beads):
        order = (np.arange(BEADS) + turn) % BEADS
        tables.append(table[:, order])
    return tables


def contract_left(table):
    out = np.zeros((ROWS, 3 * table.shape[1]))
    for c in range(KEPT):
        for k in range(3):
            out[k * KEPT + c, k * table.shape[1] : (k + 1) * table.shape[1]] = table[c]
    return out


def expand_left(table):
    return BEADS / KEPT * contract_left(table).T


def pack_rows(target, x):
    lanes = x.shape[1]
    target[:, :lanes] = x[:8]
    target[:4, lanes:] = x[8:12, : lanes // 2]
    target[4:, lanes:] = x[8:12, lanes // 2 :]


def unpacked(x):
    lanes = x.shape[1] * 2 // 3
    last = jnp.concatenate([x[:4, lanes:], x[4:, lanes:]], axis=1)
    return jnp.concatenate([x[:, :lanes], last, jnp.zeros_like(last)], axis=0)


def begin_kernel(chunks, bead, left, strengths, pos, *refs):
    mine, theirs, straight = refs[:3]
    whole, table, rows, spare, sems = refs[-5:]
    blocks = list(refs[3:-5]) + [spare.at[i] for i in range(chunks)]
    lanes = blocks[0].shape[2]
    slab = whole.shape[1]
    starts, copies = [], []
    for i in range(2 * chunks):
        owner = bead[0] if i < chunks else 1 - bead[0]
        starts.append(pl.multiple_of((owner * chunks + i % chunks) * lanes, TILE))
    for i, block in enumerate(blocks):
        copy = pltpu.make_async_copy(
            pos.at[:, :, pl.ds(starts[i], lanes)], block, sems.at[i]
        )
        copy.start()
        copies.append(copy)
    small = [
        pltpu.make_async_copy(left.at[bead[0]], table, sems.at[len(copies)]),
        pltpu.make_async_copy(strengths, rows, sems.at[len(copies) + 1]),
    ]
    for copy in small:
        copy.start()
    for copy in small:
        copy.wait()
    logs = math.log2(math.e) * jnp.log(rows[...])
    for t in range(slab // TILE):
        whole[LOGS : LOGS + 1, t * TILE : (t + 1) * TILE] = logs[t : t + 1]
    for i, block in enumerate(blocks):
        copies[i].wait()
        x = jnp.concatenate([block[c] for c in range(3)], axis=0)
        where = pl.ds(starts[i], lanes)
        row = lax.broadcasted_iota(jnp.int32, (ROWS, lanes), 0)
        whole[:, where] = jnp.where(row == LOGS, whole[:, where], exact(table[...], x))

    block, rim = slab // 2, GT * TILE
    size = block + rim

    def sides(which):
        first, other = (0, block - rim) if which == 0 else (block - rim, 0)
        mine[...] = whole[:, first : first + size]
        head, tail = whole[:, :rim], whole[:, slab - rim :]
        straight[...] = tail if which == 0 else head
        relay = head if which == 0 else tail
        pack_rows(theirs, jnp.concatenate([whole[:, other : other + size], relay], axis=1))

    for which in range(2):
        pl.when(bead[0] == which)(functools.partial(sides, which))


def fetch_kernel(moves, chunks, bead, pos, mom, *refs):
    *blocks, sems = refs
    lanes = blocks[0].shape[2]
    copies = []
    for i, (block, plane, source, comp, comps, owner, chunk) in enumerate(moves):
        side = bead[0] if owner == 0 else 1 - bead[0]
        start = pl.multiple_of((side * chunks + chunk) * lanes, TILE)
        copy = pltpu.make_async_copy(
            (pos, mom)[source].at[pl.ds(comp, comps), :, pl.ds(start, lanes)],
            blocks[block].at[pl.ds(plane, comps)],
            sems.at[i],
        )
        copy.start()
        copies.append(copy)
    for copy in copies:
        copy.wait()


def fetch(moves, planes, chunks, bead, pos, mom):
    beads, slab = mom.shape[1:]
    lanes = slab // (2 * chunks)
    return pl.pallas_call(
        functools.partial(fetch_kernel, moves, chunks),
        in_specs=[IN_SMEM] + [pl.BlockSpec(memory_space=pl.ANY)] * 2,
        out_specs=[IN_VMEM] * len(planes),
        out_shape=[vmem_out((n, beads, lanes), F32) for n in planes],
        scratch_shapes=[pltpu.SemaphoreType.DMA((len(moves),))],
        compiler_params=PARAMS,
        cost_estimate=COST,
        name="fetch",
    )(bead, far(pos), far(mom))


def begin(chunks, bead, left, strengths, pos):
    beads, slab = pos.shape[1:]
    block, rim = slab // 2, GT * TILE
    lanes = block // chunks
    shapes = [(ROWS, block + rim), (8, 3 * (block + 2 * rim) // 2), (ROWS, rim)]
    shapes += [(3, beads, lanes)] * chunks
    return pl.pallas_call(
        functools.partial(begin_kernel, chunks),
        in_specs=[IN_SMEM] + [pl.BlockSpec(memory_space=pl.ANY)] * 3,
        out_specs=[IN_VMEM] * len(shapes),
        out_shape=[vmem_out(s, F32) for s in shapes],
        scratch_shapes=[
            pltpu.VMEM((ROWS, slab), F32),
            pltpu.VMEM(left.shape[1:], left.dtype),
            pltpu.VMEM(strengths.shape, F32),
            pltpu.VMEM((chunks, 3, beads, lanes), F32),
            pltpu.SemaphoreType.DMA((2 * chunks + 2,)),
        ],
        compiler_params=PARAMS,
        cost_estimate=COST,
        name="begin",
    )(bead, far(left), far(strengths), far(pos))


def relay_kernel(own, received, out):
    rim = GT * TILE
    size = received.shape[1] * 2 // 3
    more = jnp.concatenate([received[:, size - rim : size], received[4:, -rim:]], axis=0)
    out[...] = own[...] + jnp.concatenate([more, jnp.zeros_like(more[:4])], axis=0)


def relay(own, received):
    return pl.pallas_call(
        relay_kernel,
        in_specs=[IN_VMEM] * 2,
        out_specs=IN_VMEM,
        out_shape=vmem_out(own.shape, F32),
        compiler_params=PARAMS,
        cost_estimate=COST,
        name="relay",
    )(near(own), near(received))


def partial_kernel(bead, left, strengths, pos, out):
    comps, _, lanes = pos.shape
    logs = math.log2(math.e) * jnp.log(strengths[...])
    logs = jnp.concatenate([logs[t : t + 1] for t in range(lanes // TILE)], axis=1)
    row = lax.broadcasted_iota(jnp.int32, (ROWS, lanes), 0)
    x = jnp.concatenate([pos[c] for c in range(comps)], axis=0)
    out[...] = jnp.where(row == LOGS, logs, exact(left[bead[0]], x))


def partial_rows(bead, left, strengths, pos):
    beads, slab = pos.shape[1:]
    lanes = math.gcd(slab, 1024)
    return pl.pallas_call(
        partial_kernel,
        grid=(slab // lanes,),
        in_specs=[
            IN_SMEM,
            IN_VMEM,
            pl.BlockSpec((lanes // TILE, TILE), lambda i: (i, 0)),
            pl.BlockSpec((3, beads, lanes), lambda i: (0, 0, i)),
        ],
        out_specs=pl.BlockSpec((ROWS, lanes), lambda i: (0, i)),
        out_shape=jax.ShapeDtypeStruct((ROWS, slab), F32),
        name="partial_rows",
    )(bead, left, strengths, pos)


def prepare_kernel(group, bead, bonds, angles, hot):
    lane = lax.broadcasted_iota(jnp.int32, (1, TILE), 1)
    atom = lax.broadcasted_iota(jnp.int32, (TILE, 2 * TILE), 0)
    low = lane < APT

    def merge(first, second, odd):
        a = pltpu.roll(first, APT, 1) if odd else first
        b = second if odd else pltpu.roll(second, APT, 1)
        return jnp.where(low, a, b)

    def tiles(i, carry):
        at = (bead[0] * (hot.shape[0] // group) + i) * group
        bond_rows = bonds[:, pl.ds(pl.multiple_of(at * BPT, BPT), group * BPT)]
        angle_rows = angles[:, pl.ds(pl.multiple_of(at * APT, TILE), group * APT)]
        for t in range(group):
            one = bond_rows[0:1, t * TILE : (t + 1) * TILE]
            other = bond_rows[1:2, t * TILE : (t + 1) * TILE]
            odd = t % 2
            window = slice((t // 2) * TILE, (t // 2 + 1) * TILE)
            first, middle, last = [angle_rows[e : e + 1, window] for e in range(3)]
            opposite = merge(last, first, odd)
            centre = merge(middle, middle, odd)
            gains = jnp.concatenate([other, centre], axis=1)
            losses = jnp.concatenate([one, opposite], axis=1)
            table = (atom == gains).astype(F32) - (atom == losses).astype(F32)
            hot[i * group + t] = table.astype(BF16)
        return carry

    lax.fori_loop(0, hot.shape[0] // group, tiles, 0)


def prepare(bead, bond_ends, angle_ends, block_tiles):
    return pl.pallas_call(
        functools.partial(prepare_kernel, math.gcd(block_tiles, 4)),
        in_specs=[IN_SMEM, IN_VMEM, IN_VMEM],
        out_specs=IN_VMEM,
        out_shape=vmem_out((block_tiles, TILE, 2 * TILE), BF16),
        compiler_params=PARAMS,
        cost_estimate=COST,
        name="prepare",
    )(bead, bond_ends, angle_ends)


def pair_kernel(spots, seg_sizes, own_count, packed, bead, space, nbr, *refs):
    total = sum(n for *_, n in seg_sizes)
    count = sum(n for n, *_ in seg_sizes)
    seg_refs = refs[:count]
    target, feat_i, feat_m, feat_p, base, *weights, held = refs[count:]
    out = held if packed else target
    column, own_spot, spot = spots((bead[0], space[0]))
    row = lax.broadcasted_iota(jnp.int32, (ROWS, TILE), 0)
    slot = row // KEPT
    scale = math.sqrt(2.0 * math.log2(math.e) / range_sq)
    same = (
        lax.broadcasted_iota(jnp.int32, (ROWS, ROWS), 0) % KEPT
        == lax.broadcasted_iota(jnp.int32, (ROWS, ROWS), 1) % KEPT
    ).astype(F32)

    def features(tile, c16):
        base[tile] = c16
        logs = c16[LOGS : LOGS + 1]
        place = jnp.where(slot == 3, 0.0, c16)
        scaled = place * scale
        high, low = [piece.astype(F32) for piece in split(scaled, 2)]
        square = jnp.dot(same, scaled * scaled, precision=HIGH, preferred_element_type=F32)
        half = -0.5 * square

        def three(x):
            a, b, c = [piece.astype(F32) for piece in split(x, 3)]
            return jnp.where(slot == 0, a, jnp.where(slot == 1, b, jnp.where(slot == 2, c, 0.0)))

        ones = jnp.where(slot == 3, 0.0, 1.0)
        mine = jnp.concatenate([high, high, low, low, three(half), ones], axis=0)
        theirs = jnp.concatenate(
            [high, low, high, low, ones, three(half + logs), ones, ones], axis=0
        )
        feat_i[tile] = mine.astype(BF16)
        feat_m[tile] = jnp.transpose(theirs, (1, 0)).astype(BF16)
        one = jnp.ones((ROWS, TILE), F32)
        p_high, p_low = [piece.astype(F32) for piece in split(place, 2)]
        feat_p[tile] = jnp.concatenate([one, p_high, p_low], axis=0).astype(BF16)

    def piece(ref, begins, i):
        moving = callable(begins)
        at = (begins(bead[0]) if moving else begins) + i

        def lanes(tile):
            if moving:
                return pl.ds(pl.multiple_of(tile * TILE, TILE), TILE)
            return slice(tile * TILE, (tile + 1) * TILE)

        if ref.shape[0] == ROWS:
            return ref[:, lanes(at)]
        tiles = ref.shape[1] * 2 // 3 // TILE
        half = tiles // 2
        upper = at >= half
        last = ref[:, lanes(tiles + jnp.where(upper, at - half, at))]
        last = jnp.where(upper, last[4:], last[:4])
        return jnp.concatenate([ref[:, lanes(at)], last, jnp.zeros_like(last)], axis=0)

    tile = 0
    at = 0
    for number, begins, tiles in seg_sizes:
        group = seg_refs[at : at + number]
        at += number
        for i in range(tiles):
            c16 = piece(group[0], begins, i)
            for other in group[1:]:
                c16 = c16 + piece(other, begins, i)
            features(tile, c16)
            tile += 1
    assert tile == total

    groups = 6
    wide_row = lax.broadcasted_iota(jnp.int32, (groups * ROWS, TILE), 0)
    pick = [(wide_row % KEPT == c).astype(BF16) for c in range(KEPT)]
    owner = row % KEPT

    def close(t, u):
        return spot(nbr[u, column(t)])

    def weigh(t, weights):
        features_i = feat_i[own_spot(t)]
        right = jnp.concatenate([features_i * pick[c] for c in range(KEPT)], axis=1)
        right = jnp.concatenate([right, jnp.zeros((2 * ROWS, KEPT * TILE), BF16)], axis=0)
        left = jnp.concatenate([feat_m[close(t, u)] for u in range(3)], axis=0)
        power = mm(left, right)
        for u in range(3):
            high, low = split(jnp.exp2(power[u * TILE : (u + 1) * TILE]), 2)
            weights[2 * u * TILE : (2 * u + 1) * TILE] = high
            weights[(2 * u + 1) * TILE : (2 * u + 2) * TILE] = low

    def pull(t, weights):
        left = []
        for u in range(3):
            piece = feat_p[close(t, u)]
            left += [piece, piece]
        total_p = mm(jnp.concatenate(left, axis=1), weights[...])
        sums = total_p[:ROWS]
        pulls = total_p[ROWS : 2 * ROWS] + total_p[2 * ROWS :]
        c16 = base[own_spot(t)]
        factor = (2.0 / range_sq) * jnp.exp2(c16[LOGS : LOGS + 1])
        result = jnp.zeros((ROWS, TILE), F32)
        for c in range(KEPT):
            lanes = slice(c * TILE, (c + 1) * TILE)
            force = factor * (c16 * sums[:, lanes] - pulls[:, lanes])
            result = jnp.where((owner == c) & (slot < 3), force, result)
        lane = t * TILE if isinstance(t, int) else pl.multiple_of(t * TILE, TILE)
        out[:, pl.ds(lane, TILE)] = result

    unroll = own_count if own_count <= 6 else math.gcd(own_count, 4)
    weigh(0, weights[0])

    def some_tiles(t, last):
        for j in range(unroll):
            if not (last and j == unroll - 1):
                weigh(t + j + 1, weights[(j + 1) % 2])
            pull(t + j, weights[j % 2])

    def loop(i, carry):
        some_tiles(unroll * i, False)
        return carry

    lax.fori_loop(0, own_count // unroll - 1, loop, 0)
    some_tiles(own_count - unroll, True)
    if packed:
        pack_rows(target, held[...])


def pair_forces(spots, segments, own_count, bead, space, neighbour_tiles, packed=False):
    sizes = tuple((len(group), start, tiles) for group, start, tiles in segments)
    total = sum(n for *_, n in sizes)
    assert own_count % 2 == 0
    flat = [array for group, *_ in segments for array in group]
    return pl.pallas_call(
        functools.partial(pair_kernel, spots, sizes, own_count, packed),
        in_specs=[IN_SMEM] * 3 + [IN_VMEM] * len(flat),
        out_specs=IN_VMEM,
        out_shape=vmem_out(
            (8, 3 * own_count * TILE // 2) if packed else (ROWS, own_count * TILE), F32
        ),
        scratch_shapes=[
            pltpu.VMEM((total, 6 * ROWS, TILE), BF16),
            pltpu.VMEM((total, TILE, 8 * ROWS), BF16),
            pltpu.VMEM((total, 3 * ROWS, TILE), BF16),
            pltpu.VMEM((total, ROWS, TILE), F32),
            pltpu.VMEM((6 * TILE, KEPT * TILE), BF16),
            pltpu.VMEM((6 * TILE, KEPT * TILE), BF16),
            pltpu.VMEM((ROWS, own_count * TILE), F32),
        ],
        compiler_params=PARAMS,
        cost_estimate=COST,
        name="pair_forces",
    )(bead, space, far(neighbour_tiles), *[near(x) for x in flat])


def whole_force(inner, outer):
    rim = GT * TILE
    inner, outer = unpacked(inner[...]), unpacked(outer[...])
    return jnp.concatenate([outer[:, :rim], inner, outer[:, rim:]], axis=1)


def step_kernel(parts, count, forces, chunk, chunks, group, edge, bead, *refs):
    pieces = refs[:count]
    at = count
    force = refs[at : at + forces]
    at += forces
    mass_rows, strength_rows, hot, motion, expand, contract = refs[at : at + 6]
    before = refs[at + 6] if edge and chunk else None
    outs = refs[len(refs) - parts - 1 - 2 * edge :]
    c_out = outs[parts]
    interval = time_step / SUBS
    width = group * TILE
    first = chunk * group
    motion_l = motion[...]

    def per_atom(rows):
        at = (bead[0] * chunks + chunk) * group
        return jnp.concatenate([rows[pl.ds(at + t, 1), :] for t in range(group)], axis=1)

    masses = per_atom(mass_rows)
    inverse = 1.0 / masses

    planes = [(piece, plane) for piece in pieces for plane in range(piece.shape[0])]

    def gathered(kind, c):
        found = [planes[6 * part + 3 * kind + c] for part in range(parts)]
        found = [piece[plane] for piece, plane in found]
        return found[0] if parts == 1 else jnp.concatenate(found, axis=0)

    q = [gathered(0, c) for c in range(3)]
    p = [gathered(1, c) for c in range(3)]
    if force[0].shape[0] == ROWS:
        kicks = force[0][:, first * TILE : first * TILE + width]
    else:
        kicks = jnp.concatenate([unpacked(x[...]) for x in force], axis=1)
    kick = exact(expand[bead[0]], kicks)
    v = [
        (p[c] + 0.5 * time_step * kick[c * BEADS : (c + 1) * BEADS]) * inverse for c in range(3)
    ]

    def bonded(q):
        forces = []
        for t in range(group):
            lanes = slice(t * TILE, (t + 1) * TILE)
            rows = jnp.concatenate([q[c][:, lanes] for c in range(3)], axis=0)
            seen = mm(jnp.concatenate(split(rows, 2), axis=0), hot[first + t])
            seen = seen[: 3 * BEADS] + seen[3 * BEADS :]
            stretch, arms = seen[:, :TILE], seen[:, TILE:]
            s = [stretch[c * BEADS : (c + 1) * BEADS] for c in range(3)]
            a = [arms[c * BEADS : (c + 1) * BEADS] for c in range(3)]
            length = s[0] * s[0] + s[1] * s[1] + s[2] * s[2]
            g = bond_stiff * (bond_rest - length)
            turned = [pltpu.roll(x, APT, 1) for x in a]
            inner = a[0] * turned[0] + a[1] * turned[1] + a[2] * turned[2]
            h = angle_stiff * (angle_rest - inner)
            bonds = jnp.concatenate([g * x for x in s], axis=0)
            angles = jnp.concatenate([h * x for x in turned], axis=0)
            both = jnp.concatenate([bonds, angles], axis=1)
            out = lax.dot_general(
                jnp.concatenate(split(both, 2), axis=0),
                hot[first + t],
                (((1,), (1,)), ((), ())),
                preferred_element_type=F32,
            )
            forces.append(out[: 3 * BEADS] + out[3 * BEADS :])
        return [
            jnp.concatenate([f[c * BEADS : (c + 1) * BEADS] for f in forces], axis=1)
            for c in range(3)
        ]

    for sub in range(SUBS):
        pushed = bonded(q)
        factor = (0.5 if sub == 0 else 1.0) * interval * inverse
        v = [v[c] + factor * pushed[c] for c in range(3)]
        for c in range(3):
            moved = packed_exact(motion_l, jnp.concatenate([q[c], v[c]], axis=0))
            q[c], v[c] = moved[:BEADS], moved[BEADS:]
    pushed = bonded(q)
    p = [masses * v[c] + (0.5 * interval) * pushed[c] for c in range(3)]
    beads = BEADS // parts
    for i in range(parts):
        for c in range(3):
            outs[i][c] = q[c][i * beads : (i + 1) * beads]
            outs[i][3 + c] = p[c][i * beads : (i + 1) * beads]
    rows = jnp.concatenate(q, axis=0)
    c16 = exact(contract[bead[0]], rows, 2)
    row = lax.broadcasted_iota(jnp.int32, (ROWS, width), 0)
    logs = math.log2(math.e) * jnp.log(per_atom(strength_rows))
    c16 = jnp.where(row == LOGS, logs, c16)
    c_out[...] = c16
    if edge:
        rim = GT * TILE
        head = c16[:, :rim] if before is None else before[:, :rim]
        tail = c16[:, width - rim :]
        outs[-2][...] = jnp.where(bead[0] == 0, tail, head)
        outs[-1][...] = jnp.where(bead[0] == 0, head, tail)


def substeps(chunk, chunks, bead, pieces, force, mass, strength, hot, motion, expand, contract, edge, before):
    beads, lanes = pieces[0].shape[1:]
    parts = BEADS // beads
    extra = [before] if edge and chunk else []
    shapes = [(6, beads, lanes)] * parts + [(ROWS, lanes)]
    if edge:
        shapes += [(ROWS, GT * TILE)] * 2
    return pl.pallas_call(
        functools.partial(
            step_kernel, parts, len(pieces), len(force), chunk, chunks, lanes // TILE, int(edge)
        ),
        in_specs=[IN_SMEM] + [IN_VMEM] * (len(pieces) + len(force) + 6 + len(extra)),
        out_specs=[IN_VMEM] * len(shapes),
        out_shape=[vmem_out(s, F32) for s in shapes],
        compiler_params=PARAMS,
        cost_estimate=COST,
        name="substeps",
    )(
        bead,
        *[near(x) for x in pieces + force],
        mass,
        strength,
        near(hot),
        motion,
        expand,
        contract,
        *[near(x) for x in extra],
    )


def finish_kernel(chunks, bead, expand, force, *refs):
    pos, mom = refs[-2:]
    parts = refs[:-2]
    bead_count = len(parts) // chunks
    lanes = parts[0].shape[2]
    comp = pl.program_id(0)
    table = expand[bead[0], comp]
    for i, part in enumerate(parts):
        chunk, distance = divmod(i, bead_count)
        block = lax.rem(bead[0] + bead_count - distance, bead_count)
        start = pl.multiple_of(block * (chunks * lanes) + chunk * lanes, TILE)
        where = pl.ds(start, lanes)
        pos[0, :, where] = part[comp]
        mom[0, :, where] = part[3 + comp] + 0.5 * time_step * exact(table, force[:, where])


def finish(chunks, bead, parts, expand, force):
    slab = force.shape[1]
    beads = parts[0].shape[1]
    return pl.pallas_call(
        functools.partial(finish_kernel, chunks),
        grid=(3,),
        in_specs=[IN_SMEM] + [IN_VMEM] * (2 + len(parts)),
        out_specs=[pl.BlockSpec((1, beads, slab), lambda i: (i, 0, 0))] * 2,
        out_shape=[jax.ShapeDtypeStruct((3, beads, slab), F32)] * 2,
        compiler_params=PARAMS,
        cost_estimate=COST,
        name="finish",
    )(bead, expand, near(force), *[near(x) for x in parts])


def finish_block_kernel(chunks, owner, moves, count, bead, expand, inner, outer, *refs):
    parts = refs[:count]
    pos, mom, held, sems = refs[-4:]
    lanes = parts[0].shape[2]
    blocks = [bead[0], 1 - bead[0]]

    def where(owner, chunk):
        return pl.ds(pl.multiple_of((blocks[owner] * chunks + chunk) * lanes, TILE), lanes)

    copies = []

    def copy(source, target):
        copies.append(pltpu.make_async_copy(source, target, sems.at[len(copies)]))
        copies[-1].start()

    for part, move_owner, chunk in moves:
        copy(parts[part].at[pl.ds(0, 3)], pos.at[:, :, where(move_owner, chunk)])
    force = whole_force(inner, outer)
    for chunk in range(chunks):
        lane = slice(chunk * lanes, (chunk + 1) * lanes)
        for c in range(3):
            kick = 0.5 * time_step * exact(expand[bead[0], c], force[:, lane])
            held[c, :, lane] = parts[chunk][3 + c] + kick
        copy(held.at[:, :, pl.ds(chunk * lanes, lanes)], mom.at[:, :, where(owner, chunk)])
    for waiting in copies:
        waiting.wait()


def finish_block(chunks, owner, moves, bead, parts, expand, inner, outer, before):
    beads, lanes = parts[0].shape[1:]
    block = lanes * chunks
    anywhere = pl.BlockSpec(memory_space=pl.ANY)
    at = 4 + len(parts)
    return pl.pallas_call(
        functools.partial(finish_block_kernel, chunks, owner, moves, len(parts)),
        in_specs=[IN_SMEM] + [IN_VMEM] * (3 + len(parts)) + [anywhere] * len(before),
        out_specs=[anywhere] * 2,
        out_shape=[pltpu.MemorySpace.HBM((3, beads, 2 * block), F32)] * 2,
        scratch_shapes=[
            pltpu.VMEM((3, beads, block), F32),
            pltpu.SemaphoreType.DMA((len(moves) + chunks,)),
        ],
        input_output_aliases={at + i: i for i in range(len(before))},
        compiler_params=PARAMS,
        cost_estimate=COST,
        name="finish_block",
    )(
        bead,
        expand,
        near(inner),
        near(outer),
        *[near(x) for x in parts],
        *[far(x) for x in before],
    )


def body(positions, momenta, masses, strengths, bond_ends, angle_ends, neighbour_tiles):
    beads, _, slab = positions.shape
    bead_count = lax.axis_size("bead")
    bead = lax.axis_index("bead")
    space_count = lax.axis_size("space")
    space = lax.axis_index("space")
    block = slab // bead_count
    slab_tiles = slab // TILE
    block_tiles = block // TILE
    all_tiles = slab_tiles * space_count
    rim = GT * TILE
    chunks = 2 if block_tiles % 4 == 0 else 1
    lanes = block // chunks
    interval = time_step / SUBS
    pair = bead_count == 2

    pos = positions.transpose(1, 0, 2)
    mom = momenta.transpose(1, 0, 2)
    bead_at = jnp.reshape(bead, (1,)).astype(jnp.int32)
    space_at = jnp.reshape(space, (1,)).astype(jnp.int32)
    mass = masses.reshape(slab_tiles, TILE)
    strength = strengths.reshape(slab_tiles, TILE)
    turned = contract_rows(beads)
    table = contract_table(BEADS, KEPT)
    own_tables = [table[:, i * beads : (i + 1) * beads] for i in range(bead_count)]

    def stack(tables):
        return jnp.asarray(np.stack(tables))

    begin_left = stack([stacked_left(contract_left(t)) for t in own_tables])
    finish_left = stack(
        [
            np.stack(
                [stacked_left(expand_left(t)[c * beads : (c + 1) * beads]) for c in range(3)]
            )
            for t in own_tables
        ]
    )
    contract_l = stack([stacked_left(contract_left(t), 2) for t in turned])
    expand_l = stack([stacked_left(expand_left(t)) for t in turned])
    motion = jnp.asarray(packed_left(motion_table(BEADS, interval)))

    def lanes_of(x, start, size):
        return lax.dynamic_slice_in_dim(x, start, size, x.ndim - 1)

    def permutation(step, flip):
        return [
            (s * 2 + b, ((s + step(b)) % space_count) * 2 + (b ^ flip))
            for s in range(space_count)
            for b in range(2)
        ]

    def rims(x):
        up = [(i, (i + 1) % space_count) for i in range(space_count)]
        down = [((i + 1) % space_count, i) for i in range(space_count)]
        return (
            lax.ppermute(x[:, slab - rim :], "space", up),
            lax.ppermute(x[:, :rim], "space", down),
        )

    def relative(tile, info):
        x = tile - info[1] * slab_tiles
        x = jnp.where(x >= all_tiles - GT, x - all_tiles, x)
        return jnp.where(x < -GT, x + all_tiles, x)

    def spots_inner(info):
        def spot(tile):
            return relative(tile, info) - info[0] * block_tiles

        return lambda t: t + GT + info[0] * block_tiles, lambda t: t + GT, spot

    def spots_start(info):
        left_at = 2 * GT + jnp.where(info[0] == 0, GT, 0)

        def spot(tile):
            x = relative(tile, info) - info[0] * block_tiles
            return jnp.where(x < 0, x + GT + left_at, x)

        return lambda t: t + info[0] * block_tiles, lambda t: t, spot

    def spots_late(info):
        chunk_tiles = lanes // TILE
        right_at = block_tiles - chunk_tiles + GT + jnp.where(info[0] == 0, 0, GT)

        def place(x):
            return x - chunk_tiles + GT

        def spot(tile):
            x = relative(tile, info) - info[0] * block_tiles
            return jnp.where(x >= block_tiles, x - block_tiles + right_at, place(x))

        def own(t):
            return t + chunk_tiles

        return lambda t: own(t) + info[0] * block_tiles, lambda t: place(own(t)), spot

    def spots_outer(info):
        bead_at = 4 * GT
        far_at = bead_at + GT
        left_at = jnp.where(info[0] == 0, far_at, bead_at)
        right_at = jnp.where(info[0] == 0, bead_at, far_at)

        def own(t):
            return jnp.where(t < GT, t, t + block_tiles - 2 * GT)

        def place(x):
            return jnp.where(x < 2 * GT, x, x - (block_tiles - 4 * GT))

        def spot(tile):
            x = relative(tile, info) - info[0] * block_tiles
            right = jnp.where(x >= block_tiles, x - block_tiles + right_at, place(x))
            return jnp.where(x < 0, x + GT + left_at, right)

        return lambda t: own(t) + info[0] * block_tiles, lambda t: place(own(t)), spot

    def spots_slab(first):
        def spots(info):
            start = info[0] * block_tiles if first else 0

            def spot(tile):
                x = relative(tile, info)
                return jnp.where(x < 0, x + GT + slab_tiles, jnp.where(x >= slab_tiles, x + GT, x))

            return lambda t: t + start, lambda t: t + start, spot

        return spots

    pieces = [[] for _ in range(chunks)]
    if pair:
        (lead,) = fetch([(0, 0, 0, 0, 2, 1, 0)], [2], chunks, bead_at, pos, mom)
        other = lax.ppermute(lead, "bead", SWAP)
        mine, theirs, straight, *own_q = begin(chunks, bead_at, begin_left, strength, pos)
        theirs = lax.ppermute(theirs, "bead", SWAP)
        moves = [(0, 0, 0, 2, 1, 1, 0), (0, 1, 1, 0, 3, 1, 0)]
        blocks = fetch(moves, [4], chunks, bead_at, pos, mom)
        moves = []
        for chunk in range(1, chunks):
            moves += [(chunk - 1, 0, 0, 0, 3, 1, chunk), (chunk - 1, 3, 1, 0, 3, 1, chunk)]
        moves += [(chunks - 1 + chunk, 0, 1, 0, 3, 0, chunk) for chunk in range(chunks)]
        planes = [6] * (chunks - 1) + [3] * chunks
        blocks += fetch(moves, planes, chunks, bead_at, pos, mom)
        for chunk in range(chunks):
            moment = lax.ppermute(blocks[chunk], "bead", SWAP)
            pieces[chunk] = [own_q[chunk], blocks[chunks + chunk]]
            pieces[chunk] += [moment] if chunk else [other, moment]
        straight = relay(straight, theirs)
        straight = lax.ppermute(
            straight, ("space", "bead"), permutation(lambda b: -1 if b else 1, 0)
        )
        both = [mine, theirs]
        edge_tiles = [(both, lambda b: (1 - b) * block_tiles, GT), ([straight], 0, GT)]
        chunk_tiles = lanes // TILE
        early = [(both, lambda b: b * GT, chunk_tiles + GT)]
        start_tiles = [(both, lambda b: b * GT, 2 * GT)] + edge_tiles
        late = [(both, lambda b: b * GT + chunk_tiles - GT, block_tiles - chunk_tiles + GT)]
        late += edge_tiles
    else:
        part = partial_rows(bead_at, begin_left, strength, pos)
        summed = lax.psum(part, "bead")
        logs_row = lax.broadcasted_iota(jnp.int32, summed.shape, 0) == LOGS
        summed = jnp.where(logs_row, jnp.log2(strengths)[None, :], summed)
        segments = [([summed], 0, slab_tiles), *[([x], 0, GT) for x in rims(summed)]]
        spots = spots_slab(True)
        for chunk in range(chunks):
            parts = []
            for d in range(bead_count):
                start = jnp.mod(bead - d, bead_count) * block + chunk * lanes
                piece = jnp.concatenate(
                    [lanes_of(pos, start, lanes), lanes_of(mom, start, lanes)], 0
                )
                back = [(i, (i - d) % bead_count) for i in range(bead_count)]
                parts.append(lax.ppermute(piece, "bead", back) if d else piece)
            pieces[chunk] = [jnp.concatenate(parts, 1)]

    hot = prepare(bead_at, bond_ends, angle_ends, block_tiles)
    if pair:
        ids = bead_at, space_at, neighbour_tiles
        inner = pair_forces(spots_inner, early, chunk_tiles - GT, *ids, True)
        outer = pair_forces(spots_start, start_tiles, GT, *ids, True)
        force = [outer, inner]
    else:
        force = [pair_forces(spots, segments, block_tiles, bead_at, space_at, neighbour_tiles)]

    own_out, returned, contracted = [], [], []
    for chunk in range(chunks):
        if pair and chunk:
            count = block_tiles - chunk_tiles
            force = [pair_forces(spots_late, late, count, *ids, True)]
        last = pair and chunk == chunks - 1
        outs = substeps(
            chunk, chunks, bead_at, pieces[chunk], force, mass, strength, hot, motion,
            expand_l, contract_l, last, contracted[0] if contracted else None,
        )
        if last:
            *outs, bead_edge, far_edge = outs
        *outs, c16 = outs
        if not pair:
            outs = [outs[0][:, d * beads : (d + 1) * beads] for d in range(bead_count)]
        own_out.append(outs[0])
        contracted.append(c16)
        back = []
        for d in range(1, bead_count):
            on = [(i, (i + d) % bead_count) for i in range(bead_count)]
            back.append(lax.ppermute(outs[d], "bead", on))
        returned.append(back)

    if not pair:
        c16 = jnp.concatenate(contracted, 1) if chunks > 1 else contracted[0]
        everyone = lax.all_gather(c16, "bead", axis=1, tiled=True)
        segments = [([everyone], 0, slab_tiles), *[([x], 0, GT) for x in rims(everyone)]]
        force = pair_forces(
            spots_slab(False), segments, slab_tiles, bead_at, space_at, neighbour_tiles
        )
        parts = [x for chunk in range(chunks) for x in [own_out[chunk]] + returned[chunk]]
        new_pos, new_mom = finish(chunks, bead_at, parts, finish_left, force)
        return new_pos.transpose(1, 0, 2), new_mom.transpose(1, 0, 2)

    beside = lax.ppermute(bead_edge, "bead", SWAP)
    across = lax.ppermute(
        far_edge, ("space", "bead"), permutation(lambda b: 1 if b else -1, 1)
    )
    segments = [([x], 0, chunk_tiles) for x in contracted]
    inner = pair_forces(spots_inner, segments, block_tiles - 2 * GT, *ids, True)
    segments = [
        ([contracted[0]], 0, 2 * GT),
        ([contracted[-1]], chunk_tiles - 2 * GT, 2 * GT),
        ([beside], 0, GT),
        ([across], 0, GT),
    ]
    outer = pair_forces(spots_outer, segments, 2 * GT, *ids, True)
    others = [x[0] for x in returned]
    moves = [(i, 0, i) for i in range(chunks)]
    moves += [(chunks + i, 1, i) for i in range(chunks - 1)]
    result = finish_block(
        chunks, 0, moves, bead_at, own_out + others[:-1], finish_left, inner, outer, []
    )
    inner = lax.ppermute(inner, "bead", SWAP)
    outer = lax.ppermute(outer, "bead", SWAP)
    moves = [(chunks - 1, 1, chunks - 1)]
    new_pos, new_mom = finish_block(
        chunks, 1, moves, bead_at, others, finish_left, inner, outer, result
    )
    return new_pos.transpose(1, 0, 2), new_mom.transpose(1, 0, 2)


SWAP = [(0, 1), (1, 0)]


def solution(mesh):
    placed = (
        P("bead", None, "space"),
        P("bead", None, "space"),
        P("space"),
        P("space"),
        P(None, "space"),
        P(None, "space"),
        P(None, "space"),
    )

    return jax.shard_map(
        body,
        mesh=mesh,
        in_specs=placed,
        out_specs=(P("bead", None, "space"), P("bead", None, "space")),
        check_vma=False,
    )
```

```python
import functools
import math

import jax
import jax.numpy as jnp
import numpy as np
from jax import lax
from jax.experimental import pallas as pl
from jax.experimental.pallas import tpu as pltpu
from jax.sharding import PartitionSpec as P


BEADS = 32
KEPT = 4
SUBS = 3
TILE = 128
GT = 2
BPT = 128
APT = 64
ROWS = 4 * KEPT
LOGS = 3 * KEPT

time_step = 0.3
spring_freq = 80.0
bond_stiff = 0.2
bond_rest = 1.0
angle_stiff = 0.1
angle_rest = 0.5
range_sq = 4.0
HIGH = lax.Precision.HIGHEST
IN_VMEM = pl.BlockSpec(memory_space=pltpu.VMEM)
IN_SMEM = pl.BlockSpec(memory_space=pltpu.SMEM)
IN_SPACE = pltpu.MemorySpace.VMEM


def near(x):
    return pltpu.with_memory_space_constraint(x, IN_SPACE)


def far(x):
    return pltpu.with_memory_space_constraint(x, pltpu.MemorySpace.HBM)


def vmem_out(shape, dtype):
    return IN_SPACE(shape, dtype)


PARAMS = pltpu.CompilerParams(vmem_limit_bytes=20 * 1024 * 1024)
COST = pl.CostEstimate(flops=10_000_000, bytes_accessed=100_000, transcendentals=0)
F32 = jnp.float32
BF16 = jnp.bfloat16


def mode_table(number):
    within = np.arange(number)
    result = np.zeros((number, number))
    for column in range(number):
        if column == 0:
            result[:, column] = 1.0 / math.sqrt(number)
        elif 2 * column < number:
            result[:, column] = math.sqrt(2.0 / number) * np.cos(
                2 * np.pi * within * column / number
            )
        elif 2 * column == number:
            result[:, column] = (-1.0) ** within / math.sqrt(number)
        else:
            result[:, column] = math.sqrt(2.0 / number) * np.sin(
                2 * np.pi * within * column / number
            )
    return result


def contract_table(number, kept):
    larger = mode_table(number)
    smaller = mode_table(kept)
    chosen = [column if 2 * column <= kept else number - kept + column for column in range(kept)]
    return math.sqrt(kept / number) * smaller @ larger[:, chosen].T


def motion_table(number, interval):
    freqs = 2.0 * spring_freq * np.sin(np.pi * np.arange(number) / number)
    modes = mode_table(number)
    safe = np.where(freqs > 0, freqs, 1.0)
    gains = np.where(freqs > 0, np.sin(freqs * interval) / safe, interval)
    drags = freqs * np.sin(freqs * interval)
    stay = modes @ np.diag(np.cos(freqs * interval)) @ modes.T
    gain = modes @ np.diag(gains) @ modes.T
    drag = modes @ np.diag(drags) @ modes.T
    return np.block([[stay, gain], [-drag, stay]])


def np_split(table, parts):
    out, rest = [], np.asarray(table, np.float64)
    for _ in range(parts):
        piece = rest.astype(np.float32).astype(jnp.bfloat16)
        out.append(piece)
        rest = rest - piece.astype(np.float64)
    return out


def stacked_left(table, parts=3):
    pieces = np_split(table, parts)
    zero = np.zeros_like(pieces[0])
    return np.concatenate(
        [
            np.concatenate([pieces[i]] * (parts - i) + [zero] * i, axis=1)
            for i in range(parts)
        ],
        axis=0,
    )


def split(x, parts):
    out = []
    for i in range(parts):
        piece = x.astype(BF16)
        out.append(piece)
        if i < parts - 1:
            x = x - piece.astype(F32)
    return out


def mm(left, right):
    return jnp.dot(left, right, preferred_element_type=F32)


def exact(left, x, parts=3):
    out = mm(left, jnp.concatenate(split(x, parts), axis=0))
    rows = out.shape[0] // parts
    total = out[:rows]
    for i in range(1, parts):
        total = total + out[i * rows : (i + 1) * rows]
    return total


def packed_left(table):
    high, mid, low = np_split(table, 3)
    zero = np.zeros_like(high)
    return np.concatenate(
        [
            np.concatenate([high, high, high, mid], axis=1),
            np.concatenate([low, mid, zero, zero], axis=1),
        ],
        axis=0,
    )


def packed_exact(left, x):
    high, mid, low = split(x, 3)
    out = mm(left, jnp.concatenate([high, mid, low, high], axis=0))
    rows = out.shape[0] // 2
    return out[:rows] + out[rows:]


def contract_rows(beads):
    table = contract_table(BEADS, KEPT)
    tables = []
    for turn in range(0, BEADS, beads):
        order = (np.arange(BEADS) + turn) % BEADS
        tables.append(table[:, order])
    return tables


def contract_left(table):
    out = np.zeros((ROWS, 3 * table.shape[1]))
    for c in range(KEPT):
        for k in range(3):
            out[k * KEPT + c, k * table.shape[1] : (k + 1) * table.shape[1]] = table[c]
    return out


def expand_left(table):
    return BEADS / KEPT * contract_left(table).T


def pack_rows(target, x):
    lanes = x.shape[1]
    target[:, :lanes] = x[:8]
    target[:4, lanes:] = x[8:12, : lanes // 2]
    target[4:, lanes:] = x[8:12, lanes // 2 :]


def unpacked(x):
    lanes = x.shape[1] * 2 // 3
    last = jnp.concatenate([x[:4, lanes:], x[4:, lanes:]], axis=1)
    return jnp.concatenate([x[:, :lanes], last, jnp.zeros_like(last)], axis=0)


def begin_kernel(chunks, bead, left, strengths, pos, *refs):
    mine, theirs, straight = refs[:3]
    whole, table, rows, spare, sems = refs[-5:]
    blocks = list(refs[3:-5]) + [spare.at[i] for i in range(chunks)]
    lanes = blocks[0].shape[2]
    slab = whole.shape[1]
    starts, copies = [], []
    for i in range(2 * chunks):
        owner = bead[0] if i < chunks else 1 - bead[0]
        starts.append(pl.multiple_of((owner * chunks + i % chunks) * lanes, TILE))
    for i, block in enumerate(blocks):
        copy = pltpu.make_async_copy(
            pos.at[:, :, pl.ds(starts[i], lanes)], block, sems.at[i]
        )
        copy.start()
        copies.append(copy)
    small = [
        pltpu.make_async_copy(left.at[bead[0]], table, sems.at[len(copies)]),
        pltpu.make_async_copy(strengths, rows, sems.at[len(copies) + 1]),
    ]
    for copy in small:
        copy.start()
    for copy in small:
        copy.wait()
    logs = math.log2(math.e) * jnp.log(rows[...])
    for t in range(slab // TILE):
        whole[LOGS : LOGS + 1, t * TILE : (t + 1) * TILE] = logs[t : t + 1]
    for i, block in enumerate(blocks):
        copies[i].wait()
        x = jnp.concatenate([block[c] for c in range(3)], axis=0)
        where = pl.ds(starts[i], lanes)
        row = lax.broadcasted_iota(jnp.int32, (ROWS, lanes), 0)
        whole[:, where] = jnp.where(row == LOGS, whole[:, where], exact(table[...], x))

    block, rim = slab // 2, GT * TILE
    size = block + rim

    def sides(which):
        first, other = (0, block - rim) if which == 0 else (block - rim, 0)
        mine[...] = whole[:, first : first + size]
        head, tail = whole[:, :rim], whole[:, slab - rim :]
        straight[...] = tail if which == 0 else head
        relay = head if which == 0 else tail
        pack_rows(theirs, jnp.concatenate([whole[:, other : other + size], relay], axis=1))

    for which in range(2):
        pl.when(bead[0] == which)(functools.partial(sides, which))


def fetch_kernel(moves, chunks, bead, pos, mom, *refs):
    *blocks, sems = refs
    lanes = blocks[0].shape[2]
    copies = []
    for i, (block, plane, source, comp, comps, owner, chunk) in enumerate(moves):
        side = bead[0] if owner == 0 else 1 - bead[0]
        start = pl.multiple_of((side * chunks + chunk) * lanes, TILE)
        copy = pltpu.make_async_copy(
            (pos, mom)[source].at[pl.ds(comp, comps), :, pl.ds(start, lanes)],
            blocks[block].at[pl.ds(plane, comps)],
            sems.at[i],
        )
        copy.start()
        copies.append(copy)
    for copy in copies:
        copy.wait()


def fetch(moves, planes, chunks, bead, pos, mom):
    beads, slab = mom.shape[1:]
    lanes = slab // (2 * chunks)
    return pl.pallas_call(
        functools.partial(fetch_kernel, moves, chunks),
        in_specs=[IN_SMEM] + [pl.BlockSpec(memory_space=pl.ANY)] * 2,
        out_specs=[IN_VMEM] * len(planes),
        out_shape=[vmem_out((n, beads, lanes), F32) for n in planes],
        scratch_shapes=[pltpu.SemaphoreType.DMA((len(moves),))],
        compiler_params=PARAMS,
        cost_estimate=COST,
        name="fetch",
    )(bead, far(pos), far(mom))


def begin(chunks, bead, left, strengths, pos):
    beads, slab = pos.shape[1:]
    block, rim = slab // 2, GT * TILE
    lanes = block // chunks
    shapes = [(ROWS, block + rim), (8, 3 * (block + 2 * rim) // 2), (ROWS, rim)]
    shapes += [(3, beads, lanes)] * chunks
    return pl.pallas_call(
        functools.partial(begin_kernel, chunks),
        in_specs=[IN_SMEM] + [pl.BlockSpec(memory_space=pl.ANY)] * 3,
        out_specs=[IN_VMEM] * len(shapes),
        out_shape=[vmem_out(s, F32) for s in shapes],
        scratch_shapes=[
            pltpu.VMEM((ROWS, slab), F32),
            pltpu.VMEM(left.shape[1:], left.dtype),
            pltpu.VMEM(strengths.shape, F32),
            pltpu.VMEM((chunks, 3, beads, lanes), F32),
            pltpu.SemaphoreType.DMA((2 * chunks + 2,)),
        ],
        compiler_params=PARAMS,
        cost_estimate=COST,
        name="begin",
    )(bead, far(left), far(strengths), far(pos))


def relay_kernel(own, received, out):
    rim = GT * TILE
    size = received.shape[1] * 2 // 3
    more = jnp.concatenate([received[:, size - rim : size], received[4:, -rim:]], axis=0)
    out[...] = own[...] + jnp.concatenate([more, jnp.zeros_like(more[:4])], axis=0)


def relay(own, received):
    return pl.pallas_call(
        relay_kernel,
        in_specs=[IN_VMEM] * 2,
        out_specs=IN_VMEM,
        out_shape=vmem_out(own.shape, F32),
        compiler_params=PARAMS,
        cost_estimate=COST,
        name="relay",
    )(near(own), near(received))


def partial_kernel(bead, left, strengths, pos, out):
    comps, _, lanes = pos.shape
    logs = math.log2(math.e) * jnp.log(strengths[...])
    logs = jnp.concatenate([logs[t : t + 1] for t in range(lanes // TILE)], axis=1)
    row = lax.broadcasted_iota(jnp.int32, (ROWS, lanes), 0)
    x = jnp.concatenate([pos[c] for c in range(comps)], axis=0)
    out[...] = jnp.where(row == LOGS, logs, exact(left[bead[0]], x))


def partial_rows(bead, left, strengths, pos):
    beads, slab = pos.shape[1:]
    lanes = math.gcd(slab, 1024)
    return pl.pallas_call(
        partial_kernel,
        grid=(slab // lanes,),
        in_specs=[
            IN_SMEM,
            IN_VMEM,
            pl.BlockSpec((lanes // TILE, TILE), lambda i: (i, 0)),
            pl.BlockSpec((3, beads, lanes), lambda i: (0, 0, i)),
        ],
        out_specs=pl.BlockSpec((ROWS, lanes), lambda i: (0, i)),
        out_shape=jax.ShapeDtypeStruct((ROWS, slab), F32),
        name="partial_rows",
    )(bead, left, strengths, pos)


def prepare_kernel(group, bead, bonds, angles, hot):
    lane = lax.broadcasted_iota(jnp.int32, (1, TILE), 1)
    atom = lax.broadcasted_iota(jnp.int32, (TILE, 2 * TILE), 0)
    low = lane < APT

    def merge(first, second, odd):
        a = pltpu.roll(first, APT, 1) if odd else first
        b = second if odd else pltpu.roll(second, APT, 1)
        return jnp.where(low, a, b)

    def tiles(i, carry):
        at = (bead[0] * (hot.shape[0] // group) + i) * group
        bond_rows = bonds[:, pl.ds(pl.multiple_of(at * BPT, BPT), group * BPT)]
        angle_rows = angles[:, pl.ds(pl.multiple_of(at * APT, TILE), group * APT)]
        for t in range(group):
            one = bond_rows[0:1, t * TILE : (t + 1) * TILE]
            other = bond_rows[1:2, t * TILE : (t + 1) * TILE]
            odd = t % 2
            window = slice((t // 2) * TILE, (t // 2 + 1) * TILE)
            first, middle, last = [angle_rows[e : e + 1, window] for e in range(3)]
            opposite = merge(last, first, odd)
            centre = merge(middle, middle, odd)
            gains = jnp.concatenate([other, centre], axis=1)
            losses = jnp.concatenate([one, opposite], axis=1)
            table = (atom == gains).astype(F32) - (atom == losses).astype(F32)
            hot[i * group + t] = table.astype(BF16)
        return carry

    lax.fori_loop(0, hot.shape[0] // group, tiles, 0)


def prepare(bead, bond_ends, angle_ends, block_tiles):
    return pl.pallas_call(
        functools.partial(prepare_kernel, math.gcd(block_tiles, 4)),
        in_specs=[IN_SMEM, IN_VMEM, IN_VMEM],
        out_specs=IN_VMEM,
        out_shape=vmem_out((block_tiles, TILE, 2 * TILE), BF16),
        compiler_params=PARAMS,
        cost_estimate=COST,
        name="prepare",
    )(bead, bond_ends, angle_ends)


def pair_kernel(spots, seg_sizes, own_count, packed, bead, space, nbr, *refs):
    total = sum(n for *_, n in seg_sizes)
    count = sum(n for n, *_ in seg_sizes)
    seg_refs = refs[:count]
    target, feat_i, feat_m, feat_p, base, *weights, held = refs[count:]
    out = held if packed else target
    column, own_spot, spot = spots((bead[0], space[0]))
    row = lax.broadcasted_iota(jnp.int32, (ROWS, TILE), 0)
    slot = row // KEPT
    scale = math.sqrt(2.0 * math.log2(math.e) / range_sq)
    same = (
        lax.broadcasted_iota(jnp.int32, (ROWS, ROWS), 0) % KEPT
        == lax.broadcasted_iota(jnp.int32, (ROWS, ROWS), 1) % KEPT
    ).astype(F32)

    def features(tile, c16):
        base[tile] = c16
        logs = c16[LOGS : LOGS + 1]
        place = jnp.where(slot == 3, 0.0, c16)
        scaled = place * scale
        high, low = [piece.astype(F32) for piece in split(scaled, 2)]
        square = jnp.dot(same, scaled * scaled, precision=HIGH, preferred_element_type=F32)
        half = -0.5 * square

        def three(x):
            a, b, c = [piece.astype(F32) for piece in split(x, 3)]
            return jnp.where(slot == 0, a, jnp.where(slot == 1, b, jnp.where(slot == 2, c, 0.0)))

        ones = jnp.where(slot == 3, 0.0, 1.0)
        mine = jnp.concatenate([high, high, low, low, three(half), ones], axis=0)
        theirs = jnp.concatenate(
            [high, low, high, low, ones, three(half + logs), ones, ones], axis=0
        )
        feat_i[tile] = mine.astype(BF16)
        feat_m[tile] = jnp.transpose(theirs, (1, 0)).astype(BF16)
        one = jnp.ones((ROWS, TILE), F32)
        p_high, p_low = [piece.astype(F32) for piece in split(place, 2)]
        feat_p[tile] = jnp.concatenate([one, p_high, p_low], axis=0).astype(BF16)

    def piece(ref, begins, i):
        moving = callable(begins)
        at = (begins(bead[0]) if moving else begins) + i

        def lanes(tile):
            if moving:
                return pl.ds(pl.multiple_of(tile * TILE, TILE), TILE)
            return slice(tile * TILE, (tile + 1) * TILE)

        if ref.shape[0] == ROWS:
            return ref[:, lanes(at)]
        tiles = ref.shape[1] * 2 // 3 // TILE
        half = tiles // 2
        upper = at >= half
        last = ref[:, lanes(tiles + jnp.where(upper, at - half, at))]
        last = jnp.where(upper, last[4:], last[:4])
        return jnp.concatenate([ref[:, lanes(at)], last, jnp.zeros_like(last)], axis=0)

    tile = 0
    at = 0
    for number, begins, tiles in seg_sizes:
        group = seg_refs[at : at + number]
        at += number
        for i in range(tiles):
            c16 = piece(group[0], begins, i)
            for other in group[1:]:
                c16 = c16 + piece(other, begins, i)
            features(tile, c16)
            tile += 1
    assert tile == total

    groups = 6
    wide_row = lax.broadcasted_iota(jnp.int32, (groups * ROWS, TILE), 0)
    pick = [(wide_row % KEPT == c).astype(BF16) for c in range(KEPT)]
    owner = row % KEPT

    def close(t, u):
        return spot(nbr[u, column(t)])

    def weigh(t, weights):
        features_i = feat_i[own_spot(t)]
        right = jnp.concatenate([features_i * pick[c] for c in range(KEPT)], axis=1)
        right = jnp.concatenate([right, jnp.zeros((2 * ROWS, KEPT * TILE), BF16)], axis=0)
        left = jnp.concatenate([feat_m[close(t, u)] for u in range(3)], axis=0)
        power = mm(left, right)
        for u in range(3):
            high, low = split(jnp.exp2(power[u * TILE : (u + 1) * TILE]), 2)
            weights[2 * u * TILE : (2 * u + 1) * TILE] = high
            weights[(2 * u + 1) * TILE : (2 * u + 2) * TILE] = low

    def pull(t, weights):
        left = []
        for u in range(3):
            piece = feat_p[close(t, u)]
            left += [piece, piece]
        total_p = mm(jnp.concatenate(left, axis=1), weights[...])
        sums = total_p[:ROWS]
        pulls = total_p[ROWS : 2 * ROWS] + total_p[2 * ROWS :]
        c16 = base[own_spot(t)]
        factor = (2.0 / range_sq) * jnp.exp2(c16[LOGS : LOGS + 1])
        result = jnp.zeros((ROWS, TILE), F32)
        for c in range(KEPT):
            lanes = slice(c * TILE, (c + 1) * TILE)
            force = factor * (c16 * sums[:, lanes] - pulls[:, lanes])
            result = jnp.where((owner == c) & (slot < 3), force, result)
        lane = t * TILE if isinstance(t, int) else pl.multiple_of(t * TILE, TILE)
        out[:, pl.ds(lane, TILE)] = result

    unroll = math.gcd(own_count, 4)
    weigh(0, weights[0])

    def some_tiles(t, last):
        for j in range(unroll):
            if not (last and j == unroll - 1):
                weigh(t + j + 1, weights[(j + 1) % 2])
            pull(t + j, weights[j % 2])

    def loop(i, carry):
        some_tiles(unroll * i, False)
        return carry

    lax.fori_loop(0, own_count // unroll - 1, loop, 0)
    some_tiles(own_count - unroll, True)
    if packed:
        pack_rows(target, held[...])


def pair_forces(spots, segments, own_count, bead, space, neighbour_tiles, packed=False):
    sizes = tuple((len(group), start, tiles) for group, start, tiles in segments)
    total = sum(n for *_, n in sizes)
    assert own_count % 2 == 0
    flat = [array for group, *_ in segments for array in group]
    return pl.pallas_call(
        functools.partial(pair_kernel, spots, sizes, own_count, packed),
        in_specs=[IN_SMEM] * 3 + [IN_VMEM] * len(flat),
        out_specs=IN_VMEM,
        out_shape=vmem_out(
            (8, 3 * own_count * TILE // 2) if packed else (ROWS, own_count * TILE), F32
        ),
        scratch_shapes=[
            pltpu.VMEM((total, 6 * ROWS, TILE), BF16),
            pltpu.VMEM((total, TILE, 8 * ROWS), BF16),
            pltpu.VMEM((total, 3 * ROWS, TILE), BF16),
            pltpu.VMEM((total, ROWS, TILE), F32),
            pltpu.VMEM((6 * TILE, KEPT * TILE), BF16),
            pltpu.VMEM((6 * TILE, KEPT * TILE), BF16),
            pltpu.VMEM((ROWS, own_count * TILE), F32),
        ],
        compiler_params=PARAMS,
        cost_estimate=COST,
        name="pair_forces",
    )(bead, space, far(neighbour_tiles), *[near(x) for x in flat])


def whole_force(inner, outer):
    rim = GT * TILE
    inner, outer = unpacked(inner[...]), unpacked(outer[...])
    return jnp.concatenate([outer[:, :rim], inner, outer[:, rim:]], axis=1)


def step_kernel(parts, count, forces, chunk, chunks, group, edge, bead, *refs):
    pieces = list(refs[:count])
    at = count
    force = refs[at] if forces == 1 else whole_force(*refs[at : at + 2])
    at += forces
    mass_rows, strength_rows, hot, motion, expand, contract = refs[at : at + 6]
    at += 6
    before = refs[at] if edge and chunk else None
    at += 1 if edge and chunk else 0
    if parts > 1:
        held, sem = refs[-2:]
        start = pl.multiple_of((bead[0] * chunks + chunk) * (group * TILE), TILE)
        own_momenta = pltpu.make_async_copy(
            refs[at].at[:, :, pl.ds(start, group * TILE)], held, sem
        )
        own_momenta.start()
        pieces.insert(1, held)
        at += 1
    outs = refs[at : at + parts + 1 + 2 * edge]
    c_out = outs[parts]
    interval = time_step / SUBS
    width = group * TILE
    first = chunk * group
    motion_l = motion[...]

    def per_atom(rows):
        at = (bead[0] * chunks + chunk) * group
        return jnp.concatenate([rows[pl.ds(at + t, 1), :] for t in range(group)], axis=1)

    masses = per_atom(mass_rows)
    inverse = 1.0 / masses

    planes = [(piece, plane) for piece in pieces for plane in range(piece.shape[0])]

    def gathered(kind, c):
        found = [planes[6 * part + 3 * kind + c] for part in range(parts)]
        found = [piece[plane] for piece, plane in found]
        return found[0] if parts == 1 else jnp.concatenate(found, axis=0)

    q = [gathered(0, c) for c in range(3)]

    def bonded(q):
        forces = []
        for t in range(group):
            lanes = slice(t * TILE, (t + 1) * TILE)
            rows = jnp.concatenate([q[c][:, lanes] for c in range(3)], axis=0)
            seen = mm(jnp.concatenate(split(rows, 2), axis=0), hot[first + t])
            seen = seen[: 3 * BEADS] + seen[3 * BEADS :]
            stretch, arms = seen[:, :TILE], seen[:, TILE:]
            s = [stretch[c * BEADS : (c + 1) * BEADS] for c in range(3)]
            a = [arms[c * BEADS : (c + 1) * BEADS] for c in range(3)]
            length = s[0] * s[0] + s[1] * s[1] + s[2] * s[2]
            g = bond_stiff * (bond_rest - length)
            turned = [pltpu.roll(x, APT, 1) for x in a]
            inner = a[0] * turned[0] + a[1] * turned[1] + a[2] * turned[2]
            h = angle_stiff * (angle_rest - inner)
            bonds = jnp.concatenate([g * x for x in s], axis=0)
            angles = jnp.concatenate([h * x for x in turned], axis=0)
            both = jnp.concatenate([bonds, angles], axis=1)
            out = lax.dot_general(
                jnp.concatenate(split(both, 2), axis=0),
                hot[first + t],
                (((1,), (1,)), ((), ())),
                preferred_element_type=F32,
            )
            forces.append(out[: 3 * BEADS] + out[3 * BEADS :])
        return [
            jnp.concatenate([f[c * BEADS : (c + 1) * BEADS] for f in forces], axis=1)
            for c in range(3)
        ]

    pushed = bonded(q)
    if parts > 1:
        own_momenta.wait()
    p = [gathered(1, c) for c in range(3)]
    kick = exact(expand[bead[0]], force[:, first * TILE : first * TILE + width])
    v = [
        (p[c] + 0.5 * time_step * kick[c * BEADS : (c + 1) * BEADS]) * inverse for c in range(3)
    ]
    for sub in range(SUBS):
        pushed = bonded(q) if sub else pushed
        factor = (0.5 if sub == 0 else 1.0) * interval * inverse
        v = [v[c] + factor * pushed[c] for c in range(3)]
        for c in range(3):
            moved = packed_exact(motion_l, jnp.concatenate([q[c], v[c]], axis=0))
            q[c], v[c] = moved[:BEADS], moved[BEADS:]
    pushed = bonded(q)
    p = [masses * v[c] + (0.5 * interval) * pushed[c] for c in range(3)]
    beads = BEADS // parts
    for i in range(parts):
        for c in range(3):
            outs[i][c] = q[c][i * beads : (i + 1) * beads]
            outs[i][3 + c] = p[c][i * beads : (i + 1) * beads]
    rows = jnp.concatenate(q, axis=0)
    c16 = exact(contract[bead[0]], rows, 2)
    row = lax.broadcasted_iota(jnp.int32, (ROWS, width), 0)
    logs = math.log2(math.e) * jnp.log(per_atom(strength_rows))
    c16 = jnp.where(row == LOGS, logs, c16)
    c_out[...] = c16
    if edge:
        rim = GT * TILE
        head = c16[:, :rim] if before is None else before[:, :rim]
        tail = c16[:, width - rim :]
        outs[-2][...] = jnp.where(bead[0] == 0, tail, head)
        outs[-1][...] = jnp.where(bead[0] == 0, head, tail)


def substeps(chunk, chunks, bead, pieces, force, mass, strength, hot, motion, expand, contract, edge, before, mom):
    beads, lanes = pieces[0].shape[1:]
    parts = BEADS // beads
    extra = [near(before)] if edge and chunk else []
    scratch = []
    if parts > 1:
        extra.append(far(mom))
        scratch = [pltpu.VMEM((3, beads, lanes), F32), pltpu.SemaphoreType.DMA]
    shapes = [(6, beads, lanes)] * parts + [(ROWS, lanes)]
    if edge:
        shapes += [(ROWS, GT * TILE)] * 2
    return pl.pallas_call(
        functools.partial(
            step_kernel, parts, len(pieces), len(force), chunk, chunks, lanes // TILE, int(edge)
        ),
        in_specs=[IN_SMEM]
        + [IN_VMEM] * (len(pieces) + len(force) + 5 + len(extra) + (parts == 1))
        + [pl.BlockSpec(memory_space=pl.ANY)] * (parts > 1),
        scratch_shapes=scratch,
        out_specs=[IN_VMEM] * len(shapes),
        out_shape=[vmem_out(s, F32) for s in shapes],
        compiler_params=PARAMS,
        cost_estimate=COST,
        name="substeps",
    )(
        bead,
        *[near(x) for x in pieces + force],
        mass,
        strength,
        near(hot),
        motion,
        expand,
        contract,
        *extra,
    )


def finish_kernel(chunks, bead, expand, force, *refs):
    pos, mom = refs[-2:]
    parts = refs[:-2]
    bead_count = len(parts) // chunks
    lanes = parts[0].shape[2]
    comp = pl.program_id(0)
    table = expand[bead[0], comp]
    for i, part in enumerate(parts):
        chunk, distance = divmod(i, bead_count)
        block = lax.rem(bead[0] + bead_count - distance, bead_count)
        start = pl.multiple_of(block * (chunks * lanes) + chunk * lanes, TILE)
        where = pl.ds(start, lanes)
        pos[0, :, where] = part[comp]
        mom[0, :, where] = part[3 + comp] + 0.5 * time_step * exact(table, force[:, where])


def finish(chunks, bead, parts, expand, force):
    slab = force.shape[1]
    beads = parts[0].shape[1]
    return pl.pallas_call(
        functools.partial(finish_kernel, chunks),
        grid=(3,),
        in_specs=[IN_SMEM] + [IN_VMEM] * (2 + len(parts)),
        out_specs=[pl.BlockSpec((1, beads, slab), lambda i: (i, 0, 0))] * 2,
        out_shape=[jax.ShapeDtypeStruct((3, beads, slab), F32)] * 2,
        compiler_params=PARAMS,
        cost_estimate=COST,
        name="finish",
    )(bead, expand, near(force), *[near(x) for x in parts])


def finish_block_kernel(chunks, owner, moves, count, bead, expand, inner, outer, *refs):
    parts = refs[:count]
    pos, mom, held, sems = refs[-4:]
    lanes = parts[0].shape[2]
    blocks = [bead[0], 1 - bead[0]]

    def where(owner, chunk):
        return pl.ds(pl.multiple_of((blocks[owner] * chunks + chunk) * lanes, TILE), lanes)

    copies = []

    def copy(source, target):
        copies.append(pltpu.make_async_copy(source, target, sems.at[len(copies)]))
        copies[-1].start()

    for part, move_owner, chunk in moves:
        copy(parts[part].at[pl.ds(0, 3)], pos.at[:, :, where(move_owner, chunk)])
    force = whole_force(inner, outer)
    for chunk in range(chunks):
        lane = slice(chunk * lanes, (chunk + 1) * lanes)
        for c in range(3):
            kick = 0.5 * time_step * exact(expand[bead[0], c], force[:, lane])
            held[c, :, lane] = parts[chunk][3 + c] + kick
        copy(held.at[:, :, pl.ds(chunk * lanes, lanes)], mom.at[:, :, where(owner, chunk)])
    for waiting in copies:
        waiting.wait()


def finish_block(chunks, owner, moves, bead, parts, expand, inner, outer, before):
    beads, lanes = parts[0].shape[1:]
    block = lanes * chunks
    anywhere = pl.BlockSpec(memory_space=pl.ANY)
    at = 4 + len(parts)
    return pl.pallas_call(
        functools.partial(finish_block_kernel, chunks, owner, moves, len(parts)),
        in_specs=[IN_SMEM] + [IN_VMEM] * (3 + len(parts)) + [anywhere] * len(before),
        out_specs=[anywhere] * 2,
        out_shape=[pltpu.MemorySpace.HBM((3, beads, 2 * block), F32)] * 2,
        scratch_shapes=[
            pltpu.VMEM((3, beads, block), F32),
            pltpu.SemaphoreType.DMA((len(moves) + chunks,)),
        ],
        input_output_aliases={at + i: i for i in range(len(before))},
        compiler_params=PARAMS,
        cost_estimate=COST,
        name="finish_block",
    )(
        bead,
        expand,
        near(inner),
        near(outer),
        *[near(x) for x in parts],
        *[far(x) for x in before],
    )


def body(positions, momenta, masses, strengths, bond_ends, angle_ends, neighbour_tiles):
    beads, _, slab = positions.shape
    bead_count = lax.axis_size("bead")
    bead = lax.axis_index("bead")
    space_count = lax.axis_size("space")
    space = lax.axis_index("space")
    block = slab // bead_count
    slab_tiles = slab // TILE
    block_tiles = block // TILE
    all_tiles = slab_tiles * space_count
    rim = GT * TILE
    chunks = 2 if block_tiles % 4 == 0 else 1
    lanes = block // chunks
    interval = time_step / SUBS
    pair = bead_count == 2

    pos = positions.transpose(1, 0, 2)
    mom = momenta.transpose(1, 0, 2)
    bead_at = jnp.reshape(bead, (1,)).astype(jnp.int32)
    space_at = jnp.reshape(space, (1,)).astype(jnp.int32)
    mass = masses.reshape(slab_tiles, TILE)
    strength = strengths.reshape(slab_tiles, TILE)
    turned = contract_rows(beads)
    table = contract_table(BEADS, KEPT)
    own_tables = [table[:, i * beads : (i + 1) * beads] for i in range(bead_count)]

    def stack(tables):
        return jnp.asarray(np.stack(tables))

    begin_left = stack([stacked_left(contract_left(t)) for t in own_tables])
    finish_left = stack(
        [
            np.stack(
                [stacked_left(expand_left(t)[c * beads : (c + 1) * beads]) for c in range(3)]
            )
            for t in own_tables
        ]
    )
    contract_l = stack([stacked_left(contract_left(t), 2) for t in turned])
    expand_l = stack([stacked_left(expand_left(t)) for t in turned])
    motion = jnp.asarray(packed_left(motion_table(BEADS, interval)))

    def lanes_of(x, start, size):
        return lax.dynamic_slice_in_dim(x, start, size, x.ndim - 1)

    def permutation(step, flip):
        return [
            (s * 2 + b, ((s + step(b)) % space_count) * 2 + (b ^ flip))
            for s in range(space_count)
            for b in range(2)
        ]

    def rims(x):
        up = [(i, (i + 1) % space_count) for i in range(space_count)]
        down = [((i + 1) % space_count, i) for i in range(space_count)]
        return (
            lax.ppermute(x[:, slab - rim :], "space", up),
            lax.ppermute(x[:, :rim], "space", down),
        )

    def relative(tile, info):
        x = tile - info[1] * slab_tiles
        x = jnp.where(x >= all_tiles - GT, x - all_tiles, x)
        return jnp.where(x < -GT, x + all_tiles, x)

    def spots_inner(info):
        def spot(tile):
            return relative(tile, info) - info[0] * block_tiles

        return lambda t: t + GT + info[0] * block_tiles, lambda t: t + GT, spot

    def spots_outer(info):
        bead_at = 4 * GT
        far_at = bead_at + GT
        left_at = jnp.where(info[0] == 0, far_at, bead_at)
        right_at = jnp.where(info[0] == 0, bead_at, far_at)

        def own(t):
            return jnp.where(t < GT, t, t + block_tiles - 2 * GT)

        def place(x):
            return jnp.where(x < 2 * GT, x, x - (block_tiles - 4 * GT))

        def spot(tile):
            x = relative(tile, info) - info[0] * block_tiles
            right = jnp.where(x >= block_tiles, x - block_tiles + right_at, place(x))
            return jnp.where(x < 0, x + GT + left_at, right)

        return lambda t: own(t) + info[0] * block_tiles, lambda t: place(own(t)), spot

    def spots_slab(first):
        def spots(info):
            start = info[0] * block_tiles if first else 0

            def spot(tile):
                x = relative(tile, info)
                return jnp.where(x < 0, x + GT + slab_tiles, jnp.where(x >= slab_tiles, x + GT, x))

            return lambda t: t + start, lambda t: t + start, spot

        return spots

    pieces = [[] for _ in range(chunks)]
    if pair:
        (lead,) = fetch([(0, 0, 0, 0, 2, 1, 0)], [2], chunks, bead_at, pos, mom)
        other = lax.ppermute(lead, "bead", SWAP)
        mine, theirs, straight, *own_q = begin(chunks, bead_at, begin_left, strength, pos)
        theirs = lax.ppermute(theirs, "bead", SWAP)
        moves = [(0, 0, 0, 2, 1, 1, 0), (0, 1, 1, 0, 3, 1, 0)]
        blocks = fetch(moves, [4], chunks, bead_at, pos, mom)
        moves = []
        for chunk in range(1, chunks):
            moves += [(chunk - 1, 0, 0, 0, 3, 1, chunk), (chunk - 1, 3, 1, 0, 3, 1, chunk)]
        planes = [6] * (chunks - 1)
        blocks += fetch(moves, planes, chunks, bead_at, pos, mom)
        for chunk in range(chunks):
            moment = lax.ppermute(blocks[chunk], "bead", SWAP)
            pieces[chunk] = [own_q[chunk]]
            pieces[chunk] += [moment] if chunk else [other, moment]
        straight = relay(straight, theirs)
        straight = lax.ppermute(
            straight, ("space", "bead"), permutation(lambda b: -1 if b else 1, 0)
        )
        both = [mine, theirs]
        inside = [(both, lambda b: b * GT, block_tiles)]
        rim_tiles = [
            (both, lambda b: b * GT, 2 * GT),
            (both, lambda b: b * GT + block_tiles - 2 * GT, 2 * GT),
            (both, lambda b: (1 - b) * block_tiles, GT),
            ([straight], 0, GT),
        ]
    else:
        part = partial_rows(bead_at, begin_left, strength, pos)
        summed = lax.psum(part, "bead")
        logs_row = lax.broadcasted_iota(jnp.int32, summed.shape, 0) == LOGS
        summed = jnp.where(logs_row, jnp.log2(strengths)[None, :], summed)
        segments = [([summed], 0, slab_tiles), *[([x], 0, GT) for x in rims(summed)]]
        spots = spots_slab(True)
        for chunk in range(chunks):
            parts = []
            for d in range(bead_count):
                start = jnp.mod(bead - d, bead_count) * block + chunk * lanes
                piece = jnp.concatenate(
                    [lanes_of(pos, start, lanes), lanes_of(mom, start, lanes)], 0
                )
                back = [(i, (i - d) % bead_count) for i in range(bead_count)]
                parts.append(lax.ppermute(piece, "bead", back) if d else piece)
            pieces[chunk] = [jnp.concatenate(parts, 1)]

    hot = prepare(bead_at, bond_ends, angle_ends, block_tiles)
    if pair:
        ids = bead_at, space_at, neighbour_tiles
        inner = pair_forces(spots_inner, inside, block_tiles - 2 * GT, *ids, True)
        outer = pair_forces(spots_outer, rim_tiles, 2 * GT, *ids, True)
        force = [inner, outer]
    else:
        force = [pair_forces(spots, segments, block_tiles, bead_at, space_at, neighbour_tiles)]

    own_out, returned, contracted = [], [], []
    for chunk in range(chunks):
        last = pair and chunk == chunks - 1
        outs = substeps(
            chunk, chunks, bead_at, pieces[chunk], force, mass, strength, hot, motion,
            expand_l, contract_l, last, contracted[0] if contracted else None, mom,
        )
        if last:
            *outs, bead_edge, far_edge = outs
        *outs, c16 = outs
        if not pair:
            outs = [outs[0][:, d * beads : (d + 1) * beads] for d in range(bead_count)]
        own_out.append(outs[0])
        contracted.append(c16)
        back = []
        for d in range(1, bead_count):
            on = [(i, (i + d) % bead_count) for i in range(bead_count)]
            back.append(lax.ppermute(outs[d], "bead", on))
        returned.append(back)

    if not pair:
        c16 = jnp.concatenate(contracted, 1) if chunks > 1 else contracted[0]
        everyone = lax.all_gather(c16, "bead", axis=1, tiled=True)
        segments = [([everyone], 0, slab_tiles), *[([x], 0, GT) for x in rims(everyone)]]
        force = pair_forces(
            spots_slab(False), segments, slab_tiles, bead_at, space_at, neighbour_tiles
        )
        parts = [x for chunk in range(chunks) for x in [own_out[chunk]] + returned[chunk]]
        new_pos, new_mom = finish(chunks, bead_at, parts, finish_left, force)
        return new_pos.transpose(1, 0, 2), new_mom.transpose(1, 0, 2)

    beside = lax.ppermute(bead_edge, "bead", SWAP)
    across = lax.ppermute(
        far_edge, ("space", "bead"), permutation(lambda b: 1 if b else -1, 1)
    )
    chunk_tiles = lanes // TILE
    segments = [([x], 0, chunk_tiles) for x in contracted]
    inner = pair_forces(spots_inner, segments, block_tiles - 2 * GT, *ids, True)
    segments = [
        ([contracted[0]], 0, 2 * GT),
        ([contracted[-1]], chunk_tiles - 2 * GT, 2 * GT),
        ([beside], 0, GT),
        ([across], 0, GT),
    ]
    outer = pair_forces(spots_outer, segments, 2 * GT, *ids, True)
    others = [x[0] for x in returned]
    moves = [(i, 0, i) for i in range(chunks)]
    moves += [(chunks + i, 1, i) for i in range(chunks - 1)]
    result = finish_block(
        chunks, 0, moves, bead_at, own_out + others[:-1], finish_left, inner, outer, []
    )
    inner = lax.ppermute(inner, "bead", SWAP)
    outer = lax.ppermute(outer, "bead", SWAP)
    moves = [(chunks - 1, 1, chunks - 1)]
    new_pos, new_mom = finish_block(
        chunks, 1, moves, bead_at, others, finish_left, inner, outer, result
    )
    return new_pos.transpose(1, 0, 2), new_mom.transpose(1, 0, 2)


SWAP = [(0, 1), (1, 0)]


def solution(mesh):
    placed = (
        P("bead", None, "space"),
        P("bead", None, "space"),
        P("space"),
        P("space"),
        P(None, "space"),
        P(None, "space"),
        P(None, "space"),
    )

    return jax.shard_map(
        body,
        mesh=mesh,
        in_specs=placed,
        out_specs=(P("bead", None, "space"), P("bead", None, "space")),
        check_vma=False,
    )
```

```python
import functools
import math

import jax
import jax.numpy as jnp
import numpy as np
from jax import lax
from jax.experimental import pallas as pl
from jax.experimental.pallas import tpu as pltpu
from jax.sharding import PartitionSpec as P


BEADS = 32
KEPT = 4
SUBS = 3
TILE = 128
GT = 2
BPT = 128
APT = 64
ROWS = 4 * KEPT
LOGS = 3 * KEPT

time_step = 0.3
spring_freq = 80.0
bond_stiff = 0.2
bond_rest = 1.0
angle_stiff = 0.1
angle_rest = 0.5
range_sq = 4.0
HIGH = lax.Precision.HIGHEST
IN_VMEM = pl.BlockSpec(memory_space=pltpu.VMEM)
IN_SMEM = pl.BlockSpec(memory_space=pltpu.SMEM)
IN_SPACE = pltpu.MemorySpace.VMEM


def near(x):
    return pltpu.with_memory_space_constraint(x, IN_SPACE)


def far(x):
    return pltpu.with_memory_space_constraint(x, pltpu.MemorySpace.HBM)


def vmem_out(shape, dtype):
    return IN_SPACE(shape, dtype)


PARAMS = pltpu.CompilerParams(vmem_limit_bytes=20 * 1024 * 1024)
COST = pl.CostEstimate(flops=10_000_000, bytes_accessed=100_000, transcendentals=0)
F32 = jnp.float32
BF16 = jnp.bfloat16


def mode_table(number):
    within = np.arange(number)
    result = np.zeros((number, number))
    for column in range(number):
        if column == 0:
            result[:, column] = 1.0 / math.sqrt(number)
        elif 2 * column < number:
            result[:, column] = math.sqrt(2.0 / number) * np.cos(
                2 * np.pi * within * column / number
            )
        elif 2 * column == number:
            result[:, column] = (-1.0) ** within / math.sqrt(number)
        else:
            result[:, column] = math.sqrt(2.0 / number) * np.sin(
                2 * np.pi * within * column / number
            )
    return result


def contract_table(number, kept):
    larger = mode_table(number)
    smaller = mode_table(kept)
    chosen = [column if 2 * column <= kept else number - kept + column for column in range(kept)]
    return math.sqrt(kept / number) * smaller @ larger[:, chosen].T


def motion_table(number, interval):
    freqs = 2.0 * spring_freq * np.sin(np.pi * np.arange(number) / number)
    modes = mode_table(number)
    safe = np.where(freqs > 0, freqs, 1.0)
    gains = np.where(freqs > 0, np.sin(freqs * interval) / safe, interval)
    drags = freqs * np.sin(freqs * interval)
    stay = modes @ np.diag(np.cos(freqs * interval)) @ modes.T
    gain = modes @ np.diag(gains) @ modes.T
    drag = modes @ np.diag(drags) @ modes.T
    return np.block([[stay, gain], [-drag, stay]])


def np_split(table, parts):
    out, rest = [], np.asarray(table, np.float64)
    for _ in range(parts):
        piece = rest.astype(np.float32).astype(jnp.bfloat16)
        out.append(piece)
        rest = rest - piece.astype(np.float64)
    return out


def stacked_left(table, parts=3):
    pieces = np_split(table, parts)
    zero = np.zeros_like(pieces[0])
    return np.concatenate(
        [
            np.concatenate([pieces[i]] * (parts - i) + [zero] * i, axis=1)
            for i in range(parts)
        ],
        axis=0,
    )


def split(x, parts):
    out = []
    for i in range(parts):
        piece = x.astype(BF16)
        out.append(piece)
        if i < parts - 1:
            x = x - piece.astype(F32)
    return out


def mm(left, right):
    return jnp.dot(left, right, preferred_element_type=F32)


def exact(left, x, parts=3):
    out = mm(left, jnp.concatenate(split(x, parts), axis=0))
    rows = out.shape[0] // parts
    total = out[:rows]
    for i in range(1, parts):
        total = total + out[i * rows : (i + 1) * rows]
    return total


def packed_left(table):
    high, mid, low = np_split(table, 3)
    zero = np.zeros_like(high)
    return np.concatenate(
        [
            np.concatenate([high, high, high, mid], axis=1),
            np.concatenate([low, mid, zero, zero], axis=1),
        ],
        axis=0,
    )


def packed_exact(left, x):
    high, mid, low = split(x, 3)
    out = mm(left, jnp.concatenate([high, mid, low, high], axis=0))
    rows = out.shape[0] // 2
    return out[:rows] + out[rows:]


def contract_rows(beads):
    table = contract_table(BEADS, KEPT)
    tables = []
    for turn in range(0, BEADS, beads):
        order = (np.arange(BEADS) + turn) % BEADS
        tables.append(table[:, order])
    return tables


def contract_left(table):
    out = np.zeros((ROWS, 3 * table.shape[1]))
    for c in range(KEPT):
        for k in range(3):
            out[k * KEPT + c, k * table.shape[1] : (k + 1) * table.shape[1]] = table[c]
    return out


def expand_left(table):
    return BEADS / KEPT * contract_left(table).T


def pack_rows(target, x):
    lanes = x.shape[1]
    target[:, :lanes] = x[:8]
    target[:4, lanes:] = x[8:12, : lanes // 2]
    target[4:, lanes:] = x[8:12, lanes // 2 :]


def unpacked(x):
    lanes = x.shape[1] * 2 // 3
    last = jnp.concatenate([x[:4, lanes:], x[4:, lanes:]], axis=1)
    return jnp.concatenate([x[:, :lanes], last, jnp.zeros_like(last)], axis=0)


def begin_kernel(chunks, bead, left, strengths, pos, *refs):
    mine, theirs, straight = refs[:3]
    whole, table, rows, spare, sems = refs[-5:]
    blocks = list(refs[3:-5]) + [spare.at[i] for i in range(chunks)]
    lanes = blocks[0].shape[2]
    slab = whole.shape[1]
    starts, copies = [], []
    for i in range(2 * chunks):
        owner = bead[0] if i < chunks else 1 - bead[0]
        starts.append(pl.multiple_of((owner * chunks + i % chunks) * lanes, TILE))
    small = [
        pltpu.make_async_copy(left.at[bead[0]], table, sems.at[2 * chunks]),
        pltpu.make_async_copy(strengths, rows, sems.at[2 * chunks + 1]),
    ]
    for copy in small:
        copy.start()
    for i, block in enumerate(blocks):
        copy = pltpu.make_async_copy(
            pos.at[:, :, pl.ds(starts[i], lanes)], block, sems.at[i]
        )
        copy.start()
        copies.append(copy)
    for copy in small:
        copy.wait()
    logs = math.log2(math.e) * jnp.log(rows[...])
    for t in range(slab // TILE):
        whole[LOGS : LOGS + 1, t * TILE : (t + 1) * TILE] = logs[t : t + 1]
    for i, block in enumerate(blocks):
        copies[i].wait()
        x = jnp.concatenate([block[c] for c in range(3)], axis=0)
        where = pl.ds(starts[i], lanes)
        row = lax.broadcasted_iota(jnp.int32, (ROWS, lanes), 0)
        whole[:, where] = jnp.where(row == LOGS, whole[:, where], exact(table[...], x))

    block, rim = slab // 2, GT * TILE
    size = block + rim

    def sides(which):
        first, other = (0, block - rim) if which == 0 else (block - rim, 0)
        mine[...] = whole[:, first : first + size]
        head, tail = whole[:, :rim], whole[:, slab - rim :]
        straight[...] = tail if which == 0 else head
        relay = head if which == 0 else tail
        pack_rows(theirs, jnp.concatenate([whole[:, other : other + size], relay], axis=1))

    for which in range(2):
        pl.when(bead[0] == which)(functools.partial(sides, which))


def fetch_kernel(moves, chunks, bead, pos, mom, *refs):
    *blocks, sems = refs
    lanes = blocks[0].shape[2]
    copies = []
    for i, (block, plane, source, comp, comps, owner, chunk) in enumerate(moves):
        side = bead[0] if owner == 0 else 1 - bead[0]
        start = pl.multiple_of((side * chunks + chunk) * lanes, TILE)
        copy = pltpu.make_async_copy(
            (pos, mom)[source].at[pl.ds(comp, comps), :, pl.ds(start, lanes)],
            blocks[block].at[pl.ds(plane, comps)],
            sems.at[i],
        )
        copy.start()
        copies.append(copy)
    for copy in copies:
        copy.wait()


def fetch(moves, planes, chunks, bead, pos, mom):
    beads, slab = mom.shape[1:]
    lanes = slab // (2 * chunks)
    return pl.pallas_call(
        functools.partial(fetch_kernel, moves, chunks),
        in_specs=[IN_SMEM] + [pl.BlockSpec(memory_space=pl.ANY)] * 2,
        out_specs=[IN_VMEM] * len(planes),
        out_shape=[vmem_out((n, beads, lanes), F32) for n in planes],
        scratch_shapes=[pltpu.SemaphoreType.DMA((len(moves),))],
        compiler_params=PARAMS,
        cost_estimate=COST,
        name="fetch",
    )(bead, far(pos), far(mom))


def begin(chunks, bead, left, strengths, pos):
    beads, slab = pos.shape[1:]
    block, rim = slab // 2, GT * TILE
    lanes = block // chunks
    shapes = [(ROWS, block + rim), (8, 3 * (block + 2 * rim) // 2), (ROWS, rim)]
    shapes += [(3, beads, lanes)] * chunks
    return pl.pallas_call(
        functools.partial(begin_kernel, chunks),
        in_specs=[IN_SMEM] + [pl.BlockSpec(memory_space=pl.ANY)] * 3,
        out_specs=[IN_VMEM] * len(shapes),
        out_shape=[vmem_out(s, F32) for s in shapes],
        scratch_shapes=[
            pltpu.VMEM((ROWS, slab), F32),
            pltpu.VMEM(left.shape[1:], left.dtype),
            pltpu.VMEM(strengths.shape, F32),
            pltpu.VMEM((chunks, 3, beads, lanes), F32),
            pltpu.SemaphoreType.DMA((2 * chunks + 2,)),
        ],
        compiler_params=PARAMS,
        cost_estimate=COST,
        name="begin",
    )(bead, far(left), far(strengths), far(pos))


def relay_kernel(own, received, out):
    rim = GT * TILE
    size = received.shape[1] * 2 // 3
    more = jnp.concatenate([received[:, size - rim : size], received[4:, -rim:]], axis=0)
    out[...] = own[...] + jnp.concatenate([more, jnp.zeros_like(more[:4])], axis=0)


def relay(own, received):
    return pl.pallas_call(
        relay_kernel,
        in_specs=[IN_VMEM] * 2,
        out_specs=IN_VMEM,
        out_shape=vmem_out(own.shape, F32),
        compiler_params=PARAMS,
        cost_estimate=COST,
        name="relay",
    )(near(own), near(received))


def partial_kernel(bead, left, strengths, pos, out):
    comps, _, lanes = pos.shape
    logs = math.log2(math.e) * jnp.log(strengths[...])
    logs = jnp.concatenate([logs[t : t + 1] for t in range(lanes // TILE)], axis=1)
    row = lax.broadcasted_iota(jnp.int32, (ROWS, lanes), 0)
    x = jnp.concatenate([pos[c] for c in range(comps)], axis=0)
    out[...] = jnp.where(row == LOGS, logs, exact(left[bead[0]], x))


def partial_rows(bead, left, strengths, pos):
    beads, slab = pos.shape[1:]
    lanes = math.gcd(slab, 1024)
    return pl.pallas_call(
        partial_kernel,
        grid=(slab // lanes,),
        in_specs=[
            IN_SMEM,
            IN_VMEM,
            pl.BlockSpec((lanes // TILE, TILE), lambda i: (i, 0)),
            pl.BlockSpec((3, beads, lanes), lambda i: (0, 0, i)),
        ],
        out_specs=pl.BlockSpec((ROWS, lanes), lambda i: (0, i)),
        out_shape=jax.ShapeDtypeStruct((ROWS, slab), F32),
        name="partial_rows",
    )(bead, left, strengths, pos)


def prepare_kernel(group, bead, bonds, angles, hot):
    lane = lax.broadcasted_iota(jnp.int32, (1, TILE), 1)
    atom = lax.broadcasted_iota(jnp.int32, (TILE, 2 * TILE), 0)
    low = lane < APT

    def merge(first, second, odd):
        a = pltpu.roll(first, APT, 1) if odd else first
        b = second if odd else pltpu.roll(second, APT, 1)
        return jnp.where(low, a, b)

    def tiles(i, carry):
        at = (bead[0] * (hot.shape[0] // group) + i) * group
        bond_rows = bonds[:, pl.ds(pl.multiple_of(at * BPT, BPT), group * BPT)]
        angle_rows = angles[:, pl.ds(pl.multiple_of(at * APT, TILE), group * APT)]
        for t in range(group):
            one = bond_rows[0:1, t * TILE : (t + 1) * TILE]
            other = bond_rows[1:2, t * TILE : (t + 1) * TILE]
            odd = t % 2
            window = slice((t // 2) * TILE, (t // 2 + 1) * TILE)
            first, middle, last = [angle_rows[e : e + 1, window] for e in range(3)]
            opposite = merge(last, first, odd)
            centre = merge(middle, middle, odd)
            gains = jnp.concatenate([other, centre], axis=1)
            losses = jnp.concatenate([one, opposite], axis=1)
            table = (atom == gains).astype(F32) - (atom == losses).astype(F32)
            hot[i * group + t] = table.astype(BF16)
        return carry

    lax.fori_loop(0, hot.shape[0] // group, tiles, 0)


def prepare(bead, bond_ends, angle_ends, block_tiles):
    return pl.pallas_call(
        functools.partial(prepare_kernel, math.gcd(block_tiles, 4)),
        in_specs=[IN_SMEM, IN_VMEM, IN_VMEM],
        out_specs=IN_VMEM,
        out_shape=vmem_out((block_tiles, TILE, 2 * TILE), BF16),
        compiler_params=PARAMS,
        cost_estimate=COST,
        name="prepare",
    )(bead, bond_ends, angle_ends)


def pair_kernel(spots, seg_sizes, own_count, packed, bead, space, nbr, *refs):
    total = sum(n for *_, n in seg_sizes)
    count = sum(n for n, *_ in seg_sizes)
    seg_refs = refs[:count]
    target, feat_i, feat_m, feat_p, base, *weights, held = refs[count:]
    out = held if packed else target
    column, own_spot, spot = spots((bead[0], space[0]))
    row = lax.broadcasted_iota(jnp.int32, (ROWS, TILE), 0)
    slot = row // KEPT
    scale = math.sqrt(2.0 * math.log2(math.e) / range_sq)
    same = (
        lax.broadcasted_iota(jnp.int32, (ROWS, ROWS), 0) % KEPT
        == lax.broadcasted_iota(jnp.int32, (ROWS, ROWS), 1) % KEPT
    ).astype(F32)

    def features(tile, c16):
        base[tile] = c16
        logs = c16[LOGS : LOGS + 1]
        place = jnp.where(slot == 3, 0.0, c16)
        scaled = place * scale
        high, low = [piece.astype(F32) for piece in split(scaled, 2)]
        square = jnp.dot(same, scaled * scaled, precision=HIGH, preferred_element_type=F32)
        half = -0.5 * square

        def three(x):
            a, b, c = [piece.astype(F32) for piece in split(x, 3)]
            return jnp.where(slot == 0, a, jnp.where(slot == 1, b, jnp.where(slot == 2, c, 0.0)))

        ones = jnp.where(slot == 3, 0.0, 1.0)
        mine = jnp.concatenate([high, high, low, low, three(half), ones], axis=0)
        theirs = jnp.concatenate(
            [high, low, high, low, ones, three(half + logs), ones, ones], axis=0
        )
        feat_i[tile] = mine.astype(BF16)
        feat_m[tile] = jnp.transpose(theirs, (1, 0)).astype(BF16)
        one = jnp.ones((ROWS, TILE), F32)
        p_high, p_low = [piece.astype(F32) for piece in split(place, 2)]
        feat_p[tile] = jnp.concatenate([one, p_high, p_low], axis=0).astype(BF16)

    def piece(ref, begins, i):
        moving = callable(begins)
        at = (begins(bead[0]) if moving else begins) + i

        def lanes(tile):
            if moving:
                return pl.ds(pl.multiple_of(tile * TILE, TILE), TILE)
            return slice(tile * TILE, (tile + 1) * TILE)

        if ref.shape[0] == ROWS:
            return ref[:, lanes(at)]
        tiles = ref.shape[1] * 2 // 3 // TILE
        half = tiles // 2
        upper = at >= half
        last = ref[:, lanes(tiles + jnp.where(upper, at - half, at))]
        last = jnp.where(upper, last[4:], last[:4])
        return jnp.concatenate([ref[:, lanes(at)], last, jnp.zeros_like(last)], axis=0)

    tile = 0
    at = 0
    for number, begins, tiles in seg_sizes:
        group = seg_refs[at : at + number]
        at += number
        for i in range(tiles):
            c16 = piece(group[0], begins, i)
            for other in group[1:]:
                c16 = c16 + piece(other, begins, i)
            features(tile, c16)
            tile += 1
    assert tile == total

    groups = 6
    wide_row = lax.broadcasted_iota(jnp.int32, (groups * ROWS, TILE), 0)
    pick = [(wide_row % KEPT == c).astype(BF16) for c in range(KEPT)]
    owner = row % KEPT

    def close(t, u):
        return spot(nbr[u, column(t)])

    def weigh(t, weights):
        features_i = feat_i[own_spot(t)]
        right = jnp.concatenate([features_i * pick[c] for c in range(KEPT)], axis=1)
        right = jnp.concatenate([right, jnp.zeros((2 * ROWS, KEPT * TILE), BF16)], axis=0)
        left = jnp.concatenate([feat_m[close(t, u)] for u in range(3)], axis=0)
        power = mm(left, right)
        for u in range(3):
            high, low = split(jnp.exp2(power[u * TILE : (u + 1) * TILE]), 2)
            weights[2 * u * TILE : (2 * u + 1) * TILE] = high
            weights[(2 * u + 1) * TILE : (2 * u + 2) * TILE] = low

    def pull(t, weights):
        left = []
        for u in range(3):
            piece = feat_p[close(t, u)]
            left += [piece, piece]
        total_p = mm(jnp.concatenate(left, axis=1), weights[...])
        sums = total_p[:ROWS]
        pulls = total_p[ROWS : 2 * ROWS] + total_p[2 * ROWS :]
        c16 = base[own_spot(t)]
        factor = (2.0 / range_sq) * jnp.exp2(c16[LOGS : LOGS + 1])
        result = jnp.zeros((ROWS, TILE), F32)
        for c in range(KEPT):
            lanes = slice(c * TILE, (c + 1) * TILE)
            force = factor * (c16 * sums[:, lanes] - pulls[:, lanes])
            result = jnp.where((owner == c) & (slot < 3), force, result)
        lane = t * TILE if isinstance(t, int) else pl.multiple_of(t * TILE, TILE)
        out[:, pl.ds(lane, TILE)] = result

    unroll = math.gcd(own_count, 4)
    weigh(0, weights[0])

    def some_tiles(t, last):
        for j in range(unroll):
            if not (last and j == unroll - 1):
                weigh(t + j + 1, weights[(j + 1) % 2])
            pull(t + j, weights[j % 2])

    def loop(i, carry):
        some_tiles(unroll * i, False)
        return carry

    lax.fori_loop(0, own_count // unroll - 1, loop, 0)
    some_tiles(own_count - unroll, True)
    if packed:
        pack_rows(target, held[...])


def pair_forces(spots, segments, own_count, bead, space, neighbour_tiles, packed=False):
    sizes = tuple((len(group), start, tiles) for group, start, tiles in segments)
    total = sum(n for *_, n in sizes)
    assert own_count % 2 == 0
    flat = [array for group, *_ in segments for array in group]
    return pl.pallas_call(
        functools.partial(pair_kernel, spots, sizes, own_count, packed),
        in_specs=[IN_SMEM] * 3 + [IN_VMEM] * len(flat),
        out_specs=IN_VMEM,
        out_shape=vmem_out(
            (8, 3 * own_count * TILE // 2) if packed else (ROWS, own_count * TILE), F32
        ),
        scratch_shapes=[
            pltpu.VMEM((total, 6 * ROWS, TILE), BF16),
            pltpu.VMEM((total, TILE, 8 * ROWS), BF16),
            pltpu.VMEM((total, 3 * ROWS, TILE), BF16),
            pltpu.VMEM((total, ROWS, TILE), F32),
            pltpu.VMEM((6 * TILE, KEPT * TILE), BF16),
            pltpu.VMEM((6 * TILE, KEPT * TILE), BF16),
            pltpu.VMEM((ROWS, own_count * TILE), F32),
        ],
        compiler_params=PARAMS,
        cost_estimate=COST,
        name="pair_forces",
    )(bead, space, far(neighbour_tiles), *[near(x) for x in flat])


def whole_force(inner, outer):
    rim = GT * TILE
    inner, outer = unpacked(inner[...]), unpacked(outer[...])
    return jnp.concatenate([outer[:, :rim], inner, outer[:, rim:]], axis=1)


def step_kernel(parts, count, forces, chunk, chunks, group, edge, bead, *refs):
    pieces = refs[:count]
    at = count
    force = refs[at] if forces == 1 else whole_force(*refs[at : at + 2])
    at += forces
    mass_rows, strength_rows, hot, motion, expand, contract = refs[at : at + 6]
    before = refs[at + 6] if edge and chunk else None
    outs = refs[len(refs) - parts - 1 - 2 * edge :]
    c_out = outs[parts]
    interval = time_step / SUBS
    width = group * TILE
    first = chunk * group
    motion_l = motion[...]

    def per_atom(rows):
        at = (bead[0] * chunks + chunk) * group
        return jnp.concatenate([rows[pl.ds(at + t, 1), :] for t in range(group)], axis=1)

    masses = per_atom(mass_rows)
    inverse = 1.0 / masses

    planes = [(piece, plane) for piece in pieces for plane in range(piece.shape[0])]

    def gathered(kind, c):
        found = [planes[6 * part + 3 * kind + c] for part in range(parts)]
        found = [piece[plane] for piece, plane in found]
        return found[0] if parts == 1 else jnp.concatenate(found, axis=0)

    q = [gathered(0, c) for c in range(3)]
    p = [gathered(1, c) for c in range(3)]
    kick = exact(expand[bead[0]], force[:, first * TILE : first * TILE + width])
    v = [
        (p[c] + 0.5 * time_step * kick[c * BEADS : (c + 1) * BEADS]) * inverse for c in range(3)
    ]

    def bonded(q):
        forces = []
        for t in range(group):
            lanes = slice(t * TILE, (t + 1) * TILE)
            rows = jnp.concatenate([q[c][:, lanes] for c in range(3)], axis=0)
            seen = mm(jnp.concatenate(split(rows, 2), axis=0), hot[first + t])
            seen = seen[: 3 * BEADS] + seen[3 * BEADS :]
            stretch, arms = seen[:, :TILE], seen[:, TILE:]
            s = [stretch[c * BEADS : (c + 1) * BEADS] for c in range(3)]
            a = [arms[c * BEADS : (c + 1) * BEADS] for c in range(3)]
            length = s[0] * s[0] + s[1] * s[1] + s[2] * s[2]
            g = bond_stiff * (bond_rest - length)
            turned = [pltpu.roll(x, APT, 1) for x in a]
            inner = a[0] * turned[0] + a[1] * turned[1] + a[2] * turned[2]
            h = angle_stiff * (angle_rest - inner)
            bonds = jnp.concatenate([g * x for x in s], axis=0)
            angles = jnp.concatenate([h * x for x in turned], axis=0)
            both = jnp.concatenate([bonds, angles], axis=1)
            out = lax.dot_general(
                jnp.concatenate(split(both, 2), axis=0),
                hot[first + t],
                (((1,), (1,)), ((), ())),
                preferred_element_type=F32,
            )
            forces.append(out[: 3 * BEADS] + out[3 * BEADS :])
        return [
            jnp.concatenate([f[c * BEADS : (c + 1) * BEADS] for f in forces], axis=1)
            for c in range(3)
        ]

    for sub in range(SUBS):
        pushed = bonded(q)
        factor = (0.5 if sub == 0 else 1.0) * interval * inverse
        v = [v[c] + factor * pushed[c] for c in range(3)]
        for c in range(3):
            moved = packed_exact(motion_l, jnp.concatenate([q[c], v[c]], axis=0))
            q[c], v[c] = moved[:BEADS], moved[BEADS:]
    pushed = bonded(q)
    p = [masses * v[c] + (0.5 * interval) * pushed[c] for c in range(3)]
    beads = BEADS // parts
    for i in range(parts):
        for c in range(3):
            outs[i][c] = q[c][i * beads : (i + 1) * beads]
            outs[i][3 + c] = p[c][i * beads : (i + 1) * beads]
    rows = jnp.concatenate(q, axis=0)
    c16 = exact(contract[bead[0]], rows, 2)
    row = lax.broadcasted_iota(jnp.int32, (ROWS, width), 0)
    logs = math.log2(math.e) * jnp.log(per_atom(strength_rows))
    c16 = jnp.where(row == LOGS, logs, c16)
    c_out[...] = c16
    if edge:
        rim = GT * TILE
        head = c16[:, :rim] if before is None else before[:, :rim]
        tail = c16[:, width - rim :]
        outs[-2][...] = jnp.where(bead[0] == 0, tail, head)
        outs[-1][...] = jnp.where(bead[0] == 0, head, tail)


def substeps(chunk, chunks, bead, pieces, force, mass, strength, hot, motion, expand, contract, edge, before):
    beads, lanes = pieces[0].shape[1:]
    parts = BEADS // beads
    extra = [before] if edge and chunk else []
    shapes = [(6, beads, lanes)] * parts + [(ROWS, lanes)]
    if edge:
        shapes += [(ROWS, GT * TILE)] * 2
    return pl.pallas_call(
        functools.partial(
            step_kernel, parts, len(pieces), len(force), chunk, chunks, lanes // TILE, int(edge)
        ),
        in_specs=[IN_SMEM] + [IN_VMEM] * (len(pieces) + len(force) + 6 + len(extra)),
        out_specs=[IN_VMEM] * len(shapes),
        out_shape=[vmem_out(s, F32) for s in shapes],
        compiler_params=PARAMS,
        cost_estimate=COST,
        name="substeps",
    )(
        bead,
        *[near(x) for x in pieces + force],
        mass,
        strength,
        near(hot),
        motion,
        expand,
        contract,
        *[near(x) for x in extra],
    )


def finish_kernel(chunks, bead, expand, force, *refs):
    pos, mom = refs[-2:]
    parts = refs[:-2]
    bead_count = len(parts) // chunks
    lanes = parts[0].shape[2]
    comp = pl.program_id(0)
    table = expand[bead[0], comp]
    for i, part in enumerate(parts):
        chunk, distance = divmod(i, bead_count)
        block = lax.rem(bead[0] + bead_count - distance, bead_count)
        start = pl.multiple_of(block * (chunks * lanes) + chunk * lanes, TILE)
        where = pl.ds(start, lanes)
        pos[0, :, where] = part[comp]
        mom[0, :, where] = part[3 + comp] + 0.5 * time_step * exact(table, force[:, where])


def finish(chunks, bead, parts, expand, force):
    slab = force.shape[1]
    beads = parts[0].shape[1]
    return pl.pallas_call(
        functools.partial(finish_kernel, chunks),
        grid=(3,),
        in_specs=[IN_SMEM] + [IN_VMEM] * (2 + len(parts)),
        out_specs=[pl.BlockSpec((1, beads, slab), lambda i: (i, 0, 0))] * 2,
        out_shape=[jax.ShapeDtypeStruct((3, beads, slab), F32)] * 2,
        compiler_params=PARAMS,
        cost_estimate=COST,
        name="finish",
    )(bead, expand, near(force), *[near(x) for x in parts])


def finish_block_kernel(chunks, owner, moves, count, bead, expand, inner, outer, *refs):
    parts = refs[:count]
    pos, mom, held, sems = refs[-4:]
    lanes = parts[0].shape[2]
    blocks = [bead[0], 1 - bead[0]]

    def where(owner, chunk):
        return pl.ds(pl.multiple_of((blocks[owner] * chunks + chunk) * lanes, TILE), lanes)

    copies = []

    def copy(source, target):
        copies.append(pltpu.make_async_copy(source, target, sems.at[len(copies)]))
        copies[-1].start()

    for part, move_owner, chunk in moves:
        copy(parts[part].at[pl.ds(0, 3)], pos.at[:, :, where(move_owner, chunk)])
    force = whole_force(inner, outer)
    for chunk in range(chunks):
        lane = slice(chunk * lanes, (chunk + 1) * lanes)
        for c in range(3):
            kick = 0.5 * time_step * exact(expand[bead[0], c], force[:, lane])
            held[c, :, lane] = parts[chunk][3 + c] + kick
        copy(held.at[:, :, pl.ds(chunk * lanes, lanes)], mom.at[:, :, where(owner, chunk)])
    for waiting in copies:
        waiting.wait()


def finish_block(chunks, owner, moves, bead, parts, expand, inner, outer, before):
    beads, lanes = parts[0].shape[1:]
    block = lanes * chunks
    anywhere = pl.BlockSpec(memory_space=pl.ANY)
    at = 4 + len(parts)
    return pl.pallas_call(
        functools.partial(finish_block_kernel, chunks, owner, moves, len(parts)),
        in_specs=[IN_SMEM] + [IN_VMEM] * (3 + len(parts)) + [anywhere] * len(before),
        out_specs=[anywhere] * 2,
        out_shape=[pltpu.MemorySpace.HBM((3, beads, 2 * block), F32)] * 2,
        scratch_shapes=[
            pltpu.VMEM((3, beads, block), F32),
            pltpu.SemaphoreType.DMA((len(moves) + chunks,)),
        ],
        input_output_aliases={at + i: i for i in range(len(before))},
        compiler_params=PARAMS,
        cost_estimate=COST,
        name="finish_block",
    )(
        bead,
        expand,
        near(inner),
        near(outer),
        *[near(x) for x in parts],
        *[far(x) for x in before],
    )


def body(positions, momenta, masses, strengths, bond_ends, angle_ends, neighbour_tiles):
    beads, _, slab = positions.shape
    bead_count = lax.axis_size("bead")
    bead = lax.axis_index("bead")
    space_count = lax.axis_size("space")
    space = lax.axis_index("space")
    block = slab // bead_count
    slab_tiles = slab // TILE
    block_tiles = block // TILE
    all_tiles = slab_tiles * space_count
    rim = GT * TILE
    chunks = 2 if block_tiles % 4 == 0 else 1
    lanes = block // chunks
    interval = time_step / SUBS
    pair = bead_count == 2

    pos = positions.transpose(1, 0, 2)
    mom = momenta.transpose(1, 0, 2)
    bead_at = jnp.reshape(bead, (1,)).astype(jnp.int32)
    space_at = jnp.reshape(space, (1,)).astype(jnp.int32)
    mass = masses.reshape(slab_tiles, TILE)
    strength = strengths.reshape(slab_tiles, TILE)
    turned = contract_rows(beads)
    table = contract_table(BEADS, KEPT)
    own_tables = [table[:, i * beads : (i + 1) * beads] for i in range(bead_count)]

    def stack(tables):
        return jnp.asarray(np.stack(tables))

    begin_left = stack([stacked_left(contract_left(t)) for t in own_tables])
    finish_left = stack(
        [
            np.stack(
                [stacked_left(expand_left(t)[c * beads : (c + 1) * beads]) for c in range(3)]
            )
            for t in own_tables
        ]
    )
    contract_l = stack([stacked_left(contract_left(t), 2) for t in turned])
    expand_l = stack([stacked_left(expand_left(t)) for t in turned])
    motion = jnp.asarray(packed_left(motion_table(BEADS, interval)))

    def lanes_of(x, start, size):
        return lax.dynamic_slice_in_dim(x, start, size, x.ndim - 1)

    def permutation(step, flip):
        return [
            (s * 2 + b, ((s + step(b)) % space_count) * 2 + (b ^ flip))
            for s in range(space_count)
            for b in range(2)
        ]

    def rims(x):
        up = [(i, (i + 1) % space_count) for i in range(space_count)]
        down = [((i + 1) % space_count, i) for i in range(space_count)]
        return (
            lax.ppermute(x[:, slab - rim :], "space", up),
            lax.ppermute(x[:, :rim], "space", down),
        )

    def relative(tile, info):
        x = tile - info[1] * slab_tiles
        x = jnp.where(x >= all_tiles - GT, x - all_tiles, x)
        return jnp.where(x < -GT, x + all_tiles, x)

    def spots_inner(info):
        def spot(tile):
            return relative(tile, info) - info[0] * block_tiles

        return lambda t: t + GT + info[0] * block_tiles, lambda t: t + GT, spot

    def spots_outer(info):
        bead_at = 4 * GT
        far_at = bead_at + GT
        left_at = jnp.where(info[0] == 0, far_at, bead_at)
        right_at = jnp.where(info[0] == 0, bead_at, far_at)

        def own(t):
            return jnp.where(t < GT, t, t + block_tiles - 2 * GT)

        def place(x):
            return jnp.where(x < 2 * GT, x, x - (block_tiles - 4 * GT))

        def spot(tile):
            x = relative(tile, info) - info[0] * block_tiles
            right = jnp.where(x >= block_tiles, x - block_tiles + right_at, place(x))
            return jnp.where(x < 0, x + GT + left_at, right)

        return lambda t: own(t) + info[0] * block_tiles, lambda t: place(own(t)), spot

    def spots_slab(first):
        def spots(info):
            start = info[0] * block_tiles if first else 0

            def spot(tile):
                x = relative(tile, info)
                return jnp.where(x < 0, x + GT + slab_tiles, jnp.where(x >= slab_tiles, x + GT, x))

            return lambda t: t + start, lambda t: t + start, spot

        return spots

    pieces = [[] for _ in range(chunks)]
    if pair:
        mine, theirs, straight, *own_q = begin(chunks, bead_at, begin_left, strength, pos)
        theirs = lax.ppermute(theirs, "bead", SWAP)
        moves = [(0, 0, 0, 0, 3, 1, 0), (0, 3, 1, 0, 3, 1, 0)]
        blocks = fetch(moves, [6], chunks, bead_at, pos, mom)
        moves = []
        for chunk in range(1, chunks):
            moves += [(chunk - 1, 0, 0, 0, 3, 1, chunk), (chunk - 1, 3, 1, 0, 3, 1, chunk)]
        moves += [(chunks - 1 + chunk, 0, 1, 0, 3, 0, chunk) for chunk in range(chunks)]
        planes = [6] * (chunks - 1) + [3] * chunks
        blocks += fetch(moves, planes, chunks, bead_at, pos, mom)
        for chunk in range(chunks):
            moment = lax.ppermute(blocks[chunk], "bead", SWAP)
            pieces[chunk] = [own_q[chunk], blocks[chunks + chunk], moment]
        straight = relay(straight, theirs)
        straight = lax.ppermute(
            straight, ("space", "bead"), permutation(lambda b: -1 if b else 1, 0)
        )
        both = [mine, theirs]
        inside = [(both, lambda b: b * GT, block_tiles)]
        rim_tiles = [
            (both, lambda b: b * GT, 2 * GT),
            (both, lambda b: b * GT + block_tiles - 2 * GT, 2 * GT),
            (both, lambda b: (1 - b) * block_tiles, GT),
            ([straight], 0, GT),
        ]
    else:
        part = partial_rows(bead_at, begin_left, strength, pos)
        summed = lax.psum(part, "bead")
        logs_row = lax.broadcasted_iota(jnp.int32, summed.shape, 0) == LOGS
        summed = jnp.where(logs_row, jnp.log2(strengths)[None, :], summed)
        segments = [([summed], 0, slab_tiles), *[([x], 0, GT) for x in rims(summed)]]
        spots = spots_slab(True)
        for chunk in range(chunks):
            parts = []
            for d in range(bead_count):
                start = jnp.mod(bead - d, bead_count) * block + chunk * lanes
                piece = jnp.concatenate(
                    [lanes_of(pos, start, lanes), lanes_of(mom, start, lanes)], 0
                )
                back = [(i, (i - d) % bead_count) for i in range(bead_count)]
                parts.append(lax.ppermute(piece, "bead", back) if d else piece)
            pieces[chunk] = [jnp.concatenate(parts, 1)]

    hot = prepare(bead_at, bond_ends, angle_ends, block_tiles)
    if pair:
        ids = bead_at, space_at, neighbour_tiles
        inner = pair_forces(spots_inner, inside, block_tiles - 2 * GT, *ids, True)
        outer = pair_forces(spots_outer, rim_tiles, 2 * GT, *ids, True)
        force = [inner, outer]
    else:
        force = [pair_forces(spots, segments, block_tiles, bead_at, space_at, neighbour_tiles)]

    own_out, returned, contracted = [], [], []
    for chunk in range(chunks):
        last = pair and chunk == chunks - 1
        outs = substeps(
            chunk, chunks, bead_at, pieces[chunk], force, mass, strength, hot, motion,
            expand_l, contract_l, last, contracted[0] if contracted else None,
        )
        if last:
            *outs, bead_edge, far_edge = outs
        *outs, c16 = outs
        if not pair:
            outs = [outs[0][:, d * beads : (d + 1) * beads] for d in range(bead_count)]
        own_out.append(outs[0])
        contracted.append(c16)
        back = []
        for d in range(1, bead_count):
            on = [(i, (i + d) % bead_count) for i in range(bead_count)]
            back.append(lax.ppermute(outs[d], "bead", on))
        returned.append(back)

    if not pair:
        c16 = jnp.concatenate(contracted, 1) if chunks > 1 else contracted[0]
        everyone = lax.all_gather(c16, "bead", axis=1, tiled=True)
        segments = [([everyone], 0, slab_tiles), *[([x], 0, GT) for x in rims(everyone)]]
        force = pair_forces(
            spots_slab(False), segments, slab_tiles, bead_at, space_at, neighbour_tiles
        )
        parts = [x for chunk in range(chunks) for x in [own_out[chunk]] + returned[chunk]]
        new_pos, new_mom = finish(chunks, bead_at, parts, finish_left, force)
        return new_pos.transpose(1, 0, 2), new_mom.transpose(1, 0, 2)

    beside = lax.ppermute(bead_edge, "bead", SWAP)
    across = lax.ppermute(
        far_edge, ("space", "bead"), permutation(lambda b: 1 if b else -1, 1)
    )
    chunk_tiles = lanes // TILE
    segments = [([x], 0, chunk_tiles) for x in contracted]
    inner = pair_forces(spots_inner, segments, block_tiles - 2 * GT, *ids, True)
    segments = [
        ([contracted[0]], 0, 2 * GT),
        ([contracted[-1]], chunk_tiles - 2 * GT, 2 * GT),
        ([beside], 0, GT),
        ([across], 0, GT),
    ]
    outer = pair_forces(spots_outer, segments, 2 * GT, *ids, True)
    others = [x[0] for x in returned]
    moves = [(i, 0, i) for i in range(chunks)]
    moves += [(chunks + i, 1, i) for i in range(chunks - 1)]
    result = finish_block(
        chunks, 0, moves, bead_at, own_out + others[:-1], finish_left, inner, outer, []
    )
    inner = lax.ppermute(inner, "bead", SWAP)
    outer = lax.ppermute(outer, "bead", SWAP)
    moves = [(chunks - 1, 1, chunks - 1)]
    new_pos, new_mom = finish_block(
        chunks, 1, moves, bead_at, others, finish_left, inner, outer, result
    )
    return new_pos.transpose(1, 0, 2), new_mom.transpose(1, 0, 2)


SWAP = [(0, 1), (1, 0)]


def solution(mesh):
    placed = (
        P("bead", None, "space"),
        P("bead", None, "space"),
        P("space"),
        P("space"),
        P(None, "space"),
        P(None, "space"),
        P(None, "space"),
    )

    return jax.shard_map(
        body,
        mesh=mesh,
        in_specs=placed,
        out_specs=(P("bead", None, "space"), P("bead", None, "space")),
        check_vma=False,
    )
```
